32 devices in a mesh: groups: 2 (over x), right: 4 (over y, core), left: 4 (over z).
Axes of the slice: x: 2, y: 2, z: 4, core: 2. Of those that a mesh axis runs over, the one named last changes fastest.
Arguments:
- left_act: bfloat16 [4096, 8192], P(('groups', 'right'), 'left'), parts along dimension 0, may hold values from -15 to 15
- right_act: bfloat16 [4096, 4096], P(('groups', 'left'), 'right'), parts along dimension 0, may hold values from -15 to 15
- counts: int32 [512, 128], P(('groups', 'left'), 'right'), parts along dimension 0, may hold values from 512 to 2048
- w_out: bfloat16 [1024, 128], replicated, may hold values from -0.1875 to 0.1875
Outputs:
- pair_update: float32 [512, 128, 128], P(('groups', 'left'), 'right'), parts along dimension 0
The draws below stay inside these ranges and needn't reach their ends.
There are 2 independent parts, one for each index of `groups`. The reference program is written for one: setup_inputs(seed, part) draws one part's arguments, and reference() takes and returns one part's arrays. A program takes and returns all parts, laid end to end along the dimension named above; an argument that names none is the same for every part. Nothing has to cross between parts.
All inputs are finite; a program needn't handle non-finite values.
Results may differ from the reference program's by a relative error of at most 0.0029.
Values may be sent and summed in bfloat16 or wider, within the bound.
A program may use at most 128 MiB of HBM per device.

```python
import jax
import jax.numpy as jnp
from jax import lax

CH = 32
PAIR = 128
SEQS = 2048
LEFT = 256
RIGHT = 128


def place_ends(array, key, smallest, top_value):
    longest = array.shape.index(max(array.shape))
    spots = []
    for shift in (0, 1):
        where = [jax.random.randint(jax.random.fold_in(key, axis), (), 0, length) for axis, length in enumerate(array.shape)]
        where[longest] = (where[longest] + shift) % array.shape[longest]
        spots.append(tuple(where))
    return array.at[spots[0]].set(smallest).at[spots[1]].set(top_value)


def shard_levels(key, dims, pieces, least, largest):
    level, own = 1.0, jax.random.fold_in(key, 6)
    for position, shards_of in pieces:
        heights = jnp.exp(jax.random.uniform(jax.random.fold_in(own, position), (shards_of,), jnp.float32, least / len(pieces), largest / len(pieces)))
        level = level * jnp.repeat(heights, dims[position] // shards_of).reshape([-1 if axis == position else 1 for axis in range(len(dims))])
    return level


def bell_draw(rng, dims, spread, most, split=(), kind=jnp.bfloat16):
    values = jax.random.normal(rng, dims, jnp.float32) * spread
    if len(split) > 0:
        values = shard_levels(rng, dims, split, -0.22, 0.18) * values
    return jnp.clip(values, min=-most, max=most).astype(kind)


def setup_inputs(seed: int = 0, part: int = 0) -> dict:
    splits = jax.random.split(jax.random.key(seed), 5)
    own_keys = jax.random.split(jax.random.fold_in(splits[4], part), 5)
    left_act = bell_draw(own_keys[0], (SEQS, LEFT * CH), 3.0, 15.0, ((0, 4), (1, 4)))
    right_act = bell_draw(own_keys[1], (SEQS, RIGHT * CH), 3.0, 15.0, ((0, 4), (1, 4)))
    counts = place_ends(jax.random.randint(own_keys[2], (LEFT, RIGHT), SEQS // 4, SEQS + 1), jax.random.fold_in(own_keys[2], 1), SEQS // 4, SEQS).astype(jnp.int32)
    w_out = bell_draw(splits[3], (CH * CH, PAIR), (CH * CH) ** -0.5, 0.1875)
    return dict(left_act=left_act, right_act=right_act, counts=counts, w_out=w_out)


def reference(left_act, right_act, counts, w_out):
    block = 16 if LEFT % 16 == 0 else 2
    width = block * CH

    def one_block(index):
        columns = lax.dynamic_slice_in_dim(left_act, (index * width).astype(jnp.int32), width, 1)
        outer = lax.dot_general(columns, right_act, (((0,), (0,)), ((), ())), preferred_element_type=jnp.float32)
        outer = outer.reshape(block, CH, RIGHT, CH).transpose(0, 2, 1, 3).reshape(block * RIGHT, CH * CH)
        flat = outer.astype(jnp.bfloat16)
        projected = jnp.dot(flat, w_out, preferred_element_type=jnp.float32).reshape(block, RIGHT, PAIR)
        cover = lax.dynamic_slice_in_dim(counts, (index * block).astype(jnp.int32), block, 0)
        return projected / cover.astype(jnp.float32)[:, :, None]

    blocks = lax.map(one_block, jnp.arange(LEFT // block, dtype=jnp.int32))
    return blocks.reshape(LEFT, RIGHT, PAIR)
```

```python
import functools

import jax
import jax.numpy as jnp
from jax import lax
from jax.experimental import pallas as pl
from jax.experimental.pallas import tpu as pltpu
from jax.sharding import PartitionSpec as P

CH = 32
CORES = 2
TILE = 256
MESH = pl.DeviceIdType.MESH


def lane_quads(tiles):
    lane = lax.broadcasted_iota(jnp.int32, tiles[0].shape, 1)
    low = lane < 64
    even = (lane % 64) < 32
    stage = [None] * 4
    for c in range(2):
        a, b = tiles[c], tiles[c + 2]
        stage[c] = jnp.where(low, a, pltpu.roll(b, 64, 1))
        stage[c + 2] = jnp.where(low, pltpu.roll(a, 64, 1), b)
    outs = [None] * 4
    for half in range(2):
        a, b = stage[2 * half], stage[2 * half + 1]
        outs[2 * half] = jnp.where(even, a, pltpu.roll(b, 32, 1))
        outs[2 * half + 1] = jnp.where(even, pltpu.roll(a, 96, 1), b)
    return outs


def kernel(sizes, left_ref, right_ref, counts_ref, w_hbm, out_ref, w_ref, counts_in, cover, out_v, left_full, right_full, left_t, acc, flat,
           z_send, z_recv, y_send, y_recv, s_send, s_recv, own_sem, out_sem):
    n_z, n_r, q_z, q_y = sizes
    n_y = n_r // CORES
    rows_l, width_l = left_ref.shape
    rows_r, width_r = right_ref.shape
    piece_r = width_r // q_z
    piece_l = rows_l // q_y
    left_dev = width_l // CH
    right_dev = width_r // CH
    seqs = left_t.shape[1]
    z = lax.axis_index("left")
    r = lax.axis_index("right")
    y = r // CORES
    k = r % CORES

    def z_dev(pos):
        return {"left": pos}

    def y_dev(pos):
        return {"right": pos * CORES + k}

    sib_dev = {"right": y * CORES + (1 - k)}

    barrier = pltpu.get_barrier_semaphore()

    def greet(dev):
        pl.semaphore_signal(barrier, inc=1, device_id=dev, device_id_type=MESH)

    greet(sib_dev)
    for pos, n, dev in ((z, n_z, z_dev), (y, n_y, y_dev)):
        pl.when(pos + 1 < n)(functools.partial(greet, dev(pos + 1)))
        pl.when(pos >= 1)(functools.partial(greet, dev(pos - 1)))
    total = 1 + (z + 1 < n_z).astype(jnp.int32) + (z >= 1).astype(jnp.int32)
    total = total + (y + 1 < n_y).astype(jnp.int32) + (y >= 1).astype(jnp.int32)
    pl.semaphore_wait(barrier, total)

    def z_slot(chunk, q):
        return right_full.at[pl.ds(pl.multiple_of(chunk * rows_r, rows_r), rows_r), pl.ds(q * piece_r, piece_r)]

    def z_copy(side, step, q):
        sign = 1 - 2 * side
        chunk = z - sign * step
        src = right_ref.at[:, pl.ds(q * piece_r, piece_r)] if step == 0 else z_slot(chunk, q)
        at = step * q_z + q
        return pltpu.make_async_remote_copy(
            src_ref=src, dst_ref=z_slot(chunk, q), send_sem=z_send.at[side, at], recv_sem=z_recv.at[side, at],
            device_id=z_dev(z + sign), device_id_type=MESH)

    def z_sends(side, step):
        near = z + 1 < n_z if side == 0 else z >= 1
        far = z - step >= 0 if side == 0 else z + step < n_z
        return jnp.logical_and(near, far)

    def z_arrives(side, step):
        return z - step - 1 >= 0 if side == 0 else z + step + 1 < n_z

    def z_wait(side, step, q):
        sign = 1 - 2 * side
        slot = z_slot(z - sign * (step + 1), q)
        pltpu.make_async_copy(slot, slot, z_recv.at[side, step * q_z + q]).wait()

    def l_slot(chunk, q):
        return left_full.at[pl.ds(pl.multiple_of(chunk * rows_l + q * piece_l, piece_l), piece_l), :]

    def l_own(q):
        return left_ref.at[pl.ds(q * piece_l, piece_l), :]

    def y_copy(side, step, q):
        sign = 1 - 2 * side
        chunk = (y - sign * step) * CORES + k
        at = step * q_y + q
        return pltpu.make_async_remote_copy(
            src_ref=l_own(q) if step == 0 else l_slot(chunk, q), dst_ref=l_slot(chunk, q),
            send_sem=y_send.at[side, at], recv_sem=y_recv.at[side, at],
            device_id=y_dev(y + sign), device_id_type=MESH)

    def y_sends(side, step):
        near = y + 1 < n_y if side == 0 else y >= 1
        far = y - step >= 0 if side == 0 else y + step < n_y
        return jnp.logical_and(near, far)

    def y_arrives(side, step):
        return y - step - 1 >= 0 if side == 0 else y + step + 1 < n_y

    def y_wait(side, step, q):
        sign = 1 - 2 * side
        slot = l_slot((y - sign * (step + 1)) * CORES + k, q)
        pltpu.make_async_copy(slot, slot, y_recv.at[side, step * q_y + q]).wait()

    def s_at(side, step, q):
        if step < 0:
            return q
        return (1 + side * (n_y - 1) + step) * q_y + q

    def s_copy(side, step, q):
        sign = 1 - 2 * side
        chunk = (y - sign * (step + 1)) * CORES + k if step >= 0 else r
        at = s_at(side, step, q)
        return pltpu.make_async_remote_copy(
            src_ref=l_own(q) if step < 0 else l_slot(chunk, q), dst_ref=l_slot(chunk, q),
            send_sem=s_send.at[at], recv_sem=s_recv.at[at],
            device_id=sib_dev, device_id_type=MESH)

    def s_wait(side, step, q):
        sign = 1 - 2 * side
        y_from = y - sign * (step + 1) if step >= 0 else y
        slot = l_slot(y_from * CORES + (1 - k), q)
        pltpu.make_async_copy(slot, slot, s_recv.at[s_at(side, step, q)]).wait()

    tile = 256

    def turn(src, first_row, chunk, q):
        col = pl.multiple_of(chunk * rows_l + q * piece_l, piece_l)

        def body(m, carry):
            at = pl.multiple_of(m * tile, tile)
            left_t[pl.ds(at, tile), pl.ds(col, piece_l)] = src[pl.ds(first_row, piece_l), pl.ds(at, tile)].T
            return carry

        lax.fori_loop(0, width_l // tile, body, 0)

    def turn_full(chunk, q):
        turn(left_full, pl.multiple_of(chunk * rows_l + q * piece_l, piece_l), chunk, q)

    for q in range(max(q_z, q_y)):
        for side in range(2):
            if q < q_z:
                pl.when(z_sends(side, 0))(lambda side=side, q=q: z_copy(side, 0, q).start())
            if q < q_y:
                pl.when(y_sends(side, 0))(lambda side=side, q=q: y_copy(side, 0, q).start())
    own_left = pltpu.make_async_copy(left_ref, left_full.at[pl.ds(pl.multiple_of(r * rows_l, rows_l), rows_l), :], own_sem.at[0])
    own = pltpu.make_async_copy(right_ref, right_full.at[pl.ds(pl.multiple_of(z * rows_r, rows_r), rows_r), :], own_sem.at[1])
    weights = pltpu.make_async_copy(w_hbm, w_ref, own_sem.at[2])
    counts_copy = pltpu.make_async_copy(counts_ref, counts_in, own_sem.at[3])
    for copy in (own_left, own, weights, counts_copy):
        copy.start()
    for q in range(q_y):
        s_copy(0, -1, q).start()
    own_left.wait()
    for q in range(q_y):
        turn_full(r, q)
    counts_copy.wait()
    counted = counts_in[...].astype(jnp.float32)
    for j in range(right_dev):
        cover[j] = jnp.broadcast_to(counted[:, j:j + 1], (left_dev, cover.shape[2]))
    for q in range(q_y):
        s_wait(0, -1, q)
        turn_full(y * CORES + (1 - k), q)

    def z_tick(step, q):
        for side in range(2):
            @pl.when(z_arrives(side, step))
            def _():
                z_wait(side, step, q)
                if step + 1 < n_z - 1:
                    pl.when(z_sends(side, step + 1))(lambda: z_copy(side, step + 1, q).start())

    def y_tick(step, q):
        for side in range(2):
            @pl.when(y_arrives(side, step))
            def _():
                y_wait(side, step, q)
                s_copy(side, step, q).start()
                if step + 1 < n_y - 1:
                    pl.when(y_sends(side, step + 1))(lambda: y_copy(side, step + 1, q).start())

        for side in range(2):
            @pl.when(y_arrives(side, step))
            def _():
                sign = 1 - 2 * side
                y_from = y - sign * (step + 1)
                turn_full(y_from * CORES + k, q)
                s_wait(side, step, q)
                turn_full(y_from * CORES + (1 - k), q)

    y_ticks = [(step, q) for step in range(n_y - 1) for q in range(q_y)]
    for t in range((n_z - 2) * q_z):
        z_tick(t // q_z, t % q_z)
        if t % 2 == 1 and y_ticks:
            y_tick(*y_ticks.pop(0))
    for tick in y_ticks:
        y_tick(*tick)
    own.wait()
    weights.wait()

    block = 1024
    at_end = jnp.logical_or(z == 0, z == n_z - 1)
    base = jnp.where(z == 0, 0, rows_r)
    base = pl.multiple_of(base, rows_r)

    def product(q, first, depth, add):
        cols = pl.ds(q * piece_r, piece_r)

        def body(m, carry):
            rows = pl.ds(pl.multiple_of(m * block, block), block)
            value = jnp.dot(left_t[rows, pl.ds(first, depth)], right_full[pl.ds(first, depth), cols],
                            preferred_element_type=jnp.float32)
            for part in range(piece_r // 128):
                some = value[:, part * 128:(part + 1) * 128]
                slab = q * (piece_r // 128) + part
                acc[slab, rows, :] = acc[slab, rows, :] + some if add else some
            return carry

        lax.fori_loop(0, width_l // block, body, 0)

    def first_part(q):
        @pl.when(at_end)
        def _():
            product(q, base, seqs - rows_r, False)

        @pl.when(jnp.logical_not(at_end))
        def _():
            product(q, 0, seqs, False)

    for q in range(q_z):
        first_part(q)

    def finish(q):
        heads = piece_r // CH
        for quad in range(heads // 4):
            slab = acc.at[q * (piece_r // 128) + quad]
            for cq in range(CH // 4):
                tiles = [slab[pl.ds(cq * 4 + c, left_dev, stride=CH), :].astype(jnp.bfloat16) for c in range(4)]
                for j, value in enumerate(lane_quads(tiles)):
                    flat[pl.ds((quad * 4 + j) * left_dev, left_dev), pl.ds(cq * 128, 128)] = value
        projected = jnp.dot(flat[...], w_ref[...], preferred_element_type=jnp.float32)
        for j in range(heads):
            value = projected[j * left_dev:(j + 1) * left_dev, :] / cover[q * heads + j]
            out_v.at[q].reshape(left_dev * heads, value.shape[1])[pl.ds(j, left_dev, stride=heads), :] = value
        out_copy(q).start()

    def out_copy(q):
        return pltpu.make_async_copy(out_v.at[q], out_ref.at[:, pl.ds(q * heads_q, heads_q), :], out_sem.at[q])

    heads_q = piece_r // CH
    last = n_z - 2
    for q in range(q_z):
        z_tick(last, q)

        @pl.when(at_end)
        def _():
            far = jnp.where(z == 0, (n_z - 1) * rows_r, 0)
            product(q, pl.multiple_of(far, rows_r), rows_r, True)

        finish(q)

    for side in range(2):
        for step in range(n_z - 1):
            for q in range(q_z):
                pl.when(z_sends(side, step))(lambda side=side, step=step, q=q: z_copy(side, step, q).wait_send())
        for step in range(n_y - 1):
            for q in range(q_y):
                pl.when(y_sends(side, step))(lambda side=side, step=step, q=q: y_copy(side, step, q).wait_send())
                pl.when(y_arrives(side, step))(lambda side=side, step=step, q=q: s_copy(side, step, q).wait_send())
    for q in range(q_y):
        s_copy(0, -1, q).wait_send()
    for q in range(q_z):
        out_copy(q).wait()


def folded(left_ref, right_ref, counts_ref, w_hbm, out_ref, w_in, w_wide, w_ref, counts_in, cover, order, left_full, left_far, right_full, right_t,
           acc, acc_far, flat, part, out_v, in_send, in_recv, fwd_send, far_send, far_recv, end_send, end_recv, own_send, own_recv,
           y_send, y_recv, s_send, s_recv, a_send, a_recv, p_send, p_recv, own_sem, out_sem):
    rows, width_l = left_ref.shape
    width_r = right_ref.shape[1]
    steps = width_r // TILE
    piece = rows // steps
    half = width_l // CORES
    quads = width_l // 128
    heads = TILE // CH
    z = lax.axis_index("left")
    r = lax.axis_index("right")
    y, k = r // CORES, r % CORES
    up = z // 2
    sign = 2 * up - 1

    def fold(n, at):
        return up * at + (1 - up) * (n - 1 - at)

    zc, yc, kc = fold(4, z), fold(2, y), fold(2, k)
    inner, end = zc == 2, zc == 3
    sib_dev = {"right": r + 1 - 2 * k}
    y_dev = {"right": r + (1 - 2 * y) * CORES}

    def when(*terms):
        value = terms[0]
        for term in terms[1:]:
            value = jnp.logical_and(value, term)
        return pl.when(value)

    def z_dev(way):
        return {"left": z + way * sign}

    barrier = pltpu.get_barrier_semaphore()

    def greet(dev):
        pl.semaphore_signal(barrier, inc=1, device_id=dev, device_id_type=MESH)

    greet(sib_dev)
    greet(y_dev)
    greet(z_dev(-1))
    when(inner)(lambda: greet(z_dev(1)))
    pl.semaphore_wait(barrier, 3 + inner.astype(jnp.int32))

    def remote(src, dst, send, recv, dev):
        return pltpu.make_async_remote_copy(src_ref=src, dst_ref=dst, send_sem=send, recv_sem=recv, device_id=dev, device_id_type=MESH)

    def arrived(slot, sem):
        pltpu.make_async_copy(slot, slot, sem).wait()

    def block(at, first=0, size=rows):
        return pl.ds(pl.multiple_of(fold(4, at) * rows + first, size), size)

    def cols(q):
        return pl.ds(pl.multiple_of(q * TILE, TILE), TILE)

    def right_slot(at, q):
        return right_full.at[block(at), cols(q)]

    def in_copy(way, q):
        return remote(right_ref.at[:, cols(q)], right_slot(2, q), in_send.at[(way + 1) // 2, q], in_recv.at[0, q], z_dev(way))

    def fwd_copy(way, q):
        slot = right_slot(3 if way < 0 else 1, q)
        return remote(slot, slot, fwd_send.at[(way + 1) // 2, q], in_recv.at[1, q], z_dev(way))

    def end_copy(q):
        return remote(right_ref.at[:, cols(q)], right_slot(3, q), end_send.at[q], end_recv.at[q], z_dev(-1))

    def own_half():
        return pl.ds(pl.multiple_of(k * half, half), half)

    def far_copy(p):
        at = pl.ds(pl.multiple_of(p * piece, piece), piece)
        return remote(left_full.at[block(0, p * piece, piece), own_half()], left_far.at[at, own_half()], far_send.at[p], far_recv.at[p], z_dev(-1))

    def far_slot(p, core):
        return left_far.at[pl.ds(pl.multiple_of(p * piece, piece), piece), pl.ds(pl.multiple_of(core * half, half), half)]

    def share_copy(p):
        return remote(far_slot(p, k), far_slot(p, k), a_send.at[p], a_recv.at[p], sib_dev)

    def own_copy(p):
        at = pl.ds(pl.multiple_of(p * piece, piece), piece)
        slot = left_full.at[pl.ds(pl.multiple_of(r * rows + p * piece, piece), piece), :]
        return remote(left_ref.at[at, :], slot, own_send.at[p], own_recv.at[p], sib_dev)

    def own_arrived(p):
        other = r + 1 - 2 * k
        arrived(left_full.at[pl.ds(pl.multiple_of(other * rows + p * piece, piece), piece), :], own_recv.at[p])

    def y_slot(side, pos, p, core):
        return left_full.at[block(2 * side + pos, p * piece, piece), pl.ds(pl.multiple_of(core * half, half), half)]

    def y_copy(pos, p):
        slot = y_slot(yc, pos, p, k)
        return remote(slot, slot, y_send.at[pos, p], y_recv.at[pos, p], y_dev)

    def s_copy(pos, p):
        slot = y_slot(1 - yc, pos, p, k)
        return remote(slot, slot, s_send.at[pos, p], s_recv.at[pos, p], sib_dev)

    def part_copy(q):
        return remote(part.at[q], part.at[q], p_send.at[q], p_recv.at[q], z_dev(1))

    def each(body, first=0, last=steps):
        def step(at, carry):
            body(at)
            return carry

        lax.fori_loop(first, last, step, 0)

    @when(inner)
    def _():
        @each
        def _(q):
            in_copy(-1, q).start()
            in_copy(1, q).start()

    when(end)(lambda: end_copy(0).start())
    own_left = pltpu.make_async_copy(left_ref, left_full.at[pl.ds(pl.multiple_of(r * rows, rows), rows), :], own_sem.at[0])
    own = pltpu.make_async_copy(right_ref, right_full.at[block(zc), :], own_sem.at[1])
    weights = pltpu.make_async_copy(w_hbm, w_in, own_sem.at[2])
    counts_copy = pltpu.make_async_copy(counts_ref, counts_in, own_sem.at[3])
    own_left.start()
    each(lambda p: own_copy(p).start())
    for copy in (own, weights, counts_copy):
        copy.start()
    own_left.wait()
    first, second = kc == 0, kc == 1

    @when(first)
    def _():
        each(lambda p: y_copy(0, p).start())
        when(end, yc == 0)(lambda: each(lambda p: far_copy(p).start()))

    @each
    def _(p):
        own_arrived(p)

        @when(second)
        def _():
            y_copy(0, p).start()
            when(end, yc == 0)(lambda: far_copy(p).start())

    each(lambda p: y_copy(1, p).start())
    when(end, yc == 0)(lambda: each(lambda q: end_copy(q).start(), 1))

    row = lax.broadcasted_iota(jnp.int32, (TILE, TILE), 0)
    column = lax.broadcasted_iota(jnp.int32, (TILE, TILE), 1)
    order[...] = jnp.where(column == (row % heads) * CH + row // heads, 1.0, 0.0).astype(order.dtype)
    weights.wait()
    w_wide[...] = w_in[...].astype(jnp.float32)
    for e in range(CH):
        w_ref[pl.ds(e * CH, CH), :] = w_wide[pl.ds(e, CH, stride=CH), :].astype(w_ref.dtype)
    counts_copy.wait()
    counted = counts_in[...].astype(jnp.float32)
    for i in range(counted.shape[1]):
        cover[i // 4, i % 4] = jnp.broadcast_to(counted[:, i:i + 1], (counted.shape[0], cover.shape[3]))

    def turn(at, q):
        value = lax.dot_general(order[...], right_full[block(at), cols(q)], (((1,), (1,)), ((), ())), preferred_element_type=jnp.float32)
        right_t[cols(q), block(at)] = value.astype(right_t.dtype)

    def product(into, lines, source, left, left_rows, size, add):
        wide = 512
        lhs = right_t.at[lines, source]

        @functools.partial(each, last=width_l // wide)
        def _(n):
            value = jnp.dot(lhs[...], left[left_rows, pl.ds(pl.multiple_of(n * wide, wide), wide)], preferred_element_type=jnp.float32)
            for one in range(wide // 128):
                some = value[:, one * 128:(one + 1) * 128]
                slab = n * (wide // 128) + one
                into[slab, size, :] = into[slab, size, :] + some if add else some

    def product_all(at, add):
        every = pl.ds(0, width_r)
        product(acc, every, block(at), left_full, block(at), every, add)

    def product_one(at, q):
        product(acc, cols(q), block(at), left_full, block(at), cols(q), True)

    def project(source, first_row):
        for eq in range(CH // 4):
            tiles = []
            for e in range(4):
                tile = source[:, pl.ds(pl.multiple_of(first_row + (eq * 4 + e) * heads, heads), heads), :]
                tiles.append(tile.reshape(quads * heads, 128).astype(flat.dtype))
            for i, value in enumerate(lane_quads(tiles)):
                flat[pl.ds(i * quads * heads, quads * heads), pl.ds(eq * 128, 128)] = value
        return jnp.dot(flat[...], w_ref[...], preferred_element_type=jnp.float32)

    def settle(q, add):
        for i in range(4):
            value = out_v[q, :, i]
            if add:
                more = part[q, pl.ds(i * quads * heads, quads * heads), :]
                value = value + more.astype(jnp.float32).reshape(value.shape)
            out_v[q, :, i] = value / cover[:, i, pl.ds(pl.multiple_of(q * heads, heads), heads), :]
        out_copy(q).start()

    def out_copy(q):
        at = pl.ds(pl.multiple_of(q * heads, heads), heads)
        return pltpu.make_async_copy(out_v.at[q].reshape(4 * quads, heads, 128), out_ref.at[:, at, :], out_sem.at[q])

    own.wait()
    each(lambda q: turn(zc, q))

    @each
    def _(p):
        arrived(right_slot(zc - 1, p), in_recv.at[0, p])
        when(inner)(lambda: fwd_copy(1, p).start())
        arrived(y_slot(1 - yc, 0, p, k), y_recv.at[0, p])
        s_copy(0, p).start()
        when(end, yc == 1)(lambda: far_copy(p).start())

        @when(inner, p >= 1)
        def _():
            arrived(far_slot(p - 1, k), far_recv.at[p - 1])
            share_copy(p - 1).start()

        turn(zc - 1, p)

    when(end, yc == 1)(lambda: each(lambda q: end_copy(q).start(), 1))

    def end_arrived(q):
        arrived(right_slot(3, q), end_recv.at[q])
        fwd_copy(-1, q).start()
        turn(3, q)

    when(inner)(lambda: end_arrived(0))
    each(lambda p: arrived(y_slot(1 - yc, 0, p, 1 - k), s_recv.at[0, p]))
    product_all(2, False)
    near, late = 1 + 2 * yc, 3 - 2 * yc

    def far(q):
        arrived(right_slot(0, q), in_recv.at[1, q])
        turn(0, q)
        product(acc_far, cols(q), block(0), left_far, pl.ds(0, rows), pl.ds(0, TILE), False)
        part[q] = project(acc_far, 0).astype(part.dtype)
        product_one(0, q)
        part_copy(q).start()

    @each
    def _(q):
        when(inner, q >= 1)(lambda: end_arrived(q))
        arrived(y_slot(1 - yc, 1, q, k), y_recv.at[1, q])
        s_copy(1, q).start()

        @when(end)
        def _():
            arrived(right_slot(1, q), in_recv.at[1, q])
            turn(1, q)

        product_one(near, q)

        @when(inner, q == 0)
        def _():
            arrived(far_slot(steps - 1, k), far_recv.at[steps - 1])
            share_copy(steps - 1).start()
            each(lambda p: arrived(far_slot(p, 1 - k), a_recv.at[p]))

        when(inner, q >= 1)(lambda: far(q - 1))

    each(lambda p: arrived(y_slot(1 - yc, 1, p, 1 - k), s_recv.at[1, p]))
    product_all(late, True)

    @each
    def _(q):
        when(inner, q == steps - 1)(lambda: far(q))
        value = project(acc, q * TILE)
        for i in range(4):
            out_v[q, :, i] = value[i * quads * heads:(i + 1) * quads * heads].reshape(quads, heads, 128)
        when(inner)(lambda: settle(q, False))

    @when(end)
    def _():
        @each
        def _(q):
            arrived(part.at[q], p_recv.at[q])
            settle(q, True)

    @each
    def _(q):
        own_copy(q).wait_send()
        for pos in range(2):
            y_copy(pos, q).wait_send()
            s_copy(pos, q).wait_send()

        @when(inner)
        def _():
            for way in (-1, 1):
                in_copy(way, q).wait_send()
                fwd_copy(way, q).wait_send()
            share_copy(q).wait_send()
            part_copy(q).wait_send()

        @when(end)
        def _():
            end_copy(q).wait_send()
            far_copy(q).wait_send()

        out_copy(q).wait()


def folded_call(left_act, right_act, counts, w_out):
    rows, width_l = left_act.shape
    width_r = right_act.shape[1]
    left_dev, right_dev = counts.shape
    pair = w_out.shape[1]
    steps = width_r // TILE
    heads = TILE // CH
    full = 4 * rows
    dma = pltpu.SemaphoreType.DMA
    return pl.pallas_call(
        folded,
        out_shape=jax.ShapeDtypeStruct((left_dev, right_dev, pair), jnp.float32),
        in_specs=[pl.BlockSpec(memory_space=pl.ANY)] * 4,
        out_specs=pl.BlockSpec(memory_space=pl.ANY),
        scratch_shapes=[
            pltpu.VMEM(w_out.shape, w_out.dtype),
            pltpu.VMEM(w_out.shape, jnp.float32),
            pltpu.VMEM(w_out.shape, w_out.dtype),
            pltpu.VMEM((right_dev, left_dev), counts.dtype),
            pltpu.VMEM((left_dev // 4, 4, right_dev, pair), jnp.float32),
            pltpu.VMEM((TILE, TILE), jnp.bfloat16),
            pltpu.VMEM((full, width_l), jnp.bfloat16),
            pltpu.VMEM((rows, width_l), jnp.bfloat16),
            pltpu.VMEM((full, width_r), jnp.bfloat16),
            pltpu.VMEM((width_r, full), jnp.bfloat16),
            pltpu.VMEM((width_l // 128, width_r, 128), jnp.float32),
            pltpu.VMEM((width_l // 128, TILE, 128), jnp.float32),
            pltpu.VMEM((left_dev * heads, CH * CH), jnp.bfloat16),
            pltpu.VMEM((steps, left_dev * heads, pair), jnp.bfloat16),
            pltpu.VMEM((steps, left_dev // 4, 4, heads, pair), jnp.float32),
            dma((2, steps)), dma((2, steps)), dma((2, steps)), dma((steps,)), dma((steps,)), dma((steps,)), dma((steps,)), dma((steps,)),
            dma((steps,)), dma((2, steps)), dma((2, steps)), dma((2, steps)), dma((2, steps)), dma((steps,)), dma((steps,)), dma((steps,)),
            dma((steps,)), dma((4,)), dma((steps,)),
        ],
        compiler_params=pltpu.CompilerParams(collective_id=0, has_side_effects=True, vmem_limit_bytes=56 * 1024 * 1024),
        name="pair_mean",
    )(left_act, right_act, counts.T, w_out)


def solution(mesh):
    n_z, n_r = mesh.shape["left"], mesh.shape["right"]
    n_y = n_r // CORES

    def shards(left_act, right_act, counts, w_out):
        if (n_z, n_y) == (4, 2):
            return folded_call(left_act, right_act, counts, w_out)
        rows_l, width_l = left_act.shape
        rows_r, width_r = right_act.shape
        seqs = rows_r * n_z
        left_dev, right_dev = counts.shape
        pair = w_out.shape[1]
        q_z = width_r // 256
        q_y = rows_l // max(128, rows_l // 4)
        projected = pl.pallas_call(
            functools.partial(kernel, (n_z, n_r, q_z, q_y)),
            out_shape=jax.ShapeDtypeStruct((left_dev, right_dev, pair), jnp.float32),
            in_specs=[pl.BlockSpec(memory_space=pl.ANY)] * 4,
            out_specs=pl.BlockSpec(memory_space=pl.ANY),
            scratch_shapes=[
                pltpu.VMEM(w_out.shape, w_out.dtype),
                pltpu.VMEM(counts.shape, counts.dtype),
                pltpu.VMEM((right_dev, left_dev, pair), jnp.float32),
                pltpu.VMEM((q_z, left_dev, right_dev // q_z, pair), jnp.float32),
                pltpu.VMEM((seqs, width_l), jnp.bfloat16),
                pltpu.VMEM((seqs, width_r), jnp.bfloat16),
                pltpu.VMEM((width_l, seqs), jnp.bfloat16),
                pltpu.VMEM((width_r // 128, width_l, 128), jnp.float32),
                pltpu.VMEM((width_r // q_z // CH * left_dev, CH * CH), jnp.bfloat16),
                pltpu.SemaphoreType.DMA((2, (n_z - 1) * q_z)),
                pltpu.SemaphoreType.DMA((2, (n_z - 1) * q_z)),
                pltpu.SemaphoreType.DMA((2, (n_y - 1) * q_y)),
                pltpu.SemaphoreType.DMA((2, (n_y - 1) * q_y)),
                pltpu.SemaphoreType.DMA(((2 * n_y - 1) * q_y,)),
                pltpu.SemaphoreType.DMA(((2 * n_y - 1) * q_y,)),
                pltpu.SemaphoreType.DMA((4,)),
                pltpu.SemaphoreType.DMA((q_z,)),
            ],
            compiler_params=pltpu.CompilerParams(
                collective_id=0, has_side_effects=True, vmem_limit_bytes=56 * 1024 * 1024
            ),
            name="pair_mean",
        )(left_act, right_act, counts, w_out)
        return projected

    in_specs = (
        P(("groups", "right"), "left"),
        P(("groups", "left"), "right"),
        P(("groups", "left"), "right"),
        P(),
    )
    out_specs = P(("groups", "left"), "right", None)
    return jax.shard_map(shards, mesh=mesh, in_specs=in_specs, out_specs=out_specs, check_vma=False)
```

```python
import functools

import jax
import jax.numpy as jnp
from jax import lax
from jax.experimental import pallas as pl
from jax.experimental.pallas import tpu as pltpu
from jax.sharding import PartitionSpec as P

CH = 32
CORES = 2
TILE = 256
MESH = pl.DeviceIdType.MESH


def lane_quads(tiles):
    lane = lax.broadcasted_iota(jnp.int32, tiles[0].shape, 1)
    low = lane < 64
    even = (lane % 64) < 32
    stage = [None] * 4
    for c in range(2):
        a, b = tiles[c], tiles[c + 2]
        stage[c] = jnp.where(low, a, pltpu.roll(b, 64, 1))
        stage[c + 2] = jnp.where(low, pltpu.roll(a, 64, 1), b)
    outs = [None] * 4
    for half in range(2):
        a, b = stage[2 * half], stage[2 * half + 1]
        outs[2 * half] = jnp.where(even, a, pltpu.roll(b, 32, 1))
        outs[2 * half + 1] = jnp.where(even, pltpu.roll(a, 96, 1), b)
    return outs


def kernel(sizes, left_ref, right_ref, counts_ref, w_hbm, out_ref, w_ref, counts_in, cover, out_v, left_full, right_full, left_t, acc, flat,
           z_send, z_recv, y_send, y_recv, s_send, s_recv, own_sem, out_sem):
    n_z, n_r, q_z, q_y = sizes
    n_y = n_r // CORES
    rows_l, width_l = left_ref.shape
    rows_r, width_r = right_ref.shape
    piece_r = width_r // q_z
    piece_l = rows_l // q_y
    left_dev = width_l // CH
    right_dev = width_r // CH
    seqs = left_t.shape[1]
    z = lax.axis_index("left")
    r = lax.axis_index("right")
    y = r // CORES
    k = r % CORES

    def z_dev(pos):
        return {"left": pos}

    def y_dev(pos):
        return {"right": pos * CORES + k}

    sib_dev = {"right": y * CORES + (1 - k)}

    barrier = pltpu.get_barrier_semaphore()

    def greet(dev):
        pl.semaphore_signal(barrier, inc=1, device_id=dev, device_id_type=MESH)

    greet(sib_dev)
    for pos, n, dev in ((z, n_z, z_dev), (y, n_y, y_dev)):
        pl.when(pos + 1 < n)(functools.partial(greet, dev(pos + 1)))
        pl.when(pos >= 1)(functools.partial(greet, dev(pos - 1)))
    total = 1 + (z + 1 < n_z).astype(jnp.int32) + (z >= 1).astype(jnp.int32)
    total = total + (y + 1 < n_y).astype(jnp.int32) + (y >= 1).astype(jnp.int32)
    pl.semaphore_wait(barrier, total)

    def z_slot(chunk, q):
        return right_full.at[pl.ds(pl.multiple_of(chunk * rows_r, rows_r), rows_r), pl.ds(q * piece_r, piece_r)]

    def z_copy(side, step, q):
        sign = 1 - 2 * side
        chunk = z - sign * step
        src = right_ref.at[:, pl.ds(q * piece_r, piece_r)] if step == 0 else z_slot(chunk, q)
        at = step * q_z + q
        return pltpu.make_async_remote_copy(
            src_ref=src, dst_ref=z_slot(chunk, q), send_sem=z_send.at[side, at], recv_sem=z_recv.at[side, at],
            device_id=z_dev(z + sign), device_id_type=MESH)

    def z_sends(side, step):
        near = z + 1 < n_z if side == 0 else z >= 1
        far = z - step >= 0 if side == 0 else z + step < n_z
        return jnp.logical_and(near, far)

    def z_arrives(side, step):
        return z - step - 1 >= 0 if side == 0 else z + step + 1 < n_z

    def z_wait(side, step, q):
        sign = 1 - 2 * side
        slot = z_slot(z - sign * (step + 1), q)
        pltpu.make_async_copy(slot, slot, z_recv.at[side, step * q_z + q]).wait()

    def l_slot(chunk, q):
        return left_full.at[pl.ds(pl.multiple_of(chunk * rows_l + q * piece_l, piece_l), piece_l), :]

    def l_own(q):
        return left_ref.at[pl.ds(q * piece_l, piece_l), :]

    def y_copy(side, step, q):
        sign = 1 - 2 * side
        chunk = (y - sign * step) * CORES + k
        at = step * q_y + q
        return pltpu.make_async_remote_copy(
            src_ref=l_own(q) if step == 0 else l_slot(chunk, q), dst_ref=l_slot(chunk, q),
            send_sem=y_send.at[side, at], recv_sem=y_recv.at[side, at],
            device_id=y_dev(y + sign), device_id_type=MESH)

    def y_sends(side, step):
        near = y + 1 < n_y if side == 0 else y >= 1
        far = y - step >= 0 if side == 0 else y + step < n_y
        return jnp.logical_and(near, far)

    def y_arrives(side, step):
        return y - step - 1 >= 0 if side == 0 else y + step + 1 < n_y

    def y_wait(side, step, q):
        sign = 1 - 2 * side
        slot = l_slot((y - sign * (step + 1)) * CORES + k, q)
        pltpu.make_async_copy(slot, slot, y_recv.at[side, step * q_y + q]).wait()

    def s_at(side, step, q):
        if step < 0:
            return q
        return (1 + side * (n_y - 1) + step) * q_y + q

    def s_copy(side, step, q):
        sign = 1 - 2 * side
        chunk = (y - sign * (step + 1)) * CORES + k if step >= 0 else r
        at = s_at(side, step, q)
        return pltpu.make_async_remote_copy(
            src_ref=l_own(q) if step < 0 else l_slot(chunk, q), dst_ref=l_slot(chunk, q),
            send_sem=s_send.at[at], recv_sem=s_recv.at[at],
            device_id=sib_dev, device_id_type=MESH)

    def s_wait(side, step, q):
        sign = 1 - 2 * side
        y_from = y - sign * (step + 1) if step >= 0 else y
        slot = l_slot(y_from * CORES + (1 - k), q)
        pltpu.make_async_copy(slot, slot, s_recv.at[s_at(side, step, q)]).wait()

    tile = 256

    def turn(src, first_row, chunk, q):
        col = pl.multiple_of(chunk * rows_l + q * piece_l, piece_l)

        def body(m, carry):
            at = pl.multiple_of(m * tile, tile)
            left_t[pl.ds(at, tile), pl.ds(col, piece_l)] = src[pl.ds(first_row, piece_l), pl.ds(at, tile)].T
            return carry

        lax.fori_loop(0, width_l // tile, body, 0)

    def turn_full(chunk, q):
        turn(left_full, pl.multiple_of(chunk * rows_l + q * piece_l, piece_l), chunk, q)

    for q in range(max(q_z, q_y)):
        for side in range(2):
            if q < q_z:
                pl.when(z_sends(side, 0))(lambda side=side, q=q: z_copy(side, 0, q).start())
            if q < q_y:
                pl.when(y_sends(side, 0))(lambda side=side, q=q: y_copy(side, 0, q).start())
    own_left = pltpu.make_async_copy(left_ref, left_full.at[pl.ds(pl.multiple_of(r * rows_l, rows_l), rows_l), :], own_sem.at[0])
    own = pltpu.make_async_copy(right_ref, right_full.at[pl.ds(pl.multiple_of(z * rows_r, rows_r), rows_r), :], own_sem.at[1])
    weights = pltpu.make_async_copy(w_hbm, w_ref, own_sem.at[2])
    counts_copy = pltpu.make_async_copy(counts_ref, counts_in, own_sem.at[3])
    for copy in (own_left, own, weights, counts_copy):
        copy.start()
    for q in range(q_y):
        s_copy(0, -1, q).start()
    own_left.wait()
    for q in range(q_y):
        turn_full(r, q)
    counts_copy.wait()
    counted = counts_in[...].astype(jnp.float32)
    for j in range(right_dev):
        cover[j] = jnp.broadcast_to(counted[:, j:j + 1], (left_dev, cover.shape[2]))
    for q in range(q_y):
        s_wait(0, -1, q)
        turn_full(y * CORES + (1 - k), q)

    def z_tick(step, q):
        for side in range(2):
            @pl.when(z_arrives(side, step))
            def _():
                z_wait(side, step, q)
                if step + 1 < n_z - 1:
                    pl.when(z_sends(side, step + 1))(lambda: z_copy(side, step + 1, q).start())

    def y_tick(step, q):
        for side in range(2):
            @pl.when(y_arrives(side, step))
            def _():
                y_wait(side, step, q)
                s_copy(side, step, q).start()
                if step + 1 < n_y - 1:
                    pl.when(y_sends(side, step + 1))(lambda: y_copy(side, step + 1, q).start())

        for side in range(2):
            @pl.when(y_arrives(side, step))
            def _():
                sign = 1 - 2 * side
                y_from = y - sign * (step + 1)
                turn_full(y_from * CORES + k, q)
                s_wait(side, step, q)
                turn_full(y_from * CORES + (1 - k), q)

    y_ticks = [(step, q) for step in range(n_y - 1) for q in range(q_y)]
    for t in range((n_z - 2) * q_z):
        z_tick(t // q_z, t % q_z)
        if t % 2 == 1 and y_ticks:
            y_tick(*y_ticks.pop(0))
    for tick in y_ticks:
        y_tick(*tick)
    own.wait()
    weights.wait()

    block = 1024
    at_end = jnp.logical_or(z == 0, z == n_z - 1)
    base = jnp.where(z == 0, 0, rows_r)
    base = pl.multiple_of(base, rows_r)

    def product(q, first, depth, add):
        cols = pl.ds(q * piece_r, piece_r)

        def body(m, carry):
            rows = pl.ds(pl.multiple_of(m * block, block), block)
            value = jnp.dot(left_t[rows, pl.ds(first, depth)], right_full[pl.ds(first, depth), cols],
                            preferred_element_type=jnp.float32)
            for part in range(piece_r // 128):
                some = value[:, part * 128:(part + 1) * 128]
                slab = q * (piece_r // 128) + part
                acc[slab, rows, :] = acc[slab, rows, :] + some if add else some
            return carry

        lax.fori_loop(0, width_l // block, body, 0)

    def first_part(q):
        @pl.when(at_end)
        def _():
            product(q, base, seqs - rows_r, False)

        @pl.when(jnp.logical_not(at_end))
        def _():
            product(q, 0, seqs, False)

    for q in range(q_z):
        first_part(q)

    def finish(q):
        heads = piece_r // CH
        for quad in range(heads // 4):
            slab = acc.at[q * (piece_r // 128) + quad]
            for cq in range(CH // 4):
                tiles = [slab[pl.ds(cq * 4 + c, left_dev, stride=CH), :].astype(jnp.bfloat16) for c in range(4)]
                for j, value in enumerate(lane_quads(tiles)):
                    flat[pl.ds((quad * 4 + j) * left_dev, left_dev), pl.ds(cq * 128, 128)] = value
        projected = jnp.dot(flat[...], w_ref[...], preferred_element_type=jnp.float32)
        for j in range(heads):
            value = projected[j * left_dev:(j + 1) * left_dev, :] / cover[q * heads + j]
            out_v.at[q].reshape(left_dev * heads, value.shape[1])[pl.ds(j, left_dev, stride=heads), :] = value
        out_copy(q).start()

    def out_copy(q):
        return pltpu.make_async_copy(out_v.at[q], out_ref.at[:, pl.ds(q * heads_q, heads_q), :], out_sem.at[q])

    heads_q = piece_r // CH
    last = n_z - 2
    for q in range(q_z):
        z_tick(last, q)

        @pl.when(at_end)
        def _():
            far = jnp.where(z == 0, (n_z - 1) * rows_r, 0)
            product(q, pl.multiple_of(far, rows_r), rows_r, True)

        finish(q)

    for side in range(2):
        for step in range(n_z - 1):
            for q in range(q_z):
                pl.when(z_sends(side, step))(lambda side=side, step=step, q=q: z_copy(side, step, q).wait_send())
        for step in range(n_y - 1):
            for q in range(q_y):
                pl.when(y_sends(side, step))(lambda side=side, step=step, q=q: y_copy(side, step, q).wait_send())
                pl.when(y_arrives(side, step))(lambda side=side, step=step, q=q: s_copy(side, step, q).wait_send())
    for q in range(q_y):
        s_copy(0, -1, q).wait_send()
    for q in range(q_z):
        out_copy(q).wait()


def folded(left_ref, right_ref, counts_ref, w_hbm, out_ref, w_in, w_wide, w_ref, counts_in, cover, order, left_full, left_far, right_full, right_t,
           acc, acc_far, flat, part, out_v, in_send, in_recv, fwd_send, far_send, far_recv, end_send, end_recv, own_send, own_recv,
           y_send, y_recv, s_send, s_recv, a_send, a_recv, p_send, p_recv, own_sem, out_sem):
    rows, width_l = left_ref.shape
    width_r = right_ref.shape[1]
    steps = width_r // TILE
    piece = rows // steps
    half = width_l // CORES
    quads = width_l // 128
    heads = TILE // CH
    early = steps // 2
    z = lax.axis_index("left")
    r = lax.axis_index("right")
    y, k = r // CORES, r % CORES
    up = z // 2
    sign = 2 * up - 1

    def fold(n, at):
        return up * at + (1 - up) * (n - 1 - at)

    zc, yc, kc = fold(4, z), fold(2, y), fold(2, k)
    inner, end = zc == 2, zc == 3
    sib_dev = {"right": r + 1 - 2 * k}
    y_dev = {"right": r + (1 - 2 * y) * CORES}

    def when(*terms):
        value = terms[0]
        for term in terms[1:]:
            value = jnp.logical_and(value, term)
        return pl.when(value)

    def z_dev(way):
        return {"left": z + way * sign}

    barrier = pltpu.get_barrier_semaphore()

    def greet(dev):
        pl.semaphore_signal(barrier, inc=1, device_id=dev, device_id_type=MESH)

    greet(sib_dev)
    greet(y_dev)
    greet(z_dev(-1))
    when(inner)(lambda: greet(z_dev(1)))
    pl.semaphore_wait(barrier, 3 + inner.astype(jnp.int32))

    def remote(src, dst, send, recv, dev):
        return pltpu.make_async_remote_copy(src_ref=src, dst_ref=dst, send_sem=send, recv_sem=recv, device_id=dev, device_id_type=MESH)

    def arrived(slot, sem):
        pltpu.make_async_copy(slot, slot, sem).wait()

    def block(at, first=0, size=rows):
        return pl.ds(pl.multiple_of(fold(4, at) * rows + first, size), size)

    def cols(q):
        return pl.ds(pl.multiple_of(q * TILE, TILE), TILE)

    def right_slot(at, q):
        return right_full.at[block(at), cols(q)]

    def in_copy(way, q):
        return remote(right_ref.at[:, cols(q)], right_slot(2, q), in_send.at[(way + 1) // 2, q], in_recv.at[0, q], z_dev(way))

    def fwd_copy(way, q):
        slot = right_slot(3 if way < 0 else 1, q)
        return remote(slot, slot, fwd_send.at[(way + 1) // 2, q], in_recv.at[1, q], z_dev(way))

    def end_copy(q):
        return remote(right_ref.at[:, cols(q)], right_slot(3, q), end_send.at[q], end_recv.at[q], z_dev(-1))

    def own_half():
        return pl.ds(pl.multiple_of(k * half, half), half)

    def far_copy(p):
        at = pl.ds(pl.multiple_of(p * piece, piece), piece)
        return remote(left_full.at[block(0, p * piece, piece), own_half()], left_far.at[at, own_half()], far_send.at[p], far_recv.at[p], z_dev(-1))

    def far_slot(p, core):
        return left_far.at[pl.ds(pl.multiple_of(p * piece, piece), piece), pl.ds(pl.multiple_of(core * half, half), half)]

    def share_copy(p):
        return remote(far_slot(p, k), far_slot(p, k), a_send.at[p], a_recv.at[p], sib_dev)

    def own_copy(p):
        at = pl.ds(pl.multiple_of(p * piece, piece), piece)
        slot = left_full.at[pl.ds(pl.multiple_of(r * rows + p * piece, piece), piece), :]
        return remote(left_ref.at[at, :], slot, own_send.at[p], own_recv.at[p], sib_dev)

    def own_arrived(p):
        other = r + 1 - 2 * k
        arrived(left_full.at[pl.ds(pl.multiple_of(other * rows + p * piece, piece), piece), :], own_recv.at[p])

    def y_slot(side, pos, p, core):
        at = 3 * side if pos == 0 else 1 + side
        return left_full.at[block(at, p * piece, piece), pl.ds(pl.multiple_of(core * half, half), half)]

    def y_copy(pos, p, own=False):
        slot = y_slot(yc, pos, p, k)
        source = left_ref.at[pl.ds(pl.multiple_of(p * piece, piece), piece), own_half()] if own else slot
        return remote(source, slot, y_send.at[pos, p], y_recv.at[pos, p], y_dev)

    def s_copy(pos, p):
        slot = y_slot(1 - yc, pos, p, k)
        return remote(slot, slot, s_send.at[pos, p], s_recv.at[pos, p], sib_dev)

    def part_copy(q):
        return remote(part.at[q], part.at[q], p_send.at[q], p_recv.at[q], z_dev(1))

    def each(body, first=0, last=steps):
        def step(at, carry):
            body(at)
            return carry

        lax.fori_loop(first, last, step, 0)

    first = kc == yc
    when(first)(lambda: each(lambda p: y_copy(0, p, True).start()))

    @when(inner)
    def _():
        @each
        def _(q):
            in_copy(-1, q).start()
            in_copy(1, q).start()

    when(end)(lambda: each(lambda q: end_copy(q).start(), 0, early))
    own_left = pltpu.make_async_copy(left_ref, left_full.at[pl.ds(pl.multiple_of(r * rows, rows), rows), :], own_sem.at[0])
    own = pltpu.make_async_copy(right_ref, right_full.at[block(zc), :], own_sem.at[1])
    weights = pltpu.make_async_copy(w_hbm, w_in, own_sem.at[2])
    counts_copy = pltpu.make_async_copy(counts_ref, counts_in, own_sem.at[3])
    each(lambda p: own_copy(p).start())
    for copy in (own_left, own, weights, counts_copy):
        copy.start()

    @each
    def _(p):
        own_arrived(p)
        when(jnp.logical_not(first))(lambda: y_copy(0, p).start())
        when(end, yc == 0, kc == 1)(lambda: far_copy(p).start())

    own_left.wait()
    when(end, yc == 0, kc == 0)(lambda: each(lambda p: far_copy(p).start()))
    each(lambda p: y_copy(1, p).start())
    when(end, yc == 0)(lambda: each(lambda q: end_copy(q).start(), early))

    row = lax.broadcasted_iota(jnp.int32, (TILE, TILE), 0)
    column = lax.broadcasted_iota(jnp.int32, (TILE, TILE), 1)
    order[...] = jnp.where(column == (row % heads) * CH + row // heads, 1.0, 0.0).astype(order.dtype)
    weights.wait()
    w_wide[...] = w_in[...].astype(jnp.float32)
    for e in range(CH):
        w_ref[pl.ds(e * CH, CH), :] = w_wide[pl.ds(e, CH, stride=CH), :].astype(w_ref.dtype)
    counts_copy.wait()
    counted = counts_in[...].astype(jnp.float32)
    for i in range(counted.shape[1]):
        cover[i // 4, i % 4] = jnp.broadcast_to(counted[:, i:i + 1], (counted.shape[0], cover.shape[3]))

    def turn(at, q):
        value = lax.dot_general(order[...], right_full[block(at), cols(q)], (((1,), (1,)), ((), ())), preferred_element_type=jnp.float32)
        right_t[cols(q), block(at)] = value.astype(right_t.dtype)

    def product(into, lines, source, left, left_rows, size, wide, add):
        for n in range(width_l // wide):
            value = jnp.dot(right_t[lines, source], left[left_rows, pl.ds(n * wide, wide)], preferred_element_type=jnp.float32)
            for one in range(wide // 128):
                some = value[:, one * 128:(one + 1) * 128]
                slab = n * (wide // 128) + one
                into[slab, size, :] = into[slab, size, :] + some if add else some

    def product_all(at, add, first=0, depth=rows):
        every = pl.ds(0, width_r)
        product(acc, every, block(at, first, depth), left_full, block(at, first, depth), every, 256, add)

    def product_one(at, q):
        product(acc, cols(q), block(at), left_full, block(at), cols(q), 512, True)

    def project(source, first_row):
        for eq in range(CH // 4):
            tiles = []
            for e in range(4):
                tile = source[:, pl.ds(pl.multiple_of(first_row + (eq * 4 + e) * heads, heads), heads), :]
                tiles.append(tile.reshape(quads * heads, 128).astype(flat.dtype))
            for i, value in enumerate(lane_quads(tiles)):
                flat[pl.ds(i * quads * heads, quads * heads), pl.ds(eq * 128, 128)] = value
        return jnp.dot(flat[...], w_ref[...], preferred_element_type=jnp.float32)

    def settle(q, add):
        for i in range(4):
            value = out_v[q, :, i]
            if add:
                more = part[q, pl.ds(i * quads * heads, quads * heads), :]
                value = value + more.astype(jnp.float32).reshape(value.shape)
            out_v[q, :, i] = value / cover[:, i, pl.ds(pl.multiple_of(q * heads, heads), heads), :]
        out_copy(q).start()

    def out_copy(q):
        at = pl.ds(pl.multiple_of(q * heads, heads), heads)
        return pltpu.make_async_copy(out_v.at[q].reshape(4 * quads, heads, 128), out_ref.at[:, at, :], out_sem.at[q])

    own.wait()
    each(lambda q: turn(zc, q))

    def end_arrived(q):
        arrived(right_slot(3, q), end_recv.at[q])
        fwd_copy(-1, q).start()
        turn(3, q)

    def share(p):
        arrived(far_slot(p, k), far_recv.at[p])
        share_copy(p).start()

    @each
    def _(p):
        arrived(y_slot(1 - yc, 0, p, k), y_recv.at[0, p])
        s_copy(0, p).start()
        when(end, yc == 1)(lambda: far_copy(p).start())
        arrived(right_slot(zc - 1, p), in_recv.at[0, p])
        when(inner)(lambda: fwd_copy(1, p).start())
        turn(zc - 1, p)
        when(inner, p >= 1, p <= early)(lambda: end_arrived(p - 1))

    when(end, yc == 1)(lambda: each(lambda q: end_copy(q).start(), early))
    when(inner)(lambda: each(share, 0, early))
    each(lambda p: arrived(y_slot(1 - yc, 0, p, 1 - k), s_recv.at[0, p]))
    is_inner = 3 - zc
    product_all(is_inner * (1 + yc) + (1 - is_inner) * 3, False)
    near, late = is_inner * 3 + (1 - is_inner) * (1 + yc), 2 - yc

    def far(q):
        arrived(right_slot(0, q), in_recv.at[1, q])
        turn(0, q)
        product(acc_far, cols(q), block(0), left_far, pl.ds(0, rows), pl.ds(0, TILE), 512, False)
        part[q] = project(acc_far, 0).astype(part.dtype)
        part_copy(q).start()
        product_one(0, q)

    def late_half(at):
        each(lambda p: arrived(y_slot(1 - yc, 1, p, 1 - k), s_recv.at[1, p]), at * steps // 2, (at + 1) * steps // 2)
        product_all(late, True, at * (rows // 2), rows // 2)

    @each
    def _(q):
        when(inner, q >= early)(lambda: end_arrived(q))
        arrived(y_slot(1 - yc, 1, q, k), y_recv.at[1, q])
        s_copy(1, q).start()
        when(inner, q < steps - early)(lambda: share(q + early))

        @when(end)
        def _():
            arrived(right_slot(1, q), in_recv.at[1, q])
            turn(1, q)

        product_one(near, q)
        when(inner, q == steps - early - 1)(lambda: each(lambda p: arrived(far_slot(p, 1 - k), a_recv.at[p])))
        when(inner, q >= 1)(lambda: far(q - 1))
        when(inner, q == early)(lambda: late_half(0))

    when(end)(lambda: late_half(0))
    late_half(1)

    @each
    def _(q):
        when(inner, q == 1)(lambda: far(steps - 1))
        value = project(acc, q * TILE)
        for i in range(4):
            out_v[q, :, i] = value[i * quads * heads:(i + 1) * quads * heads].reshape(quads, heads, 128)
        when(inner)(lambda: settle(q, False))

    @when(end)
    def _():
        @each
        def _(q):
            arrived(part.at[q], p_recv.at[q])
            settle(q, True)

    @each
    def _(q):
        own_copy(q).wait_send()
        for pos in range(2):
            y_copy(pos, q).wait_send()
            s_copy(pos, q).wait_send()

        @when(inner)
        def _():
            for way in (-1, 1):
                in_copy(way, q).wait_send()
                fwd_copy(way, q).wait_send()
            share_copy(q).wait_send()
            part_copy(q).wait_send()

        @when(end)
        def _():
            end_copy(q).wait_send()
            far_copy(q).wait_send()

        out_copy(q).wait()


def folded_call(left_act, right_act, counts, w_out):
    rows, width_l = left_act.shape
    width_r = right_act.shape[1]
    left_dev, right_dev = counts.shape
    pair = w_out.shape[1]
    steps = width_r // TILE
    heads = TILE // CH
    full = 4 * rows
    dma = pltpu.SemaphoreType.DMA
    return pl.pallas_call(
        folded,
        out_shape=jax.ShapeDtypeStruct((left_dev, right_dev, pair), jnp.float32),
        in_specs=[pl.BlockSpec(memory_space=pl.ANY)] * 4,
        out_specs=pl.BlockSpec(memory_space=pl.ANY),
        scratch_shapes=[
            pltpu.VMEM(w_out.shape, w_out.dtype),
            pltpu.VMEM(w_out.shape, jnp.float32),
            pltpu.VMEM(w_out.shape, w_out.dtype),
            pltpu.VMEM((right_dev, left_dev), counts.dtype),
            pltpu.VMEM((left_dev // 4, 4, right_dev, pair), jnp.float32),
            pltpu.VMEM((TILE, TILE), jnp.bfloat16),
            pltpu.VMEM((full, width_l), jnp.bfloat16),
            pltpu.VMEM((rows, width_l), jnp.bfloat16),
            pltpu.VMEM((full, width_r), jnp.bfloat16),
            pltpu.VMEM((width_r, full), jnp.bfloat16),
            pltpu.VMEM((width_l // 128, width_r, 128), jnp.float32),
            pltpu.VMEM((width_l // 128, TILE, 128), jnp.float32),
            pltpu.VMEM((left_dev * heads, CH * CH), jnp.bfloat16),
            pltpu.VMEM((steps, left_dev * heads, pair), jnp.bfloat16),
            pltpu.VMEM((steps, left_dev // 4, 4, heads, pair), jnp.float32),
            dma((2, steps)), dma((2, steps)), dma((2, steps)), dma((steps,)), dma((steps,)), dma((steps,)), dma((steps,)), dma((steps,)),
            dma((steps,)), dma((2, steps)), dma((2, steps)), dma((2, steps)), dma((2, steps)), dma((steps,)), dma((steps,)), dma((steps,)),
            dma((steps,)), dma((4,)), dma((steps,)),
        ],
        compiler_params=pltpu.CompilerParams(collective_id=0, has_side_effects=True, vmem_limit_bytes=56 * 1024 * 1024),
        name="pair_mean",
    )(left_act, right_act, counts.T, w_out)


def solution(mesh):
    n_z, n_r = mesh.shape["left"], mesh.shape["right"]
    n_y = n_r // CORES

    def shards(left_act, right_act, counts, w_out):
        if (n_z, n_y) == (4, 2):
            return folded_call(left_act, right_act, counts, w_out)
        rows_l, width_l = left_act.shape
        rows_r, width_r = right_act.shape
        seqs = rows_r * n_z
        left_dev, right_dev = counts.shape
        pair = w_out.shape[1]
        q_z = width_r // 256
        q_y = rows_l // max(128, rows_l // 4)
        projected = pl.pallas_call(
            functools.partial(kernel, (n_z, n_r, q_z, q_y)),
            out_shape=jax.ShapeDtypeStruct((left_dev, right_dev, pair), jnp.float32),
            in_specs=[pl.BlockSpec(memory_space=pl.ANY)] * 4,
            out_specs=pl.BlockSpec(memory_space=pl.ANY),
            scratch_shapes=[
                pltpu.VMEM(w_out.shape, w_out.dtype),
                pltpu.VMEM(counts.shape, counts.dtype),
                pltpu.VMEM((right_dev, left_dev, pair), jnp.float32),
                pltpu.VMEM((q_z, left_dev, right_dev // q_z, pair), jnp.float32),
                pltpu.VMEM((seqs, width_l), jnp.bfloat16),
                pltpu.VMEM((seqs, width_r), jnp.bfloat16),
                pltpu.VMEM((width_l, seqs), jnp.bfloat16),
                pltpu.VMEM((width_r // 128, width_l, 128), jnp.float32),
                pltpu.VMEM((width_r // q_z // CH * left_dev, CH * CH), jnp.bfloat16),
                pltpu.SemaphoreType.DMA((2, (n_z - 1) * q_z)),
                pltpu.SemaphoreType.DMA((2, (n_z - 1) * q_z)),
                pltpu.SemaphoreType.DMA((2, (n_y - 1) * q_y)),
                pltpu.SemaphoreType.DMA((2, (n_y - 1) * q_y)),
                pltpu.SemaphoreType.DMA(((2 * n_y - 1) * q_y,)),
                pltpu.SemaphoreType.DMA(((2 * n_y - 1) * q_y,)),
                pltpu.SemaphoreType.DMA((4,)),
                pltpu.SemaphoreType.DMA((q_z,)),
            ],
            compiler_params=pltpu.CompilerParams(
                collective_id=0, has_side_effects=True, vmem_limit_bytes=56 * 1024 * 1024
            ),
            name="pair_mean",
        )(left_act, right_act, counts, w_out)
        return projected

    in_specs = (
        P(("groups", "right"), "left"),
        P(("groups", "left"), "right"),
        P(("groups", "left"), "right"),
        P(),
    )
    out_specs = P(("groups", "left"), "right", None)
    return jax.shard_map(shards, mesh=mesh, in_specs=in_specs, out_specs=out_specs, check_vma=False)
```

```python
import functools

import jax
import jax.numpy as jnp
from jax import lax
from jax.experimental import pallas as pl
from jax.experimental.pallas import tpu as pltpu
from jax.sharding import PartitionSpec as P

CH = 32
CORES = 2
TILE = 256
MESH = pl.DeviceIdType.MESH


def lane_quads(tiles):
    lane = lax.broadcasted_iota(jnp.int32, tiles[0].shape, 1)
    low = lane < 64
    even = (lane % 64) < 32
    stage = [None] * 4
    for c in range(2):
        a, b = tiles[c], tiles[c + 2]
        stage[c] = jnp.where(low, a, pltpu.roll(b, 64, 1))
        stage[c + 2] = jnp.where(low, pltpu.roll(a, 64, 1), b)
    outs = [None] * 4
    for half in range(2):
        a, b = stage[2 * half], stage[2 * half + 1]
        outs[2 * half] = jnp.where(even, a, pltpu.roll(b, 32, 1))
        outs[2 * half + 1] = jnp.where(even, pltpu.roll(a, 96, 1), b)
    return outs


def kernel(sizes, left_ref, right_ref, counts_ref, w_hbm, out_ref, w_ref, counts_in, cover, out_v, left_full, right_full, left_t, acc, flat,
           z_send, z_recv, y_send, y_recv, s_send, s_recv, own_sem, out_sem):
    n_z, n_r, q_z, q_y = sizes
    n_y = n_r // CORES
    rows_l, width_l = left_ref.shape
    rows_r, width_r = right_ref.shape
    piece_r = width_r // q_z
    piece_l = rows_l // q_y
    left_dev = width_l // CH
    right_dev = width_r // CH
    seqs = left_t.shape[1]
    z = lax.axis_index("left")
    r = lax.axis_index("right")
    y = r // CORES
    k = r % CORES

    def z_dev(pos):
        return {"left": pos}

    def y_dev(pos):
        return {"right": pos * CORES + k}

    sib_dev = {"right": y * CORES + (1 - k)}

    barrier = pltpu.get_barrier_semaphore()

    def greet(dev):
        pl.semaphore_signal(barrier, inc=1, device_id=dev, device_id_type=MESH)

    greet(sib_dev)
    for pos, n, dev in ((z, n_z, z_dev), (y, n_y, y_dev)):
        pl.when(pos + 1 < n)(functools.partial(greet, dev(pos + 1)))
        pl.when(pos >= 1)(functools.partial(greet, dev(pos - 1)))
    total = 1 + (z + 1 < n_z).astype(jnp.int32) + (z >= 1).astype(jnp.int32)
    total = total + (y + 1 < n_y).astype(jnp.int32) + (y >= 1).astype(jnp.int32)
    pl.semaphore_wait(barrier, total)

    def z_slot(chunk, q):
        return right_full.at[pl.ds(pl.multiple_of(chunk * rows_r, rows_r), rows_r), pl.ds(q * piece_r, piece_r)]

    def z_copy(side, step, q):
        sign = 1 - 2 * side
        chunk = z - sign * step
        src = right_ref.at[:, pl.ds(q * piece_r, piece_r)] if step == 0 else z_slot(chunk, q)
        at = step * q_z + q
        return pltpu.make_async_remote_copy(
            src_ref=src, dst_ref=z_slot(chunk, q), send_sem=z_send.at[side, at], recv_sem=z_recv.at[side, at],
            device_id=z_dev(z + sign), device_id_type=MESH)

    def z_sends(side, step):
        near = z + 1 < n_z if side == 0 else z >= 1
        far = z - step >= 0 if side == 0 else z + step < n_z
        return jnp.logical_and(near, far)

    def z_arrives(side, step):
        return z - step - 1 >= 0 if side == 0 else z + step + 1 < n_z

    def z_wait(side, step, q):
        sign = 1 - 2 * side
        slot = z_slot(z - sign * (step + 1), q)
        pltpu.make_async_copy(slot, slot, z_recv.at[side, step * q_z + q]).wait()

    def l_slot(chunk, q):
        return left_full.at[pl.ds(pl.multiple_of(chunk * rows_l + q * piece_l, piece_l), piece_l), :]

    def l_own(q):
        return left_ref.at[pl.ds(q * piece_l, piece_l), :]

    def y_copy(side, step, q):
        sign = 1 - 2 * side
        chunk = (y - sign * step) * CORES + k
        at = step * q_y + q
        return pltpu.make_async_remote_copy(
            src_ref=l_own(q) if step == 0 else l_slot(chunk, q), dst_ref=l_slot(chunk, q),
            send_sem=y_send.at[side, at], recv_sem=y_recv.at[side, at],
            device_id=y_dev(y + sign), device_id_type=MESH)

    def y_sends(side, step):
        near = y + 1 < n_y if side == 0 else y >= 1
        far = y - step >= 0 if side == 0 else y + step < n_y
        return jnp.logical_and(near, far)

    def y_arrives(side, step):
        return y - step - 1 >= 0 if side == 0 else y + step + 1 < n_y

    def y_wait(side, step, q):
        sign = 1 - 2 * side
        slot = l_slot((y - sign * (step + 1)) * CORES + k, q)
        pltpu.make_async_copy(slot, slot, y_recv.at[side, step * q_y + q]).wait()

    def s_at(side, step, q):
        if step < 0:
            return q
        return (1 + side * (n_y - 1) + step) * q_y + q

    def s_copy(side, step, q):
        sign = 1 - 2 * side
        chunk = (y - sign * (step + 1)) * CORES + k if step >= 0 else r
        at = s_at(side, step, q)
        return pltpu.make_async_remote_copy(
            src_ref=l_own(q) if step < 0 else l_slot(chunk, q), dst_ref=l_slot(chunk, q),
            send_sem=s_send.at[at], recv_sem=s_recv.at[at],
            device_id=sib_dev, device_id_type=MESH)

    def s_wait(side, step, q):
        sign = 1 - 2 * side
        y_from = y - sign * (step + 1) if step >= 0 else y
        slot = l_slot(y_from * CORES + (1 - k), q)
        pltpu.make_async_copy(slot, slot, s_recv.at[s_at(side, step, q)]).wait()

    tile = 256

    def turn(src, first_row, chunk, q):
        col = pl.multiple_of(chunk * rows_l + q * piece_l, piece_l)

        def body(m, carry):
            at = pl.multiple_of(m * tile, tile)
            left_t[pl.ds(at, tile), pl.ds(col, piece_l)] = src[pl.ds(first_row, piece_l), pl.ds(at, tile)].T
            return carry

        lax.fori_loop(0, width_l // tile, body, 0)

    def turn_full(chunk, q):
        turn(left_full, pl.multiple_of(chunk * rows_l + q * piece_l, piece_l), chunk, q)

    for q in range(max(q_z, q_y)):
        for side in range(2):
            if q < q_z:
                pl.when(z_sends(side, 0))(lambda side=side, q=q: z_copy(side, 0, q).start())
            if q < q_y:
                pl.when(y_sends(side, 0))(lambda side=side, q=q: y_copy(side, 0, q).start())
    own_left = pltpu.make_async_copy(left_ref, left_full.at[pl.ds(pl.multiple_of(r * rows_l, rows_l), rows_l), :], own_sem.at[0])
    own = pltpu.make_async_copy(right_ref, right_full.at[pl.ds(pl.multiple_of(z * rows_r, rows_r), rows_r), :], own_sem.at[1])
    weights = pltpu.make_async_copy(w_hbm, w_ref, own_sem.at[2])
    counts_copy = pltpu.make_async_copy(counts_ref, counts_in, own_sem.at[3])
    for copy in (own_left, own, weights, counts_copy):
        copy.start()
    for q in range(q_y):
        s_copy(0, -1, q).start()
    own_left.wait()
    for q in range(q_y):
        turn_full(r, q)
    counts_copy.wait()
    counted = counts_in[...].astype(jnp.float32)
    for j in range(right_dev):
        cover[j] = jnp.broadcast_to(counted[:, j:j + 1], (left_dev, cover.shape[2]))
    for q in range(q_y):
        s_wait(0, -1, q)
        turn_full(y * CORES + (1 - k), q)

    def z_tick(step, q):
        for side in range(2):
            @pl.when(z_arrives(side, step))
            def _():
                z_wait(side, step, q)
                if step + 1 < n_z - 1:
                    pl.when(z_sends(side, step + 1))(lambda: z_copy(side, step + 1, q).start())

    def y_tick(step, q):
        for side in range(2):
            @pl.when(y_arrives(side, step))
            def _():
                y_wait(side, step, q)
                s_copy(side, step, q).start()
                if step + 1 < n_y - 1:
                    pl.when(y_sends(side, step + 1))(lambda: y_copy(side, step + 1, q).start())

        for side in range(2):
            @pl.when(y_arrives(side, step))
            def _():
                sign = 1 - 2 * side
                y_from = y - sign * (step + 1)
                turn_full(y_from * CORES + k, q)
                s_wait(side, step, q)
                turn_full(y_from * CORES + (1 - k), q)

    y_ticks = [(step, q) for step in range(n_y - 1) for q in range(q_y)]
    for t in range((n_z - 2) * q_z):
        z_tick(t // q_z, t % q_z)
        if t % 2 == 1 and y_ticks:
            y_tick(*y_ticks.pop(0))
    for tick in y_ticks:
        y_tick(*tick)
    own.wait()
    weights.wait()

    block = 1024
    at_end = jnp.logical_or(z == 0, z == n_z - 1)
    base = jnp.where(z == 0, 0, rows_r)
    base = pl.multiple_of(base, rows_r)

    def product(q, first, depth, add):
        cols = pl.ds(q * piece_r, piece_r)

        def body(m, carry):
            rows = pl.ds(pl.multiple_of(m * block, block), block)
            value = jnp.dot(left_t[rows, pl.ds(first, depth)], right_full[pl.ds(first, depth), cols],
                            preferred_element_type=jnp.float32)
            for part in range(piece_r // 128):
                some = value[:, part * 128:(part + 1) * 128]
                slab = q * (piece_r // 128) + part
                acc[slab, rows, :] = acc[slab, rows, :] + some if add else some
            return carry

        lax.fori_loop(0, width_l // block, body, 0)

    def first_part(q):
        @pl.when(at_end)
        def _():
            product(q, base, seqs - rows_r, False)

        @pl.when(jnp.logical_not(at_end))
        def _():
            product(q, 0, seqs, False)

    for q in range(q_z):
        first_part(q)

    def finish(q):
        heads = piece_r // CH
        for quad in range(heads // 4):
            slab = acc.at[q * (piece_r // 128) + quad]
            for cq in range(CH // 4):
                tiles = [slab[pl.ds(cq * 4 + c, left_dev, stride=CH), :].astype(jnp.bfloat16) for c in range(4)]
                for j, value in enumerate(lane_quads(tiles)):
                    flat[pl.ds((quad * 4 + j) * left_dev, left_dev), pl.ds(cq * 128, 128)] = value
        projected = jnp.dot(flat[...], w_ref[...], preferred_element_type=jnp.float32)
        for j in range(heads):
            value = projected[j * left_dev:(j + 1) * left_dev, :] / cover[q * heads + j]
            out_v.at[q].reshape(left_dev * heads, value.shape[1])[pl.ds(j, left_dev, stride=heads), :] = value
        out_copy(q).start()

    def out_copy(q):
        return pltpu.make_async_copy(out_v.at[q], out_ref.at[:, pl.ds(q * heads_q, heads_q), :], out_sem.at[q])

    heads_q = piece_r // CH
    last = n_z - 2
    for q in range(q_z):
        z_tick(last, q)

        @pl.when(at_end)
        def _():
            far = jnp.where(z == 0, (n_z - 1) * rows_r, 0)
            product(q, pl.multiple_of(far, rows_r), rows_r, True)

        finish(q)

    for side in range(2):
        for step in range(n_z - 1):
            for q in range(q_z):
                pl.when(z_sends(side, step))(lambda side=side, step=step, q=q: z_copy(side, step, q).wait_send())
        for step in range(n_y - 1):
            for q in range(q_y):
                pl.when(y_sends(side, step))(lambda side=side, step=step, q=q: y_copy(side, step, q).wait_send())
                pl.when(y_arrives(side, step))(lambda side=side, step=step, q=q: s_copy(side, step, q).wait_send())
    for q in range(q_y):
        s_copy(0, -1, q).wait_send()
    for q in range(q_z):
        out_copy(q).wait()


def folded(left_ref, right_ref, counts_ref, w_hbm, out_ref, w_in, w_wide, w_ref, counts_in, cover, order, left_full, left_far, right_full, right_t,
           acc, acc_far, flat, part, out_v, in_send, in_recv, fwd_send, mid_send, mid_recv, far_send, far_recv, end_send, end_recv, own_send, own_recv,
           y_send, y_recv, s_send, s_recv, a_send, a_recv, p_send, p_recv, own_sem):
    rows, width_l = left_ref.shape
    width_r = right_ref.shape[1]
    steps = width_r // TILE
    piece = rows // steps
    half = width_l // CORES
    quads = width_l // 128
    heads = TILE // CH
    early = steps // 2
    z = lax.axis_index("left")
    r = lax.axis_index("right")
    y, k = r // CORES, r % CORES
    up = z // 2
    sign = 2 * up - 1

    def fold(n, at):
        return up * at + (1 - up) * (n - 1 - at)

    zc, yc, kc = fold(4, z), fold(2, y), fold(2, k)
    inner, end = zc == 2, zc == 3
    sib_dev = {"right": r + 1 - 2 * k}
    y_dev = {"right": r + (1 - 2 * y) * CORES}

    def when(*terms):
        value = terms[0]
        for term in terms[1:]:
            value = jnp.logical_and(value, term)
        return pl.when(value)

    def z_dev(way):
        return {"left": z + way * sign}

    barrier = pltpu.get_barrier_semaphore()

    def greet(dev):
        pl.semaphore_signal(barrier, inc=1, device_id=dev, device_id_type=MESH)

    greet(sib_dev)
    greet(y_dev)
    greet(z_dev(-1))
    when(inner)(lambda: greet(z_dev(1)))
    pl.semaphore_wait(barrier, 3 + inner.astype(jnp.int32))

    def remote(src, dst, send, recv, dev):
        return pltpu.make_async_remote_copy(src_ref=src, dst_ref=dst, send_sem=send, recv_sem=recv, device_id=dev, device_id_type=MESH)

    def arrived(slot, sem):
        pltpu.make_async_copy(slot, slot, sem).wait()

    def block(at, first=0, size=rows):
        return pl.ds(pl.multiple_of(fold(4, at) * rows + first, size), size)

    def cols(q):
        return pl.ds(pl.multiple_of(q * TILE, TILE), TILE)

    def right_slot(at, q):
        return right_full.at[block(at), cols(q)]

    def in_copy(way, q):
        return remote(right_ref.at[:, cols(q)], right_slot(2, q), in_send.at[(way + 1) // 2, q], in_recv.at[0, q], z_dev(way))

    def fwd_copy(q):
        slot = right_slot(1, q)
        return remote(slot, slot, fwd_send.at[q], in_recv.at[1, q], z_dev(1))

    def half_slot(at, q, h):
        return right_full.at[block(at, h * (rows // 2), rows // 2), cols(q)]

    def mid_copy(q, h):
        slot = half_slot(3, q, h)
        return remote(slot, slot, mid_send.at[q, h], mid_recv.at[q, h], z_dev(-1))

    def end_copy(q, h):
        source = right_ref.at[pl.ds(h * (rows // 2), rows // 2), cols(q)]
        return remote(source, half_slot(3, q, h), end_send.at[q, h], end_recv.at[q, h], z_dev(-1))

    def end_start(q):
        for h in range(2):
            end_copy(q, h).start()

    def own_half():
        return pl.ds(pl.multiple_of(k * half, half), half)

    def far_copy(p):
        at = pl.ds(pl.multiple_of(p * piece, piece), piece)
        return remote(left_full.at[block(0, p * piece, piece), own_half()], left_far.at[at, own_half()], far_send.at[p], far_recv.at[p], z_dev(-1))

    def far_slot(p, core):
        return left_far.at[pl.ds(pl.multiple_of(p * piece, piece), piece), pl.ds(pl.multiple_of(core * half, half), half)]

    def share_copy(p):
        return remote(far_slot(p, k), far_slot(p, k), a_send.at[p], a_recv.at[p], sib_dev)

    def own_copy(p):
        at = pl.ds(pl.multiple_of(p * piece, piece), piece)
        slot = left_full.at[pl.ds(pl.multiple_of(r * rows + p * piece, piece), piece), :]
        return remote(left_ref.at[at, :], slot, own_send.at[p], own_recv.at[p], sib_dev)

    def own_arrived(p):
        other = r + 1 - 2 * k
        arrived(left_full.at[pl.ds(pl.multiple_of(other * rows + p * piece, piece), piece), :], own_recv.at[p])

    def y_slot(side, pos, p, core):
        at = 3 * side if pos == 0 else 1 + side
        return left_full.at[block(at, p * piece, piece), pl.ds(pl.multiple_of(core * half, half), half)]

    def y_copy(pos, p, own=False):
        slot = y_slot(yc, pos, p, k)
        source = left_ref.at[pl.ds(pl.multiple_of(p * piece, piece), piece), own_half()] if own else slot
        return remote(source, slot, y_send.at[pos, p], y_recv.at[pos, p], y_dev)

    def s_copy(pos, p):
        slot = y_slot(1 - yc, pos, p, k)
        return remote(slot, slot, s_send.at[pos, p], s_recv.at[pos, p], sib_dev)

    def part_copy(q):
        return remote(part.at[q], part.at[q], p_send.at[q], p_recv.at[q], z_dev(1))

    def each(body, first=0, last=steps):
        def step(at, carry):
            body(at)
            return carry

        lax.fori_loop(first, last, step, 0)

    first = kc == yc
    when(first)(lambda: each(lambda p: y_copy(0, p, True).start()))

    @when(inner)
    def _():
        @each
        def _(q):
            in_copy(-1, q).start()
            in_copy(1, q).start()

    when(end)(lambda: each(end_start, 0, early))
    own_left = pltpu.make_async_copy(left_ref, left_full.at[pl.ds(pl.multiple_of(r * rows, rows), rows), :], own_sem.at[0])
    own = pltpu.make_async_copy(right_ref, right_full.at[block(zc), :], own_sem.at[1])
    weights = pltpu.make_async_copy(w_hbm, w_in, own_sem.at[2])
    counts_copy = pltpu.make_async_copy(counts_ref, counts_in, own_sem.at[3])
    each(lambda p: own_copy(p).start())
    for copy in (own_left, own, weights, counts_copy):
        copy.start()

    @each
    def _(p):
        own_arrived(p)
        when(jnp.logical_not(first))(lambda: y_copy(0, p).start())
        when(end, yc == 0, kc == 1)(lambda: far_copy(p).start())

    own_left.wait()
    when(end, yc == 0, kc == 0)(lambda: each(lambda p: far_copy(p).start()))
    each(lambda p: y_copy(1, p).start())
    when(end, yc == 0)(lambda: each(end_start, early))

    row = lax.broadcasted_iota(jnp.int32, (TILE, TILE), 0)
    column = lax.broadcasted_iota(jnp.int32, (TILE, TILE), 1)
    order[...] = jnp.where(column == (row % heads) * CH + row // heads, 1.0, 0.0).astype(order.dtype)
    weights.wait()
    w_wide[...] = w_in[...].astype(jnp.float32)
    for e in range(CH):
        w_ref[pl.ds(e * CH, CH), :] = w_wide[pl.ds(e, CH, stride=CH), :].astype(w_ref.dtype)
    counts_copy.wait()
    counted = counts_in[...].astype(jnp.float32)
    for i in range(counted.shape[1]):
        cover[i // 4, i % 4] = jnp.broadcast_to(counted[:, i:i + 1], (counted.shape[0], cover.shape[3]))

    def turn(at, q):
        value = lax.dot_general(order[...], right_full[block(at), cols(q)], (((1,), (1,)), ((), ())), preferred_element_type=jnp.float32)
        right_t[cols(q), block(at)] = value.astype(right_t.dtype)

    def product(into, lines, source, left, left_rows, size, wide, add):
        for n in range(width_l // wide):
            value = jnp.dot(right_t[lines, source], left[left_rows, pl.ds(n * wide, wide)], preferred_element_type=jnp.float32)
            for one in range(wide // 128):
                some = value[:, one * 128:(one + 1) * 128]
                slab = n * (wide // 128) + one
                into[slab, size, :] = into[slab, size, :] + some if add else some

    def product_all(at, add, first=0, depth=rows):
        every = pl.ds(0, width_r)
        product(acc, every, block(at, first, depth), left_full, block(at, first, depth), every, 256, add)

    def product_one(at, q):
        product(acc, cols(q), block(at), left_full, block(at), cols(q), 512, True)

    def project(source, first_row):
        for eq in range(CH // 4):
            tiles = []
            for e in range(4):
                tile = source[:, pl.ds(pl.multiple_of(first_row + (eq * 4 + e) * heads, heads), heads), :]
                tiles.append(tile.reshape(quads * heads, 128).astype(flat.dtype))
            for i, value in enumerate(lane_quads(tiles)):
                flat[pl.ds(i * quads * heads, quads * heads), pl.ds(eq * 128, 128)] = value
        return jnp.dot(flat[...], w_ref[...], preferred_element_type=jnp.float32)

    def settle(q, add):
        for i in range(4):
            value = out_v[q, :, i]
            if add:
                more = part[q, pl.ds(i * quads * heads, quads * heads), :]
                value = value + more.astype(jnp.float32).reshape(value.shape)
            at = pl.ds(pl.multiple_of(q * heads, heads), heads)
            out_ref[pl.ds(i, quads, stride=4), at, :] = value / cover[:, i, at, :]

    own.wait()
    each(lambda q: turn(zc, q))

    def pass_on(q, h):
        arrived(half_slot(3, q, h), end_recv.at[q, h])
        mid_copy(q, h).start()

    def end_arrived(q):
        for h in range(2):
            pass_on(q, h)
        turn(3, q)

    def share(p):
        arrived(far_slot(p, k), far_recv.at[p])
        share_copy(p).start()

    @each
    def _(p):
        arrived(y_slot(1 - yc, 0, p, k), y_recv.at[0, p])
        s_copy(0, p).start()
        when(end, yc == 1)(lambda: far_copy(p).start())
        arrived(right_slot(zc - 1, p), in_recv.at[0, p])
        when(inner)(lambda: fwd_copy(p).start())
        turn(zc - 1, p)
        when(inner, p >= 1, p <= early)(lambda: end_arrived(p - 1))

    when(end, yc == 1)(lambda: each(end_start, early))
    each(lambda p: arrived(y_slot(1 - yc, 0, p, 1 - k), s_recv.at[0, p]))
    late = 2 - yc

    def y_arrived(p):
        arrived(y_slot(1 - yc, 1, p, k), y_recv.at[1, p])
        s_copy(1, p).start()

    def late_half(at):
        each(lambda p: arrived(y_slot(1 - yc, 1, p, 1 - k), s_recv.at[1, p]), at * steps // 2, (at + 1) * steps // 2)
        product_all(late, True, at * (rows // 2), rows // 2)

    def far_product(q):
        for h in range(2):
            arrived(half_slot(0, q, h), mid_recv.at[q, h])
        turn(0, q)
        product(acc_far, cols(q), block(0), left_far, pl.ds(0, rows), pl.ds(0, TILE), 512, False)

    def far_send_on(q):
        part[q] = project(acc_far, 0).astype(part.dtype)
        part_copy(q).start()

    def finish(q):
        value = project(acc, q * TILE)
        for i in range(4):
            out_v[q, :, i] = value[i * quads * heads:(i + 1) * quads * heads].reshape(quads, heads, 128)

    def sent(q):
        own_copy(q).wait_send()
        for pos in range(2):
            y_copy(pos, q).wait_send()
            s_copy(pos, q).wait_send()

    @when(inner)
    def _():
        each(share, 0, early)
        product_all(1 + yc, False)
        each(lambda q: product_one(3, q), 0, early)
        each(y_arrived, 0, early - 1)
        each(share, early)
        y_arrived(early - 1)
        each(lambda p: arrived(far_slot(p, 1 - k), a_recv.at[p]))
        for q in range(early):
            far_product(q)
            far_send_on(q)
            pass_on(early, q)
            product_one(0, q)
        turn(3, early)
        y_arrived(early)
        product_one(3, early)
        pass_on(early + 1, 0)
        late_half(0)
        far_product(early)
        pass_on(early + 1, 1)
        far_send_on(early)
        y_arrived(early + 1)
        turn(3, early + 1)
        product_one(3, early + 1)
        product_one(0, early)
        late_half(1)
        far_product(early + 1)
        far_send_on(early + 1)
        product_one(0, early + 1)

        @each
        def _(q):
            finish(q)
            settle(q, False)

        @each
        def _(q):
            sent(q)
            for way in (-1, 1):
                in_copy(way, q).wait_send()
            fwd_copy(q).wait_send()
            for h in range(2):
                mid_copy(q, h).wait_send()
            share_copy(q).wait_send()
            part_copy(q).wait_send()

    @when(end)
    def _():
        product_all(3, False)

        @each
        def _(q):
            y_arrived(q)
            arrived(right_slot(1, q), in_recv.at[1, q])
            turn(1, q)
            product_one(1 + yc, q)

        late_half(0)
        late_half(1)
        each(finish)

        @each
        def _(q):
            sent(q)
            for h in range(2):
                end_copy(q, h).wait_send()
            far_copy(q).wait_send()

        @each
        def _(q):
            arrived(part.at[q], p_recv.at[q])
            settle(q, True)


def folded_call(left_act, right_act, counts, w_out):
    rows, width_l = left_act.shape
    width_r = right_act.shape[1]
    left_dev, right_dev = counts.shape
    pair = w_out.shape[1]
    steps = width_r // TILE
    heads = TILE // CH
    full = 4 * rows
    dma = pltpu.SemaphoreType.DMA
    return pl.pallas_call(
        folded,
        out_shape=jax.ShapeDtypeStruct((left_dev, right_dev, pair), jnp.float32),
        in_specs=[pl.BlockSpec(memory_space=pl.ANY)] * 4,
        out_specs=pl.BlockSpec(memory_space=pltpu.VMEM),
        scratch_shapes=[
            pltpu.VMEM(w_out.shape, w_out.dtype),
            pltpu.VMEM(w_out.shape, jnp.float32),
            pltpu.VMEM(w_out.shape, w_out.dtype),
            pltpu.VMEM((right_dev, left_dev), counts.dtype),
            pltpu.VMEM((left_dev // 4, 4, right_dev, pair), jnp.float32),
            pltpu.VMEM((TILE, TILE), jnp.bfloat16),
            pltpu.VMEM((full, width_l), jnp.bfloat16),
            pltpu.VMEM((rows, width_l), jnp.bfloat16),
            pltpu.VMEM((full, width_r), jnp.bfloat16),
            pltpu.VMEM((width_r, full), jnp.bfloat16),
            pltpu.VMEM((width_l // 128, width_r, 128), jnp.float32),
            pltpu.VMEM((width_l // 128, TILE, 128), jnp.float32),
            pltpu.VMEM((left_dev * heads, CH * CH), jnp.bfloat16),
            pltpu.VMEM((steps, left_dev * heads, pair), jnp.bfloat16),
            pltpu.VMEM((steps, left_dev // 4, 4, heads, pair), jnp.float32),
            dma((2, steps)), dma((2, steps)), dma((steps,)), dma((steps, 2)), dma((steps, 2)), dma((steps,)), dma((steps,)),
            dma((steps, 2)), dma((steps, 2)), dma((steps,)),
            dma((steps,)), dma((2, steps)), dma((2, steps)), dma((2, steps)), dma((2, steps)), dma((steps,)), dma((steps,)), dma((steps,)),
            dma((steps,)), dma((4,)),
        ],
        compiler_params=pltpu.CompilerParams(collective_id=0, has_side_effects=True, vmem_limit_bytes=38000 * 1024),
        name="pair_mean",
    )(*(pltpu.with_memory_space_constraint(x, pltpu.HBM) for x in (left_act, right_act, counts.T, w_out)))


def solution(mesh):
    n_z, n_r = mesh.shape["left"], mesh.shape["right"]
    n_y = n_r // CORES

    def shards(left_act, right_act, counts, w_out):
        if (n_z, n_y) == (4, 2):
            return folded_call(left_act, right_act, counts, w_out)
        rows_l, width_l = left_act.shape
        rows_r, width_r = right_act.shape
        seqs = rows_r * n_z
        left_dev, right_dev = counts.shape
        pair = w_out.shape[1]
        q_z = width_r // 256
        q_y = rows_l // max(128, rows_l // 4)
        projected = pl.pallas_call(
            functools.partial(kernel, (n_z, n_r, q_z, q_y)),
            out_shape=jax.ShapeDtypeStruct((left_dev, right_dev, pair), jnp.float32),
            in_specs=[pl.BlockSpec(memory_space=pl.ANY)] * 4,
            out_specs=pl.BlockSpec(memory_space=pl.ANY),
            scratch_shapes=[
                pltpu.VMEM(w_out.shape, w_out.dtype),
                pltpu.VMEM(counts.shape, counts.dtype),
                pltpu.VMEM((right_dev, left_dev, pair), jnp.float32),
                pltpu.VMEM((q_z, left_dev, right_dev // q_z, pair), jnp.float32),
                pltpu.VMEM((seqs, width_l), jnp.bfloat16),
                pltpu.VMEM((seqs, width_r), jnp.bfloat16),
                pltpu.VMEM((width_l, seqs), jnp.bfloat16),
                pltpu.VMEM((width_r // 128, width_l, 128), jnp.float32),
                pltpu.VMEM((width_r // q_z // CH * left_dev, CH * CH), jnp.bfloat16),
                pltpu.SemaphoreType.DMA((2, (n_z - 1) * q_z)),
                pltpu.SemaphoreType.DMA((2, (n_z - 1) * q_z)),
                pltpu.SemaphoreType.DMA((2, (n_y - 1) * q_y)),
                pltpu.SemaphoreType.DMA((2, (n_y - 1) * q_y)),
                pltpu.SemaphoreType.DMA(((2 * n_y - 1) * q_y,)),
                pltpu.SemaphoreType.DMA(((2 * n_y - 1) * q_y,)),
                pltpu.SemaphoreType.DMA((4,)),
                pltpu.SemaphoreType.DMA((q_z,)),
            ],
            compiler_params=pltpu.CompilerParams(
                collective_id=0, has_side_effects=True, vmem_limit_bytes=56 * 1024 * 1024
            ),
            name="pair_mean",
        )(left_act, right_act, counts, w_out)
        return projected

    in_specs = (
        P(("groups", "right"), "left"),
        P(("groups", "left"), "right"),
        P(("groups", "left"), "right"),
        P(),
    )
    out_specs = P(("groups", "left"), "right", None)
    return jax.shard_map(shards, mesh=mesh, in_specs=in_specs, out_specs=out_specs, check_vma=False)
```

```python
import functools

import jax
import jax.numpy as jnp
from jax import lax
from jax.experimental import pallas as pl
from jax.experimental.pallas import tpu as pltpu
from jax.sharding import PartitionSpec as P

CH = 32
CORES = 2
TILE = 256
MESH = pl.DeviceIdType.MESH


def lane_quads(tiles):
    lane = lax.broadcasted_iota(jnp.int32, tiles[0].shape, 1)
    low = lane < 64
    even = (lane % 64) < 32
    stage = [None] * 4
    for c in range(2):
        a, b = tiles[c], tiles[c + 2]
        stage[c] = jnp.where(low, a, pltpu.roll(b, 64, 1))
        stage[c + 2] = jnp.where(low, pltpu.roll(a, 64, 1), b)
    outs = [None] * 4
    for half in range(2):
        a, b = stage[2 * half], stage[2 * half + 1]
        outs[2 * half] = jnp.where(even, a, pltpu.roll(b, 32, 1))
        outs[2 * half + 1] = jnp.where(even, pltpu.roll(a, 96, 1), b)
    return outs


def kernel(sizes, left_ref, right_ref, counts_ref, w_hbm, out_ref, w_ref, counts_in, cover, out_v, left_full, right_full, left_t, acc, flat,
           z_send, z_recv, y_send, y_recv, s_send, s_recv, own_sem, out_sem):
    n_z, n_r, q_z, q_y = sizes
    n_y = n_r // CORES
    rows_l, width_l = left_ref.shape
    rows_r, width_r = right_ref.shape
    piece_r = width_r // q_z
    piece_l = rows_l // q_y
    left_dev = width_l // CH
    right_dev = width_r // CH
    seqs = left_t.shape[1]
    z = lax.axis_index("left")
    r = lax.axis_index("right")
    y = r // CORES
    k = r % CORES

    def z_dev(pos):
        return {"left": pos}

    def y_dev(pos):
        return {"right": pos * CORES + k}

    sib_dev = {"right": y * CORES + (1 - k)}

    barrier = pltpu.get_barrier_semaphore()

    def greet(dev):
        pl.semaphore_signal(barrier, inc=1, device_id=dev, device_id_type=MESH)

    greet(sib_dev)
    for pos, n, dev in ((z, n_z, z_dev), (y, n_y, y_dev)):
        pl.when(pos + 1 < n)(functools.partial(greet, dev(pos + 1)))
        pl.when(pos >= 1)(functools.partial(greet, dev(pos - 1)))
    total = 1 + (z + 1 < n_z).astype(jnp.int32) + (z >= 1).astype(jnp.int32)
    total = total + (y + 1 < n_y).astype(jnp.int32) + (y >= 1).astype(jnp.int32)
    pl.semaphore_wait(barrier, total)

    def z_slot(chunk, q):
        return right_full.at[pl.ds(pl.multiple_of(chunk * rows_r, rows_r), rows_r), pl.ds(q * piece_r, piece_r)]

    def z_copy(side, step, q):
        sign = 1 - 2 * side
        chunk = z - sign * step
        src = right_ref.at[:, pl.ds(q * piece_r, piece_r)] if step == 0 else z_slot(chunk, q)
        at = step * q_z + q
        return pltpu.make_async_remote_copy(
            src_ref=src, dst_ref=z_slot(chunk, q), send_sem=z_send.at[side, at], recv_sem=z_recv.at[side, at],
            device_id=z_dev(z + sign), device_id_type=MESH)

    def z_sends(side, step):
        near = z + 1 < n_z if side == 0 else z >= 1
        far = z - step >= 0 if side == 0 else z + step < n_z
        return jnp.logical_and(near, far)

    def z_arrives(side, step):
        return z - step - 1 >= 0 if side == 0 else z + step + 1 < n_z

    def z_wait(side, step, q):
        sign = 1 - 2 * side
        slot = z_slot(z - sign * (step + 1), q)
        pltpu.make_async_copy(slot, slot, z_recv.at[side, step * q_z + q]).wait()

    def l_slot(chunk, q):
        return left_full.at[pl.ds(pl.multiple_of(chunk * rows_l + q * piece_l, piece_l), piece_l), :]

    def l_own(q):
        return left_ref.at[pl.ds(q * piece_l, piece_l), :]

    def y_copy(side, step, q):
        sign = 1 - 2 * side
        chunk = (y - sign * step) * CORES + k
        at = step * q_y + q
        return pltpu.make_async_remote_copy(
            src_ref=l_own(q) if step == 0 else l_slot(chunk, q), dst_ref=l_slot(chunk, q),
            send_sem=y_send.at[side, at], recv_sem=y_recv.at[side, at],
            device_id=y_dev(y + sign), device_id_type=MESH)

    def y_sends(side, step):
        near = y + 1 < n_y if side == 0 else y >= 1
        far = y - step >= 0 if side == 0 else y + step < n_y
        return jnp.logical_and(near, far)

    def y_arrives(side, step):
        return y - step - 1 >= 0 if side == 0 else y + step + 1 < n_y

    def y_wait(side, step, q):
        sign = 1 - 2 * side
        slot = l_slot((y - sign * (step + 1)) * CORES + k, q)
        pltpu.make_async_copy(slot, slot, y_recv.at[side, step * q_y + q]).wait()

    def s_at(side, step, q):
        if step < 0:
            return q
        return (1 + side * (n_y - 1) + step) * q_y + q

    def s_copy(side, step, q):
        sign = 1 - 2 * side
        chunk = (y - sign * (step + 1)) * CORES + k if step >= 0 else r
        at = s_at(side, step, q)
        return pltpu.make_async_remote_copy(
            src_ref=l_own(q) if step < 0 else l_slot(chunk, q), dst_ref=l_slot(chunk, q),
            send_sem=s_send.at[at], recv_sem=s_recv.at[at],
            device_id=sib_dev, device_id_type=MESH)

    def s_wait(side, step, q):
        sign = 1 - 2 * side
        y_from = y - sign * (step + 1) if step >= 0 else y
        slot = l_slot(y_from * CORES + (1 - k), q)
        pltpu.make_async_copy(slot, slot, s_recv.at[s_at(side, step, q)]).wait()

    tile = 256

    def turn(src, first_row, chunk, q):
        col = pl.multiple_of(chunk * rows_l + q * piece_l, piece_l)

        def body(m, carry):
            at = pl.multiple_of(m * tile, tile)
            left_t[pl.ds(at, tile), pl.ds(col, piece_l)] = src[pl.ds(first_row, piece_l), pl.ds(at, tile)].T
            return carry

        lax.fori_loop(0, width_l // tile, body, 0)

    def turn_full(chunk, q):
        turn(left_full, pl.multiple_of(chunk * rows_l + q * piece_l, piece_l), chunk, q)

    for q in range(max(q_z, q_y)):
        for side in range(2):
            if q < q_z:
                pl.when(z_sends(side, 0))(lambda side=side, q=q: z_copy(side, 0, q).start())
            if q < q_y:
                pl.when(y_sends(side, 0))(lambda side=side, q=q: y_copy(side, 0, q).start())
    own_left = pltpu.make_async_copy(left_ref, left_full.at[pl.ds(pl.multiple_of(r * rows_l, rows_l), rows_l), :], own_sem.at[0])
    own = pltpu.make_async_copy(right_ref, right_full.at[pl.ds(pl.multiple_of(z * rows_r, rows_r), rows_r), :], own_sem.at[1])
    weights = pltpu.make_async_copy(w_hbm, w_ref, own_sem.at[2])
    counts_copy = pltpu.make_async_copy(counts_ref, counts_in, own_sem.at[3])
    for copy in (own_left, own, weights, counts_copy):
        copy.start()
    for q in range(q_y):
        s_copy(0, -1, q).start()
    own_left.wait()
    for q in range(q_y):
        turn_full(r, q)
    counts_copy.wait()
    counted = counts_in[...].astype(jnp.float32)
    for j in range(right_dev):
        cover[j] = jnp.broadcast_to(counted[:, j:j + 1], (left_dev, cover.shape[2]))
    for q in range(q_y):
        s_wait(0, -1, q)
        turn_full(y * CORES + (1 - k), q)

    def z_tick(step, q):
        for side in range(2):
            @pl.when(z_arrives(side, step))
            def _():
                z_wait(side, step, q)
                if step + 1 < n_z - 1:
                    pl.when(z_sends(side, step + 1))(lambda: z_copy(side, step + 1, q).start())

    def y_tick(step, q):
        for side in range(2):
            @pl.when(y_arrives(side, step))
            def _():
                y_wait(side, step, q)
                s_copy(side, step, q).start()
                if step + 1 < n_y - 1:
                    pl.when(y_sends(side, step + 1))(lambda: y_copy(side, step + 1, q).start())

        for side in range(2):
            @pl.when(y_arrives(side, step))
            def _():
                sign = 1 - 2 * side
                y_from = y - sign * (step + 1)
                turn_full(y_from * CORES + k, q)
                s_wait(side, step, q)
                turn_full(y_from * CORES + (1 - k), q)

    y_ticks = [(step, q) for step in range(n_y - 1) for q in range(q_y)]
    for t in range((n_z - 2) * q_z):
        z_tick(t // q_z, t % q_z)
        if t % 2 == 1 and y_ticks:
            y_tick(*y_ticks.pop(0))
    for tick in y_ticks:
        y_tick(*tick)
    own.wait()
    weights.wait()

    block = 1024
    at_end = jnp.logical_or(z == 0, z == n_z - 1)
    base = jnp.where(z == 0, 0, rows_r)
    base = pl.multiple_of(base, rows_r)

    def product(q, first, depth, add):
        cols = pl.ds(q * piece_r, piece_r)

        def body(m, carry):
            rows = pl.ds(pl.multiple_of(m * block, block), block)
            value = jnp.dot(left_t[rows, pl.ds(first, depth)], right_full[pl.ds(first, depth), cols],
                            preferred_element_type=jnp.float32)
            for part in range(piece_r // 128):
                some = value[:, part * 128:(part + 1) * 128]
                slab = q * (piece_r // 128) + part
                acc[slab, rows, :] = acc[slab, rows, :] + some if add else some
            return carry

        lax.fori_loop(0, width_l // block, body, 0)

    def first_part(q):
        @pl.when(at_end)
        def _():
            product(q, base, seqs - rows_r, False)

        @pl.when(jnp.logical_not(at_end))
        def _():
            product(q, 0, seqs, False)

    for q in range(q_z):
        first_part(q)

    def finish(q):
        heads = piece_r // CH
        for quad in range(heads // 4):
            slab = acc.at[q * (piece_r // 128) + quad]
            for cq in range(CH // 4):
                tiles = [slab[pl.ds(cq * 4 + c, left_dev, stride=CH), :].astype(jnp.bfloat16) for c in range(4)]
                for j, value in enumerate(lane_quads(tiles)):
                    flat[pl.ds((quad * 4 + j) * left_dev, left_dev), pl.ds(cq * 128, 128)] = value
        projected = jnp.dot(flat[...], w_ref[...], preferred_element_type=jnp.float32)
        for j in range(heads):
            value = projected[j * left_dev:(j + 1) * left_dev, :] / cover[q * heads + j]
            out_v.at[q].reshape(left_dev * heads, value.shape[1])[pl.ds(j, left_dev, stride=heads), :] = value
        out_copy(q).start()

    def out_copy(q):
        return pltpu.make_async_copy(out_v.at[q], out_ref.at[:, pl.ds(q * heads_q, heads_q), :], out_sem.at[q])

    heads_q = piece_r // CH
    last = n_z - 2
    for q in range(q_z):
        z_tick(last, q)

        @pl.when(at_end)
        def _():
            far = jnp.where(z == 0, (n_z - 1) * rows_r, 0)
            product(q, pl.multiple_of(far, rows_r), rows_r, True)

        finish(q)

    for side in range(2):
        for step in range(n_z - 1):
            for q in range(q_z):
                pl.when(z_sends(side, step))(lambda side=side, step=step, q=q: z_copy(side, step, q).wait_send())
        for step in range(n_y - 1):
            for q in range(q_y):
                pl.when(y_sends(side, step))(lambda side=side, step=step, q=q: y_copy(side, step, q).wait_send())
                pl.when(y_arrives(side, step))(lambda side=side, step=step, q=q: s_copy(side, step, q).wait_send())
    for q in range(q_y):
        s_copy(0, -1, q).wait_send()
    for q in range(q_z):
        out_copy(q).wait()


def folded(left_ref, right_ref, counts_ref, w_hbm, out_ref, w_in, w_wide, w_ref, counts_in, cover, order, left_full, left_far, right_full, right_t,
           acc, acc_far, flat, part, out_v, send, in_recv, far_recv, end_recv, own_recv, y_recv, s_recv, a_recv, own_sem):
    rows, width_l = left_ref.shape
    width_r = right_ref.shape[1]
    steps = width_r // TILE
    piece = rows // steps
    half = width_l // CORES
    quads = width_l // 128
    heads = TILE // CH
    early = steps // 2
    z = lax.axis_index("left")
    r = lax.axis_index("right")
    y, k = r // CORES, r % CORES
    up = z // 2
    sign = 2 * up - 1

    def fold(n, at):
        return up * at + (1 - up) * (n - 1 - at)

    zc, yc, kc = fold(4, z), fold(2, y), fold(2, k)
    inner, end = zc == 2, zc == 3
    sib_dev = {"right": r + 1 - 2 * k}
    y_dev = {"right": r + (1 - 2 * y) * CORES}

    def when(*terms):
        value = terms[0]
        for term in terms[1:]:
            value = jnp.logical_and(value, term)
        return pl.when(value)

    def z_dev(way):
        return {"left": z + way * sign}

    barrier = pltpu.get_barrier_semaphore()

    def greet(dev):
        pl.semaphore_signal(barrier, inc=1, device_id=dev, device_id_type=MESH)

    greet(sib_dev)
    greet(y_dev)
    greet(z_dev(-1))
    when(inner)(lambda: greet(z_dev(1)))
    pl.semaphore_wait(barrier, 3 + inner.astype(jnp.int32))

    def remote(src, dst, send, recv, dev):
        return pltpu.make_async_remote_copy(src_ref=src, dst_ref=dst, send_sem=send, recv_sem=recv, device_id=dev, device_id_type=MESH)

    def arrived(slot, sem):
        pltpu.make_async_copy(slot, slot, sem).wait()

    def block(at, first=0, size=rows):
        return pl.ds(pl.multiple_of(fold(4, at) * rows + first, size), size)

    def cols(q):
        return pl.ds(pl.multiple_of(q * TILE, TILE), TILE)

    def right_slot(at, q):
        return right_full.at[block(at), cols(q)]

    def in_copy(way, q):
        return remote(right_ref.at[:, cols(q)], right_slot(2, q), send.at[(way + 1) // 2], in_recv.at[0, q], z_dev(way))

    def fwd_copy(q):
        slot = right_slot(1, q)
        return remote(slot, slot, send.at[2], in_recv.at[1, q], z_dev(1))

    def half_slot(at, q, h):
        return right_full.at[block(at, h * (rows // 2), rows // 2), cols(q)]

    def mid_copy(q, h):
        slot = half_slot(3, q, h)
        return remote(slot, slot, send.at[3], in_recv.at[1, q], z_dev(-1))

    def end_copy(q, h):
        source = right_ref.at[pl.ds(h * (rows // 2), rows // 2), cols(q)]
        return remote(source, half_slot(3, q, h), send.at[3], end_recv.at[q, h], z_dev(-1))

    def end_start(q):
        for h in range(2):
            end_copy(q, h).start()

    def own_half():
        return pl.ds(pl.multiple_of(k * half, half), half)

    def far_copy(p):
        at = pl.ds(pl.multiple_of(p * piece, piece), piece)
        return remote(left_full.at[block(0, p * piece, piece), own_half()], left_far.at[at, own_half()], send.at[2], far_recv.at[p], z_dev(-1))

    def far_slot(p, core):
        return left_far.at[pl.ds(pl.multiple_of(p * piece, piece), piece), pl.ds(pl.multiple_of(core * half, half), half)]

    def share_copy(p):
        return remote(far_slot(p, k), far_slot(p, k), send.at[4], a_recv.at[0], sib_dev)

    def own_copy(p):
        at = pl.ds(pl.multiple_of(p * piece, piece), piece)
        slot = left_full.at[pl.ds(pl.multiple_of(r * rows + p * piece, piece), piece), :]
        return remote(left_ref.at[at, :], slot, send.at[5], own_recv.at[p], sib_dev)

    def own_arrived(p):
        other = r + 1 - 2 * k
        arrived(left_full.at[pl.ds(pl.multiple_of(other * rows + p * piece, piece), piece), :], own_recv.at[p])

    def y_slot(side, pos, p, core, count=1):
        at = 3 * side if pos == 0 else 1 + side
        return left_full.at[block(at, p * piece, count * piece), pl.ds(pl.multiple_of(core * half, half), half)]

    def y_copy(pos, p, own=False):
        slot = y_slot(yc, pos, p, k)
        source = left_ref.at[pl.ds(pl.multiple_of(p * piece, piece), piece), own_half()] if own else slot
        return remote(source, slot, send.at[6], y_recv.at[pos, p], y_dev)

    def s_copy(pos, p, group):
        slot = y_slot(1 - yc, pos, p, k)
        return remote(slot, slot, send.at[7], s_recv.at[group], sib_dev)

    def part_copy(q):
        return remote(part.at[q], part.at[q], send.at[8], far_recv.at[q], z_dev(1))

    def each(body, first=0, last=steps):
        def step(at, carry):
            body(at)
            return carry

        lax.fori_loop(first, last, step, 0)

    @when(inner)
    def _():
        @each
        def _(q):
            in_copy(-1, q).start()
            in_copy(1, q).start()

    when(end)(lambda: each(end_start, 0, early))
    first = kc == yc
    when(first)(lambda: each(lambda p: y_copy(0, p, True).start()))
    own_left = pltpu.make_async_copy(left_ref, left_full.at[pl.ds(pl.multiple_of(r * rows, rows), rows), :], own_sem.at[0])
    own = pltpu.make_async_copy(right_ref, right_full.at[block(zc), :], own_sem.at[1])
    weights = pltpu.make_async_copy(w_hbm, w_in, own_sem.at[2])
    counts_copy = pltpu.make_async_copy(counts_ref, counts_in, own_sem.at[3])
    each(lambda p: own_copy(p).start())
    for copy in (own_left, own, weights, counts_copy):
        copy.start()

    @each
    def _(p):
        own_arrived(p)
        when(jnp.logical_not(first))(lambda: y_copy(0, p).start())
        when(end, yc == 0, kc == 1)(lambda: far_copy(p).start())

    own_left.wait()
    when(end, yc == 0, kc == 0)(lambda: each(lambda p: far_copy(p).start()))
    each(lambda p: y_copy(1, p).start())
    when(end, yc == 0)(lambda: each(end_start, early))

    row = lax.broadcasted_iota(jnp.int32, (TILE, TILE), 0)
    column = lax.broadcasted_iota(jnp.int32, (TILE, TILE), 1)
    order[...] = jnp.where(column == (row % heads) * CH + row // heads, 1.0, 0.0).astype(order.dtype)
    weights.wait()
    w_wide[...] = w_in[...].astype(jnp.float32)
    for e in range(CH):
        w_ref[pl.ds(e * CH, CH), :] = w_wide[pl.ds(e, CH, stride=CH), :].astype(w_ref.dtype)
    counts_copy.wait()
    counted = counts_in[...].astype(jnp.float32)
    for i in range(counted.shape[1]):
        cover[i // 4, i % 4] = jnp.broadcast_to(counted[:, i:i + 1], (counted.shape[0], cover.shape[3]))

    def turn(at, q):
        value = lax.dot_general(order[...], right_full[block(at), cols(q)], (((1,), (1,)), ((), ())), preferred_element_type=jnp.float32)
        right_t[cols(q), block(at)] = value.astype(right_t.dtype)

    def product(into, lines, source, left, left_rows, size, wide, add):
        for n in range(width_l // wide):
            value = jnp.dot(right_t[lines, source], left[left_rows, pl.ds(n * wide, wide)], preferred_element_type=jnp.float32)
            for one in range(wide // 128):
                some = value[:, one * 128:(one + 1) * 128]
                slab = n * (wide // 128) + one
                into[slab, size, :] = into[slab, size, :] + some if add else some

    def product_all(at, add, first=0, depth=rows):
        every = pl.ds(0, width_r)
        product(acc, every, block(at, first, depth), left_full, block(at, first, depth), every, 256, add)

    def product_one(at, q):
        product(acc, cols(q), block(at), left_full, block(at), cols(q), 512, True)

    def project(source, first_row):
        for eq in range(CH // 4):
            tiles = []
            for e in range(4):
                tile = source[:, pl.ds(pl.multiple_of(first_row + (eq * 4 + e) * heads, heads), heads), :]
                tiles.append(tile.reshape(quads * heads, 128).astype(flat.dtype))
            for i, value in enumerate(lane_quads(tiles)):
                flat[pl.ds(i * quads * heads, quads * heads), pl.ds(eq * 128, 128)] = value
        return jnp.dot(flat[...], w_ref[...], preferred_element_type=jnp.float32)

    def settle(q, add):
        for i in range(4):
            value = out_v[q, :, i]
            if add:
                more = part[q, pl.ds(i * quads * heads, quads * heads), :]
                value = value + more.astype(jnp.float32).reshape(value.shape)
            at = pl.ds(pl.multiple_of(q * heads, heads), heads)
            out_ref[pl.ds(i, quads, stride=4), at, :] = value / cover[:, i, at, :]

    own.wait()
    each(lambda q: turn(zc, q))

    def pass_on(q, h):
        arrived(half_slot(3, q, h), end_recv.at[q, h])
        mid_copy(q, h).start()

    def end_arrived(q):
        for h in range(2):
            pass_on(q, h)
        turn(3, q)

    def share(p):
        arrived(far_slot(p, k), far_recv.at[p])
        share_copy(p).start()

    @each
    def _(p):
        arrived(y_slot(1 - yc, 0, p, k), y_recv.at[0, p])
        s_copy(0, p, 0).start()
        when(end, yc == 1)(lambda: far_copy(p).start())
        arrived(right_slot(zc - 1, p), in_recv.at[0, p])
        when(inner)(lambda: fwd_copy(p).start())
        turn(zc - 1, p)
        when(inner, p >= 1, p <= early)(lambda: end_arrived(p - 1))

    when(end, yc == 1)(lambda: each(end_start, early))
    arrived(y_slot(1 - yc, 0, 0, 1 - k, steps), s_recv.at[0])
    late = 2 - yc
    groups = ((0, early), (early, early + 1), (early + 1, steps))

    def y_arrived(p):
        group = next(at for at, (_, last) in enumerate(groups) if p < last)
        arrived(y_slot(1 - yc, 1, p, k), y_recv.at[1, p])
        s_copy(1, p, 1 + group).start()

    def late_part(group):
        low, high = groups[group]
        arrived(y_slot(1 - yc, 1, low, 1 - k, high - low), s_recv.at[1 + group])
        product_all(late, True, low * piece, (high - low) * piece)

    def far_product(q):
        arrived(right_slot(0, q), in_recv.at[1, q])
        turn(0, q)
        product(acc_far, cols(q), block(0), left_far, pl.ds(0, rows), pl.ds(0, TILE), 512, False)

    def far_send_on(q):
        part[q] = project(acc_far, 0).astype(part.dtype)
        part_copy(q).start()

    def finish(q):
        value = project(acc, q * TILE)
        for i in range(4):
            out_v[q, :, i] = value[i * quads * heads:(i + 1) * quads * heads].reshape(quads, heads, 128)

    def sent(sem, count=1):
        slot = left_full.at[pl.ds(0, count * rows), pl.ds(0, half)]
        arrived(slot, send.at[sem])

    @when(inner)
    def _():
        each(share, 0, early)
        product_all(1 + yc, False)
        for q in range(early):
            product_one(3, q)
        y_arrived(0)
        each(share, early)
        arrived(left_far.at[:, pl.ds(pl.multiple_of((1 - k) * half, half), half)], a_recv.at[0])
        far_product(0)
        y_arrived(1)
        far_send_on(0)
        pass_on(2, 0)
        product_one(0, 0)
        far_product(1)
        far_send_on(1)
        pass_on(2, 1)
        product_one(0, 1)
        turn(3, 2)
        y_arrived(2)
        product_one(3, 2)
        pass_on(3, 0)
        late_part(0)
        late_part(1)
        pass_on(3, 1)
        far_product(2)
        y_arrived(3)
        far_send_on(2)
        turn(3, 3)
        product_one(3, 3)
        product_one(0, 2)
        late_part(2)
        far_product(3)
        far_send_on(3)
        product_one(0, 3)

        @each
        def _(q):
            finish(q)
            settle(q, False)

        sent(0)
        sent(1)
        sent(2)
        sent(3)
        sent(4)
        sent(5, 2)
        sent(6, 2)
        sent(7, 2)
        arrived(part, send.at[8])

    @when(end)
    def _():
        product_all(3, False)
        for q in range(steps):
            y_arrived(q)
            arrived(right_slot(1, q), in_recv.at[1, q])
            turn(1, q)
            product_one(1 + yc, q)
        for group in range(len(groups)):
            late_part(group)
        each(finish)
        sent(2)
        sent(3)
        sent(5, 2)
        sent(6, 2)
        sent(7, 2)

        @each
        def _(q):
            arrived(part.at[q], far_recv.at[q])
            settle(q, True)


def folded_call(left_act, right_act, counts, w_out):
    rows, width_l = left_act.shape
    width_r = right_act.shape[1]
    left_dev, right_dev = counts.shape
    pair = w_out.shape[1]
    steps = width_r // TILE
    heads = TILE // CH
    full = 4 * rows
    dma = pltpu.SemaphoreType.DMA
    return pl.pallas_call(
        folded,
        out_shape=jax.ShapeDtypeStruct((left_dev, right_dev, pair), jnp.float32),
        in_specs=[pl.BlockSpec(memory_space=pl.ANY)] * 4,
        out_specs=pl.BlockSpec(memory_space=pltpu.VMEM),
        scratch_shapes=[
            pltpu.VMEM(w_out.shape, w_out.dtype),
            pltpu.VMEM(w_out.shape, jnp.float32),
            pltpu.VMEM(w_out.shape, w_out.dtype),
            pltpu.VMEM((right_dev, left_dev), counts.dtype),
            pltpu.VMEM((left_dev // 4, 4, right_dev, pair), jnp.float32),
            pltpu.VMEM((TILE, TILE), jnp.bfloat16),
            pltpu.VMEM((full, width_l), jnp.bfloat16),
            pltpu.VMEM((rows, width_l), jnp.bfloat16),
            pltpu.VMEM((full, width_r), jnp.bfloat16),
            pltpu.VMEM((width_r, full), jnp.bfloat16),
            pltpu.VMEM((width_l // 128, width_r, 128), jnp.float32),
            pltpu.VMEM((width_l // 128, TILE, 128), jnp.float32),
            pltpu.VMEM((left_dev * heads, CH * CH), jnp.bfloat16),
            pltpu.VMEM((steps, left_dev * heads, pair), jnp.bfloat16),
            pltpu.VMEM((steps, left_dev // 4, 4, heads, pair), jnp.float32),
            dma((9,)), dma((2, steps)), dma((steps,)), dma((steps, 2)), dma((steps,)), dma((2, steps)), dma((4,)), dma((1,)), dma((4,)),
        ],
        compiler_params=pltpu.CompilerParams(collective_id=0, has_side_effects=True, vmem_limit_bytes=38000 * 1024),
        name="pair_mean",
    )(*(pltpu.with_memory_space_constraint(x, pltpu.HBM) for x in (left_act, right_act, counts.T, w_out)))


def solution(mesh):
    n_z, n_r = mesh.shape["left"], mesh.shape["right"]
    n_y = n_r // CORES

    def shards(left_act, right_act, counts, w_out):
        width_l, width_r = left_act.shape[1], right_act.shape[1]
        if (n_z, n_y) == (4, 2) and width_r == 4 * TILE and width_l == CORES * width_r:
            return folded_call(left_act, right_act, counts, w_out)
        rows_l, width_l = left_act.shape
        rows_r, width_r = right_act.shape
        seqs = rows_r * n_z
        left_dev, right_dev = counts.shape
        pair = w_out.shape[1]
        q_z = width_r // 256
        q_y = rows_l // max(128, rows_l // 4)
        projected = pl.pallas_call(
            functools.partial(kernel, (n_z, n_r, q_z, q_y)),
            out_shape=jax.ShapeDtypeStruct((left_dev, right_dev, pair), jnp.float32),
            in_specs=[pl.BlockSpec(memory_space=pl.ANY)] * 4,
            out_specs=pl.BlockSpec(memory_space=pl.ANY),
            scratch_shapes=[
                pltpu.VMEM(w_out.shape, w_out.dtype),
                pltpu.VMEM(counts.shape, counts.dtype),
                pltpu.VMEM((right_dev, left_dev, pair), jnp.float32),
                pltpu.VMEM((q_z, left_dev, right_dev // q_z, pair), jnp.float32),
                pltpu.VMEM((seqs, width_l), jnp.bfloat16),
                pltpu.VMEM((seqs, width_r), jnp.bfloat16),
                pltpu.VMEM((width_l, seqs), jnp.bfloat16),
                pltpu.VMEM((width_r // 128, width_l, 128), jnp.float32),
                pltpu.VMEM((width_r // q_z // CH * left_dev, CH * CH), jnp.bfloat16),
                pltpu.SemaphoreType.DMA((2, (n_z - 1) * q_z)),
                pltpu.SemaphoreType.DMA((2, (n_z - 1) * q_z)),
                pltpu.SemaphoreType.DMA((2, (n_y - 1) * q_y)),
                pltpu.SemaphoreType.DMA((2, (n_y - 1) * q_y)),
                pltpu.SemaphoreType.DMA(((2 * n_y - 1) * q_y,)),
                pltpu.SemaphoreType.DMA(((2 * n_y - 1) * q_y,)),
                pltpu.SemaphoreType.DMA((4,)),
                pltpu.SemaphoreType.DMA((q_z,)),
            ],
            compiler_params=pltpu.CompilerParams(
                collective_id=0, has_side_effects=True, vmem_limit_bytes=56 * 1024 * 1024
            ),
            name="pair_mean",
        )(left_act, right_act, counts, w_out)
        return projected

    in_specs = (
        P(("groups", "right"), "left"),
        P(("groups", "left"), "right"),
        P(("groups", "left"), "right"),
        P(),
    )
    out_specs = P(("groups", "left"), "right", None)
    return jax.shard_map(shards, mesh=mesh, in_specs=in_specs, out_specs=out_specs, check_vma=False)
```

```python
import functools

import jax
import jax.numpy as jnp
from jax import lax
from jax.experimental import pallas as pl
from jax.experimental.pallas import tpu as pltpu
from jax.sharding import PartitionSpec as P

CH = 32
CORES = 2
TILE = 256
MESH = pl.DeviceIdType.MESH


def lane_quads(tiles):
    lane = lax.broadcasted_iota(jnp.int32, tiles[0].shape, 1)
    low = lane < 64
    even = (lane % 64) < 32
    stage = [None] * 4
    for c in range(2):
        a, b = tiles[c], tiles[c + 2]
        stage[c] = jnp.where(low, a, pltpu.roll(b, 64, 1))
        stage[c + 2] = jnp.where(low, pltpu.roll(a, 64, 1), b)
    outs = [None] * 4
    for half in range(2):
        a, b = stage[2 * half], stage[2 * half + 1]
        outs[2 * half] = jnp.where(even, a, pltpu.roll(b, 32, 1))
        outs[2 * half + 1] = jnp.where(even, pltpu.roll(a, 96, 1), b)
    return outs


def kernel(sizes, left_ref, right_ref, counts_ref, w_hbm, out_ref, w_ref, counts_in, cover, out_v, left_full, right_full, left_t, acc, flat,
           z_send, z_recv, y_send, y_recv, s_send, s_recv, own_sem, out_sem):
    n_z, n_r, q_z, q_y = sizes
    n_y = n_r // CORES
    rows_l, width_l = left_ref.shape
    rows_r, width_r = right_ref.shape
    piece_r = width_r // q_z
    piece_l = rows_l // q_y
    left_dev = width_l // CH
    right_dev = width_r // CH
    seqs = left_t.shape[1]
    z = lax.axis_index("left")
    r = lax.axis_index("right")
    y = r // CORES
    k = r % CORES

    def z_dev(pos):
        return {"left": pos}

    def y_dev(pos):
        return {"right": pos * CORES + k}

    sib_dev = {"right": y * CORES + (1 - k)}

    barrier = pltpu.get_barrier_semaphore()

    def greet(dev):
        pl.semaphore_signal(barrier, inc=1, device_id=dev, device_id_type=MESH)

    greet(sib_dev)
    for pos, n, dev in ((z, n_z, z_dev), (y, n_y, y_dev)):
        pl.when(pos + 1 < n)(functools.partial(greet, dev(pos + 1)))
        pl.when(pos >= 1)(functools.partial(greet, dev(pos - 1)))
    total = 1 + (z + 1 < n_z).astype(jnp.int32) + (z >= 1).astype(jnp.int32)
    total = total + (y + 1 < n_y).astype(jnp.int32) + (y >= 1).astype(jnp.int32)
    pl.semaphore_wait(barrier, total)

    def z_slot(chunk, q):
        return right_full.at[pl.ds(pl.multiple_of(chunk * rows_r, rows_r), rows_r), pl.ds(q * piece_r, piece_r)]

    def z_copy(side, step, q):
        sign = 1 - 2 * side
        chunk = z - sign * step
        src = right_ref.at[:, pl.ds(q * piece_r, piece_r)] if step == 0 else z_slot(chunk, q)
        at = step * q_z + q
        return pltpu.make_async_remote_copy(
            src_ref=src, dst_ref=z_slot(chunk, q), send_sem=z_send.at[side, at], recv_sem=z_recv.at[side, at],
            device_id=z_dev(z + sign), device_id_type=MESH)

    def z_sends(side, step):
        near = z + 1 < n_z if side == 0 else z >= 1
        far = z - step >= 0 if side == 0 else z + step < n_z
        return jnp.logical_and(near, far)

    def z_arrives(side, step):
        return z - step - 1 >= 0 if side == 0 else z + step + 1 < n_z

    def z_wait(side, step, q):
        sign = 1 - 2 * side
        slot = z_slot(z - sign * (step + 1), q)
        pltpu.make_async_copy(slot, slot, z_recv.at[side, step * q_z + q]).wait()

    def l_slot(chunk, q):
        return left_full.at[pl.ds(pl.multiple_of(chunk * rows_l + q * piece_l, piece_l), piece_l), :]

    def l_own(q):
        return left_ref.at[pl.ds(q * piece_l, piece_l), :]

    def y_copy(side, step, q):
        sign = 1 - 2 * side
        chunk = (y - sign * step) * CORES + k
        at = step * q_y + q
        return pltpu.make_async_remote_copy(
            src_ref=l_own(q) if step == 0 else l_slot(chunk, q), dst_ref=l_slot(chunk, q),
            send_sem=y_send.at[side, at], recv_sem=y_recv.at[side, at],
            device_id=y_dev(y + sign), device_id_type=MESH)

    def y_sends(side, step):
        near = y + 1 < n_y if side == 0 else y >= 1
        far = y - step >= 0 if side == 0 else y + step < n_y
        return jnp.logical_and(near, far)

    def y_arrives(side, step):
        return y - step - 1 >= 0 if side == 0 else y + step + 1 < n_y

    def y_wait(side, step, q):
        sign = 1 - 2 * side
        slot = l_slot((y - sign * (step + 1)) * CORES + k, q)
        pltpu.make_async_copy(slot, slot, y_recv.at[side, step * q_y + q]).wait()

    def s_at(side, step, q):
        if step < 0:
            return q
        return (1 + side * (n_y - 1) + step) * q_y + q

    def s_copy(side, step, q):
        sign = 1 - 2 * side
        chunk = (y - sign * (step + 1)) * CORES + k if step >= 0 else r
        at = s_at(side, step, q)
        return pltpu.make_async_remote_copy(
            src_ref=l_own(q) if step < 0 else l_slot(chunk, q), dst_ref=l_slot(chunk, q),
            send_sem=s_send.at[at], recv_sem=s_recv.at[at],
            device_id=sib_dev, device_id_type=MESH)

    def s_wait(side, step, q):
        sign = 1 - 2 * side
        y_from = y - sign * (step + 1) if step >= 0 else y
        slot = l_slot(y_from * CORES + (1 - k), q)
        pltpu.make_async_copy(slot, slot, s_recv.at[s_at(side, step, q)]).wait()

    tile = 256

    def turn(src, first_row, chunk, q):
        col = pl.multiple_of(chunk * rows_l + q * piece_l, piece_l)

        def body(m, carry):
            at = pl.multiple_of(m * tile, tile)
            left_t[pl.ds(at, tile), pl.ds(col, piece_l)] = src[pl.ds(first_row, piece_l), pl.ds(at, tile)].T
            return carry

        lax.fori_loop(0, width_l // tile, body, 0)

    def turn_full(chunk, q):
        turn(left_full, pl.multiple_of(chunk * rows_l + q * piece_l, piece_l), chunk, q)

    for q in range(max(q_z, q_y)):
        for side in range(2):
            if q < q_z:
                pl.when(z_sends(side, 0))(lambda side=side, q=q: z_copy(side, 0, q).start())
            if q < q_y:
                pl.when(y_sends(side, 0))(lambda side=side, q=q: y_copy(side, 0, q).start())
    own_left = pltpu.make_async_copy(left_ref, left_full.at[pl.ds(pl.multiple_of(r * rows_l, rows_l), rows_l), :], own_sem.at[0])
    own = pltpu.make_async_copy(right_ref, right_full.at[pl.ds(pl.multiple_of(z * rows_r, rows_r), rows_r), :], own_sem.at[1])
    weights = pltpu.make_async_copy(w_hbm, w_ref, own_sem.at[2])
    counts_copy = pltpu.make_async_copy(counts_ref, counts_in, own_sem.at[3])
    for copy in (own_left, own, weights, counts_copy):
        copy.start()
    for q in range(q_y):
        s_copy(0, -1, q).start()
    own_left.wait()
    for q in range(q_y):
        turn_full(r, q)
    counts_copy.wait()
    counted = counts_in[...].astype(jnp.float32)
    for j in range(right_dev):
        cover[j] = jnp.broadcast_to(counted[:, j:j + 1], (left_dev, cover.shape[2]))
    for q in range(q_y):
        s_wait(0, -1, q)
        turn_full(y * CORES + (1 - k), q)

    def z_tick(step, q):
        for side in range(2):
            @pl.when(z_arrives(side, step))
            def _():
                z_wait(side, step, q)
                if step + 1 < n_z - 1:
                    pl.when(z_sends(side, step + 1))(lambda: z_copy(side, step + 1, q).start())

    def y_tick(step, q):
        for side in range(2):
            @pl.when(y_arrives(side, step))
            def _():
                y_wait(side, step, q)
                s_copy(side, step, q).start()
                if step + 1 < n_y - 1:
                    pl.when(y_sends(side, step + 1))(lambda: y_copy(side, step + 1, q).start())

        for side in range(2):
            @pl.when(y_arrives(side, step))
            def _():
                sign = 1 - 2 * side
                y_from = y - sign * (step + 1)
                turn_full(y_from * CORES + k, q)
                s_wait(side, step, q)
                turn_full(y_from * CORES + (1 - k), q)

    y_ticks = [(step, q) for step in range(n_y - 1) for q in range(q_y)]
    for t in range((n_z - 2) * q_z):
        z_tick(t // q_z, t % q_z)
        if t % 2 == 1 and y_ticks:
            y_tick(*y_ticks.pop(0))
    for tick in y_ticks:
        y_tick(*tick)
    own.wait()
    weights.wait()

    block = 1024
    at_end = jnp.logical_or(z == 0, z == n_z - 1)
    base = jnp.where(z == 0, 0, rows_r)
    base = pl.multiple_of(base, rows_r)

    def product(q, first, depth, add):
        cols = pl.ds(q * piece_r, piece_r)

        def body(m, carry):
            rows = pl.ds(pl.multiple_of(m * block, block), block)
            value = jnp.dot(left_t[rows, pl.ds(first, depth)], right_full[pl.ds(first, depth), cols],
                            preferred_element_type=jnp.float32)
            for part in range(piece_r // 128):
                some = value[:, part * 128:(part + 1) * 128]
                slab = q * (piece_r // 128) + part
                acc[slab, rows, :] = acc[slab, rows, :] + some if add else some
            return carry

        lax.fori_loop(0, width_l // block, body, 0)

    def first_part(q):
        @pl.when(at_end)
        def _():
            product(q, base, seqs - rows_r, False)

        @pl.when(jnp.logical_not(at_end))
        def _():
            product(q, 0, seqs, False)

    for q in range(q_z):
        first_part(q)

    def finish(q):
        heads = piece_r // CH
        for quad in range(heads // 4):
            slab = acc.at[q * (piece_r // 128) + quad]
            for cq in range(CH // 4):
                tiles = [slab[pl.ds(cq * 4 + c, left_dev, stride=CH), :].astype(jnp.bfloat16) for c in range(4)]
                for j, value in enumerate(lane_quads(tiles)):
                    flat[pl.ds((quad * 4 + j) * left_dev, left_dev), pl.ds(cq * 128, 128)] = value
        projected = jnp.dot(flat[...], w_ref[...], preferred_element_type=jnp.float32)
        for j in range(heads):
            value = projected[j * left_dev:(j + 1) * left_dev, :] / cover[q * heads + j]
            out_v.at[q].reshape(left_dev * heads, value.shape[1])[pl.ds(j, left_dev, stride=heads), :] = value
        out_copy(q).start()

    def out_copy(q):
        return pltpu.make_async_copy(out_v.at[q], out_ref.at[:, pl.ds(q * heads_q, heads_q), :], out_sem.at[q])

    heads_q = piece_r // CH
    last = n_z - 2
    for q in range(q_z):
        z_tick(last, q)

        @pl.when(at_end)
        def _():
            far = jnp.where(z == 0, (n_z - 1) * rows_r, 0)
            product(q, pl.multiple_of(far, rows_r), rows_r, True)

        finish(q)

    for side in range(2):
        for step in range(n_z - 1):
            for q in range(q_z):
                pl.when(z_sends(side, step))(lambda side=side, step=step, q=q: z_copy(side, step, q).wait_send())
        for step in range(n_y - 1):
            for q in range(q_y):
                pl.when(y_sends(side, step))(lambda side=side, step=step, q=q: y_copy(side, step, q).wait_send())
                pl.when(y_arrives(side, step))(lambda side=side, step=step, q=q: s_copy(side, step, q).wait_send())
    for q in range(q_y):
        s_copy(0, -1, q).wait_send()
    for q in range(q_z):
        out_copy(q).wait()


def folded(left_ref, right_ref, counts_ref, w_hbm, out_ref, w_in, w_wide, w_ref, counts_in, cover, order, left_full, left_far, right_full, right_t,
           acc, acc_far, flat, part, out_v, send, in_recv, far_recv, end_recv, own_recv, y_recv, s_recv, a_recv, own_sem):
    rows, width_l = left_ref.shape
    width_r = right_ref.shape[1]
    steps = width_r // TILE
    piece = rows // steps
    half = width_l // CORES
    quads = width_l // 128
    heads = TILE // CH
    pair = w_hbm.shape[1]
    lines = quads * heads
    early = steps // 2
    z = lax.axis_index("left")
    r = lax.axis_index("right")
    y, k = r // CORES, r % CORES
    up = z // 2
    sign = 2 * up - 1

    def fold(n, at):
        return up * at + (1 - up) * (n - 1 - at)

    zc, yc, kc = fold(4, z), fold(2, y), fold(2, k)
    inner, end = zc == 2, zc == 3
    sib_dev = {"right": r + 1 - 2 * k}
    y_dev = {"right": r + (1 - 2 * y) * CORES}

    def when(*terms):
        value = terms[0]
        for term in terms[1:]:
            value = jnp.logical_and(value, term)
        return pl.when(value)

    def z_dev(way):
        return {"left": z + way * sign}

    barrier = pltpu.get_barrier_semaphore()

    def greet(dev):
        pl.semaphore_signal(barrier, inc=1, device_id=dev, device_id_type=MESH)

    greet(sib_dev)
    greet(y_dev)
    greet(z_dev(-1))
    when(inner)(lambda: greet(z_dev(1)))
    pl.semaphore_wait(barrier, 3 + inner.astype(jnp.int32))

    def remote(src, dst, send, recv, dev):
        return pltpu.make_async_remote_copy(src_ref=src, dst_ref=dst, send_sem=send, recv_sem=recv, device_id=dev, device_id_type=MESH)

    def arrived(slot, sem):
        pltpu.make_async_copy(slot, slot, sem).wait()

    def block(at, first=0, size=rows):
        return pl.ds(pl.multiple_of(fold(4, at) * rows + first, size), size)

    def cols(q):
        return pl.ds(pl.multiple_of(q * TILE, TILE), TILE)

    def right_slot(at, q):
        return right_full.at[block(at), cols(q)]

    def in_copy(way, q):
        return remote(right_ref.at[:, cols(q)], right_slot(2, q), send.at[(way + 1) // 2], in_recv.at[0, q], z_dev(way))

    def fwd_copy(q):
        slot = right_slot(1, q)
        return remote(slot, slot, send.at[2], in_recv.at[1, q], z_dev(1))

    def half_slot(at, q, h):
        return right_full.at[block(at, h * (rows // 2), rows // 2), cols(q)]

    def mid_copy(q, h):
        slot = half_slot(3, q, h)
        return remote(slot, slot, send.at[3], in_recv.at[1, q], z_dev(-1))

    def end_copy(q, h):
        source = right_ref.at[pl.ds(h * (rows // 2), rows // 2), cols(q)]
        return remote(source, half_slot(3, q, h), send.at[3], end_recv.at[q, h], z_dev(-1))

    def end_start(q):
        for h in range(2):
            end_copy(q, h).start()

    def own_half():
        return pl.ds(pl.multiple_of(k * half, half), half)

    def far_copy(p):
        at = pl.ds(pl.multiple_of(p * piece, piece), piece)
        return remote(left_full.at[block(0, p * piece, piece), own_half()], left_far.at[at, own_half()], send.at[2], far_recv.at[p], z_dev(-1))

    def far_slot(p, core):
        return left_far.at[pl.ds(pl.multiple_of(p * piece, piece), piece), pl.ds(pl.multiple_of(core * half, half), half)]

    def share_copy(p):
        return remote(far_slot(p, k), far_slot(p, k), send.at[4], a_recv.at[0], sib_dev)

    def own_copy(p):
        at = pl.ds(pl.multiple_of(p * piece, piece), piece)
        slot = left_full.at[pl.ds(pl.multiple_of(r * rows + p * piece, piece), piece), :]
        return remote(left_ref.at[at, :], slot, send.at[5], own_recv.at[p], sib_dev)

    def own_arrived(p):
        other = r + 1 - 2 * k
        arrived(left_full.at[pl.ds(pl.multiple_of(other * rows + p * piece, piece), piece), :], own_recv.at[p])

    def y_slot(side, pos, p, core, count=1):
        at = 3 * side if pos == 0 else 1 + side
        return left_full.at[block(at, p * piece, count * piece), pl.ds(pl.multiple_of(core * half, half), half)]

    def y_copy(pos, p, own=False):
        slot = y_slot(yc, pos, p, k)
        source = left_ref.at[pl.ds(pl.multiple_of(p * piece, piece), piece), own_half()] if own else slot
        return remote(source, slot, send.at[6], y_recv.at[pos, p], y_dev)

    def s_copy(pos, p, group):
        slot = y_slot(1 - yc, pos, p, k)
        return remote(slot, slot, send.at[7], s_recv.at[group], sib_dev)

    def part_copy(q):
        return remote(part.at[q], part.at[q], send.at[8], far_recv.at[q], z_dev(1))

    def each(body, first=0, last=steps):
        def step(at, carry):
            body(at)
            return carry

        lax.fori_loop(first, last, step, 0)

    @when(inner)
    def _():
        @each
        def _(q):
            in_copy(-1, q).start()
            in_copy(1, q).start()

    when(end)(lambda: each(end_start, 0, early))
    first = kc == yc
    when(first)(lambda: each(lambda p: y_copy(0, p, True).start()))
    own_left = pltpu.make_async_copy(left_ref, left_full.at[pl.ds(pl.multiple_of(r * rows, rows), rows), :], own_sem.at[0])
    own = pltpu.make_async_copy(right_ref, right_full.at[block(zc), :], own_sem.at[1])
    weights = pltpu.make_async_copy(w_hbm, w_in, own_sem.at[2])
    counts_copy = pltpu.make_async_copy(counts_ref, counts_in, own_sem.at[3])
    each(lambda p: own_copy(p).start())
    for copy in (own_left, own, weights, counts_copy):
        copy.start()

    @each
    def _(p):
        own_arrived(p)
        when(jnp.logical_not(first))(lambda: y_copy(0, p).start())
        when(end, yc == 0, kc == 1)(lambda: far_copy(p).start())

    own_left.wait()
    when(end, yc == 0, kc == 0)(lambda: each(lambda p: far_copy(p).start()))
    each(lambda p: y_copy(1, p).start())
    when(end, yc == 0)(lambda: each(end_start, early))

    row = lax.broadcasted_iota(jnp.int32, (TILE, TILE), 0)
    column = lax.broadcasted_iota(jnp.int32, (TILE, TILE), 1)
    order[...] = jnp.where(column == (row % heads) * CH + row // heads, 1.0, 0.0).astype(order.dtype)
    weights.wait()
    w_wide[...] = w_in[...].astype(jnp.float32)
    for e in range(CH):
        some = w_wide[pl.ds(e, CH, stride=CH), :].astype(w_ref.dtype)
        for i in range(2):
            w_ref[pl.ds((2 * e + i) * CH, CH), i * pair:(i + 1) * pair] = some
            w_ref[pl.ds((2 * e + i) * CH, CH), (1 - i) * pair:(2 - i) * pair] = jnp.zeros_like(some)
    counts_copy.wait()
    counted = counts_in[...].astype(jnp.float32)
    for i in range(counted.shape[1]):
        cover[i // 4, i % 4] = jnp.broadcast_to(counted[:, i:i + 1], (counted.shape[0], cover.shape[3]))

    def turn(at, q):
        value = lax.dot_general(order[...], right_full[block(at), cols(q)], (((1,), (1,)), ((), ())), preferred_element_type=jnp.float32)
        right_t[cols(q), block(at)] = value.astype(right_t.dtype)

    def product(into, lines, source, left, left_rows, size, wide, add):
        for n in range(width_l // wide):
            value = jnp.dot(right_t[lines, source], left[left_rows, pl.ds(n * wide, wide)], preferred_element_type=jnp.float32)
            for one in range(wide // 128):
                some = value[:, one * 128:(one + 1) * 128]
                slab = n * (wide // 128) + one
                into[slab, size, :] = into[slab, size, :] + some if add else some

    def product_all(at, add, first=0, depth=rows):
        every = pl.ds(0, width_r)
        product(acc, every, block(at, first, depth), left_full, block(at, first, depth), every, 256, add)

    def product_one(at, q):
        product(acc, cols(q), block(at), left_full, block(at), cols(q), 512, True)

    def project(source, first_row):
        low = lax.broadcasted_iota(jnp.int32, (lines, 128), 1) < 64
        for two in range(CH // 2):
            a, b = (
                source[:, pl.ds(pl.multiple_of(first_row + e * heads, heads), heads), :].reshape(lines, 128).astype(flat.dtype)
                for e in (2 * two, 2 * two + 1)
            )
            at = pl.ds(two * 128, 128)
            flat[pl.ds(0, lines), at] = jnp.where(low, a, pltpu.roll(b, 64, 1))
            flat[pl.ds(lines, lines), at] = jnp.where(low, pltpu.roll(a, 64, 1), b)
        return jnp.dot(flat[...], w_ref[...], preferred_element_type=jnp.float32)

    def spot(i):
        return slice(i // 2 * lines, (i // 2 + 1) * lines), slice(i % 2 * pair, (i % 2 + 1) * pair)

    def settle(q, add):
        for i in range(4):
            value = out_v[q, :, i]
            if add:
                value = value + part[(q, *spot(i))].astype(jnp.float32).reshape(value.shape)
            at = pl.ds(pl.multiple_of(q * heads, heads), heads)
            out_ref[pl.ds(i, quads, stride=4), at, :] = value / cover[:, i, at, :]

    own.wait()
    each(lambda q: turn(zc, q))

    def pass_on(q, h):
        arrived(half_slot(3, q, h), end_recv.at[q, h])
        mid_copy(q, h).start()

    def end_arrived(q):
        for h in range(2):
            pass_on(q, h)
        turn(3, q)

    def share(p):
        arrived(far_slot(p, k), far_recv.at[p])
        share_copy(p).start()

    @each
    def _(p):
        arrived(y_slot(1 - yc, 0, p, k), y_recv.at[0, p])
        s_copy(0, p, 0).start()
        when(end, yc == 1)(lambda: far_copy(p).start())
        arrived(right_slot(zc - 1, p), in_recv.at[0, p])
        when(inner)(lambda: fwd_copy(p).start())
        turn(zc - 1, p)
        when(inner, p >= 1, p <= early)(lambda: end_arrived(p - 1))

    when(end, yc == 1)(lambda: each(end_start, early))
    arrived(y_slot(1 - yc, 0, 0, 1 - k, steps), s_recv.at[0])
    late = 2 - yc
    groups = ((0, early), (early, early + 1), (early + 1, steps))

    def y_arrived(p):
        group = next(at for at, (_, last) in enumerate(groups) if p < last)
        arrived(y_slot(1 - yc, 1, p, k), y_recv.at[1, p])
        s_copy(1, p, 1 + group).start()

    def late_part(group):
        low, high = groups[group]
        arrived(y_slot(1 - yc, 1, low, 1 - k, high - low), s_recv.at[1 + group])
        product_all(late, True, low * piece, (high - low) * piece)

    def far_turn(q):
        arrived(right_slot(0, q), in_recv.at[1, q])
        turn(0, q)

    def far_product(q):
        product(acc_far, cols(q), block(0), left_far, pl.ds(0, rows), pl.ds(0, TILE), 512, False)

    def far_send_on(q):
        part[q] = project(acc_far, 0).astype(part.dtype)
        part_copy(q).start()

    def finish(q):
        value = project(acc, q * TILE)
        for i in range(4):
            out_v[q, :, i] = value[spot(i)].reshape(quads, heads, pair)

    def sent(sem, count=1):
        slot = left_full.at[pl.ds(0, count * rows), pl.ds(0, half)]
        arrived(slot, send.at[sem])

    @when(inner)
    def _():
        each(share, 0, early)
        product_all(1 + yc, False)
        for q in range(early):
            product_one(3, q)
        y_arrived(0)
        share(2)
        far_turn(0)
        product_one(0, 0)
        share(3)
        arrived(left_far.at[:, pl.ds(pl.multiple_of((1 - k) * half, half), half)], a_recv.at[0])
        far_product(0)
        y_arrived(1)
        far_send_on(0)
        pass_on(2, 0)
        far_turn(1)
        far_product(1)
        far_send_on(1)
        pass_on(2, 1)
        product_one(0, 1)
        turn(3, 2)
        y_arrived(2)
        product_one(3, 2)
        pass_on(3, 0)
        late_part(0)
        late_part(1)
        pass_on(3, 1)
        far_turn(2)
        far_product(2)
        y_arrived(3)
        far_send_on(2)
        turn(3, 3)
        product_one(3, 3)
        product_one(0, 2)
        far_turn(3)
        far_product(3)
        far_send_on(3)
        late_part(2)
        product_one(0, 3)

        @each
        def _(q):
            finish(q)
            settle(q, False)

        sent(0)
        sent(1)
        sent(2)
        sent(3)
        sent(4)
        sent(5, 2)
        sent(6, 2)
        sent(7, 2)
        arrived(part, send.at[8])

    @when(end)
    def _():
        product_all(3, False)
        for q in range(steps):
            y_arrived(q)
            arrived(right_slot(1, q), in_recv.at[1, q])
            turn(1, q)
            product_one(1 + yc, q)
        for group in range(len(groups)):
            late_part(group)
        each(finish)
        sent(2)
        sent(3)
        sent(5, 2)
        sent(6, 2)
        sent(7, 2)

        @each
        def _(q):
            arrived(part.at[q], far_recv.at[q])
            settle(q, True)


def folded_call(left_act, right_act, counts, w_out):
    rows, width_l = left_act.shape
    width_r = right_act.shape[1]
    left_dev, right_dev = counts.shape
    pair = w_out.shape[1]
    steps = width_r // TILE
    heads = TILE // CH
    full = 4 * rows
    dma = pltpu.SemaphoreType.DMA
    return pl.pallas_call(
        folded,
        out_shape=jax.ShapeDtypeStruct((left_dev, right_dev, pair), jnp.float32),
        in_specs=[pl.BlockSpec(memory_space=pl.ANY)] * 4,
        out_specs=pl.BlockSpec(memory_space=pltpu.VMEM),
        scratch_shapes=[
            pltpu.VMEM(w_out.shape, w_out.dtype),
            pltpu.VMEM(w_out.shape, jnp.float32),
            pltpu.VMEM((2 * w_out.shape[0], 2 * pair), w_out.dtype),
            pltpu.VMEM((right_dev, left_dev), counts.dtype),
            pltpu.VMEM((left_dev // 4, 4, right_dev, pair), jnp.float32),
            pltpu.VMEM((TILE, TILE), jnp.bfloat16),
            pltpu.VMEM((full, width_l), jnp.bfloat16),
            pltpu.VMEM((rows, width_l), jnp.bfloat16),
            pltpu.VMEM((full, width_r), jnp.bfloat16),
            pltpu.VMEM((width_r, full), jnp.bfloat16),
            pltpu.VMEM((width_l // 128, width_r, 128), jnp.float32),
            pltpu.VMEM((width_l // 128, TILE, 128), jnp.float32),
            pltpu.VMEM((left_dev * heads // 2, 2 * CH * CH), jnp.bfloat16),
            pltpu.VMEM((steps, left_dev * heads // 2, 2 * pair), jnp.bfloat16),
            pltpu.VMEM((steps, left_dev // 4, 4, heads, pair), jnp.float32),
            dma((9,)), dma((2, steps)), dma((steps,)), dma((steps, 2)), dma((steps,)), dma((2, steps)), dma((4,)), dma((1,)), dma((4,)),
        ],
        compiler_params=pltpu.CompilerParams(collective_id=0, has_side_effects=True, vmem_limit_bytes=38000 * 1024),
        name="pair_mean",
    )(*(pltpu.with_memory_space_constraint(x, pltpu.HBM) for x in (left_act, right_act, counts.T, w_out)))


def solution(mesh):
    n_z, n_r = mesh.shape["left"], mesh.shape["right"]
    n_y = n_r // CORES

    def shards(left_act, right_act, counts, w_out):
        width_l, width_r = left_act.shape[1], right_act.shape[1]
        if (n_z, n_y) == (4, 2) and width_r == 4 * TILE and width_l == CORES * width_r:
            return folded_call(left_act, right_act, counts, w_out)
        rows_l, width_l = left_act.shape
        rows_r, width_r = right_act.shape
        seqs = rows_r * n_z
        left_dev, right_dev = counts.shape
        pair = w_out.shape[1]
        q_z = width_r // 256
        q_y = rows_l // max(128, rows_l // 4)
        projected = pl.pallas_call(
            functools.partial(kernel, (n_z, n_r, q_z, q_y)),
            out_shape=jax.ShapeDtypeStruct((left_dev, right_dev, pair), jnp.float32),
            in_specs=[pl.BlockSpec(memory_space=pl.ANY)] * 4,
            out_specs=pl.BlockSpec(memory_space=pl.ANY),
            scratch_shapes=[
                pltpu.VMEM(w_out.shape, w_out.dtype),
                pltpu.VMEM(counts.shape, counts.dtype),
                pltpu.VMEM((right_dev, left_dev, pair), jnp.float32),
                pltpu.VMEM((q_z, left_dev, right_dev // q_z, pair), jnp.float32),
                pltpu.VMEM((seqs, width_l), jnp.bfloat16),
                pltpu.VMEM((seqs, width_r), jnp.bfloat16),
                pltpu.VMEM((width_l, seqs), jnp.bfloat16),
                pltpu.VMEM((width_r // 128, width_l, 128), jnp.float32),
                pltpu.VMEM((width_r // q_z // CH * left_dev, CH * CH), jnp.bfloat16),
                pltpu.SemaphoreType.DMA((2, (n_z - 1) * q_z)),
                pltpu.SemaphoreType.DMA((2, (n_z - 1) * q_z)),
                pltpu.SemaphoreType.DMA((2, (n_y - 1) * q_y)),
                pltpu.SemaphoreType.DMA((2, (n_y - 1) * q_y)),
                pltpu.SemaphoreType.DMA(((2 * n_y - 1) * q_y,)),
                pltpu.SemaphoreType.DMA(((2 * n_y - 1) * q_y,)),
                pltpu.SemaphoreType.DMA((4,)),
                pltpu.SemaphoreType.DMA((q_z,)),
            ],
            compiler_params=pltpu.CompilerParams(
                collective_id=0, has_side_effects=True, vmem_limit_bytes=56 * 1024 * 1024
            ),
            name="pair_mean",
        )(left_act, right_act, counts, w_out)
        return projected

    in_specs = (
        P(("groups", "right"), "left"),
        P(("groups", "left"), "right"),
        P(("groups", "left"), "right"),
        P(),
    )
    out_specs = P(("groups", "left"), "right", None)
    return jax.shard_map(shards, mesh=mesh, in_specs=in_specs, out_specs=out_specs, check_vma=False)
```

```python
import functools

import jax
import jax.numpy as jnp
from jax import lax
from jax.experimental import pallas as pl
from jax.experimental.pallas import tpu as pltpu
from jax.sharding import PartitionSpec as P

CH = 32
CORES = 2
TILE = 256
MESH = pl.DeviceIdType.MESH


def lane_quads(tiles):
    lane = lax.broadcasted_iota(jnp.int32, tiles[0].shape, 1)
    low = lane < 64
    even = (lane % 64) < 32
    stage = [None] * 4
    for c in range(2):
        a, b = tiles[c], tiles[c + 2]
        stage[c] = jnp.where(low, a, pltpu.roll(b, 64, 1))
        stage[c + 2] = jnp.where(low, pltpu.roll(a, 64, 1), b)
    outs = [None] * 4
    for half in range(2):
        a, b = stage[2 * half], stage[2 * half + 1]
        outs[2 * half] = jnp.where(even, a, pltpu.roll(b, 32, 1))
        outs[2 * half + 1] = jnp.where(even, pltpu.roll(a, 96, 1), b)
    return outs


def kernel(sizes, left_ref, right_ref, counts_ref, w_hbm, out_ref, w_ref, counts_in, cover, out_v, left_full, right_full, left_t, acc, flat,
           z_send, z_recv, y_send, y_recv, s_send, s_recv, own_sem, out_sem):
    n_z, n_r, q_z, q_y = sizes
    n_y = n_r // CORES
    rows_l, width_l = left_ref.shape
    rows_r, width_r = right_ref.shape
    piece_r = width_r // q_z
    piece_l = rows_l // q_y
    left_dev = width_l // CH
    right_dev = width_r // CH
    seqs = left_t.shape[1]
    z = lax.axis_index("left")
    r = lax.axis_index("right")
    y = r // CORES
    k = r % CORES

    def z_dev(pos):
        return {"left": pos}

    def y_dev(pos):
        return {"right": pos * CORES + k}

    sib_dev = {"right": y * CORES + (1 - k)}

    barrier = pltpu.get_barrier_semaphore()

    def greet(dev):
        pl.semaphore_signal(barrier, inc=1, device_id=dev, device_id_type=MESH)

    greet(sib_dev)
    for pos, n, dev in ((z, n_z, z_dev), (y, n_y, y_dev)):
        pl.when(pos + 1 < n)(functools.partial(greet, dev(pos + 1)))
        pl.when(pos >= 1)(functools.partial(greet, dev(pos - 1)))
    total = 1 + (z + 1 < n_z).astype(jnp.int32) + (z >= 1).astype(jnp.int32)
    total = total + (y + 1 < n_y).astype(jnp.int32) + (y >= 1).astype(jnp.int32)
    pl.semaphore_wait(barrier, total)

    def z_slot(chunk, q):
        return right_full.at[pl.ds(pl.multiple_of(chunk * rows_r, rows_r), rows_r), pl.ds(q * piece_r, piece_r)]

    def z_copy(side, step, q):
        sign = 1 - 2 * side
        chunk = z - sign * step
        src = right_ref.at[:, pl.ds(q * piece_r, piece_r)] if step == 0 else z_slot(chunk, q)
        at = step * q_z + q
        return pltpu.make_async_remote_copy(
            src_ref=src, dst_ref=z_slot(chunk, q), send_sem=z_send.at[side, at], recv_sem=z_recv.at[side, at],
            device_id=z_dev(z + sign), device_id_type=MESH)

    def z_sends(side, step):
        near = z + 1 < n_z if side == 0 else z >= 1
        far = z - step >= 0 if side == 0 else z + step < n_z
        return jnp.logical_and(near, far)

    def z_arrives(side, step):
        return z - step - 1 >= 0 if side == 0 else z + step + 1 < n_z

    def z_wait(side, step, q):
        sign = 1 - 2 * side
        slot = z_slot(z - sign * (step + 1), q)
        pltpu.make_async_copy(slot, slot, z_recv.at[side, step * q_z + q]).wait()

    def l_slot(chunk, q):
        return left_full.at[pl.ds(pl.multiple_of(chunk * rows_l + q * piece_l, piece_l), piece_l), :]

    def l_own(q):
        return left_ref.at[pl.ds(q * piece_l, piece_l), :]

    def y_copy(side, step, q):
        sign = 1 - 2 * side
        chunk = (y - sign * step) * CORES + k
        at = step * q_y + q
        return pltpu.make_async_remote_copy(
            src_ref=l_own(q) if step == 0 else l_slot(chunk, q), dst_ref=l_slot(chunk, q),
            send_sem=y_send.at[side, at], recv_sem=y_recv.at[side, at],
            device_id=y_dev(y + sign), device_id_type=MESH)

    def y_sends(side, step):
        near = y + 1 < n_y if side == 0 else y >= 1
        far = y - step >= 0 if side == 0 else y + step < n_y
        return jnp.logical_and(near, far)

    def y_arrives(side, step):
        return y - step - 1 >= 0 if side == 0 else y + step + 1 < n_y

    def y_wait(side, step, q):
        sign = 1 - 2 * side
        slot = l_slot((y - sign * (step + 1)) * CORES + k, q)
        pltpu.make_async_copy(slot, slot, y_recv.at[side, step * q_y + q]).wait()

    def s_at(side, step, q):
        if step < 0:
            return q
        return (1 + side * (n_y - 1) + step) * q_y + q

    def s_copy(side, step, q):
        sign = 1 - 2 * side
        chunk = (y - sign * (step + 1)) * CORES + k if step >= 0 else r
        at = s_at(side, step, q)
        return pltpu.make_async_remote_copy(
            src_ref=l_own(q) if step < 0 else l_slot(chunk, q), dst_ref=l_slot(chunk, q),
            send_sem=s_send.at[at], recv_sem=s_recv.at[at],
            device_id=sib_dev, device_id_type=MESH)

    def s_wait(side, step, q):
        sign = 1 - 2 * side
        y_from = y - sign * (step + 1) if step >= 0 else y
        slot = l_slot(y_from * CORES + (1 - k), q)
        pltpu.make_async_copy(slot, slot, s_recv.at[s_at(side, step, q)]).wait()

    tile = 256

    def turn(src, first_row, chunk, q):
        col = pl.multiple_of(chunk * rows_l + q * piece_l, piece_l)

        def body(m, carry):
            at = pl.multiple_of(m * tile, tile)
            left_t[pl.ds(at, tile), pl.ds(col, piece_l)] = src[pl.ds(first_row, piece_l), pl.ds(at, tile)].T
            return carry

        lax.fori_loop(0, width_l // tile, body, 0)

    def turn_full(chunk, q):
        turn(left_full, pl.multiple_of(chunk * rows_l + q * piece_l, piece_l), chunk, q)

    for q in range(max(q_z, q_y)):
        for side in range(2):
            if q < q_z:
                pl.when(z_sends(side, 0))(lambda side=side, q=q: z_copy(side, 0, q).start())
            if q < q_y:
                pl.when(y_sends(side, 0))(lambda side=side, q=q: y_copy(side, 0, q).start())
    own_left = pltpu.make_async_copy(left_ref, left_full.at[pl.ds(pl.multiple_of(r * rows_l, rows_l), rows_l), :], own_sem.at[0])
    own = pltpu.make_async_copy(right_ref, right_full.at[pl.ds(pl.multiple_of(z * rows_r, rows_r), rows_r), :], own_sem.at[1])
    weights = pltpu.make_async_copy(w_hbm, w_ref, own_sem.at[2])
    counts_copy = pltpu.make_async_copy(counts_ref, counts_in, own_sem.at[3])
    for copy in (own_left, own, weights, counts_copy):
        copy.start()
    for q in range(q_y):
        s_copy(0, -1, q).start()
    own_left.wait()
    for q in range(q_y):
        turn_full(r, q)
    counts_copy.wait()
    counted = counts_in[...].astype(jnp.float32)
    for j in range(right_dev):
        cover[j] = jnp.broadcast_to(counted[:, j:j + 1], (left_dev, cover.shape[2]))
    for q in range(q_y):
        s_wait(0, -1, q)
        turn_full(y * CORES + (1 - k), q)

    def z_tick(step, q):
        for side in range(2):
            @pl.when(z_arrives(side, step))
            def _():
                z_wait(side, step, q)
                if step + 1 < n_z - 1:
                    pl.when(z_sends(side, step + 1))(lambda: z_copy(side, step + 1, q).start())

    def y_tick(step, q):
        for side in range(2):
            @pl.when(y_arrives(side, step))
            def _():
                y_wait(side, step, q)
                s_copy(side, step, q).start()
                if step + 1 < n_y - 1:
                    pl.when(y_sends(side, step + 1))(lambda: y_copy(side, step + 1, q).start())

        for side in range(2):
            @pl.when(y_arrives(side, step))
            def _():
                sign = 1 - 2 * side
                y_from = y - sign * (step + 1)
                turn_full(y_from * CORES + k, q)
                s_wait(side, step, q)
                turn_full(y_from * CORES + (1 - k), q)

    y_ticks = [(step, q) for step in range(n_y - 1) for q in range(q_y)]
    for t in range((n_z - 2) * q_z):
        z_tick(t // q_z, t % q_z)
        if t % 2 == 1 and y_ticks:
            y_tick(*y_ticks.pop(0))
    for tick in y_ticks:
        y_tick(*tick)
    own.wait()
    weights.wait()

    block = 1024
    at_end = jnp.logical_or(z == 0, z == n_z - 1)
    base = jnp.where(z == 0, 0, rows_r)
    base = pl.multiple_of(base, rows_r)

    def product(q, first, depth, add):
        cols = pl.ds(q * piece_r, piece_r)

        def body(m, carry):
            rows = pl.ds(pl.multiple_of(m * block, block), block)
            value = jnp.dot(left_t[rows, pl.ds(first, depth)], right_full[pl.ds(first, depth), cols],
                            preferred_element_type=jnp.float32)
            for part in range(piece_r // 128):
                some = value[:, part * 128:(part + 1) * 128]
                slab = q * (piece_r // 128) + part
                acc[slab, rows, :] = acc[slab, rows, :] + some if add else some
            return carry

        lax.fori_loop(0, width_l // block, body, 0)

    def first_part(q):
        @pl.when(at_end)
        def _():
            product(q, base, seqs - rows_r, False)

        @pl.when(jnp.logical_not(at_end))
        def _():
            product(q, 0, seqs, False)

    for q in range(q_z):
        first_part(q)

    def finish(q):
        heads = piece_r // CH
        for quad in range(heads // 4):
            slab = acc.at[q * (piece_r // 128) + quad]
            for cq in range(CH // 4):
                tiles = [slab[pl.ds(cq * 4 + c, left_dev, stride=CH), :].astype(jnp.bfloat16) for c in range(4)]
                for j, value in enumerate(lane_quads(tiles)):
                    flat[pl.ds((quad * 4 + j) * left_dev, left_dev), pl.ds(cq * 128, 128)] = value
        projected = jnp.dot(flat[...], w_ref[...], preferred_element_type=jnp.float32)
        for j in range(heads):
            value = projected[j * left_dev:(j + 1) * left_dev, :] / cover[q * heads + j]
            out_v.at[q].reshape(left_dev * heads, value.shape[1])[pl.ds(j, left_dev, stride=heads), :] = value
        out_copy(q).start()

    def out_copy(q):
        return pltpu.make_async_copy(out_v.at[q], out_ref.at[:, pl.ds(q * heads_q, heads_q), :], out_sem.at[q])

    heads_q = piece_r // CH
    last = n_z - 2
    for q in range(q_z):
        z_tick(last, q)

        @pl.when(at_end)
        def _():
            far = jnp.where(z == 0, (n_z - 1) * rows_r, 0)
            product(q, pl.multiple_of(far, rows_r), rows_r, True)

        finish(q)

    for side in range(2):
        for step in range(n_z - 1):
            for q in range(q_z):
                pl.when(z_sends(side, step))(lambda side=side, step=step, q=q: z_copy(side, step, q).wait_send())
        for step in range(n_y - 1):
            for q in range(q_y):
                pl.when(y_sends(side, step))(lambda side=side, step=step, q=q: y_copy(side, step, q).wait_send())
                pl.when(y_arrives(side, step))(lambda side=side, step=step, q=q: s_copy(side, step, q).wait_send())
    for q in range(q_y):
        s_copy(0, -1, q).wait_send()
    for q in range(q_z):
        out_copy(q).wait()


def folded(left_ref, right_ref, counts_ref, w_hbm, out_ref, w_in, w_wide, w_ref, counts_in, cover, order, left_full, left_far, right_full, right_t,
           acc, acc_far, flat, part, out_v, send, in_recv, far_recv, end_recv, own_recv, y_recv, s_recv, a_recv, own_sem):
    rows, width_l = left_ref.shape
    width_r = right_ref.shape[1]
    steps = width_r // TILE
    piece = rows // steps
    half = width_l // CORES
    quads = width_l // 128
    heads = TILE // CH
    pair = w_hbm.shape[1]
    lines = quads * heads
    early = steps // 2
    z = lax.axis_index("left")
    r = lax.axis_index("right")
    y, k = r // CORES, r % CORES
    up = z // 2
    sign = 2 * up - 1

    def fold(n, at):
        return up * at + (1 - up) * (n - 1 - at)

    zc, yc, kc = fold(4, z), fold(2, y), fold(2, k)
    inner, end = zc == 2, zc == 3
    sib_dev = {"right": r + 1 - 2 * k}
    y_dev = {"right": r + (1 - 2 * y) * CORES}

    def when(*terms):
        value = terms[0]
        for term in terms[1:]:
            value = jnp.logical_and(value, term)
        return pl.when(value)

    def z_dev(way):
        return {"left": z + way * sign}

    barrier = pltpu.get_barrier_semaphore()

    def greet(dev):
        pl.semaphore_signal(barrier, inc=1, device_id=dev, device_id_type=MESH)

    greet(sib_dev)
    greet(y_dev)
    greet(z_dev(-1))
    when(inner)(lambda: greet(z_dev(1)))
    pl.semaphore_wait(barrier, 3 + inner.astype(jnp.int32))

    def remote(src, dst, send, recv, dev):
        return pltpu.make_async_remote_copy(src_ref=src, dst_ref=dst, send_sem=send, recv_sem=recv, device_id=dev, device_id_type=MESH)

    def arrived(slot, sem):
        pltpu.make_async_copy(slot, slot, sem).wait()

    def block(at, first=0, size=rows):
        return pl.ds(pl.multiple_of(fold(4, at) * rows + first, size), size)

    def cols(q):
        return pl.ds(pl.multiple_of(q * TILE, TILE), TILE)

    def right_slot(at, q):
        return right_full.at[block(at), cols(q)]

    def in_copy(way, q):
        return remote(right_ref.at[:, cols(q)], right_slot(2, q), send.at[(way + 1) // 2], in_recv.at[0, q], z_dev(way))

    def fwd_copy(q):
        slot = right_slot(1, q)
        return remote(slot, slot, send.at[2], in_recv.at[1, q], z_dev(1))

    def cut(q):
        return ((1, 0), (1, 1), (2, 2), (4, 4))[q]

    def cut_slot(at, q, h, n):
        return right_full.at[block(at, h * (rows // n), rows // n), cols(q)]

    def mid_copy(q, h=0, n=1):
        slot = cut_slot(3, q, h, n)
        return remote(slot, slot, send.at[3], in_recv.at[1, q], z_dev(-1))

    def end_start(q):
        n, at = cut(q)
        for h in range(n):
            source = right_ref.at[pl.ds(h * (rows // n), rows // n), cols(q)]
            remote(source, cut_slot(3, q, h, n), send.at[3], end_recv.at[at + h], z_dev(-1)).start()

    def own_half():
        return pl.ds(pl.multiple_of(k * half, half), half)

    def far_copy(p):
        at = pl.ds(pl.multiple_of(p * piece, piece), piece)
        return remote(left_full.at[block(0, p * piece, piece), own_half()], left_far.at[at, own_half()], send.at[2], far_recv.at[p], z_dev(-1))

    def far_slot(p, core):
        return left_far.at[pl.ds(pl.multiple_of(p * piece, piece), piece), pl.ds(pl.multiple_of(core * half, half), half)]

    def share_copy(p):
        return remote(far_slot(p, k), far_slot(p, k), send.at[4], a_recv.at[0], sib_dev)

    def own_copy(p):
        at = pl.ds(pl.multiple_of(p * piece, piece), piece)
        slot = left_full.at[pl.ds(pl.multiple_of(r * rows + p * piece, piece), piece), :]
        return remote(left_ref.at[at, :], slot, send.at[5], own_recv.at[p], sib_dev)

    def own_arrived(p):
        other = r + 1 - 2 * k
        arrived(left_full.at[pl.ds(pl.multiple_of(other * rows + p * piece, piece), piece), :], own_recv.at[p])

    def y_slot(side, pos, p, core, count=1):
        at = 3 * side if pos == 0 else 1 + side
        return left_full.at[block(at, p * piece, count * piece), pl.ds(pl.multiple_of(core * half, half), half)]

    def y_copy(pos, p, own=False):
        slot = y_slot(yc, pos, p, k)
        source = left_ref.at[pl.ds(pl.multiple_of(p * piece, piece), piece), own_half()] if own else slot
        return remote(source, slot, send.at[6], y_recv.at[pos, p], y_dev)

    def s_copy(pos, p, group):
        slot = y_slot(1 - yc, pos, p, k)
        return remote(slot, slot, send.at[7], s_recv.at[group], sib_dev)

    def part_copy(q):
        return remote(part.at[q], part.at[q], send.at[8], far_recv.at[q], z_dev(1))

    def each(body, first=0, last=steps):
        def step(at, carry):
            body(at)
            return carry

        lax.fori_loop(first, last, step, 0)

    @when(inner)
    def _():
        @each
        def _(q):
            in_copy(-1, q).start()
            in_copy(1, q).start()


    @when(end)
    def _():
        end_start(0)
        end_start(1)

    first = kc == yc
    when(first)(lambda: each(lambda p: y_copy(0, p, True).start()))
    own_left = pltpu.make_async_copy(left_ref, left_full.at[pl.ds(pl.multiple_of(r * rows, rows), rows), :], own_sem.at[0])
    own = pltpu.make_async_copy(right_ref, right_full.at[block(zc), :], own_sem.at[1])
    weights = pltpu.make_async_copy(w_hbm, w_in, own_sem.at[2])
    counts_copy = pltpu.make_async_copy(counts_ref, counts_in, own_sem.at[3])
    each(lambda p: own_copy(p).start())
    for copy in (own_left, own, weights, counts_copy):
        copy.start()

    @each
    def _(p):
        own_arrived(p)
        when(jnp.logical_not(first))(lambda: y_copy(0, p).start())
        when(end, yc == 0, kc == 1)(lambda: far_copy(p).start())
        when(end, yc == 0, kc == 1, p == steps - 2)(lambda: end_start(2))

    own_left.wait()

    @when(end, yc == 0, kc == 0)
    def _():
        each(lambda p: far_copy(p).start(), 0, steps - 1)
        end_start(2)
        far_copy(steps - 1).start()

    each(lambda p: y_copy(1, p).start())
    when(end, yc == 0)(lambda: end_start(3))

    row = lax.broadcasted_iota(jnp.int32, (TILE, TILE), 0)
    column = lax.broadcasted_iota(jnp.int32, (TILE, TILE), 1)
    order[...] = jnp.where(column == (row % heads) * CH + row // heads, 1.0, 0.0).astype(order.dtype)
    weights.wait()
    w_wide[...] = w_in[...].astype(jnp.float32)
    for e in range(CH):
        some = w_wide[pl.ds(e, CH, stride=CH), :].astype(w_ref.dtype)
        for i in range(2):
            w_ref[pl.ds((2 * e + i) * CH, CH), i * pair:(i + 1) * pair] = some
            w_ref[pl.ds((2 * e + i) * CH, CH), (1 - i) * pair:(2 - i) * pair] = jnp.zeros_like(some)
    counts_copy.wait()
    counted = counts_in[...].astype(jnp.float32)
    for i in range(counted.shape[1]):
        cover[i // 4, i % 4] = jnp.broadcast_to(counted[:, i:i + 1], (counted.shape[0], cover.shape[3]))

    def turn(at, q):
        value = lax.dot_general(order[...], right_full[block(at), cols(q)], (((1,), (1,)), ((), ())), preferred_element_type=jnp.float32)
        right_t[cols(q), block(at)] = value.astype(right_t.dtype)

    def product(into, lines, source, left, left_rows, size, wide, add):
        for n in range(width_l // wide):
            value = jnp.dot(right_t[lines, source], left[left_rows, pl.ds(n * wide, wide)], preferred_element_type=jnp.float32)
            for one in range(wide // 128):
                some = value[:, one * 128:(one + 1) * 128]
                slab = n * (wide // 128) + one
                into[slab, size, :] = into[slab, size, :] + some if add else some

    def product_all(at, add, first=0, depth=rows):
        every = pl.ds(0, width_r)
        product(acc, every, block(at, first, depth), left_full, block(at, first, depth), every, 256, add)

    def product_one(at, q):
        product(acc, cols(q), block(at), left_full, block(at), cols(q), 512, True)

    def project(source, first_row):
        low = lax.broadcasted_iota(jnp.int32, (lines, 128), 1) < 64
        for two in range(CH // 2):
            a, b = (
                source[:, pl.ds(pl.multiple_of(first_row + e * heads, heads), heads), :].reshape(lines, 128).astype(flat.dtype)
                for e in (2 * two, 2 * two + 1)
            )
            at = pl.ds(two * 128, 128)
            flat[pl.ds(0, lines), at] = jnp.where(low, a, pltpu.roll(b, 64, 1))
            flat[pl.ds(lines, lines), at] = jnp.where(low, pltpu.roll(a, 64, 1), b)
        return jnp.dot(flat[...], w_ref[...], preferred_element_type=jnp.float32)

    def spot(i):
        return slice(i // 2 * lines, (i // 2 + 1) * lines), slice(i % 2 * pair, (i % 2 + 1) * pair)

    def settle(q, add):
        for i in range(4):
            value = out_v[q, :, i]
            if add:
                value = value + part[(q, *spot(i))].astype(jnp.float32).reshape(value.shape)
            at = pl.ds(pl.multiple_of(q * heads, heads), heads)
            out_ref[pl.ds(i, quads, stride=4), at, :] = value / cover[:, i, at, :]

    own.wait()
    each(lambda q: turn(zc, q))

    def pass_on(q, h):
        n, at = cut(q)
        arrived(cut_slot(3, q, h, n), end_recv.at[at + h])
        mid_copy(q, h, n).start()

    def end_arrived(q):
        arrived(right_slot(3, q), end_recv.at[q])
        mid_copy(q).start()
        turn(3, q)

    def share(p):
        arrived(far_slot(p, k), far_recv.at[p])
        share_copy(p).start()

    @each
    def _(p):
        arrived(y_slot(1 - yc, 0, p, k), y_recv.at[0, p])
        s_copy(0, p, 0).start()
        when(end, yc == 1)(lambda: far_copy(p).start())
        when(end, yc == 1, p == steps - 2)(lambda: end_start(2))
        arrived(right_slot(zc - 1, p), in_recv.at[0, p])
        when(inner)(lambda: fwd_copy(p).start())
        turn(zc - 1, p)
        when(inner, p >= 1, p <= early)(lambda: end_arrived(p - 1))

    when(end, yc == 1)(lambda: end_start(3))
    arrived(y_slot(1 - yc, 0, 0, 1 - k, steps), s_recv.at[0])
    late = 2 - yc
    groups = ((0, early), (early, early + 1), (early + 1, steps))

    def y_arrived(p):
        group = next(at for at, (_, last) in enumerate(groups) if p < last)
        arrived(y_slot(1 - yc, 1, p, k), y_recv.at[1, p])
        s_copy(1, p, 1 + group).start()

    def late_part(group):
        low, high = groups[group]
        arrived(y_slot(1 - yc, 1, low, 1 - k, high - low), s_recv.at[1 + group])
        product_all(late, True, low * piece, (high - low) * piece)

    def far_turn(q):
        arrived(right_slot(0, q), in_recv.at[1, q])
        turn(0, q)

    def far_product(q):
        product(acc_far, cols(q), block(0), left_far, pl.ds(0, rows), pl.ds(0, TILE), 512, False)

    def far_send_on(q):
        part[q] = project(acc_far, 0).astype(part.dtype)
        part_copy(q).start()

    def finish(q):
        value = project(acc, q * TILE)
        for i in range(4):
            out_v[q, :, i] = value[spot(i)].reshape(quads, heads, pair)

    def sent(sem, count=1):
        slot = left_full.at[pl.ds(0, count * rows), pl.ds(0, half)]
        arrived(slot, send.at[sem])

    @when(inner)
    def _():
        each(share, 0, early)
        product_all(1 + yc, False)
        for q in range(early):
            product_one(3, q)
        y_arrived(0)
        share(2)
        far_turn(0)
        product_one(0, 0)
        pass_on(2, 0)
        pass_on(2, 1)
        turn(3, 2)
        product_one(3, 2)
        y_arrived(1)
        far_turn(1)
        product_one(0, 1)
        late_part(0)
        share(3)
        arrived(left_far.at[:, pl.ds(pl.multiple_of((1 - k) * half, half), half)], a_recv.at[0])
        far_product(0)
        y_arrived(2)
        far_send_on(0)
        pass_on(3, 0)
        far_product(1)
        far_send_on(1)
        pass_on(3, 1)
        far_turn(2)
        far_product(2)
        pass_on(3, 2)
        far_send_on(2)
        pass_on(3, 3)
        late_part(1)
        y_arrived(3)
        turn(3, 3)
        product_one(3, 3)
        product_one(0, 2)
        far_turn(3)
        far_product(3)
        far_send_on(3)
        late_part(2)
        product_one(0, 3)

        @each
        def _(q):
            finish(q)
            settle(q, False)

        sent(0)
        sent(1)
        sent(2)
        sent(3)
        sent(4)
        sent(5, 2)
        sent(6, 2)
        sent(7, 2)
        arrived(part, send.at[8])

    @when(end)
    def _():
        product_all(3, False)
        for q in range(steps):
            y_arrived(q)
            arrived(right_slot(1, q), in_recv.at[1, q])
            turn(1, q)
            product_one(1 + yc, q)
        for group in range(len(groups)):
            late_part(group)
        each(finish)
        sent(2)
        sent(3)
        sent(5, 2)
        sent(6, 2)
        sent(7, 2)

        @each
        def _(q):
            arrived(part.at[q], far_recv.at[q])
            settle(q, True)


def folded_call(left_act, right_act, counts, w_out):
    rows, width_l = left_act.shape
    width_r = right_act.shape[1]
    left_dev, right_dev = counts.shape
    pair = w_out.shape[1]
    steps = width_r // TILE
    heads = TILE // CH
    full = 4 * rows
    dma = pltpu.SemaphoreType.DMA
    return pl.pallas_call(
        folded,
        out_shape=jax.ShapeDtypeStruct((left_dev, right_dev, pair), jnp.float32),
        in_specs=[pl.BlockSpec(memory_space=pl.ANY)] * 4,
        out_specs=pl.BlockSpec(memory_space=pltpu.VMEM),
        scratch_shapes=[
            pltpu.VMEM(w_out.shape, w_out.dtype),
            pltpu.VMEM(w_out.shape, jnp.float32),
            pltpu.VMEM((2 * w_out.shape[0], 2 * pair), w_out.dtype),
            pltpu.VMEM((right_dev, left_dev), counts.dtype),
            pltpu.VMEM((left_dev // 4, 4, right_dev, pair), jnp.float32),
            pltpu.VMEM((TILE, TILE), jnp.bfloat16),
            pltpu.VMEM((full, width_l), jnp.bfloat16),
            pltpu.VMEM((rows, width_l), jnp.bfloat16),
            pltpu.VMEM((full, width_r), jnp.bfloat16),
            pltpu.VMEM((width_r, full), jnp.bfloat16),
            pltpu.VMEM((width_l // 128, width_r, 128), jnp.float32),
            pltpu.VMEM((width_l // 128, TILE, 128), jnp.float32),
            pltpu.VMEM((left_dev * heads // 2, 2 * CH * CH), jnp.bfloat16),
            pltpu.VMEM((steps, left_dev * heads // 2, 2 * pair), jnp.bfloat16),
            pltpu.VMEM((steps, left_dev // 4, 4, heads, pair), jnp.float32),
            dma((9,)), dma((2, steps)), dma((steps,)), dma((8,)), dma((steps,)), dma((2, steps)), dma((4,)), dma((1,)), dma((4,)),
        ],
        compiler_params=pltpu.CompilerParams(collective_id=0, has_side_effects=True, vmem_limit_bytes=38000 * 1024),
        name="pair_mean",
    )(*(pltpu.with_memory_space_constraint(x, pltpu.HBM) for x in (left_act, right_act, counts.T, w_out)))


def solution(mesh):
    n_z, n_r = mesh.shape["left"], mesh.shape["right"]
    n_y = n_r // CORES

    def shards(left_act, right_act, counts, w_out):
        width_l, width_r = left_act.shape[1], right_act.shape[1]
        if (n_z, n_y) == (4, 2) and width_r == 4 * TILE and width_l == CORES * width_r:
            return folded_call(left_act, right_act, counts, w_out)
        rows_l, width_l = left_act.shape
        rows_r, width_r = right_act.shape
        seqs = rows_r * n_z
        left_dev, right_dev = counts.shape
        pair = w_out.shape[1]
        q_z = width_r // 256
        q_y = rows_l // max(128, rows_l // 4)
        projected = pl.pallas_call(
            functools.partial(kernel, (n_z, n_r, q_z, q_y)),
            out_shape=jax.ShapeDtypeStruct((left_dev, right_dev, pair), jnp.float32),
            in_specs=[pl.BlockSpec(memory_space=pl.ANY)] * 4,
            out_specs=pl.BlockSpec(memory_space=pl.ANY),
            scratch_shapes=[
                pltpu.VMEM(w_out.shape, w_out.dtype),
                pltpu.VMEM(counts.shape, counts.dtype),
                pltpu.VMEM((right_dev, left_dev, pair), jnp.float32),
                pltpu.VMEM((q_z, left_dev, right_dev // q_z, pair), jnp.float32),
                pltpu.VMEM((seqs, width_l), jnp.bfloat16),
                pltpu.VMEM((seqs, width_r), jnp.bfloat16),
                pltpu.VMEM((width_l, seqs), jnp.bfloat16),
                pltpu.VMEM((width_r // 128, width_l, 128), jnp.float32),
                pltpu.VMEM((width_r // q_z // CH * left_dev, CH * CH), jnp.bfloat16),
                pltpu.SemaphoreType.DMA((2, (n_z - 1) * q_z)),
                pltpu.SemaphoreType.DMA((2, (n_z - 1) * q_z)),
                pltpu.SemaphoreType.DMA((2, (n_y - 1) * q_y)),
                pltpu.SemaphoreType.DMA((2, (n_y - 1) * q_y)),
                pltpu.SemaphoreType.DMA(((2 * n_y - 1) * q_y,)),
                pltpu.SemaphoreType.DMA(((2 * n_y - 1) * q_y,)),
                pltpu.SemaphoreType.DMA((4,)),
                pltpu.SemaphoreType.DMA((q_z,)),
            ],
            compiler_params=pltpu.CompilerParams(
                collective_id=0, has_side_effects=True, vmem_limit_bytes=56 * 1024 * 1024
            ),
            name="pair_mean",
        )(left_act, right_act, counts, w_out)
        return projected

    in_specs = (
        P(("groups", "right"), "left"),
        P(("groups", "left"), "right"),
        P(("groups", "left"), "right"),
        P(),
    )
    out_specs = P(("groups", "left"), "right", None)
    return jax.shard_map(shards, mesh=mesh, in_specs=in_specs, out_specs=out_specs, check_vma=False)
```

```python
import functools

import jax
import jax.numpy as jnp
from jax import lax
from jax.experimental import pallas as pl
from jax.experimental.pallas import tpu as pltpu
from jax.sharding import PartitionSpec as P

CH = 32
CORES = 2
TILE = 256
MESH = pl.DeviceIdType.MESH


def lane_quads(tiles):
    lane = lax.broadcasted_iota(jnp.int32, tiles[0].shape, 1)
    low = lane < 64
    even = (lane % 64) < 32
    stage = [None] * 4
    for c in range(2):
        a, b = tiles[c], tiles[c + 2]
        stage[c] = jnp.where(low, a, pltpu.roll(b, 64, 1))
        stage[c + 2] = jnp.where(low, pltpu.roll(a, 64, 1), b)
    outs = [None] * 4
    for half in range(2):
        a, b = stage[2 * half], stage[2 * half + 1]
        outs[2 * half] = jnp.where(even, a, pltpu.roll(b, 32, 1))
        outs[2 * half + 1] = jnp.where(even, pltpu.roll(a, 96, 1), b)
    return outs


def kernel(sizes, left_ref, right_ref, counts_ref, w_hbm, out_ref, w_ref, counts_in, cover, out_v, left_full, right_full, left_t, acc, flat,
           z_send, z_recv, y_send, y_recv, s_send, s_recv, own_sem, out_sem):
    n_z, n_r, q_z, q_y = sizes
    n_y = n_r // CORES
    rows_l, width_l = left_ref.shape
    rows_r, width_r = right_ref.shape
    piece_r = width_r // q_z
    piece_l = rows_l // q_y
    left_dev = width_l // CH
    right_dev = width_r // CH
    seqs = left_t.shape[1]
    z = lax.axis_index("left")
    r = lax.axis_index("right")
    y = r // CORES
    k = r % CORES

    def z_dev(pos):
        return {"left": pos}

    def y_dev(pos):
        return {"right": pos * CORES + k}

    sib_dev = {"right": y * CORES + (1 - k)}

    barrier = pltpu.get_barrier_semaphore()

    def greet(dev):
        pl.semaphore_signal(barrier, inc=1, device_id=dev, device_id_type=MESH)

    greet(sib_dev)
    for pos, n, dev in ((z, n_z, z_dev), (y, n_y, y_dev)):
        pl.when(pos + 1 < n)(functools.partial(greet, dev(pos + 1)))
        pl.when(pos >= 1)(functools.partial(greet, dev(pos - 1)))
    total = 1 + (z + 1 < n_z).astype(jnp.int32) + (z >= 1).astype(jnp.int32)
    total = total + (y + 1 < n_y).astype(jnp.int32) + (y >= 1).astype(jnp.int32)
    pl.semaphore_wait(barrier, total)

    def z_slot(chunk, q):
        return right_full.at[pl.ds(pl.multiple_of(chunk * rows_r, rows_r), rows_r), pl.ds(q * piece_r, piece_r)]

    def z_copy(side, step, q):
        sign = 1 - 2 * side
        chunk = z - sign * step
        src = right_ref.at[:, pl.ds(q * piece_r, piece_r)] if step == 0 else z_slot(chunk, q)
        at = step * q_z + q
        return pltpu.make_async_remote_copy(
            src_ref=src, dst_ref=z_slot(chunk, q), send_sem=z_send.at[side, at], recv_sem=z_recv.at[side, at],
            device_id=z_dev(z + sign), device_id_type=MESH)

    def z_sends(side, step):
        near = z + 1 < n_z if side == 0 else z >= 1
        far = z - step >= 0 if side == 0 else z + step < n_z
        return jnp.logical_and(near, far)

    def z_arrives(side, step):
        return z - step - 1 >= 0 if side == 0 else z + step + 1 < n_z

    def z_wait(side, step, q):
        sign = 1 - 2 * side
        slot = z_slot(z - sign * (step + 1), q)
        pltpu.make_async_copy(slot, slot, z_recv.at[side, step * q_z + q]).wait()

    def l_slot(chunk, q):
        return left_full.at[pl.ds(pl.multiple_of(chunk * rows_l + q * piece_l, piece_l), piece_l), :]

    def l_own(q):
        return left_ref.at[pl.ds(q * piece_l, piece_l), :]

    def y_copy(side, step, q):
        sign = 1 - 2 * side
        chunk = (y - sign * step) * CORES + k
        at = step * q_y + q
        return pltpu.make_async_remote_copy(
            src_ref=l_own(q) if step == 0 else l_slot(chunk, q), dst_ref=l_slot(chunk, q),
            send_sem=y_send.at[side, at], recv_sem=y_recv.at[side, at],
            device_id=y_dev(y + sign), device_id_type=MESH)

    def y_sends(side, step):
        near = y + 1 < n_y if side == 0 else y >= 1
        far = y - step >= 0 if side == 0 else y + step < n_y
        return jnp.logical_and(near, far)

    def y_arrives(side, step):
        return y - step - 1 >= 0 if side == 0 else y + step + 1 < n_y

    def y_wait(side, step, q):
        sign = 1 - 2 * side
        slot = l_slot((y - sign * (step + 1)) * CORES + k, q)
        pltpu.make_async_copy(slot, slot, y_recv.at[side, step * q_y + q]).wait()

    def s_at(side, step, q):
        if step < 0:
            return q
        return (1 + side * (n_y - 1) + step) * q_y + q

    def s_copy(side, step, q):
        sign = 1 - 2 * side
        chunk = (y - sign * (step + 1)) * CORES + k if step >= 0 else r
        at = s_at(side, step, q)
        return pltpu.make_async_remote_copy(
            src_ref=l_own(q) if step < 0 else l_slot(chunk, q), dst_ref=l_slot(chunk, q),
            send_sem=s_send.at[at], recv_sem=s_recv.at[at],
            device_id=sib_dev, device_id_type=MESH)

    def s_wait(side, step, q):
        sign = 1 - 2 * side
        y_from = y - sign * (step + 1) if step >= 0 else y
        slot = l_slot(y_from * CORES + (1 - k), q)
        pltpu.make_async_copy(slot, slot, s_recv.at[s_at(side, step, q)]).wait()

    tile = 256

    def turn(src, first_row, chunk, q):
        col = pl.multiple_of(chunk * rows_l + q * piece_l, piece_l)

        def body(m, carry):
            at = pl.multiple_of(m * tile, tile)
            left_t[pl.ds(at, tile), pl.ds(col, piece_l)] = src[pl.ds(first_row, piece_l), pl.ds(at, tile)].T
            return carry

        lax.fori_loop(0, width_l // tile, body, 0)

    def turn_full(chunk, q):
        turn(left_full, pl.multiple_of(chunk * rows_l + q * piece_l, piece_l), chunk, q)

    for q in range(max(q_z, q_y)):
        for side in range(2):
            if q < q_z:
                pl.when(z_sends(side, 0))(lambda side=side, q=q: z_copy(side, 0, q).start())
            if q < q_y:
                pl.when(y_sends(side, 0))(lambda side=side, q=q: y_copy(side, 0, q).start())
    own_left = pltpu.make_async_copy(left_ref, left_full.at[pl.ds(pl.multiple_of(r * rows_l, rows_l), rows_l), :], own_sem.at[0])
    own = pltpu.make_async_copy(right_ref, right_full.at[pl.ds(pl.multiple_of(z * rows_r, rows_r), rows_r), :], own_sem.at[1])
    weights = pltpu.make_async_copy(w_hbm, w_ref, own_sem.at[2])
    counts_copy = pltpu.make_async_copy(counts_ref, counts_in, own_sem.at[3])
    for copy in (own_left, own, weights, counts_copy):
        copy.start()
    for q in range(q_y):
        s_copy(0, -1, q).start()
    own_left.wait()
    for q in range(q_y):
        turn_full(r, q)
    counts_copy.wait()
    counted = counts_in[...].astype(jnp.float32)
    for j in range(right_dev):
        cover[j] = jnp.broadcast_to(counted[:, j:j + 1], (left_dev, cover.shape[2]))
    for q in range(q_y):
        s_wait(0, -1, q)
        turn_full(y * CORES + (1 - k), q)

    def z_tick(step, q):
        for side in range(2):
            @pl.when(z_arrives(side, step))
            def _():
                z_wait(side, step, q)
                if step + 1 < n_z - 1:
                    pl.when(z_sends(side, step + 1))(lambda: z_copy(side, step + 1, q).start())

    def y_tick(step, q):
        for side in range(2):
            @pl.when(y_arrives(side, step))
            def _():
                y_wait(side, step, q)
                s_copy(side, step, q).start()
                if step + 1 < n_y - 1:
                    pl.when(y_sends(side, step + 1))(lambda: y_copy(side, step + 1, q).start())

        for side in range(2):
            @pl.when(y_arrives(side, step))
            def _():
                sign = 1 - 2 * side
                y_from = y - sign * (step + 1)
                turn_full(y_from * CORES + k, q)
                s_wait(side, step, q)
                turn_full(y_from * CORES + (1 - k), q)

    y_ticks = [(step, q) for step in range(n_y - 1) for q in range(q_y)]
    for t in range((n_z - 2) * q_z):
        z_tick(t // q_z, t % q_z)
        if t % 2 == 1 and y_ticks:
            y_tick(*y_ticks.pop(0))
    for tick in y_ticks:
        y_tick(*tick)
    own.wait()
    weights.wait()

    block = 1024
    at_end = jnp.logical_or(z == 0, z == n_z - 1)
    base = jnp.where(z == 0, 0, rows_r)
    base = pl.multiple_of(base, rows_r)

    def product(q, first, depth, add):
        cols = pl.ds(q * piece_r, piece_r)

        def body(m, carry):
            rows = pl.ds(pl.multiple_of(m * block, block), block)
            value = jnp.dot(left_t[rows, pl.ds(first, depth)], right_full[pl.ds(first, depth), cols],
                            preferred_element_type=jnp.float32)
            for part in range(piece_r // 128):
                some = value[:, part * 128:(part + 1) * 128]
                slab = q * (piece_r // 128) + part
                acc[slab, rows, :] = acc[slab, rows, :] + some if add else some
            return carry

        lax.fori_loop(0, width_l // block, body, 0)

    def first_part(q):
        @pl.when(at_end)
        def _():
            product(q, base, seqs - rows_r, False)

        @pl.when(jnp.logical_not(at_end))
        def _():
            product(q, 0, seqs, False)

    for q in range(q_z):
        first_part(q)

    def finish(q):
        heads = piece_r // CH
        for quad in range(heads // 4):
            slab = acc.at[q * (piece_r // 128) + quad]
            for cq in range(CH // 4):
                tiles = [slab[pl.ds(cq * 4 + c, left_dev, stride=CH), :].astype(jnp.bfloat16) for c in range(4)]
                for j, value in enumerate(lane_quads(tiles)):
                    flat[pl.ds((quad * 4 + j) * left_dev, left_dev), pl.ds(cq * 128, 128)] = value
        projected = jnp.dot(flat[...], w_ref[...], preferred_element_type=jnp.float32)
        for j in range(heads):
            value = projected[j * left_dev:(j + 1) * left_dev, :] / cover[q * heads + j]
            out_v.at[q].reshape(left_dev * heads, value.shape[1])[pl.ds(j, left_dev, stride=heads), :] = value
        out_copy(q).start()

    def out_copy(q):
        return pltpu.make_async_copy(out_v.at[q], out_ref.at[:, pl.ds(q * heads_q, heads_q), :], out_sem.at[q])

    heads_q = piece_r // CH
    last = n_z - 2
    for q in range(q_z):
        z_tick(last, q)

        @pl.when(at_end)
        def _():
            far = jnp.where(z == 0, (n_z - 1) * rows_r, 0)
            product(q, pl.multiple_of(far, rows_r), rows_r, True)

        finish(q)

    for side in range(2):
        for step in range(n_z - 1):
            for q in range(q_z):
                pl.when(z_sends(side, step))(lambda side=side, step=step, q=q: z_copy(side, step, q).wait_send())
        for step in range(n_y - 1):
            for q in range(q_y):
                pl.when(y_sends(side, step))(lambda side=side, step=step, q=q: y_copy(side, step, q).wait_send())
                pl.when(y_arrives(side, step))(lambda side=side, step=step, q=q: s_copy(side, step, q).wait_send())
    for q in range(q_y):
        s_copy(0, -1, q).wait_send()
    for q in range(q_z):
        out_copy(q).wait()


def folded(left_ref, right_ref, counts_ref, w_hbm, out_ref, w_in, w_wide, w_ref, counts_in, cover, order, left_full, left_far, right_full, right_t,
           acc, acc_far, flat, part, out_v, send, in_recv, far_recv, end_recv, own_recv, y_recv, s_recv, a_recv, own_sem):
    rows, width_l = left_ref.shape
    width_r = right_ref.shape[1]
    steps = width_r // TILE
    piece = rows // steps
    half = width_l // CORES
    quads = width_l // 128
    heads = TILE // CH
    pair = w_hbm.shape[1]
    lines = quads * heads
    early = steps // 2
    z = lax.axis_index("left")
    r = lax.axis_index("right")
    y, k = r // CORES, r % CORES
    up = z // 2
    sign = 2 * up - 1

    def fold(n, at):
        return up * at + (1 - up) * (n - 1 - at)

    zc, yc, kc = fold(4, z), fold(2, y), fold(2, k)
    inner, end = zc == 2, zc == 3
    sib_dev = {"right": r + 1 - 2 * k}
    y_dev = {"right": r + (1 - 2 * y) * CORES}

    def when(*terms):
        value = terms[0]
        for term in terms[1:]:
            value = jnp.logical_and(value, term)
        return pl.when(value)

    def z_dev(way):
        return {"left": z + way * sign}

    barrier = pltpu.get_barrier_semaphore()

    def greet(dev):
        pl.semaphore_signal(barrier, inc=1, device_id=dev, device_id_type=MESH)

    greet(sib_dev)
    greet(y_dev)
    greet(z_dev(-1))
    when(inner)(lambda: greet(z_dev(1)))
    pl.semaphore_wait(barrier, 3 + inner.astype(jnp.int32))

    def remote(src, dst, send, recv, dev):
        return pltpu.make_async_remote_copy(src_ref=src, dst_ref=dst, send_sem=send, recv_sem=recv, device_id=dev, device_id_type=MESH)

    def arrived(slot, sem):
        pltpu.make_async_copy(slot, slot, sem).wait()

    def block(at, first=0, size=rows):
        return pl.ds(pl.multiple_of(fold(4, at) * rows + first, size), size)

    def cols(q):
        return pl.ds(pl.multiple_of(q * TILE, TILE), TILE)

    def right_slot(at, q):
        return right_full.at[block(at), cols(q)]

    def in_copy(way, q):
        return remote(right_ref.at[:, cols(q)], right_slot(2, q), send.at[(way + 1) // 2], in_recv.at[0, q], z_dev(way))

    def fwd_copy(q):
        slot = right_slot(1, q)
        return remote(slot, slot, send.at[2], in_recv.at[1, q], z_dev(1))

    def cut(q):
        return ((1, 0), (1, 1), (2, 2), (4, 4))[q]

    def cut_slot(at, q, h, n):
        return right_full.at[block(at, h * (rows // n), rows // n), cols(q)]

    def mid_copy(q, h=0, n=1):
        slot = cut_slot(3, q, h, n)
        return remote(slot, slot, send.at[3], in_recv.at[1, q], z_dev(-1))

    def end_start(q):
        n, at = cut(q)
        for h in range(n):
            source = right_ref.at[pl.ds(h * (rows // n), rows // n), cols(q)]
            remote(source, cut_slot(3, q, h, n), send.at[3], end_recv.at[at + h], z_dev(-1)).start()

    def own_half():
        return pl.ds(pl.multiple_of(k * half, half), half)

    def far_copy(p):
        at = pl.ds(pl.multiple_of(p * piece, piece), piece)
        return remote(left_full.at[block(0, p * piece, piece), own_half()], left_far.at[at, own_half()], send.at[2], far_recv.at[p], z_dev(-1))

    def far_slot(p, core):
        return left_far.at[pl.ds(pl.multiple_of(p * piece, piece), piece), pl.ds(pl.multiple_of(core * half, half), half)]

    def share_copy(p):
        return remote(far_slot(p, k), far_slot(p, k), send.at[4], a_recv.at[0], sib_dev)

    def own_copy(p):
        at = pl.ds(pl.multiple_of(p * piece, piece), piece)
        slot = left_full.at[pl.ds(pl.multiple_of(r * rows + p * piece, piece), piece), :]
        return remote(left_ref.at[at, :], slot, send.at[5], own_recv.at[p], sib_dev)

    def own_arrived(p):
        other = r + 1 - 2 * k
        arrived(left_full.at[pl.ds(pl.multiple_of(other * rows + p * piece, piece), piece), :], own_recv.at[p])

    def y_slot(side, pos, p, core, count=1):
        at = 3 * side if pos == 0 else 1 + side
        return left_full.at[block(at, p * piece, count * piece), pl.ds(pl.multiple_of(core * half, half), half)]

    def y_copy(pos, p, own=False):
        slot = y_slot(yc, pos, p, k)
        source = left_ref.at[pl.ds(pl.multiple_of(p * piece, piece), piece), own_half()] if own else slot
        return remote(source, slot, send.at[6], y_recv.at[pos, p], y_dev)

    def s_copy(pos, p, group):
        slot = y_slot(1 - yc, pos, p, k)
        return remote(slot, slot, send.at[7], s_recv.at[group], sib_dev)

    def part_copy(q):
        return remote(part.at[q], part.at[q], send.at[8], far_recv.at[q], z_dev(1))

    def each(body, first=0, last=steps):
        def step(at, carry):
            body(at)
            return carry

        lax.fori_loop(first, last, step, 0)

    @when(inner)
    def _():
        @each
        def _(q):
            in_copy(-1, q).start()
            in_copy(1, q).start()


    @when(end)
    def _():
        end_start(0)
        end_start(1)

    first = kc == yc
    when(first)(lambda: each(lambda p: y_copy(0, p, True).start()))
    own_left = pltpu.make_async_copy(left_ref, left_full.at[pl.ds(pl.multiple_of(r * rows, rows), rows), :], own_sem.at[0])
    own = pltpu.make_async_copy(right_ref, right_full.at[block(zc), :], own_sem.at[1])
    weights = pltpu.make_async_copy(w_hbm, w_in, own_sem.at[2])
    counts_copy = pltpu.make_async_copy(counts_ref, counts_in, own_sem.at[3])
    each(lambda p: own_copy(p).start())
    for copy in (own_left, own, weights, counts_copy):
        copy.start()

    @each
    def _(p):
        own_arrived(p)
        when(jnp.logical_not(first))(lambda: y_copy(0, p).start())
        when(end, yc == 0, kc == 1)(lambda: far_copy(p).start())
        when(end, yc == 0, kc == 1, p == steps - 2)(lambda: end_start(2))

    own_left.wait()

    @when(end, yc == 0, kc == 0)
    def _():
        each(lambda p: far_copy(p).start(), 0, steps - 1)
        end_start(2)
        far_copy(steps - 1).start()

    each(lambda p: y_copy(1, p).start())
    when(end, yc == 0)(lambda: end_start(3))

    row = lax.broadcasted_iota(jnp.int32, (TILE, TILE), 0)
    column = lax.broadcasted_iota(jnp.int32, (TILE, TILE), 1)
    order[...] = jnp.where(column == (row % heads) * CH + row // heads, 1.0, 0.0).astype(order.dtype)
    weights.wait()
    w_wide[...] = w_in[...].astype(jnp.float32)
    for e in range(CH):
        some = w_wide[pl.ds(e, CH, stride=CH), :].astype(w_ref.dtype)
        for i in range(2):
            w_ref[pl.ds((2 * e + i) * CH, CH), i * pair:(i + 1) * pair] = some
            w_ref[pl.ds((2 * e + i) * CH, CH), (1 - i) * pair:(2 - i) * pair] = jnp.zeros_like(some)
    counts_copy.wait()
    counted = counts_in[...].astype(jnp.float32)
    for i in range(counted.shape[1]):
        cover[i // 4, i % 4] = jnp.broadcast_to(counted[:, i:i + 1], (counted.shape[0], cover.shape[3]))

    def turn(at, q):
        value = lax.dot_general(order[...], right_full[block(at), cols(q)], (((1,), (1,)), ((), ())), preferred_element_type=jnp.float32)
        right_t[cols(q), block(at)] = value.astype(right_t.dtype)

    def product(into, lines, source, left, left_rows, size, wide, add):
        for n in range(width_l // wide):
            value = jnp.dot(right_t[lines, source], left[left_rows, pl.ds(n * wide, wide)], preferred_element_type=jnp.float32)
            for one in range(wide // 128):
                some = value[:, one * 128:(one + 1) * 128]
                slab = n * (wide // 128) + one
                into[slab, size, :] = into[slab, size, :] + some if add else some

    def product_all(at, add, first=0, depth=rows):
        every = pl.ds(0, width_r)
        product(acc, every, block(at, first, depth), left_full, block(at, first, depth), every, 256, add)

    def product_one(at, q):
        product(acc, cols(q), block(at), left_full, block(at), cols(q), 512, True)

    def project(source, first_row):
        low = lax.broadcasted_iota(jnp.int32, (lines, 128), 1) < 64
        for two in range(CH // 2):
            a, b = (
                source[:, pl.ds(pl.multiple_of(first_row + e * heads, heads), heads), :].reshape(lines, 128).astype(flat.dtype)
                for e in (2 * two, 2 * two + 1)
            )
            at = pl.ds(two * 128, 128)
            flat[pl.ds(0, lines), at] = jnp.where(low, a, pltpu.roll(b, 64, 1))
            flat[pl.ds(lines, lines), at] = jnp.where(low, pltpu.roll(a, 64, 1), b)
        return jnp.dot(flat[...], w_ref[...], preferred_element_type=jnp.float32)

    def spot(i):
        return slice(i // 2 * lines, (i // 2 + 1) * lines), slice(i % 2 * pair, (i % 2 + 1) * pair)

    def settle(q, add):
        for i in range(4):
            value = out_v[q, :, i]
            if add:
                value = value + part[(q, *spot(i))].astype(jnp.float32).reshape(value.shape)
            at = pl.ds(pl.multiple_of(q * heads, heads), heads)
            out_ref[pl.ds(i, quads, stride=4), at, :] = value / cover[:, i, at, :]

    own.wait()
    each(lambda q: turn(zc, q))

    def pass_on(q, h):
        n, at = cut(q)
        arrived(cut_slot(3, q, h, n), end_recv.at[at + h])
        mid_copy(q, h, n).start()

    def end_arrived(q):
        arrived(right_slot(3, q), end_recv.at[q])
        mid_copy(q).start()
        turn(3, q)

    def share(p):
        arrived(far_slot(p, k), far_recv.at[p])
        share_copy(p).start()

    @each
    def _(p):
        arrived(y_slot(1 - yc, 0, p, k), y_recv.at[0, p])
        s_copy(0, p, 0).start()
        when(end, yc == 1)(lambda: far_copy(p).start())
        when(end, yc == 1, p == steps - 2)(lambda: end_start(2))
        arrived(right_slot(zc - 1, p), in_recv.at[0, p])
        when(inner)(lambda: fwd_copy(p).start())
        turn(zc - 1, p)
        when(inner, p >= 1, p <= early)(lambda: end_arrived(p - 1))

    when(end, yc == 1)(lambda: end_start(3))
    arrived(y_slot(1 - yc, 0, 0, 1 - k, steps), s_recv.at[0])
    late = 2 - yc
    groups = ((0, early), (early, early + 1), (early + 1, steps))

    def y_arrived(p):
        group = next(at for at, (_, last) in enumerate(groups) if p < last)
        arrived(y_slot(1 - yc, 1, p, k), y_recv.at[1, p])
        s_copy(1, p, 1 + group).start()

    def late_part(group):
        low, high = groups[group]
        arrived(y_slot(1 - yc, 1, low, 1 - k, high - low), s_recv.at[1 + group])
        product_all(late, True, low * piece, (high - low) * piece)

    def far_turn(q):
        arrived(right_slot(0, q), in_recv.at[1, q])
        turn(0, q)

    def far_product(q):
        product(acc_far, cols(q), block(0), left_far, pl.ds(0, rows), pl.ds(0, TILE), 512, False)

    def far_send_on(q):
        part[q] = project(acc_far, 0).astype(part.dtype)
        part_copy(q).start()

    def finish(q):
        value = project(acc, q * TILE)
        for i in range(4):
            out_v[q, :, i] = value[spot(i)].reshape(quads, heads, pair)

    def sent(sem, count=1):
        slot = left_full.at[pl.ds(0, count * rows), pl.ds(0, half)]
        arrived(slot, send.at[sem])

    @when(inner)
    def _():
        each(share, 0, early)
        product_all(1 + yc, False)
        for q in range(early):
            product_one(3, q)
        y_arrived(0)
        share(2)
        far_turn(0)
        product_one(0, 0)
        pass_on(2, 0)
        pass_on(2, 1)
        turn(3, 2)
        product_one(3, 2)
        y_arrived(1)
        far_turn(1)
        product_one(0, 1)
        late_part(0)
        share(3)
        pass_on(3, 0)
        arrived(left_far.at[:, pl.ds(pl.multiple_of((1 - k) * half, half), half)], a_recv.at[0])
        far_product(0)
        y_arrived(2)
        pass_on(3, 1)
        far_send_on(0)
        far_product(1)
        pass_on(3, 2)
        far_send_on(1)
        pass_on(3, 3)
        far_turn(2)
        far_product(2)
        far_send_on(2)
        late_part(1)
        y_arrived(3)
        turn(3, 3)
        product_one(3, 3)
        far_turn(3)
        far_product(3)
        far_send_on(3)
        product_one(0, 2)
        late_part(2)
        product_one(0, 3)

        @each
        def _(q):
            finish(q)
            settle(q, False)

        sent(0)
        sent(1)
        sent(2)
        sent(3)
        sent(4)
        sent(5, 2)
        sent(6, 2)
        sent(7, 2)
        arrived(part, send.at[8])

    @when(end)
    def _():
        product_all(3, False)
        for q in range(steps):
            y_arrived(q)
            arrived(right_slot(1, q), in_recv.at[1, q])
            turn(1, q)
            product_one(1 + yc, q)
        for group in range(len(groups)):
            late_part(group)
        each(finish)
        sent(2)
        sent(3)
        sent(5, 2)
        sent(6, 2)
        sent(7, 2)

        @each
        def _(q):
            arrived(part.at[q], far_recv.at[q])
            settle(q, True)


def folded_call(left_act, right_act, counts, w_out):
    rows, width_l = left_act.shape
    width_r = right_act.shape[1]
    left_dev, right_dev = counts.shape
    pair = w_out.shape[1]
    steps = width_r // TILE
    heads = TILE // CH
    full = 4 * rows
    dma = pltpu.SemaphoreType.DMA
    return pl.pallas_call(
        folded,
        out_shape=jax.ShapeDtypeStruct((left_dev, right_dev, pair), jnp.float32),
        in_specs=[pl.BlockSpec(memory_space=pl.ANY)] * 4,
        out_specs=pl.BlockSpec(memory_space=pltpu.VMEM),
        scratch_shapes=[
            pltpu.VMEM(w_out.shape, w_out.dtype),
            pltpu.VMEM(w_out.shape, jnp.float32),
            pltpu.VMEM((2 * w_out.shape[0], 2 * pair), w_out.dtype),
            pltpu.VMEM((right_dev, left_dev), counts.dtype),
            pltpu.VMEM((left_dev // 4, 4, right_dev, pair), jnp.float32),
            pltpu.VMEM((TILE, TILE), jnp.bfloat16),
            pltpu.VMEM((full, width_l), jnp.bfloat16),
            pltpu.VMEM((rows, width_l), jnp.bfloat16),
            pltpu.VMEM((full, width_r), jnp.bfloat16),
            pltpu.VMEM((width_r, full), jnp.bfloat16),
            pltpu.VMEM((width_l // 128, width_r, 128), jnp.float32),
            pltpu.VMEM((width_l // 128, TILE, 128), jnp.float32),
            pltpu.VMEM((left_dev * heads // 2, 2 * CH * CH), jnp.bfloat16),
            pltpu.VMEM((steps, left_dev * heads // 2, 2 * pair), jnp.bfloat16),
            pltpu.VMEM((steps, left_dev // 4, 4, heads, pair), jnp.float32),
            dma((9,)), dma((2, steps)), dma((steps,)), dma((8,)), dma((steps,)), dma((2, steps)), dma((4,)), dma((1,)), dma((4,)),
        ],
        compiler_params=pltpu.CompilerParams(collective_id=0, has_side_effects=True, vmem_limit_bytes=38000 * 1024),
        name="pair_mean",
    )(*(pltpu.with_memory_space_constraint(x, pltpu.HBM) for x in (left_act, right_act, counts.T, w_out)))


def solution(mesh):
    n_z, n_r = mesh.shape["left"], mesh.shape["right"]
    n_y = n_r // CORES

    def shards(left_act, right_act, counts, w_out):
        width_l, width_r = left_act.shape[1], right_act.shape[1]
        if (n_z, n_y) == (4, 2) and width_r == 4 * TILE and width_l == CORES * width_r:
            return folded_call(left_act, right_act, counts, w_out)
        rows_l, width_l = left_act.shape
        rows_r, width_r = right_act.shape
        seqs = rows_r * n_z
        left_dev, right_dev = counts.shape
        pair = w_out.shape[1]
        q_z = width_r // 256
        q_y = rows_l // max(128, rows_l // 4)
        projected = pl.pallas_call(
            functools.partial(kernel, (n_z, n_r, q_z, q_y)),
            out_shape=jax.ShapeDtypeStruct((left_dev, right_dev, pair), jnp.float32),
            in_specs=[pl.BlockSpec(memory_space=pl.ANY)] * 4,
            out_specs=pl.BlockSpec(memory_space=pl.ANY),
            scratch_shapes=[
                pltpu.VMEM(w_out.shape, w_out.dtype),
                pltpu.VMEM(counts.shape, counts.dtype),
                pltpu.VMEM((right_dev, left_dev, pair), jnp.float32),
                pltpu.VMEM((q_z, left_dev, right_dev // q_z, pair), jnp.float32),
                pltpu.VMEM((seqs, width_l), jnp.bfloat16),
                pltpu.VMEM((seqs, width_r), jnp.bfloat16),
                pltpu.VMEM((width_l, seqs), jnp.bfloat16),
                pltpu.VMEM((width_r // 128, width_l, 128), jnp.float32),
                pltpu.VMEM((width_r // q_z // CH * left_dev, CH * CH), jnp.bfloat16),
                pltpu.SemaphoreType.DMA((2, (n_z - 1) * q_z)),
                pltpu.SemaphoreType.DMA((2, (n_z - 1) * q_z)),
                pltpu.SemaphoreType.DMA((2, (n_y - 1) * q_y)),
                pltpu.SemaphoreType.DMA((2, (n_y - 1) * q_y)),
                pltpu.SemaphoreType.DMA(((2 * n_y - 1) * q_y,)),
                pltpu.SemaphoreType.DMA(((2 * n_y - 1) * q_y,)),
                pltpu.SemaphoreType.DMA((4,)),
                pltpu.SemaphoreType.DMA((q_z,)),
            ],
            compiler_params=pltpu.CompilerParams(
                collective_id=0, has_side_effects=True, vmem_limit_bytes=56 * 1024 * 1024
            ),
            name="pair_mean",
        )(left_act, right_act, counts, w_out)
        return projected

    in_specs = (
        P(("groups", "right"), "left"),
        P(("groups", "left"), "right"),
        P(("groups", "left"), "right"),
        P(),
    )
    out_specs = P(("groups", "left"), "right", None)
    return jax.shard_map(shards, mesh=mesh, in_specs=in_specs, out_specs=out_specs, check_vma=False)
```

```python
import functools

import jax
import jax.numpy as jnp
from jax import lax
from jax.experimental import pallas as pl
from jax.experimental.pallas import tpu as pltpu
from jax.sharding import PartitionSpec as P

CH = 32
CORES = 2
TILE = 256
MESH = pl.DeviceIdType.MESH


def lane_quads(tiles):
    lane = lax.broadcasted_iota(jnp.int32, tiles[0].shape, 1)
    low = lane < 64
    even = (lane % 64) < 32
    stage = [None] * 4
    for c in range(2):
        a, b = tiles[c], tiles[c + 2]
        stage[c] = jnp.where(low, a, pltpu.roll(b, 64, 1))
        stage[c + 2] = jnp.where(low, pltpu.roll(a, 64, 1), b)
    outs = [None] * 4
    for half in range(2):
        a, b = stage[2 * half], stage[2 * half + 1]
        outs[2 * half] = jnp.where(even, a, pltpu.roll(b, 32, 1))
        outs[2 * half + 1] = jnp.where(even, pltpu.roll(a, 96, 1), b)
    return outs


def kernel(sizes, left_ref, right_ref, counts_ref, w_hbm, out_ref, w_ref, counts_in, cover, out_v, left_full, right_full, left_t, acc, flat,
           z_send, z_recv, y_send, y_recv, s_send, s_recv, own_sem, out_sem):
    n_z, n_r, q_z, q_y = sizes
    n_y = n_r // CORES
    rows_l, width_l = left_ref.shape
    rows_r, width_r = right_ref.shape
    piece_r = width_r // q_z
    piece_l = rows_l // q_y
    left_dev = width_l // CH
    right_dev = width_r // CH
    seqs = left_t.shape[1]
    z = lax.axis_index("left")
    r = lax.axis_index("right")
    y = r // CORES
    k = r % CORES

    def z_dev(pos):
        return {"left": pos}

    def y_dev(pos):
        return {"right": pos * CORES + k}

    sib_dev = {"right": y * CORES + (1 - k)}

    barrier = pltpu.get_barrier_semaphore()

    def greet(dev):
        pl.semaphore_signal(barrier, inc=1, device_id=dev, device_id_type=MESH)

    greet(sib_dev)
    for pos, n, dev in ((z, n_z, z_dev), (y, n_y, y_dev)):
        pl.when(pos + 1 < n)(functools.partial(greet, dev(pos + 1)))
        pl.when(pos >= 1)(functools.partial(greet, dev(pos - 1)))
    total = 1 + (z + 1 < n_z).astype(jnp.int32) + (z >= 1).astype(jnp.int32)
    total = total + (y + 1 < n_y).astype(jnp.int32) + (y >= 1).astype(jnp.int32)
    pl.semaphore_wait(barrier, total)

    def z_slot(chunk, q):
        return right_full.at[pl.ds(pl.multiple_of(chunk * rows_r, rows_r), rows_r), pl.ds(q * piece_r, piece_r)]

    def z_copy(side, step, q):
        sign = 1 - 2 * side
        chunk = z - sign * step
        src = right_ref.at[:, pl.ds(q * piece_r, piece_r)] if step == 0 else z_slot(chunk, q)
        at = step * q_z + q
        return pltpu.make_async_remote_copy(
            src_ref=src, dst_ref=z_slot(chunk, q), send_sem=z_send.at[side, at], recv_sem=z_recv.at[side, at],
            device_id=z_dev(z + sign), device_id_type=MESH)

    def z_sends(side, step):
        near = z + 1 < n_z if side == 0 else z >= 1
        far = z - step >= 0 if side == 0 else z + step < n_z
        return jnp.logical_and(near, far)

    def z_arrives(side, step):
        return z - step - 1 >= 0 if side == 0 else z + step + 1 < n_z

    def z_wait(side, step, q):
        sign = 1 - 2 * side
        slot = z_slot(z - sign * (step + 1), q)
        pltpu.make_async_copy(slot, slot, z_recv.at[side, step * q_z + q]).wait()

    def l_slot(chunk, q):
        return left_full.at[pl.ds(pl.multiple_of(chunk * rows_l + q * piece_l, piece_l), piece_l), :]

    def l_own(q):
        return left_ref.at[pl.ds(q * piece_l, piece_l), :]

    def y_copy(side, step, q):
        sign = 1 - 2 * side
        chunk = (y - sign * step) * CORES + k
        at = step * q_y + q
        return pltpu.make_async_remote_copy(
            src_ref=l_own(q) if step == 0 else l_slot(chunk, q), dst_ref=l_slot(chunk, q),
            send_sem=y_send.at[side, at], recv_sem=y_recv.at[side, at],
            device_id=y_dev(y + sign), device_id_type=MESH)

    def y_sends(side, step):
        near = y + 1 < n_y if side == 0 else y >= 1
        far = y - step >= 0 if side == 0 else y + step < n_y
        return jnp.logical_and(near, far)

    def y_arrives(side, step):
        return y - step - 1 >= 0 if side == 0 else y + step + 1 < n_y

    def y_wait(side, step, q):
        sign = 1 - 2 * side
        slot = l_slot((y - sign * (step + 1)) * CORES + k, q)
        pltpu.make_async_copy(slot, slot, y_recv.at[side, step * q_y + q]).wait()

    def s_at(side, step, q):
        if step < 0:
            return q
        return (1 + side * (n_y - 1) + step) * q_y + q

    def s_copy(side, step, q):
        sign = 1 - 2 * side
        chunk = (y - sign * (step + 1)) * CORES + k if step >= 0 else r
        at = s_at(side, step, q)
        return pltpu.make_async_remote_copy(
            src_ref=l_own(q) if step < 0 else l_slot(chunk, q), dst_ref=l_slot(chunk, q),
            send_sem=s_send.at[at], recv_sem=s_recv.at[at],
            device_id=sib_dev, device_id_type=MESH)

    def s_wait(side, step, q):
        sign = 1 - 2 * side
        y_from = y - sign * (step + 1) if step >= 0 else y
        slot = l_slot(y_from * CORES + (1 - k), q)
        pltpu.make_async_copy(slot, slot, s_recv.at[s_at(side, step, q)]).wait()

    tile = 256

    def turn(src, first_row, chunk, q):
        col = pl.multiple_of(chunk * rows_l + q * piece_l, piece_l)

        def body(m, carry):
            at = pl.multiple_of(m * tile, tile)
            left_t[pl.ds(at, tile), pl.ds(col, piece_l)] = src[pl.ds(first_row, piece_l), pl.ds(at, tile)].T
            return carry

        lax.fori_loop(0, width_l // tile, body, 0)

    def turn_full(chunk, q):
        turn(left_full, pl.multiple_of(chunk * rows_l + q * piece_l, piece_l), chunk, q)

    for q in range(max(q_z, q_y)):
        for side in range(2):
            if q < q_z:
                pl.when(z_sends(side, 0))(lambda side=side, q=q: z_copy(side, 0, q).start())
            if q < q_y:
                pl.when(y_sends(side, 0))(lambda side=side, q=q: y_copy(side, 0, q).start())
    own_left = pltpu.make_async_copy(left_ref, left_full.at[pl.ds(pl.multiple_of(r * rows_l, rows_l), rows_l), :], own_sem.at[0])
    own = pltpu.make_async_copy(right_ref, right_full.at[pl.ds(pl.multiple_of(z * rows_r, rows_r), rows_r), :], own_sem.at[1])
    weights = pltpu.make_async_copy(w_hbm, w_ref, own_sem.at[2])
    counts_copy = pltpu.make_async_copy(counts_ref, counts_in, own_sem.at[3])
    for copy in (own_left, own, weights, counts_copy):
        copy.start()
    for q in range(q_y):
        s_copy(0, -1, q).start()
    own_left.wait()
    for q in range(q_y):
        turn_full(r, q)
    counts_copy.wait()
    counted = counts_in[...].astype(jnp.float32)
    for j in range(right_dev):
        cover[j] = jnp.broadcast_to(counted[:, j:j + 1], (left_dev, cover.shape[2]))
    for q in range(q_y):
        s_wait(0, -1, q)
        turn_full(y * CORES + (1 - k), q)

    def z_tick(step, q):
        for side in range(2):
            @pl.when(z_arrives(side, step))
            def _():
                z_wait(side, step, q)
                if step + 1 < n_z - 1:
                    pl.when(z_sends(side, step + 1))(lambda: z_copy(side, step + 1, q).start())

    def y_tick(step, q):
        for side in range(2):
            @pl.when(y_arrives(side, step))
            def _():
                y_wait(side, step, q)
                s_copy(side, step, q).start()
                if step + 1 < n_y - 1:
                    pl.when(y_sends(side, step + 1))(lambda: y_copy(side, step + 1, q).start())

        for side in range(2):
            @pl.when(y_arrives(side, step))
            def _():
                sign = 1 - 2 * side
                y_from = y - sign * (step + 1)
                turn_full(y_from * CORES + k, q)
                s_wait(side, step, q)
                turn_full(y_from * CORES + (1 - k), q)

    y_ticks = [(step, q) for step in range(n_y - 1) for q in range(q_y)]
    for t in range((n_z - 2) * q_z):
        z_tick(t // q_z, t % q_z)
        if t % 2 == 1 and y_ticks:
            y_tick(*y_ticks.pop(0))
    for tick in y_ticks:
        y_tick(*tick)
    own.wait()
    weights.wait()

    block = 1024
    at_end = jnp.logical_or(z == 0, z == n_z - 1)
    base = jnp.where(z == 0, 0, rows_r)
    base = pl.multiple_of(base, rows_r)

    def product(q, first, depth, add):
        cols = pl.ds(q * piece_r, piece_r)

        def body(m, carry):
            rows = pl.ds(pl.multiple_of(m * block, block), block)
            value = jnp.dot(left_t[rows, pl.ds(first, depth)], right_full[pl.ds(first, depth), cols],
                            preferred_element_type=jnp.float32)
            for part in range(piece_r // 128):
                some = value[:, part * 128:(part + 1) * 128]
                slab = q * (piece_r // 128) + part
                acc[slab, rows, :] = acc[slab, rows, :] + some if add else some
            return carry

        lax.fori_loop(0, width_l // block, body, 0)

    def first_part(q):
        @pl.when(at_end)
        def _():
            product(q, base, seqs - rows_r, False)

        @pl.when(jnp.logical_not(at_end))
        def _():
            product(q, 0, seqs, False)

    for q in range(q_z):
        first_part(q)

    def finish(q):
        heads = piece_r // CH
        for quad in range(heads // 4):
            slab = acc.at[q * (piece_r // 128) + quad]
            for cq in range(CH // 4):
                tiles = [slab[pl.ds(cq * 4 + c, left_dev, stride=CH), :].astype(jnp.bfloat16) for c in range(4)]
                for j, value in enumerate(lane_quads(tiles)):
                    flat[pl.ds((quad * 4 + j) * left_dev, left_dev), pl.ds(cq * 128, 128)] = value
        projected = jnp.dot(flat[...], w_ref[...], preferred_element_type=jnp.float32)
        for j in range(heads):
            value = projected[j * left_dev:(j + 1) * left_dev, :] / cover[q * heads + j]
            out_v.at[q].reshape(left_dev * heads, value.shape[1])[pl.ds(j, left_dev, stride=heads), :] = value
        out_copy(q).start()

    def out_copy(q):
        return pltpu.make_async_copy(out_v.at[q], out_ref.at[:, pl.ds(q * heads_q, heads_q), :], out_sem.at[q])

    heads_q = piece_r // CH
    last = n_z - 2
    for q in range(q_z):
        z_tick(last, q)

        @pl.when(at_end)
        def _():
            far = jnp.where(z == 0, (n_z - 1) * rows_r, 0)
            product(q, pl.multiple_of(far, rows_r), rows_r, True)

        finish(q)

    for side in range(2):
        for step in range(n_z - 1):
            for q in range(q_z):
                pl.when(z_sends(side, step))(lambda side=side, step=step, q=q: z_copy(side, step, q).wait_send())
        for step in range(n_y - 1):
            for q in range(q_y):
                pl.when(y_sends(side, step))(lambda side=side, step=step, q=q: y_copy(side, step, q).wait_send())
                pl.when(y_arrives(side, step))(lambda side=side, step=step, q=q: s_copy(side, step, q).wait_send())
    for q in range(q_y):
        s_copy(0, -1, q).wait_send()
    for q in range(q_z):
        out_copy(q).wait()


def folded(left_ref, right_ref, counts_ref, w_hbm, out_ref, w_in, w_wide, w_ref, counts_in, cover, order, left_full, left_far, right_full, right_t,
           acc, acc_far, flat, part, out_v, send, in_recv, far_recv, end_recv, own_recv, y_recv, s_recv, a_recv, own_sem):
    rows, width_l = left_ref.shape
    width_r = right_ref.shape[1]
    steps = width_r // TILE
    piece = rows // steps
    half = width_l // CORES
    quads = width_l // 128
    heads = TILE // CH
    pair = w_hbm.shape[1]
    lines = quads * heads
    early = steps // 2
    z = lax.axis_index("left")
    r = lax.axis_index("right")
    y, k = r // CORES, r % CORES
    up = z // 2
    sign = 2 * up - 1

    def fold(n, at):
        return up * at + (1 - up) * (n - 1 - at)

    zc, yc, kc = fold(4, z), fold(2, y), fold(2, k)
    inner, end = zc == 2, zc == 3
    sib_dev = {"right": r + 1 - 2 * k}
    y_dev = {"right": r + (1 - 2 * y) * CORES}

    def when(*terms):
        value = terms[0]
        for term in terms[1:]:
            value = jnp.logical_and(value, term)
        return pl.when(value)

    def z_dev(way):
        return {"left": z + way * sign}

    barrier = pltpu.get_barrier_semaphore()

    def greet(dev):
        pl.semaphore_signal(barrier, inc=1, device_id=dev, device_id_type=MESH)

    greet(sib_dev)
    greet(y_dev)
    greet(z_dev(-1))
    when(inner)(lambda: greet(z_dev(1)))
    pl.semaphore_wait(barrier, 3 + inner.astype(jnp.int32))

    def remote(src, dst, send, recv, dev):
        return pltpu.make_async_remote_copy(src_ref=src, dst_ref=dst, send_sem=send, recv_sem=recv, device_id=dev, device_id_type=MESH)

    def arrived(slot, sem):
        pltpu.make_async_copy(slot, slot, sem).wait()

    def block(at, first=0, size=rows):
        return pl.ds(pl.multiple_of(fold(4, at) * rows + first, size), size)

    def cols(q):
        return pl.ds(pl.multiple_of(q * TILE, TILE), TILE)

    def right_slot(at, q):
        return right_full.at[block(at), cols(q)]

    def in_copy(way, q):
        return remote(right_ref.at[:, cols(q)], right_slot(2, q), send.at[(way + 1) // 2], in_recv.at[0, q], z_dev(way))

    def fwd_copy(q):
        slot = right_slot(1, q)
        return remote(slot, slot, send.at[2], in_recv.at[1, q], z_dev(1))

    def cut(q):
        return ((1, 0), (1, 1), (2, 2), (4, 4))[q]

    def cut_slot(at, q, h, n):
        return right_full.at[block(at, h * (rows // n), rows // n), cols(q)]

    def mid_copy(q, h=0, n=1):
        slot = cut_slot(3, q, h, n)
        return remote(slot, slot, send.at[3], in_recv.at[1, q], z_dev(-1))

    def end_start(q):
        n, at = cut(q)
        for h in range(n):
            source = right_ref.at[pl.ds(h * (rows // n), rows // n), cols(q)]
            remote(source, cut_slot(3, q, h, n), send.at[3], end_recv.at[at + h], z_dev(-1)).start()

    def own_half():
        return pl.ds(pl.multiple_of(k * half, half), half)

    def far_copy(p):
        at = pl.ds(pl.multiple_of(p * piece, piece), piece)
        return remote(left_full.at[block(0, p * piece, piece), own_half()], left_far.at[at, own_half()], send.at[2], far_recv.at[p], z_dev(-1))

    def far_slot(p, core):
        return left_far.at[pl.ds(pl.multiple_of(p * piece, piece), piece), pl.ds(pl.multiple_of(core * half, half), half)]

    def share_copy(p):
        return remote(far_slot(p, k), far_slot(p, k), send.at[4], a_recv.at[0], sib_dev)

    def own_copy(p):
        at = pl.ds(pl.multiple_of(p * piece, piece), piece)
        slot = left_full.at[pl.ds(pl.multiple_of(r * rows + p * piece, piece), piece), :]
        return remote(left_ref.at[at, :], slot, send.at[5], own_recv.at[p], sib_dev)

    def own_arrived(p):
        other = r + 1 - 2 * k
        arrived(left_full.at[pl.ds(pl.multiple_of(other * rows + p * piece, piece), piece), :], own_recv.at[p])

    def y_slot(side, pos, p, core, count=1):
        at = 3 * side if pos == 0 else 1 + side
        return left_full.at[block(at, p * piece, count * piece), pl.ds(pl.multiple_of(core * half, half), half)]

    def y_copy(pos, p, own=False):
        slot = y_slot(yc, pos, p, k)
        source = left_ref.at[pl.ds(pl.multiple_of(p * piece, piece), piece), own_half()] if own else slot
        return remote(source, slot, send.at[6], y_recv.at[pos, p], y_dev)

    def s_copy(pos, p, group):
        slot = y_slot(1 - yc, pos, p, k)
        return remote(slot, slot, send.at[7], s_recv.at[group], sib_dev)

    def part_copy(q):
        return remote(part.at[q], part.at[q], send.at[8], far_recv.at[q], z_dev(1))

    def each(body, first=0, last=steps):
        def step(at, carry):
            body(at)
            return carry

        lax.fori_loop(first, last, step, 0)

    def z_start():
        @when(inner)
        def _():
            @each
            def _(q):
                in_copy(-1, q).start()
                in_copy(1, q).start()

        @when(end)
        def _():
            end_start(0)
            end_start(1)

    when(k == 0)(z_start)
    first = kc == yc
    when(first)(lambda: each(lambda p: y_copy(0, p, True).start()))
    own_left = pltpu.make_async_copy(left_ref, left_full.at[pl.ds(pl.multiple_of(r * rows, rows), rows), :], own_sem.at[0])
    own = pltpu.make_async_copy(right_ref, right_full.at[block(zc), :], own_sem.at[1])
    weights = pltpu.make_async_copy(w_hbm, w_in, own_sem.at[2])
    counts_copy = pltpu.make_async_copy(counts_ref, counts_in, own_sem.at[3])
    each(lambda p: own_copy(p).start())
    when(k == 1)(z_start)
    for copy in (own_left, own, weights, counts_copy):
        copy.start()

    @each
    def _(p):
        own_arrived(p)
        when(jnp.logical_not(first))(lambda: y_copy(0, p).start())
        when(end, yc == 0, kc == 1)(lambda: far_copy(p).start())
        when(end, yc == 0, kc == 1, p == steps - 2)(lambda: end_start(2))

    own_left.wait()

    @when(end, yc == 0, kc == 0)
    def _():
        each(lambda p: far_copy(p).start(), 0, steps - 1)
        end_start(2)
        far_copy(steps - 1).start()

    each(lambda p: y_copy(1, p).start())
    when(end, yc == 0)(lambda: end_start(3))

    row = lax.broadcasted_iota(jnp.int32, (TILE, TILE), 0)
    column = lax.broadcasted_iota(jnp.int32, (TILE, TILE), 1)
    order[...] = jnp.where(column == (row % heads) * CH + row // heads, 1.0, 0.0).astype(order.dtype)
    weights.wait()
    w_wide[...] = w_in[...].astype(jnp.float32)
    for e in range(CH):
        some = w_wide[pl.ds(e, CH, stride=CH), :].astype(w_ref.dtype)
        for i in range(2):
            w_ref[pl.ds((2 * e + i) * CH, CH), i * pair:(i + 1) * pair] = some
            w_ref[pl.ds((2 * e + i) * CH, CH), (1 - i) * pair:(2 - i) * pair] = jnp.zeros_like(some)
    counts_copy.wait()
    counted = counts_in[...].astype(jnp.float32)
    for i in range(counted.shape[1]):
        cover[i // 4, i % 4] = jnp.broadcast_to(counted[:, i:i + 1], (counted.shape[0], cover.shape[3]))

    def turn(at, q):
        value = lax.dot_general(order[...], right_full[block(at), cols(q)], (((1,), (1,)), ((), ())), preferred_element_type=jnp.float32)
        right_t[cols(q), block(at)] = value.astype(right_t.dtype)

    def product(into, lines, source, left, left_rows, size, wide, add):
        for n in range(width_l // wide):
            value = jnp.dot(right_t[lines, source], left[left_rows, pl.ds(n * wide, wide)], preferred_element_type=jnp.float32)
            for one in range(wide // 128):
                some = value[:, one * 128:(one + 1) * 128]
                slab = n * (wide // 128) + one
                into[slab, size, :] = into[slab, size, :] + some if add else some

    def product_all(at, add, first=0, depth=rows):
        every = pl.ds(0, width_r)
        product(acc, every, block(at, first, depth), left_full, block(at, first, depth), every, 256, add)

    def product_one(at, q):
        product(acc, cols(q), block(at), left_full, block(at), cols(q), 512, True)

    def project(source, first_row):
        low = lax.broadcasted_iota(jnp.int32, (lines, 128), 1) < 64
        for two in range(CH // 2):
            a, b = (
                source[:, pl.ds(pl.multiple_of(first_row + e * heads, heads), heads), :].reshape(lines, 128).astype(flat.dtype)
                for e in (2 * two, 2 * two + 1)
            )
            at = pl.ds(two * 128, 128)
            flat[pl.ds(0, lines), at] = jnp.where(low, a, pltpu.roll(b, 64, 1))
            flat[pl.ds(lines, lines), at] = jnp.where(low, pltpu.roll(a, 64, 1), b)
        return jnp.dot(flat[...], w_ref[...], preferred_element_type=jnp.float32)

    def spot(i):
        return slice(i // 2 * lines, (i // 2 + 1) * lines), slice(i % 2 * pair, (i % 2 + 1) * pair)

    def emit(q, i, value):
        at = pl.ds(pl.multiple_of(q * heads, heads), heads)
        out_ref[pl.ds(i, quads, stride=4), at, :] = value / cover[:, i, at, :]

    def settle(q):
        for i in range(4):
            value = out_v[q, :, i]
            emit(q, i, value + part[(q, *spot(i))].astype(jnp.float32).reshape(value.shape))

    own.wait()
    each(lambda q: turn(zc, q))

    def pass_on(q, h):
        n, at = cut(q)
        arrived(cut_slot(3, q, h, n), end_recv.at[at + h])
        mid_copy(q, h, n).start()

    def end_arrived(q):
        arrived(right_slot(3, q), end_recv.at[q])
        mid_copy(q).start()
        turn(3, q)

    def share(p):
        arrived(far_slot(p, k), far_recv.at[p])
        share_copy(p).start()

    @each
    def _(p):
        arrived(y_slot(1 - yc, 0, p, k), y_recv.at[0, p])
        s_copy(0, p, 0).start()
        when(end, yc == 1)(lambda: far_copy(p).start())
        when(end, yc == 1, p == steps - 2)(lambda: end_start(2))
        arrived(right_slot(zc - 1, p), in_recv.at[0, p])
        when(inner)(lambda: fwd_copy(p).start())
        turn(zc - 1, p)
        when(inner, p >= 1, p <= early)(lambda: end_arrived(p - 1))

    when(end, yc == 1)(lambda: end_start(3))
    arrived(y_slot(1 - yc, 0, 0, 1 - k, steps), s_recv.at[0])
    late = 2 - yc
    groups = ((0, early), (early, early + 1), (early + 1, steps))

    def y_arrived(p):
        group = next(at for at, (_, last) in enumerate(groups) if p < last)
        arrived(y_slot(1 - yc, 1, p, k), y_recv.at[1, p])
        s_copy(1, p, 1 + group).start()

    def late_part(group):
        low, high = groups[group]
        arrived(y_slot(1 - yc, 1, low, 1 - k, high - low), s_recv.at[1 + group])
        product_all(late, True, low * piece, (high - low) * piece)

    def far_turn(q):
        arrived(right_slot(0, q), in_recv.at[1, q])
        turn(0, q)

    def far_product(q):
        product(acc_far, cols(q), block(0), left_far, pl.ds(0, rows), pl.ds(0, TILE), 512, False)

    def far_send_on(q):
        part[q] = project(acc_far, 0).astype(part.dtype)
        part_copy(q).start()

    def finish(q):
        value = project(acc, q * TILE)
        for i in range(4):
            out_v[q, :, i] = value[spot(i)].reshape(quads, heads, pair)

    def sent(sem, count=1):
        slot = left_full.at[pl.ds(0, count * rows), pl.ds(0, half)]
        arrived(slot, send.at[sem])

    @when(inner)
    def _():
        each(share, 0, early)
        product_all(1 + yc, False)
        for q in range(early):
            product_one(3, q)
        y_arrived(0)
        share(2)
        far_turn(0)
        product_one(0, 0)
        pass_on(2, 0)
        pass_on(2, 1)
        turn(3, 2)
        product_one(3, 2)
        y_arrived(1)
        far_turn(1)
        product_one(0, 1)
        late_part(0)
        share(3)
        pass_on(3, 0)
        far_turn(2)
        product_one(0, 2)
        pass_on(3, 1)
        arrived(left_far.at[:, pl.ds(pl.multiple_of((1 - k) * half, half), half)], a_recv.at[0])
        far_product(0)
        y_arrived(2)
        far_send_on(0)
        pass_on(3, 2)
        far_product(1)
        far_send_on(1)
        pass_on(3, 3)
        far_product(2)
        far_send_on(2)
        late_part(1)
        y_arrived(3)
        turn(3, 3)
        product_one(3, 3)
        far_turn(3)
        far_product(3)
        far_send_on(3)
        late_part(2)
        product_one(0, 3)

        @each
        def _(q):
            value = project(acc, q * TILE)
            for i in range(4):
                emit(q, i, value[spot(i)].reshape(quads, heads, pair))

        sent(0)
        sent(1)
        sent(2)
        sent(3)
        sent(4)
        sent(5, 2)
        sent(6, 2)
        sent(7, 2)
        arrived(part, send.at[8])

    @when(end)
    def _():
        product_all(3, False)
        for q in range(steps):
            y_arrived(q)
            arrived(right_slot(1, q), in_recv.at[1, q])
            turn(1, q)
            product_one(1 + yc, q)
        for group in range(len(groups)):
            late_part(group)
        each(finish)
        sent(2)
        sent(3)
        sent(5, 2)
        sent(6, 2)
        sent(7, 2)

        @each
        def _(q):
            arrived(part.at[q], far_recv.at[q])
            settle(q)


def folded_call(left_act, right_act, counts, w_out):
    rows, width_l = left_act.shape
    width_r = right_act.shape[1]
    left_dev, right_dev = counts.shape
    pair = w_out.shape[1]
    steps = width_r // TILE
    heads = TILE // CH
    full = 4 * rows
    dma = pltpu.SemaphoreType.DMA
    return pl.pallas_call(
        folded,
        out_shape=jax.ShapeDtypeStruct((left_dev, right_dev, pair), jnp.float32),
        in_specs=[pl.BlockSpec(memory_space=pl.ANY)] * 4,
        out_specs=pl.BlockSpec(memory_space=pltpu.VMEM),
        scratch_shapes=[
            pltpu.VMEM(w_out.shape, w_out.dtype),
            pltpu.VMEM(w_out.shape, jnp.float32),
            pltpu.VMEM((2 * w_out.shape[0], 2 * pair), w_out.dtype),
            pltpu.VMEM((right_dev, left_dev), counts.dtype),
            pltpu.VMEM((left_dev // 4, 4, right_dev, pair), jnp.float32),
            pltpu.VMEM((TILE, TILE), jnp.bfloat16),
            pltpu.VMEM((full, width_l), jnp.bfloat16),
            pltpu.VMEM((rows, width_l), jnp.bfloat16),
            pltpu.VMEM((full, width_r), jnp.bfloat16),
            pltpu.VMEM((width_r, full), jnp.bfloat16),
            pltpu.VMEM((width_l // 128, width_r, 128), jnp.float32),
            pltpu.VMEM((width_l // 128, TILE, 128), jnp.float32),
            pltpu.VMEM((left_dev * heads // 2, 2 * CH * CH), jnp.bfloat16),
            pltpu.VMEM((steps, left_dev * heads // 2, 2 * pair), jnp.bfloat16),
            pltpu.VMEM((steps, left_dev // 4, 4, heads, pair), jnp.float32),
            dma((9,)), dma((2, steps)), dma((steps,)), dma((8,)), dma((steps,)), dma((2, steps)), dma((4,)), dma((1,)), dma((4,)),
        ],
        compiler_params=pltpu.CompilerParams(collective_id=0, has_side_effects=True, vmem_limit_bytes=38000 * 1024),
        name="pair_mean",
    )(*(pltpu.with_memory_space_constraint(x, pltpu.HBM) for x in (left_act, right_act, counts.T, w_out)))


def solution(mesh):
    n_z, n_r = mesh.shape["left"], mesh.shape["right"]
    n_y = n_r // CORES

    def shards(left_act, right_act, counts, w_out):
        width_l, width_r = left_act.shape[1], right_act.shape[1]
        if (n_z, n_y) == (4, 2) and width_r == 4 * TILE and width_l == CORES * width_r:
            return folded_call(left_act, right_act, counts, w_out)
        rows_l, width_l = left_act.shape
        rows_r, width_r = right_act.shape
        seqs = rows_r * n_z
        left_dev, right_dev = counts.shape
        pair = w_out.shape[1]
        q_z = width_r // 256
        q_y = rows_l // max(128, rows_l // 4)
        projected = pl.pallas_call(
            functools.partial(kernel, (n_z, n_r, q_z, q_y)),
            out_shape=jax.ShapeDtypeStruct((left_dev, right_dev, pair), jnp.float32),
            in_specs=[pl.BlockSpec(memory_space=pl.ANY)] * 4,
            out_specs=pl.BlockSpec(memory_space=pl.ANY),
            scratch_shapes=[
                pltpu.VMEM(w_out.shape, w_out.dtype),
                pltpu.VMEM(counts.shape, counts.dtype),
                pltpu.VMEM((right_dev, left_dev, pair), jnp.float32),
                pltpu.VMEM((q_z, left_dev, right_dev // q_z, pair), jnp.float32),
                pltpu.VMEM((seqs, width_l), jnp.bfloat16),
                pltpu.VMEM((seqs, width_r), jnp.bfloat16),
                pltpu.VMEM((width_l, seqs), jnp.bfloat16),
                pltpu.VMEM((width_r // 128, width_l, 128), jnp.float32),
                pltpu.VMEM((width_r // q_z // CH * left_dev, CH * CH), jnp.bfloat16),
                pltpu.SemaphoreType.DMA((2, (n_z - 1) * q_z)),
                pltpu.SemaphoreType.DMA((2, (n_z - 1) * q_z)),
                pltpu.SemaphoreType.DMA((2, (n_y - 1) * q_y)),
                pltpu.SemaphoreType.DMA((2, (n_y - 1) * q_y)),
                pltpu.SemaphoreType.DMA(((2 * n_y - 1) * q_y,)),
                pltpu.SemaphoreType.DMA(((2 * n_y - 1) * q_y,)),
                pltpu.SemaphoreType.DMA((4,)),
                pltpu.SemaphoreType.DMA((q_z,)),
            ],
            compiler_params=pltpu.CompilerParams(
                collective_id=0, has_side_effects=True, vmem_limit_bytes=56 * 1024 * 1024
            ),
            name="pair_mean",
        )(left_act, right_act, counts, w_out)
        return projected

    in_specs = (
        P(("groups", "right"), "left"),
        P(("groups", "left"), "right"),
        P(("groups", "left"), "right"),
        P(),
    )
    out_specs = P(("groups", "left"), "right", None)
    return jax.shard_map(shards, mesh=mesh, in_specs=in_specs, out_specs=out_specs, check_vma=False)
```

```python
import functools

import jax
import jax.numpy as jnp
from jax import lax
from jax.experimental import pallas as pl
from jax.experimental.pallas import tpu as pltpu
from jax.sharding import PartitionSpec as P

CH = 32
CORES = 2
TILE = 256
MESH = pl.DeviceIdType.MESH


def lane_quads(tiles):
    lane = lax.broadcasted_iota(jnp.int32, tiles[0].shape, 1)
    low = lane < 64
    even = (lane % 64) < 32
    stage = [None] * 4
    for c in range(2):
        a, b = tiles[c], tiles[c + 2]
        stage[c] = jnp.where(low, a, pltpu.roll(b, 64, 1))
        stage[c + 2] = jnp.where(low, pltpu.roll(a, 64, 1), b)
    outs = [None] * 4
    for half in range(2):
        a, b = stage[2 * half], stage[2 * half + 1]
        outs[2 * half] = jnp.where(even, a, pltpu.roll(b, 32, 1))
        outs[2 * half + 1] = jnp.where(even, pltpu.roll(a, 96, 1), b)
    return outs


def kernel(sizes, left_ref, right_ref, counts_ref, w_hbm, out_ref, w_ref, counts_in, cover, out_v, left_full, right_full, left_t, acc, flat,
           z_send, z_recv, y_send, y_recv, s_send, s_recv, own_sem, out_sem):
    n_z, n_r, q_z, q_y = sizes
    n_y = n_r // CORES
    rows_l, width_l = left_ref.shape
    rows_r, width_r = right_ref.shape
    piece_r = width_r // q_z
    piece_l = rows_l // q_y
    left_dev = width_l // CH
    right_dev = width_r // CH
    seqs = left_t.shape[1]
    z = lax.axis_index("left")
    r = lax.axis_index("right")
    y = r // CORES
    k = r % CORES

    def z_dev(pos):
        return {"left": pos}

    def y_dev(pos):
        return {"right": pos * CORES + k}

    sib_dev = {"right": y * CORES + (1 - k)}

    barrier = pltpu.get_barrier_semaphore()

    def greet(dev):
        pl.semaphore_signal(barrier, inc=1, device_id=dev, device_id_type=MESH)

    greet(sib_dev)
    for pos, n, dev in ((z, n_z, z_dev), (y, n_y, y_dev)):
        pl.when(pos + 1 < n)(functools.partial(greet, dev(pos + 1)))
        pl.when(pos >= 1)(functools.partial(greet, dev(pos - 1)))
    total = 1 + (z + 1 < n_z).astype(jnp.int32) + (z >= 1).astype(jnp.int32)
    total = total + (y + 1 < n_y).astype(jnp.int32) + (y >= 1).astype(jnp.int32)
    pl.semaphore_wait(barrier, total)

    def z_slot(chunk, q):
        return right_full.at[pl.ds(pl.multiple_of(chunk * rows_r, rows_r), rows_r), pl.ds(q * piece_r, piece_r)]

    def z_copy(side, step, q):
        sign = 1 - 2 * side
        chunk = z - sign * step
        src = right_ref.at[:, pl.ds(q * piece_r, piece_r)] if step == 0 else z_slot(chunk, q)
        at = step * q_z + q
        return pltpu.make_async_remote_copy(
            src_ref=src, dst_ref=z_slot(chunk, q), send_sem=z_send.at[side, at], recv_sem=z_recv.at[side, at],
            device_id=z_dev(z + sign), device_id_type=MESH)

    def z_sends(side, step):
        near = z + 1 < n_z if side == 0 else z >= 1
        far = z - step >= 0 if side == 0 else z + step < n_z
        return jnp.logical_and(near, far)

    def z_arrives(side, step):
        return z - step - 1 >= 0 if side == 0 else z + step + 1 < n_z

    def z_wait(side, step, q):
        sign = 1 - 2 * side
        slot = z_slot(z - sign * (step + 1), q)
        pltpu.make_async_copy(slot, slot, z_recv.at[side, step * q_z + q]).wait()

    def l_slot(chunk, q):
        return left_full.at[pl.ds(pl.multiple_of(chunk * rows_l + q * piece_l, piece_l), piece_l), :]

    def l_own(q):
        return left_ref.at[pl.ds(q * piece_l, piece_l), :]

    def y_copy(side, step, q):
        sign = 1 - 2 * side
        chunk = (y - sign * step) * CORES + k
        at = step * q_y + q
        return pltpu.make_async_remote_copy(
            src_ref=l_own(q) if step == 0 else l_slot(chunk, q), dst_ref=l_slot(chunk, q),
            send_sem=y_send.at[side, at], recv_sem=y_recv.at[side, at],
            device_id=y_dev(y + sign), device_id_type=MESH)

    def y_sends(side, step):
        near = y + 1 < n_y if side == 0 else y >= 1
        far = y - step >= 0 if side == 0 else y + step < n_y
        return jnp.logical_and(near, far)

    def y_arrives(side, step):
        return y - step - 1 >= 0 if side == 0 else y + step + 1 < n_y

    def y_wait(side, step, q):
        sign = 1 - 2 * side
        slot = l_slot((y - sign * (step + 1)) * CORES + k, q)
        pltpu.make_async_copy(slot, slot, y_recv.at[side, step * q_y + q]).wait()

    def s_at(side, step, q):
        if step < 0:
            return q
        return (1 + side * (n_y - 1) + step) * q_y + q

    def s_copy(side, step, q):
        sign = 1 - 2 * side
        chunk = (y - sign * (step + 1)) * CORES + k if step >= 0 else r
        at = s_at(side, step, q)
        return pltpu.make_async_remote_copy(
            src_ref=l_own(q) if step < 0 else l_slot(chunk, q), dst_ref=l_slot(chunk, q),
            send_sem=s_send.at[at], recv_sem=s_recv.at[at],
            device_id=sib_dev, device_id_type=MESH)

    def s_wait(side, step, q):
        sign = 1 - 2 * side
        y_from = y - sign * (step + 1) if step >= 0 else y
        slot = l_slot(y_from * CORES + (1 - k), q)
        pltpu.make_async_copy(slot, slot, s_recv.at[s_at(side, step, q)]).wait()

    tile = 256

    def turn(src, first_row, chunk, q):
        col = pl.multiple_of(chunk * rows_l + q * piece_l, piece_l)

        def body(m, carry):
            at = pl.multiple_of(m * tile, tile)
            left_t[pl.ds(at, tile), pl.ds(col, piece_l)] = src[pl.ds(first_row, piece_l), pl.ds(at, tile)].T
            return carry

        lax.fori_loop(0, width_l // tile, body, 0)

    def turn_full(chunk, q):
        turn(left_full, pl.multiple_of(chunk * rows_l + q * piece_l, piece_l), chunk, q)

    for q in range(max(q_z, q_y)):
        for side in range(2):
            if q < q_z:
                pl.when(z_sends(side, 0))(lambda side=side, q=q: z_copy(side, 0, q).start())
            if q < q_y:
                pl.when(y_sends(side, 0))(lambda side=side, q=q: y_copy(side, 0, q).start())
    own_left = pltpu.make_async_copy(left_ref, left_full.at[pl.ds(pl.multiple_of(r * rows_l, rows_l), rows_l), :], own_sem.at[0])
    own = pltpu.make_async_copy(right_ref, right_full.at[pl.ds(pl.multiple_of(z * rows_r, rows_r), rows_r), :], own_sem.at[1])
    weights = pltpu.make_async_copy(w_hbm, w_ref, own_sem.at[2])
    counts_copy = pltpu.make_async_copy(counts_ref, counts_in, own_sem.at[3])
    for copy in (own_left, own, weights, counts_copy):
        copy.start()
    for q in range(q_y):
        s_copy(0, -1, q).start()
    own_left.wait()
    for q in range(q_y):
        turn_full(r, q)
    counts_copy.wait()
    counted = counts_in[...].astype(jnp.float32)
    for j in range(right_dev):
        cover[j] = jnp.broadcast_to(counted[:, j:j + 1], (left_dev, cover.shape[2]))
    for q in range(q_y):
        s_wait(0, -1, q)
        turn_full(y * CORES + (1 - k), q)

    def z_tick(step, q):
        for side in range(2):
            @pl.when(z_arrives(side, step))
            def _():
                z_wait(side, step, q)
                if step + 1 < n_z - 1:
                    pl.when(z_sends(side, step + 1))(lambda: z_copy(side, step + 1, q).start())

    def y_tick(step, q):
        for side in range(2):
            @pl.when(y_arrives(side, step))
            def _():
                y_wait(side, step, q)
                s_copy(side, step, q).start()
                if step + 1 < n_y - 1:
                    pl.when(y_sends(side, step + 1))(lambda: y_copy(side, step + 1, q).start())

        for side in range(2):
            @pl.when(y_arrives(side, step))
            def _():
                sign = 1 - 2 * side
                y_from = y - sign * (step + 1)
                turn_full(y_from * CORES + k, q)
                s_wait(side, step, q)
                turn_full(y_from * CORES + (1 - k), q)

    y_ticks = [(step, q) for step in range(n_y - 1) for q in range(q_y)]
    for t in range((n_z - 2) * q_z):
        z_tick(t // q_z, t % q_z)
        if t % 2 == 1 and y_ticks:
            y_tick(*y_ticks.pop(0))
    for tick in y_ticks:
        y_tick(*tick)
    own.wait()
    weights.wait()

    block = 1024
    at_end = jnp.logical_or(z == 0, z == n_z - 1)
    base = jnp.where(z == 0, 0, rows_r)
    base = pl.multiple_of(base, rows_r)

    def product(q, first, depth, add):
        cols = pl.ds(q * piece_r, piece_r)

        def body(m, carry):
            rows = pl.ds(pl.multiple_of(m * block, block), block)
            value = jnp.dot(left_t[rows, pl.ds(first, depth)], right_full[pl.ds(first, depth), cols],
                            preferred_element_type=jnp.float32)
            for part in range(piece_r // 128):
                some = value[:, part * 128:(part + 1) * 128]
                slab = q * (piece_r // 128) + part
                acc[slab, rows, :] = acc[slab, rows, :] + some if add else some
            return carry

        lax.fori_loop(0, width_l // block, body, 0)

    def first_part(q):
        @pl.when(at_end)
        def _():
            product(q, base, seqs - rows_r, False)

        @pl.when(jnp.logical_not(at_end))
        def _():
            product(q, 0, seqs, False)

    for q in range(q_z):
        first_part(q)

    def finish(q):
        heads = piece_r // CH
        for quad in range(heads // 4):
            slab = acc.at[q * (piece_r // 128) + quad]
            for cq in range(CH // 4):
                tiles = [slab[pl.ds(cq * 4 + c, left_dev, stride=CH), :].astype(jnp.bfloat16) for c in range(4)]
                for j, value in enumerate(lane_quads(tiles)):
                    flat[pl.ds((quad * 4 + j) * left_dev, left_dev), pl.ds(cq * 128, 128)] = value
        projected = jnp.dot(flat[...], w_ref[...], preferred_element_type=jnp.float32)
        for j in range(heads):
            value = projected[j * left_dev:(j + 1) * left_dev, :] / cover[q * heads + j]
            out_v.at[q].reshape(left_dev * heads, value.shape[1])[pl.ds(j, left_dev, stride=heads), :] = value
        out_copy(q).start()

    def out_copy(q):
        return pltpu.make_async_copy(out_v.at[q], out_ref.at[:, pl.ds(q * heads_q, heads_q), :], out_sem.at[q])

    heads_q = piece_r // CH
    last = n_z - 2
    for q in range(q_z):
        z_tick(last, q)

        @pl.when(at_end)
        def _():
            far = jnp.where(z == 0, (n_z - 1) * rows_r, 0)
            product(q, pl.multiple_of(far, rows_r), rows_r, True)

        finish(q)

    for side in range(2):
        for step in range(n_z - 1):
            for q in range(q_z):
                pl.when(z_sends(side, step))(lambda side=side, step=step, q=q: z_copy(side, step, q).wait_send())
        for step in range(n_y - 1):
            for q in range(q_y):
                pl.when(y_sends(side, step))(lambda side=side, step=step, q=q: y_copy(side, step, q).wait_send())
                pl.when(y_arrives(side, step))(lambda side=side, step=step, q=q: s_copy(side, step, q).wait_send())
    for q in range(q_y):
        s_copy(0, -1, q).wait_send()
    for q in range(q_z):
        out_copy(q).wait()


def folded(left_ref, right_ref, counts_ref, w_hbm, out_ref, w_in, w_wide, w_ref, counts_in, cover, order, left_full, left_far, right_full, right_t,
           acc, acc_far, flat, part, out_v, send, in_recv, far_recv, end_recv, own_recv, y_recv, s_recv, a_recv, own_sem):
    rows, width_l = left_ref.shape
    width_r = right_ref.shape[1]
    steps = width_r // TILE
    piece = rows // steps
    half = width_l // CORES
    quads = width_l // 128
    heads = TILE // CH
    pair = w_hbm.shape[1]
    lines = quads * heads
    early = steps // 2
    z = lax.axis_index("left")
    r = lax.axis_index("right")
    y, k = r // CORES, r % CORES
    up = z // 2
    sign = 2 * up - 1

    def fold(n, at):
        return up * at + (1 - up) * (n - 1 - at)

    zc, yc, kc = fold(4, z), fold(2, y), fold(2, k)
    inner, end = zc == 2, zc == 3
    sib_dev = {"right": r + 1 - 2 * k}
    y_dev = {"right": r + (1 - 2 * y) * CORES}

    def when(*terms):
        value = terms[0]
        for term in terms[1:]:
            value = jnp.logical_and(value, term)
        return pl.when(value)

    def z_dev(way):
        return {"left": z + way * sign}

    barrier = pltpu.get_barrier_semaphore()

    def greet(dev):
        pl.semaphore_signal(barrier, inc=1, device_id=dev, device_id_type=MESH)

    greet(sib_dev)
    greet(y_dev)
    greet(z_dev(-1))
    when(inner)(lambda: greet(z_dev(1)))
    pl.semaphore_wait(barrier, 3 + inner.astype(jnp.int32))

    def remote(src, dst, send, recv, dev):
        return pltpu.make_async_remote_copy(src_ref=src, dst_ref=dst, send_sem=send, recv_sem=recv, device_id=dev, device_id_type=MESH)

    def arrived(slot, sem):
        pltpu.make_async_copy(slot, slot, sem).wait()

    def block(at, first=0, size=rows):
        return pl.ds(pl.multiple_of(fold(4, at) * rows + first, size), size)

    def cols(q):
        return pl.ds(pl.multiple_of(q * TILE, TILE), TILE)

    def right_slot(at, q):
        return right_full.at[block(at), cols(q)]

    def in_copy(way, q):
        return remote(right_ref.at[:, cols(q)], right_slot(2, q), send.at[(way + 1) // 2], in_recv.at[0, q], z_dev(way))

    def fwd_copy(q):
        slot = right_slot(1, q)
        return remote(slot, slot, send.at[2], in_recv.at[1, q], z_dev(1))

    def cut(q):
        return ((1, 0), (1, 1), (2, 2), (4, 4))[q]

    def cut_slot(at, q, h, n):
        return right_full.at[block(at, h * (rows // n), rows // n), cols(q)]

    def mid_copy(q, h=0, n=1):
        slot = cut_slot(3, q, h, n)
        return remote(slot, slot, send.at[3], in_recv.at[1, q], z_dev(-1))

    def end_start(q):
        n, at = cut(q)
        for h in range(n):
            source = right_ref.at[pl.ds(h * (rows // n), rows // n), cols(q)]
            remote(source, cut_slot(3, q, h, n), send.at[3], end_recv.at[at + h], z_dev(-1)).start()

    def own_half():
        return pl.ds(pl.multiple_of(k * half, half), half)

    def far_copy(p):
        at = pl.ds(pl.multiple_of(p * piece, piece), piece)
        return remote(left_full.at[block(0, p * piece, piece), own_half()], left_far.at[at, own_half()], send.at[2], far_recv.at[p], z_dev(-1))

    def far_slot(p, core):
        return left_far.at[pl.ds(pl.multiple_of(p * piece, piece), piece), pl.ds(pl.multiple_of(core * half, half), half)]

    def share_copy(p):
        return remote(far_slot(p, k), far_slot(p, k), send.at[4], a_recv.at[0], sib_dev)

    def own_copy(p):
        at = pl.ds(pl.multiple_of(p * piece, piece), piece)
        slot = left_full.at[pl.ds(pl.multiple_of(r * rows + p * piece, piece), piece), :]
        return remote(left_ref.at[at, :], slot, send.at[5], own_recv.at[p], sib_dev)

    def own_arrived(p):
        other = r + 1 - 2 * k
        arrived(left_full.at[pl.ds(pl.multiple_of(other * rows + p * piece, piece), piece), :], own_recv.at[p])

    def y_slot(side, pos, p, core, count=1):
        at = 3 * side if pos == 0 else 1 + side
        return left_full.at[block(at, p * piece, count * piece), pl.ds(pl.multiple_of(core * half, half), half)]

    def y_copy(pos, p, own=False):
        slot = y_slot(yc, pos, p, k)
        source = left_ref.at[pl.ds(pl.multiple_of(p * piece, piece), piece), own_half()] if own else slot
        return remote(source, slot, send.at[6], y_recv.at[pos, p], y_dev)

    def s_copy(pos, p, group):
        slot = y_slot(1 - yc, pos, p, k)
        return remote(slot, slot, send.at[7], s_recv.at[group], sib_dev)

    def part_copy(q):
        return remote(part.at[q], part.at[q], send.at[8], far_recv.at[q], z_dev(1))

    def each(body, first=0, last=steps):
        def step(at, carry):
            body(at)
            return carry

        lax.fori_loop(first, last, step, 0)

    def z_start():
        @when(inner)
        def _():
            @each
            def _(q):
                in_copy(-1, q).start()
                in_copy(1, q).start()

        @when(end)
        def _():
            end_start(0)
            end_start(1)

    when(k == 0)(z_start)
    first = kc == yc
    when(first)(lambda: each(lambda p: y_copy(0, p, True).start()))
    own_left = pltpu.make_async_copy(left_ref, left_full.at[pl.ds(pl.multiple_of(r * rows, rows), rows), :], own_sem.at[0])
    own = pltpu.make_async_copy(right_ref, right_full.at[block(zc), :], own_sem.at[1])
    weights = pltpu.make_async_copy(w_hbm, w_in, own_sem.at[2])
    counts_copy = pltpu.make_async_copy(counts_ref, counts_in, own_sem.at[3])
    each(lambda p: own_copy(p).start())
    for copy in (own_left, own, weights, counts_copy):
        copy.start()

    @each
    def _(p):
        own_arrived(p)
        when(k == 1, p == 0)(z_start)
        when(jnp.logical_not(first))(lambda: y_copy(0, p).start())
        when(end, yc == 0, kc == 1)(lambda: far_copy(p).start())
        when(end, yc == 0, kc == 1, p == steps - 2)(lambda: end_start(2))

    own_left.wait()

    @when(end, yc == 0, kc == 0)
    def _():
        each(lambda p: far_copy(p).start(), 0, steps - 1)
        end_start(2)
        far_copy(steps - 1).start()

    each(lambda p: y_copy(1, p).start())
    when(end, yc == 0)(lambda: end_start(3))

    row = lax.broadcasted_iota(jnp.int32, (TILE, TILE), 0)
    column = lax.broadcasted_iota(jnp.int32, (TILE, TILE), 1)
    order[...] = jnp.where(column == (row % heads) * CH + row // heads, 1.0, 0.0).astype(order.dtype)
    weights.wait()
    w_wide[...] = w_in[...].astype(jnp.float32)
    for e in range(CH):
        some = w_wide[pl.ds(e, CH, stride=CH), :].astype(w_ref.dtype)
        for i in range(2):
            w_ref[pl.ds((2 * e + i) * CH, CH), i * pair:(i + 1) * pair] = some
            w_ref[pl.ds((2 * e + i) * CH, CH), (1 - i) * pair:(2 - i) * pair] = jnp.zeros_like(some)
    counts_copy.wait()
    counted = counts_in[...].astype(jnp.float32)
    for i in range(counted.shape[1]):
        cover[i // 4, i % 4] = jnp.broadcast_to(counted[:, i:i + 1], (counted.shape[0], cover.shape[3]))

    def turn(at, q):
        value = lax.dot_general(order[...], right_full[block(at), cols(q)], (((1,), (1,)), ((), ())), preferred_element_type=jnp.float32)
        right_t[cols(q), block(at)] = value.astype(right_t.dtype)

    def product(into, lines, source, left, left_rows, size, wide, add):
        for n in range(width_l // wide):
            value = jnp.dot(right_t[lines, source], left[left_rows, pl.ds(n * wide, wide)], preferred_element_type=jnp.float32)
            for one in range(wide // 128):
                some = value[:, one * 128:(one + 1) * 128]
                slab = n * (wide // 128) + one
                into[slab, size, :] = into[slab, size, :] + some if add else some

    def product_all(at, add, first=0, depth=rows):
        every = pl.ds(0, width_r)
        product(acc, every, block(at, first, depth), left_full, block(at, first, depth), every, 256, add)

    def product_one(at, q):
        product(acc, cols(q), block(at), left_full, block(at), cols(q), 512, True)

    def project(source, first_row):
        low = lax.broadcasted_iota(jnp.int32, (lines, 128), 1) < 64
        for two in range(CH // 2):
            a, b = (
                source[:, pl.ds(pl.multiple_of(first_row + e * heads, heads), heads), :].reshape(lines, 128).astype(flat.dtype)
                for e in (2 * two, 2 * two + 1)
            )
            at = pl.ds(two * 128, 128)
            flat[pl.ds(0, lines), at] = jnp.where(low, a, pltpu.roll(b, 64, 1))
            flat[pl.ds(lines, lines), at] = jnp.where(low, pltpu.roll(a, 64, 1), b)
        return jnp.dot(flat[...], w_ref[...], preferred_element_type=jnp.float32)

    def spot(i):
        return slice(i // 2 * lines, (i // 2 + 1) * lines), slice(i % 2 * pair, (i % 2 + 1) * pair)

    def emit(q, i, value):
        at = pl.ds(pl.multiple_of(q * heads, heads), heads)
        out_ref[pl.ds(i, quads, stride=4), at, :] = value / cover[:, i, at, :]

    def settle(q):
        for i in range(4):
            value = out_v[q, :, i]
            emit(q, i, value + part[(q, *spot(i))].astype(jnp.float32).reshape(value.shape))

    own.wait()
    each(lambda q: turn(zc, q))

    def pass_on(q, h):
        n, at = cut(q)
        arrived(cut_slot(3, q, h, n), end_recv.at[at + h])
        mid_copy(q, h, n).start()

    def end_arrived(q):
        arrived(right_slot(3, q), end_recv.at[q])
        mid_copy(q).start()
        turn(3, q)

    def share(p):
        arrived(far_slot(p, k), far_recv.at[p])
        share_copy(p).start()

    @each
    def _(p):
        arrived(y_slot(1 - yc, 0, p, k), y_recv.at[0, p])
        s_copy(0, p, 0).start()
        when(end, yc == 1)(lambda: far_copy(p).start())
        when(end, yc == 1, p == steps - 2)(lambda: end_start(2))
        arrived(right_slot(zc - 1, p), in_recv.at[0, p])
        when(inner)(lambda: fwd_copy(p).start())
        turn(zc - 1, p)
        when(inner, p >= 1, p <= early)(lambda: end_arrived(p - 1))

    when(end, yc == 1)(lambda: end_start(3))
    arrived(y_slot(1 - yc, 0, 0, 1 - k, steps), s_recv.at[0])
    late = 2 - yc
    groups = ((0, early), (early, early + 1), (early + 1, steps))

    def y_arrived(p):
        group = next(at for at, (_, last) in enumerate(groups) if p < last)
        arrived(y_slot(1 - yc, 1, p, k), y_recv.at[1, p])
        s_copy(1, p, 1 + group).start()

    def late_part(group):
        low, high = groups[group]
        arrived(y_slot(1 - yc, 1, low, 1 - k, high - low), s_recv.at[1 + group])
        product_all(late, True, low * piece, (high - low) * piece)

    def far_turn(q):
        arrived(right_slot(0, q), in_recv.at[1, q])
        turn(0, q)

    def far_product(q):
        product(acc_far, cols(q), block(0), left_far, pl.ds(0, rows), pl.ds(0, TILE), 512, False)

    def far_send_on(q):
        part[q] = project(acc_far, 0).astype(part.dtype)
        part_copy(q).start()

    def finish(q):
        value = project(acc, q * TILE)
        for i in range(4):
            out_v[q, :, i] = value[spot(i)].reshape(quads, heads, pair)

    def sent(sem, count=1):
        slot = left_full.at[pl.ds(0, count * rows), pl.ds(0, half)]
        arrived(slot, send.at[sem])

    @when(inner)
    def _():
        each(share, 0, early)
        product_all(1 + yc, False)
        for q in range(early):
            product_one(3, q)
        y_arrived(0)
        share(2)
        far_turn(0)
        product_one(0, 0)
        pass_on(2, 0)
        pass_on(2, 1)
        turn(3, 2)
        product_one(3, 2)
        y_arrived(1)
        far_turn(1)
        product_one(0, 1)
        late_part(0)
        share(3)
        pass_on(3, 0)
        far_turn(2)
        product_one(0, 2)
        pass_on(3, 1)
        arrived(left_far.at[:, pl.ds(pl.multiple_of((1 - k) * half, half), half)], a_recv.at[0])
        far_product(0)
        y_arrived(2)
        far_send_on(0)
        pass_on(3, 2)
        far_product(1)
        pass_on(3, 3)
        far_send_on(1)
        far_product(2)
        far_send_on(2)
        late_part(1)
        y_arrived(3)
        turn(3, 3)
        product_one(3, 3)
        far_turn(3)
        far_product(3)
        far_send_on(3)
        late_part(2)
        product_one(0, 3)

        @each
        def _(q):
            value = project(acc, q * TILE)
            for i in range(4):
                emit(q, i, value[spot(i)].reshape(quads, heads, pair))

        sent(0)
        sent(1)
        sent(2)
        sent(3)
        sent(4)
        sent(5, 2)
        sent(6, 2)
        sent(7, 2)
        arrived(part, send.at[8])

    @when(end)
    def _():
        product_all(3, False)
        for q in range(steps):
            y_arrived(q)
            arrived(right_slot(1, q), in_recv.at[1, q])
            turn(1, q)
            product_one(1 + yc, q)
        for group in range(len(groups)):
            late_part(group)
        each(finish)
        sent(2)
        sent(3)
        sent(5, 2)
        sent(6, 2)
        sent(7, 2)

        @each
        def _(q):
            arrived(part.at[q], far_recv.at[q])
            settle(q)


def folded_call(left_act, right_act, counts, w_out):
    rows, width_l = left_act.shape
    width_r = right_act.shape[1]
    left_dev, right_dev = counts.shape
    pair = w_out.shape[1]
    steps = width_r // TILE
    heads = TILE // CH
    full = 4 * rows
    dma = pltpu.SemaphoreType.DMA
    return pl.pallas_call(
        folded,
        out_shape=jax.ShapeDtypeStruct((left_dev, right_dev, pair), jnp.float32),
        in_specs=[pl.BlockSpec(memory_space=pl.ANY)] * 4,
        out_specs=pl.BlockSpec(memory_space=pltpu.VMEM),
        scratch_shapes=[
            pltpu.VMEM(w_out.shape, w_out.dtype),
            pltpu.VMEM(w_out.shape, jnp.float32),
            pltpu.VMEM((2 * w_out.shape[0], 2 * pair), w_out.dtype),
            pltpu.VMEM((right_dev, left_dev), counts.dtype),
            pltpu.VMEM((left_dev // 4, 4, right_dev, pair), jnp.float32),
            pltpu.VMEM((TILE, TILE), jnp.bfloat16),
            pltpu.VMEM((full, width_l), jnp.bfloat16),
            pltpu.VMEM((rows, width_l), jnp.bfloat16),
            pltpu.VMEM((full, width_r), jnp.bfloat16),
            pltpu.VMEM((width_r, full), jnp.bfloat16),
            pltpu.VMEM((width_l // 128, width_r, 128), jnp.float32),
            pltpu.VMEM((width_l // 128, TILE, 128), jnp.float32),
            pltpu.VMEM((left_dev * heads // 2, 2 * CH * CH), jnp.bfloat16),
            pltpu.VMEM((steps, left_dev * heads // 2, 2 * pair), jnp.bfloat16),
            pltpu.VMEM((steps, left_dev // 4, 4, heads, pair), jnp.float32),
            dma((9,)), dma((2, steps)), dma((steps,)), dma((8,)), dma((steps,)), dma((2, steps)), dma((4,)), dma((1,)), dma((4,)),
        ],
        compiler_params=pltpu.CompilerParams(collective_id=0, has_side_effects=True, vmem_limit_bytes=38000 * 1024),
        name="pair_mean",
    )(*(pltpu.with_memory_space_constraint(x, pltpu.HBM) for x in (left_act, right_act, counts.T, w_out)))


def solution(mesh):
    n_z, n_r = mesh.shape["left"], mesh.shape["right"]
    n_y = n_r // CORES

    def shards(left_act, right_act, counts, w_out):
        width_l, width_r = left_act.shape[1], right_act.shape[1]
        if (n_z, n_y) == (4, 2) and width_r == 4 * TILE and width_l == CORES * width_r:
            return folded_call(left_act, right_act, counts, w_out)
        rows_l, width_l = left_act.shape
        rows_r, width_r = right_act.shape
        seqs = rows_r * n_z
        left_dev, right_dev = counts.shape
        pair = w_out.shape[1]
        q_z = width_r // 256
        q_y = rows_l // max(128, rows_l // 4)
        projected = pl.pallas_call(
            functools.partial(kernel, (n_z, n_r, q_z, q_y)),
            out_shape=jax.ShapeDtypeStruct((left_dev, right_dev, pair), jnp.float32),
            in_specs=[pl.BlockSpec(memory_space=pl.ANY)] * 4,
            out_specs=pl.BlockSpec(memory_space=pl.ANY),
            scratch_shapes=[
                pltpu.VMEM(w_out.shape, w_out.dtype),
                pltpu.VMEM(counts.shape, counts.dtype),
                pltpu.VMEM((right_dev, left_dev, pair), jnp.float32),
                pltpu.VMEM((q_z, left_dev, right_dev // q_z, pair), jnp.float32),
                pltpu.VMEM((seqs, width_l), jnp.bfloat16),
                pltpu.VMEM((seqs, width_r), jnp.bfloat16),
                pltpu.VMEM((width_l, seqs), jnp.bfloat16),
                pltpu.VMEM((width_r // 128, width_l, 128), jnp.float32),
                pltpu.VMEM((width_r // q_z // CH * left_dev, CH * CH), jnp.bfloat16),
                pltpu.SemaphoreType.DMA((2, (n_z - 1) * q_z)),
                pltpu.SemaphoreType.DMA((2, (n_z - 1) * q_z)),
                pltpu.SemaphoreType.DMA((2, (n_y - 1) * q_y)),
                pltpu.SemaphoreType.DMA((2, (n_y - 1) * q_y)),
                pltpu.SemaphoreType.DMA(((2 * n_y - 1) * q_y,)),
                pltpu.SemaphoreType.DMA(((2 * n_y - 1) * q_y,)),
                pltpu.SemaphoreType.DMA((4,)),
                pltpu.SemaphoreType.DMA((q_z,)),
            ],
            compiler_params=pltpu.CompilerParams(
                collective_id=0, has_side_effects=True, vmem_limit_bytes=56 * 1024 * 1024
            ),
            name="pair_mean",
        )(left_act, right_act, counts, w_out)
        return projected

    in_specs = (
        P(("groups", "right"), "left"),
        P(("groups", "left"), "right"),
        P(("groups", "left"), "right"),
        P(),
    )
    out_specs = P(("groups", "left"), "right", None)
    return jax.shard_map(shards, mesh=mesh, in_specs=in_specs, out_specs=out_specs, check_vma=False)
```

```python
import functools

import jax
import jax.numpy as jnp
from jax import lax
from jax.experimental import pallas as pl
from jax.experimental.pallas import tpu as pltpu
from jax.sharding import PartitionSpec as P

CH = 32
CORES = 2
TILE = 256
MESH = pl.DeviceIdType.MESH


def lane_quads(tiles):
    lane = lax.broadcasted_iota(jnp.int32, tiles[0].shape, 1)
    low = lane < 64
    even = (lane % 64) < 32
    stage = [None] * 4
    for c in range(2):
        a, b = tiles[c], tiles[c + 2]
        stage[c] = jnp.where(low, a, pltpu.roll(b, 64, 1))
        stage[c + 2] = jnp.where(low, pltpu.roll(a, 64, 1), b)
    outs = [None] * 4
    for half in range(2):
        a, b = stage[2 * half], stage[2 * half + 1]
        outs[2 * half] = jnp.where(even, a, pltpu.roll(b, 32, 1))
        outs[2 * half + 1] = jnp.where(even, pltpu.roll(a, 96, 1), b)
    return outs


def kernel(sizes, left_ref, right_ref, counts_ref, w_hbm, out_ref, w_ref, counts_in, cover, out_v, left_full, right_full, left_t, acc, flat,
           z_send, z_recv, y_send, y_recv, s_send, s_recv, own_sem, out_sem):
    n_z, n_r, q_z, q_y = sizes
    n_y = n_r // CORES
    rows_l, width_l = left_ref.shape
    rows_r, width_r = right_ref.shape
    piece_r = width_r // q_z
    piece_l = rows_l // q_y
    left_dev = width_l // CH
    right_dev = width_r // CH
    seqs = left_t.shape[1]
    z = lax.axis_index("left")
    r = lax.axis_index("right")
    y = r // CORES
    k = r % CORES

    def z_dev(pos):
        return {"left": pos}

    def y_dev(pos):
        return {"right": pos * CORES + k}

    sib_dev = {"right": y * CORES + (1 - k)}

    barrier = pltpu.get_barrier_semaphore()

    def greet(dev):
        pl.semaphore_signal(barrier, inc=1, device_id=dev, device_id_type=MESH)

    greet(sib_dev)
    for pos, n, dev in ((z, n_z, z_dev), (y, n_y, y_dev)):
        pl.when(pos + 1 < n)(functools.partial(greet, dev(pos + 1)))
        pl.when(pos >= 1)(functools.partial(greet, dev(pos - 1)))
    total = 1 + (z + 1 < n_z).astype(jnp.int32) + (z >= 1).astype(jnp.int32)
    total = total + (y + 1 < n_y).astype(jnp.int32) + (y >= 1).astype(jnp.int32)
    pl.semaphore_wait(barrier, total)

    def z_slot(chunk, q):
        return right_full.at[pl.ds(pl.multiple_of(chunk * rows_r, rows_r), rows_r), pl.ds(q * piece_r, piece_r)]

    def z_copy(side, step, q):
        sign = 1 - 2 * side
        chunk = z - sign * step
        src = right_ref.at[:, pl.ds(q * piece_r, piece_r)] if step == 0 else z_slot(chunk, q)
        at = step * q_z + q
        return pltpu.make_async_remote_copy(
            src_ref=src, dst_ref=z_slot(chunk, q), send_sem=z_send.at[side, at], recv_sem=z_recv.at[side, at],
            device_id=z_dev(z + sign), device_id_type=MESH)

    def z_sends(side, step):
        near = z + 1 < n_z if side == 0 else z >= 1
        far = z - step >= 0 if side == 0 else z + step < n_z
        return jnp.logical_and(near, far)

    def z_arrives(side, step):
        return z - step - 1 >= 0 if side == 0 else z + step + 1 < n_z

    def z_wait(side, step, q):
        sign = 1 - 2 * side
        slot = z_slot(z - sign * (step + 1), q)
        pltpu.make_async_copy(slot, slot, z_recv.at[side, step * q_z + q]).wait()

    def l_slot(chunk, q):
        return left_full.at[pl.ds(pl.multiple_of(chunk * rows_l + q * piece_l, piece_l), piece_l), :]

    def l_own(q):
        return left_ref.at[pl.ds(q * piece_l, piece_l), :]

    def y_copy(side, step, q):
        sign = 1 - 2 * side
        chunk = (y - sign * step) * CORES + k
        at = step * q_y + q
        return pltpu.make_async_remote_copy(
            src_ref=l_own(q) if step == 0 else l_slot(chunk, q), dst_ref=l_slot(chunk, q),
            send_sem=y_send.at[side, at], recv_sem=y_recv.at[side, at],
            device_id=y_dev(y + sign), device_id_type=MESH)

    def y_sends(side, step):
        near = y + 1 < n_y if side == 0 else y >= 1
        far = y - step >= 0 if side == 0 else y + step < n_y
        return jnp.logical_and(near, far)

    def y_arrives(side, step):
        return y - step - 1 >= 0 if side == 0 else y + step + 1 < n_y

    def y_wait(side, step, q):
        sign = 1 - 2 * side
        slot = l_slot((y - sign * (step + 1)) * CORES + k, q)
        pltpu.make_async_copy(slot, slot, y_recv.at[side, step * q_y + q]).wait()

    def s_at(side, step, q):
        if step < 0:
            return q
        return (1 + side * (n_y - 1) + step) * q_y + q

    def s_copy(side, step, q):
        sign = 1 - 2 * side
        chunk = (y - sign * (step + 1)) * CORES + k if step >= 0 else r
        at = s_at(side, step, q)
        return pltpu.make_async_remote_copy(
            src_ref=l_own(q) if step < 0 else l_slot(chunk, q), dst_ref=l_slot(chunk, q),
            send_sem=s_send.at[at], recv_sem=s_recv.at[at],
            device_id=sib_dev, device_id_type=MESH)

    def s_wait(side, step, q):
        sign = 1 - 2 * side
        y_from = y - sign * (step + 1) if step >= 0 else y
        slot = l_slot(y_from * CORES + (1 - k), q)
        pltpu.make_async_copy(slot, slot, s_recv.at[s_at(side, step, q)]).wait()

    tile = 256

    def turn(src, first_row, chunk, q):
        col = pl.multiple_of(chunk * rows_l + q * piece_l, piece_l)

        def body(m, carry):
            at = pl.multiple_of(m * tile, tile)
            left_t[pl.ds(at, tile), pl.ds(col, piece_l)] = src[pl.ds(first_row, piece_l), pl.ds(at, tile)].T
            return carry

        lax.fori_loop(0, width_l // tile, body, 0)

    def turn_full(chunk, q):
        turn(left_full, pl.multiple_of(chunk * rows_l + q * piece_l, piece_l), chunk, q)

    for q in range(max(q_z, q_y)):
        for side in range(2):
            if q < q_z:
                pl.when(z_sends(side, 0))(lambda side=side, q=q: z_copy(side, 0, q).start())
            if q < q_y:
                pl.when(y_sends(side, 0))(lambda side=side, q=q: y_copy(side, 0, q).start())
    own_left = pltpu.make_async_copy(left_ref, left_full.at[pl.ds(pl.multiple_of(r * rows_l, rows_l), rows_l), :], own_sem.at[0])
    own = pltpu.make_async_copy(right_ref, right_full.at[pl.ds(pl.multiple_of(z * rows_r, rows_r), rows_r), :], own_sem.at[1])
    weights = pltpu.make_async_copy(w_hbm, w_ref, own_sem.at[2])
    counts_copy = pltpu.make_async_copy(counts_ref, counts_in, own_sem.at[3])
    for copy in (own_left, own, weights, counts_copy):
        copy.start()
    for q in range(q_y):
        s_copy(0, -1, q).start()
    own_left.wait()
    for q in range(q_y):
        turn_full(r, q)
    counts_copy.wait()
    counted = counts_in[...].astype(jnp.float32)
    for j in range(right_dev):
        cover[j] = jnp.broadcast_to(counted[:, j:j + 1], (left_dev, cover.shape[2]))
    for q in range(q_y):
        s_wait(0, -1, q)
        turn_full(y * CORES + (1 - k), q)

    def z_tick(step, q):
        for side in range(2):
            @pl.when(z_arrives(side, step))
            def _():
                z_wait(side, step, q)
                if step + 1 < n_z - 1:
                    pl.when(z_sends(side, step + 1))(lambda: z_copy(side, step + 1, q).start())

    def y_tick(step, q):
        for side in range(2):
            @pl.when(y_arrives(side, step))
            def _():
                y_wait(side, step, q)
                s_copy(side, step, q).start()
                if step + 1 < n_y - 1:
                    pl.when(y_sends(side, step + 1))(lambda: y_copy(side, step + 1, q).start())

        for side in range(2):
            @pl.when(y_arrives(side, step))
            def _():
                sign = 1 - 2 * side
                y_from = y - sign * (step + 1)
                turn_full(y_from * CORES + k, q)
                s_wait(side, step, q)
                turn_full(y_from * CORES + (1 - k), q)

    y_ticks = [(step, q) for step in range(n_y - 1) for q in range(q_y)]
    for t in range((n_z - 2) * q_z):
        z_tick(t // q_z, t % q_z)
        if t % 2 == 1 and y_ticks:
            y_tick(*y_ticks.pop(0))
    for tick in y_ticks:
        y_tick(*tick)
    own.wait()
    weights.wait()

    block = 1024
    at_end = jnp.logical_or(z == 0, z == n_z - 1)
    base = jnp.where(z == 0, 0, rows_r)
    base = pl.multiple_of(base, rows_r)

    def product(q, first, depth, add):
        cols = pl.ds(q * piece_r, piece_r)

        def body(m, carry):
            rows = pl.ds(pl.multiple_of(m * block, block), block)
            value = jnp.dot(left_t[rows, pl.ds(first, depth)], right_full[pl.ds(first, depth), cols],
                            preferred_element_type=jnp.float32)
            for part in range(piece_r // 128):
                some = value[:, part * 128:(part + 1) * 128]
                slab = q * (piece_r // 128) + part
                acc[slab, rows, :] = acc[slab, rows, :] + some if add else some
            return carry

        lax.fori_loop(0, width_l // block, body, 0)

    def first_part(q):
        @pl.when(at_end)
        def _():
            product(q, base, seqs - rows_r, False)

        @pl.when(jnp.logical_not(at_end))
        def _():
            product(q, 0, seqs, False)

    for q in range(q_z):
        first_part(q)

    def finish(q):
        heads = piece_r // CH
        for quad in range(heads // 4):
            slab = acc.at[q * (piece_r // 128) + quad]
            for cq in range(CH // 4):
                tiles = [slab[pl.ds(cq * 4 + c, left_dev, stride=CH), :].astype(jnp.bfloat16) for c in range(4)]
                for j, value in enumerate(lane_quads(tiles)):
                    flat[pl.ds((quad * 4 + j) * left_dev, left_dev), pl.ds(cq * 128, 128)] = value
        projected = jnp.dot(flat[...], w_ref[...], preferred_element_type=jnp.float32)
        for j in range(heads):
            value = projected[j * left_dev:(j + 1) * left_dev, :] / cover[q * heads + j]
            out_v.at[q].reshape(left_dev * heads, value.shape[1])[pl.ds(j, left_dev, stride=heads), :] = value
        out_copy(q).start()

    def out_copy(q):
        return pltpu.make_async_copy(out_v.at[q], out_ref.at[:, pl.ds(q * heads_q, heads_q), :], out_sem.at[q])

    heads_q = piece_r // CH
    last = n_z - 2
    for q in range(q_z):
        z_tick(last, q)

        @pl.when(at_end)
        def _():
            far = jnp.where(z == 0, (n_z - 1) * rows_r, 0)
            product(q, pl.multiple_of(far, rows_r), rows_r, True)

        finish(q)

    for side in range(2):
        for step in range(n_z - 1):
            for q in range(q_z):
                pl.when(z_sends(side, step))(lambda side=side, step=step, q=q: z_copy(side, step, q).wait_send())
        for step in range(n_y - 1):
            for q in range(q_y):
                pl.when(y_sends(side, step))(lambda side=side, step=step, q=q: y_copy(side, step, q).wait_send())
                pl.when(y_arrives(side, step))(lambda side=side, step=step, q=q: s_copy(side, step, q).wait_send())
    for q in range(q_y):
        s_copy(0, -1, q).wait_send()
    for q in range(q_z):
        out_copy(q).wait()


def folded(left_ref, right_ref, counts_ref, w_hbm, out_ref, w_in, w_wide, w_ref, counts_in, cover, order, left_full, left_far, right_full, right_t,
           acc, acc_far, flat, part, out_v, send, in_recv, far_recv, end_recv, own_recv, y_recv, s_recv, a_recv, own_sem):
    rows, width_l = left_ref.shape
    width_r = right_ref.shape[1]
    steps = width_r // TILE
    piece = rows // steps
    half = width_l // CORES
    quads = width_l // 128
    heads = TILE // CH
    pair = w_hbm.shape[1]
    lines = quads * heads
    early = steps // 2
    z = lax.axis_index("left")
    r = lax.axis_index("right")
    y, k = r // CORES, r % CORES
    up = z // 2
    sign = 2 * up - 1

    def fold(n, at):
        return up * at + (1 - up) * (n - 1 - at)

    zc, yc, kc = fold(4, z), fold(2, y), fold(2, k)
    inner, end = zc == 2, zc == 3
    sib_dev = {"right": r + 1 - 2 * k}
    y_dev = {"right": r + (1 - 2 * y) * CORES}

    def when(*terms):
        value = terms[0]
        for term in terms[1:]:
            value = jnp.logical_and(value, term)
        return pl.when(value)

    def z_dev(way):
        return {"left": z + way * sign}

    barrier = pltpu.get_barrier_semaphore()

    def greet(dev):
        pl.semaphore_signal(barrier, inc=1, device_id=dev, device_id_type=MESH)

    greet(sib_dev)
    greet(y_dev)
    greet(z_dev(-1))
    when(inner)(lambda: greet(z_dev(1)))
    pl.semaphore_wait(barrier, 3 + inner.astype(jnp.int32))

    def remote(src, dst, send, recv, dev):
        return pltpu.make_async_remote_copy(src_ref=src, dst_ref=dst, send_sem=send, recv_sem=recv, device_id=dev, device_id_type=MESH)

    def arrived(slot, sem):
        pltpu.make_async_copy(slot, slot, sem).wait()

    def block(at, first=0, size=rows):
        return pl.ds(pl.multiple_of(fold(4, at) * rows + first, size), size)

    def cols(q):
        return pl.ds(pl.multiple_of(q * TILE, TILE), TILE)

    def right_slot(at, q):
        return right_full.at[block(at), cols(q)]

    def in_copy(way, q):
        return remote(right_ref.at[:, cols(q)], right_slot(2, q), send.at[(way + 1) // 2], in_recv.at[0, q], z_dev(way))

    def fwd_copy(q):
        slot = right_slot(1, q)
        return remote(slot, slot, send.at[2], in_recv.at[1, q], z_dev(1))

    def cut(q):
        return ((1, 0), (1, 1), (2, 2), (4, 4))[q]

    def cut_slot(at, q, h, n):
        return right_full.at[block(at, h * (rows // n), rows // n), cols(q)]

    def mid_copy(q, h=0, n=1):
        slot = cut_slot(3, q, h, n)
        return remote(slot, slot, send.at[3], in_recv.at[1, q], z_dev(-1))

    def end_start(q):
        n, at = cut(q)
        for h in range(n):
            source = right_ref.at[pl.ds(h * (rows // n), rows // n), cols(q)]
            remote(source, cut_slot(3, q, h, n), send.at[3], end_recv.at[at + h], z_dev(-1)).start()

    def own_half():
        return pl.ds(pl.multiple_of(k * half, half), half)

    def far_copy(p):
        at = pl.ds(pl.multiple_of(p * piece, piece), piece)
        return remote(left_full.at[block(0, p * piece, piece), own_half()], left_far.at[at, own_half()], send.at[2], far_recv.at[p], z_dev(-1))

    def far_slot(p, core):
        return left_far.at[pl.ds(pl.multiple_of(p * piece, piece), piece), pl.ds(pl.multiple_of(core * half, half), half)]

    def share_copy(p):
        return remote(far_slot(p, k), far_slot(p, k), send.at[4], a_recv.at[0], sib_dev)

    def own_copy(p):
        at = pl.ds(pl.multiple_of(p * piece, piece), piece)
        slot = left_full.at[pl.ds(pl.multiple_of(r * rows + p * piece, piece), piece), :]
        return remote(left_ref.at[at, :], slot, send.at[5], own_recv.at[p], sib_dev)

    def own_arrived(p):
        other = r + 1 - 2 * k
        arrived(left_full.at[pl.ds(pl.multiple_of(other * rows + p * piece, piece), piece), :], own_recv.at[p])

    def y_slot(side, pos, p, core, count=1):
        at = 3 * side if pos == 0 else 1 + side
        return left_full.at[block(at, p * piece, count * piece), pl.ds(pl.multiple_of(core * half, half), half)]

    def y_copy(pos, p, own=False):
        slot = y_slot(yc, pos, p, k)
        source = left_ref.at[pl.ds(pl.multiple_of(p * piece, piece), piece), own_half()] if own else slot
        return remote(source, slot, send.at[6], y_recv.at[pos, p], y_dev)

    def s_copy(pos, p, group):
        slot = y_slot(1 - yc, pos, p, k)
        return remote(slot, slot, send.at[7], s_recv.at[group], sib_dev)

    def part_copy(q):
        return remote(part.at[q], part.at[q], send.at[8], far_recv.at[q], z_dev(1))

    def each(body, first=0, last=steps):
        def step(at, carry):
            body(at)
            return carry

        lax.fori_loop(first, last, step, 0)

    @when(inner)
    def _():
        @each
        def _(q):
            in_copy(-1, q).start()
            in_copy(1, q).start()

    @when(end)
    def _():
        end_start(0)
        end_start(1)

    first = kc == yc
    when(first)(lambda: each(lambda p: y_copy(0, p, True).start()))
    own_left = pltpu.make_async_copy(left_ref, left_full.at[pl.ds(pl.multiple_of(r * rows, rows), rows), :], own_sem.at[0])
    own = pltpu.make_async_copy(right_ref, right_full.at[block(zc), :], own_sem.at[1])
    weights = pltpu.make_async_copy(w_hbm, w_in, own_sem.at[2])
    counts_copy = pltpu.make_async_copy(counts_ref, counts_in, own_sem.at[3])
    each(lambda p: own_copy(p).start())
    for copy in (own_left, own, weights, counts_copy):
        copy.start()

    @each
    def _(p):
        own_arrived(p)
        when(jnp.logical_not(first))(lambda: y_copy(0, p).start())
        when(end, yc == 0, kc == 1)(lambda: far_copy(p).start())
        when(end, yc == 0, kc == 1, p == steps - 2)(lambda: end_start(2))

    own_left.wait()

    @when(end, yc == 0, kc == 0)
    def _():
        each(lambda p: far_copy(p).start(), 0, steps - 1)
        end_start(2)
        far_copy(steps - 1).start()

    each(lambda p: y_copy(1, p).start())
    when(end, yc == 0)(lambda: end_start(3))

    row = lax.broadcasted_iota(jnp.int32, (TILE, TILE), 0)
    column = lax.broadcasted_iota(jnp.int32, (TILE, TILE), 1)
    order[...] = jnp.where(column == (row % heads) * CH + row // heads, 1.0, 0.0).astype(order.dtype)
    weights.wait()
    w_wide[...] = w_in[...].astype(jnp.float32)
    for e in range(CH):
        some = w_wide[pl.ds(e, CH, stride=CH), :].astype(w_ref.dtype)
        for i in range(2):
            w_ref[pl.ds((2 * e + i) * CH, CH), i * pair:(i + 1) * pair] = some
            w_ref[pl.ds((2 * e + i) * CH, CH), (1 - i) * pair:(2 - i) * pair] = jnp.zeros_like(some)
    counts_copy.wait()
    counted = counts_in[...].astype(jnp.float32)
    for i in range(counted.shape[1]):
        cover[i // 4, i % 4] = jnp.broadcast_to(counted[:, i:i + 1], (counted.shape[0], cover.shape[3]))

    def turn(at, q):
        value = lax.dot_general(order[...], right_full[block(at), cols(q)], (((1,), (1,)), ((), ())), preferred_element_type=jnp.float32)
        right_t[cols(q), block(at)] = value.astype(right_t.dtype)

    def product(into, lines, source, left, left_rows, size, wide, add):
        for n in range(width_l // wide):
            value = jnp.dot(right_t[lines, source], left[left_rows, pl.ds(n * wide, wide)], preferred_element_type=jnp.float32)
            for one in range(wide // 128):
                some = value[:, one * 128:(one + 1) * 128]
                slab = n * (wide // 128) + one
                into[slab, size, :] = into[slab, size, :] + some if add else some

    def product_all(at, add, first=0, depth=rows):
        every = pl.ds(0, width_r)
        product(acc, every, block(at, first, depth), left_full, block(at, first, depth), every, 256, add)

    def product_one(at, q):
        product(acc, cols(q), block(at), left_full, block(at), cols(q), 512, True)

    def project(source, first_row):
        low = lax.broadcasted_iota(jnp.int32, (lines, 128), 1) < 64
        for two in range(CH // 2):
            a, b = (
                source[:, pl.ds(pl.multiple_of(first_row + e * heads, heads), heads), :].reshape(lines, 128).astype(flat.dtype)
                for e in (2 * two, 2 * two + 1)
            )
            at = pl.ds(two * 128, 128)
            flat[pl.ds(0, lines), at] = jnp.where(low, a, pltpu.roll(b, 64, 1))
            flat[pl.ds(lines, lines), at] = jnp.where(low, pltpu.roll(a, 64, 1), b)
        return jnp.dot(flat[...], w_ref[...], preferred_element_type=jnp.float32)

    def spot(i):
        return slice(i // 2 * lines, (i // 2 + 1) * lines), slice(i % 2 * pair, (i % 2 + 1) * pair)

    def emit(q, i, value):
        at = pl.ds(pl.multiple_of(q * heads, heads), heads)
        out_ref[pl.ds(i, quads, stride=4), at, :] = value / cover[:, i, at, :]

    def settle(q):
        for i in range(4):
            value = out_v[q, :, i]
            emit(q, i, value + part[(q, *spot(i))].astype(jnp.float32).reshape(value.shape))

    own.wait()
    each(lambda q: turn(zc, q))

    def pass_on(q, h):
        n, at = cut(q)
        arrived(cut_slot(3, q, h, n), end_recv.at[at + h])
        mid_copy(q, h, n).start()

    def end_arrived(q):
        arrived(right_slot(3, q), end_recv.at[q])
        mid_copy(q).start()
        turn(3, q)

    def share(p):
        arrived(far_slot(p, k), far_recv.at[p])
        share_copy(p).start()

    @each
    def _(p):
        arrived(y_slot(1 - yc, 0, p, k), y_recv.at[0, p])
        s_copy(0, p, 0).start()
        when(end, yc == 1)(lambda: far_copy(p).start())
        when(end, yc == 1, p == steps - 2)(lambda: end_start(2))
        arrived(right_slot(zc - 1, p), in_recv.at[0, p])
        when(inner)(lambda: fwd_copy(p).start())
        turn(zc - 1, p)
        when(inner, p >= 1, p <= early)(lambda: end_arrived(p - 1))

    when(end, yc == 1)(lambda: end_start(3))
    arrived(y_slot(1 - yc, 0, 0, 1 - k, steps), s_recv.at[0])
    late = 2 - yc
    groups = ((0, early), (early, early + 1), (early + 1, steps))

    def y_arrived(p):
        group = next(at for at, (_, last) in enumerate(groups) if p < last)
        arrived(y_slot(1 - yc, 1, p, k), y_recv.at[1, p])
        s_copy(1, p, 1 + group).start()

    def late_part(group):
        low, high = groups[group]
        arrived(y_slot(1 - yc, 1, low, 1 - k, high - low), s_recv.at[1 + group])
        product_all(late, True, low * piece, (high - low) * piece)

    def far_turn(q):
        arrived(right_slot(0, q), in_recv.at[1, q])
        turn(0, q)

    def far_product(q):
        product(acc_far, cols(q), block(0), left_far, pl.ds(0, rows), pl.ds(0, TILE), 512, False)

    def far_send_on(q):
        part[q] = project(acc_far, 0).astype(part.dtype)
        part_copy(q).start()

    def finish(q):
        value = project(acc, q * TILE)
        for i in range(4):
            out_v[q, :, i] = value[spot(i)].reshape(quads, heads, pair)

    def sent(sem, count=1):
        slot = left_full.at[pl.ds(0, count * rows), pl.ds(0, half)]
        arrived(slot, send.at[sem])

    @when(inner)
    def _():
        each(share, 0, early)
        product_all(1 + yc, False)
        for q in range(early):
            product_one(3, q)
        y_arrived(0)
        share(2)
        far_turn(0)
        product_one(0, 0)
        pass_on(2, 0)
        pass_on(2, 1)
        turn(3, 2)
        product_one(3, 2)
        y_arrived(1)
        far_turn(1)
        product_one(0, 1)
        late_part(0)
        share(3)
        pass_on(3, 0)
        far_turn(2)
        product_one(0, 2)
        pass_on(3, 1)
        arrived(left_far.at[:, pl.ds(pl.multiple_of((1 - k) * half, half), half)], a_recv.at[0])
        far_product(0)
        y_arrived(2)
        far_send_on(0)
        pass_on(3, 2)
        far_product(1)
        pass_on(3, 3)
        far_send_on(1)
        far_product(2)
        far_send_on(2)
        late_part(1)
        y_arrived(3)
        turn(3, 3)
        product_one(3, 3)
        far_turn(3)
        far_product(3)
        far_send_on(3)
        late_part(2)
        product_one(0, 3)

        @each
        def _(q):
            value = project(acc, q * TILE)
            for i in range(4):
                emit(q, i, value[spot(i)].reshape(quads, heads, pair))

        sent(0)
        sent(1)
        sent(2)
        sent(3)
        sent(4)
        sent(5, 2)
        sent(6, 2)
        sent(7, 2)
        arrived(part, send.at[8])

    @when(end)
    def _():
        product_all(3, False)
        for q in range(steps):
            y_arrived(q)
            arrived(right_slot(1, q), in_recv.at[1, q])
            turn(1, q)
            product_one(1 + yc, q)
        for group in range(len(groups)):
            late_part(group)
        each(finish)
        sent(2)
        sent(3)
        sent(5, 2)
        sent(6, 2)
        sent(7, 2)

        @each
        def _(q):
            arrived(part.at[q], far_recv.at[q])
            settle(q)


def folded_call(left_act, right_act, counts, w_out):
    rows, width_l = left_act.shape
    width_r = right_act.shape[1]
    left_dev, right_dev = counts.shape
    pair = w_out.shape[1]
    steps = width_r // TILE
    heads = TILE // CH
    full = 4 * rows
    dma = pltpu.SemaphoreType.DMA
    return pl.pallas_call(
        folded,
        out_shape=jax.ShapeDtypeStruct((left_dev, right_dev, pair), jnp.float32),
        in_specs=[pl.BlockSpec(memory_space=pl.ANY)] * 4,
        out_specs=pl.BlockSpec(memory_space=pltpu.VMEM),
        scratch_shapes=[
            pltpu.VMEM(w_out.shape, w_out.dtype),
            pltpu.VMEM(w_out.shape, jnp.float32),
            pltpu.VMEM((2 * w_out.shape[0], 2 * pair), w_out.dtype),
            pltpu.VMEM((right_dev, left_dev), counts.dtype),
            pltpu.VMEM((left_dev // 4, 4, right_dev, pair), jnp.float32),
            pltpu.VMEM((TILE, TILE), jnp.bfloat16),
            pltpu.VMEM((full, width_l), jnp.bfloat16),
            pltpu.VMEM((rows, width_l), jnp.bfloat16),
            pltpu.VMEM((full, width_r), jnp.bfloat16),
            pltpu.VMEM((width_r, full), jnp.bfloat16),
            pltpu.VMEM((width_l // 128, width_r, 128), jnp.float32),
            pltpu.VMEM((width_l // 128, TILE, 128), jnp.float32),
            pltpu.VMEM((left_dev * heads // 2, 2 * CH * CH), jnp.bfloat16),
            pltpu.VMEM((steps, left_dev * heads // 2, 2 * pair), jnp.bfloat16),
            pltpu.VMEM((steps, left_dev // 4, 4, heads, pair), jnp.float32),
            dma((9,)), dma((2, steps)), dma((steps,)), dma((8,)), dma((steps,)), dma((2, steps)), dma((4,)), dma((1,)), dma((4,)),
        ],
        compiler_params=pltpu.CompilerParams(collective_id=0, has_side_effects=True, vmem_limit_bytes=38000 * 1024),
        name="pair_mean",
    )(*(pltpu.with_memory_space_constraint(x, pltpu.HBM) for x in (left_act, right_act, counts.T, w_out)))


def solution(mesh):
    n_z, n_r = mesh.shape["left"], mesh.shape["right"]
    n_y = n_r // CORES

    def shards(left_act, right_act, counts, w_out):
        width_l, width_r = left_act.shape[1], right_act.shape[1]
        if (n_z, n_y) == (4, 2) and width_r == 4 * TILE and width_l == CORES * width_r:
            return folded_call(left_act, right_act, counts, w_out)
        rows_l, width_l = left_act.shape
        rows_r, width_r = right_act.shape
        seqs = rows_r * n_z
        left_dev, right_dev = counts.shape
        pair = w_out.shape[1]
        q_z = width_r // 256
        q_y = rows_l // max(128, rows_l // 4)
        projected = pl.pallas_call(
            functools.partial(kernel, (n_z, n_r, q_z, q_y)),
            out_shape=jax.ShapeDtypeStruct((left_dev, right_dev, pair), jnp.float32),
            in_specs=[pl.BlockSpec(memory_space=pl.ANY)] * 4,
            out_specs=pl.BlockSpec(memory_space=pl.ANY),
            scratch_shapes=[
                pltpu.VMEM(w_out.shape, w_out.dtype),
                pltpu.VMEM(counts.shape, counts.dtype),
                pltpu.VMEM((right_dev, left_dev, pair), jnp.float32),
                pltpu.VMEM((q_z, left_dev, right_dev // q_z, pair), jnp.float32),
                pltpu.VMEM((seqs, width_l), jnp.bfloat16),
                pltpu.VMEM((seqs, width_r), jnp.bfloat16),
                pltpu.VMEM((width_l, seqs), jnp.bfloat16),
                pltpu.VMEM((width_r // 128, width_l, 128), jnp.float32),
                pltpu.VMEM((width_r // q_z // CH * left_dev, CH * CH), jnp.bfloat16),
                pltpu.SemaphoreType.DMA((2, (n_z - 1) * q_z)),
                pltpu.SemaphoreType.DMA((2, (n_z - 1) * q_z)),
                pltpu.SemaphoreType.DMA((2, (n_y - 1) * q_y)),
                pltpu.SemaphoreType.DMA((2, (n_y - 1) * q_y)),
                pltpu.SemaphoreType.DMA(((2 * n_y - 1) * q_y,)),
                pltpu.SemaphoreType.DMA(((2 * n_y - 1) * q_y,)),
                pltpu.SemaphoreType.DMA((4,)),
                pltpu.SemaphoreType.DMA((q_z,)),
            ],
            compiler_params=pltpu.CompilerParams(
                collective_id=0, has_side_effects=True, vmem_limit_bytes=56 * 1024 * 1024
            ),
            name="pair_mean",
        )(left_act, right_act, counts, w_out)
        return projected

    in_specs = (
        P(("groups", "right"), "left"),
        P(("groups", "left"), "right"),
        P(("groups", "left"), "right"),
        P(),
    )
    out_specs = P(("groups", "left"), "right", None)
    return jax.shard_map(shards, mesh=mesh, in_specs=in_specs, out_specs=out_specs, check_vma=False)
```

```python
import functools

import jax
import jax.numpy as jnp
from jax import lax
from jax.experimental import pallas as pl
from jax.experimental.pallas import tpu as pltpu
from jax.sharding import PartitionSpec as P

CH = 32
CORES = 2
TILE = 256
MESH = pl.DeviceIdType.MESH


def lane_quads(tiles):
    lane = lax.broadcasted_iota(jnp.int32, tiles[0].shape, 1)
    low = lane < 64
    even = (lane % 64) < 32
    stage = [None] * 4
    for c in range(2):
        a, b = tiles[c], tiles[c + 2]
        stage[c] = jnp.where(low, a, pltpu.roll(b, 64, 1))
        stage[c + 2] = jnp.where(low, pltpu.roll(a, 64, 1), b)
    outs = [None] * 4
    for half in range(2):
        a, b = stage[2 * half], stage[2 * half + 1]
        outs[2 * half] = jnp.where(even, a, pltpu.roll(b, 32, 1))
        outs[2 * half + 1] = jnp.where(even, pltpu.roll(a, 96, 1), b)
    return outs


def kernel(sizes, left_ref, right_ref, counts_ref, w_hbm, out_ref, w_ref, counts_in, cover, out_v, left_full, right_full, left_t, acc, flat,
           z_send, z_recv, y_send, y_recv, s_send, s_recv, own_sem, out_sem):
    n_z, n_r, q_z, q_y = sizes
    n_y = n_r // CORES
    rows_l, width_l = left_ref.shape
    rows_r, width_r = right_ref.shape
    piece_r = width_r // q_z
    piece_l = rows_l // q_y
    left_dev = width_l // CH
    right_dev = width_r // CH
    seqs = left_t.shape[1]
    z = lax.axis_index("left")
    r = lax.axis_index("right")
    y = r // CORES
    k = r % CORES

    def z_dev(pos):
        return {"left": pos}

    def y_dev(pos):
        return {"right": pos * CORES + k}

    sib_dev = {"right": y * CORES + (1 - k)}

    barrier = pltpu.get_barrier_semaphore()

    def greet(dev):
        pl.semaphore_signal(barrier, inc=1, device_id=dev, device_id_type=MESH)

    greet(sib_dev)
    for pos, n, dev in ((z, n_z, z_dev), (y, n_y, y_dev)):
        pl.when(pos + 1 < n)(functools.partial(greet, dev(pos + 1)))
        pl.when(pos >= 1)(functools.partial(greet, dev(pos - 1)))
    total = 1 + (z + 1 < n_z).astype(jnp.int32) + (z >= 1).astype(jnp.int32)
    total = total + (y + 1 < n_y).astype(jnp.int32) + (y >= 1).astype(jnp.int32)
    pl.semaphore_wait(barrier, total)

    def z_slot(chunk, q):
        return right_full.at[pl.ds(pl.multiple_of(chunk * rows_r, rows_r), rows_r), pl.ds(q * piece_r, piece_r)]

    def z_copy(side, step, q):
        sign = 1 - 2 * side
        chunk = z - sign * step
        src = right_ref.at[:, pl.ds(q * piece_r, piece_r)] if step == 0 else z_slot(chunk, q)
        at = step * q_z + q
        return pltpu.make_async_remote_copy(
            src_ref=src, dst_ref=z_slot(chunk, q), send_sem=z_send.at[side, at], recv_sem=z_recv.at[side, at],
            device_id=z_dev(z + sign), device_id_type=MESH)

    def z_sends(side, step):
        near = z + 1 < n_z if side == 0 else z >= 1
        far = z - step >= 0 if side == 0 else z + step < n_z
        return jnp.logical_and(near, far)

    def z_arrives(side, step):
        return z - step - 1 >= 0 if side == 0 else z + step + 1 < n_z

    def z_wait(side, step, q):
        sign = 1 - 2 * side
        slot = z_slot(z - sign * (step + 1), q)
        pltpu.make_async_copy(slot, slot, z_recv.at[side, step * q_z + q]).wait()

    def l_slot(chunk, q):
        return left_full.at[pl.ds(pl.multiple_of(chunk * rows_l + q * piece_l, piece_l), piece_l), :]

    def l_own(q):
        return left_ref.at[pl.ds(q * piece_l, piece_l), :]

    def y_copy(side, step, q):
        sign = 1 - 2 * side
        chunk = (y - sign * step) * CORES + k
        at = step * q_y + q
        return pltpu.make_async_remote_copy(
            src_ref=l_own(q) if step == 0 else l_slot(chunk, q), dst_ref=l_slot(chunk, q),
            send_sem=y_send.at[side, at], recv_sem=y_recv.at[side, at],
            device_id=y_dev(y + sign), device_id_type=MESH)

    def y_sends(side, step):
        near = y + 1 < n_y if side == 0 else y >= 1
        far = y - step >= 0 if side == 0 else y + step < n_y
        return jnp.logical_and(near, far)

    def y_arrives(side, step):
        return y - step - 1 >= 0 if side == 0 else y + step + 1 < n_y

    def y_wait(side, step, q):
        sign = 1 - 2 * side
        slot = l_slot((y - sign * (step + 1)) * CORES + k, q)
        pltpu.make_async_copy(slot, slot, y_recv.at[side, step * q_y + q]).wait()

    def s_at(side, step, q):
        if step < 0:
            return q
        return (1 + side * (n_y - 1) + step) * q_y + q

    def s_copy(side, step, q):
        sign = 1 - 2 * side
        chunk = (y - sign * (step + 1)) * CORES + k if step >= 0 else r
        at = s_at(side, step, q)
        return pltpu.make_async_remote_copy(
            src_ref=l_own(q) if step < 0 else l_slot(chunk, q), dst_ref=l_slot(chunk, q),
            send_sem=s_send.at[at], recv_sem=s_recv.at[at],
            device_id=sib_dev, device_id_type=MESH)

    def s_wait(side, step, q):
        sign = 1 - 2 * side
        y_from = y - sign * (step + 1) if step >= 0 else y
        slot = l_slot(y_from * CORES + (1 - k), q)
        pltpu.make_async_copy(slot, slot, s_recv.at[s_at(side, step, q)]).wait()

    tile = 256

    def turn(src, first_row, chunk, q):
        col = pl.multiple_of(chunk * rows_l + q * piece_l, piece_l)

        def body(m, carry):
            at = pl.multiple_of(m * tile, tile)
            left_t[pl.ds(at, tile), pl.ds(col, piece_l)] = src[pl.ds(first_row, piece_l), pl.ds(at, tile)].T
            return carry

        lax.fori_loop(0, width_l // tile, body, 0)

    def turn_full(chunk, q):
        turn(left_full, pl.multiple_of(chunk * rows_l + q * piece_l, piece_l), chunk, q)

    for q in range(max(q_z, q_y)):
        for side in range(2):
            if q < q_z:
                pl.when(z_sends(side, 0))(lambda side=side, q=q: z_copy(side, 0, q).start())
            if q < q_y:
                pl.when(y_sends(side, 0))(lambda side=side, q=q: y_copy(side, 0, q).start())
    own_left = pltpu.make_async_copy(left_ref, left_full.at[pl.ds(pl.multiple_of(r * rows_l, rows_l), rows_l), :], own_sem.at[0])
    own = pltpu.make_async_copy(right_ref, right_full.at[pl.ds(pl.multiple_of(z * rows_r, rows_r), rows_r), :], own_sem.at[1])
    weights = pltpu.make_async_copy(w_hbm, w_ref, own_sem.at[2])
    counts_copy = pltpu.make_async_copy(counts_ref, counts_in, own_sem.at[3])
    for copy in (own_left, own, weights, counts_copy):
        copy.start()
    for q in range(q_y):
        s_copy(0, -1, q).start()
    own_left.wait()
    for q in range(q_y):
        turn_full(r, q)
    counts_copy.wait()
    counted = counts_in[...].astype(jnp.float32)
    for j in range(right_dev):
        cover[j] = jnp.broadcast_to(counted[:, j:j + 1], (left_dev, cover.shape[2]))
    for q in range(q_y):
        s_wait(0, -1, q)
        turn_full(y * CORES + (1 - k), q)

    def z_tick(step, q):
        for side in range(2):
            @pl.when(z_arrives(side, step))
            def _():
                z_wait(side, step, q)
                if step + 1 < n_z - 1:
                    pl.when(z_sends(side, step + 1))(lambda: z_copy(side, step + 1, q).start())

    def y_tick(step, q):
        for side in range(2):
            @pl.when(y_arrives(side, step))
            def _():
                y_wait(side, step, q)
                s_copy(side, step, q).start()
                if step + 1 < n_y - 1:
                    pl.when(y_sends(side, step + 1))(lambda: y_copy(side, step + 1, q).start())

        for side in range(2):
            @pl.when(y_arrives(side, step))
            def _():
                sign = 1 - 2 * side
                y_from = y - sign * (step + 1)
                turn_full(y_from * CORES + k, q)
                s_wait(side, step, q)
                turn_full(y_from * CORES + (1 - k), q)

    y_ticks = [(step, q) for step in range(n_y - 1) for q in range(q_y)]
    for t in range((n_z - 2) * q_z):
        z_tick(t // q_z, t % q_z)
        if t % 2 == 1 and y_ticks:
            y_tick(*y_ticks.pop(0))
    for tick in y_ticks:
        y_tick(*tick)
    own.wait()
    weights.wait()

    block = 1024
    at_end = jnp.logical_or(z == 0, z == n_z - 1)
    base = jnp.where(z == 0, 0, rows_r)
    base = pl.multiple_of(base, rows_r)

    def product(q, first, depth, add):
        cols = pl.ds(q * piece_r, piece_r)

        def body(m, carry):
            rows = pl.ds(pl.multiple_of(m * block, block), block)
            value = jnp.dot(left_t[rows, pl.ds(first, depth)], right_full[pl.ds(first, depth), cols],
                            preferred_element_type=jnp.float32)
            for part in range(piece_r // 128):
                some = value[:, part * 128:(part + 1) * 128]
                slab = q * (piece_r // 128) + part
                acc[slab, rows, :] = acc[slab, rows, :] + some if add else some
            return carry

        lax.fori_loop(0, width_l // block, body, 0)

    def first_part(q):
        @pl.when(at_end)
        def _():
            product(q, base, seqs - rows_r, False)

        @pl.when(jnp.logical_not(at_end))
        def _():
            product(q, 0, seqs, False)

    for q in range(q_z):
        first_part(q)

    def finish(q):
        heads = piece_r // CH
        for quad in range(heads // 4):
            slab = acc.at[q * (piece_r // 128) + quad]
            for cq in range(CH // 4):
                tiles = [slab[pl.ds(cq * 4 + c, left_dev, stride=CH), :].astype(jnp.bfloat16) for c in range(4)]
                for j, value in enumerate(lane_quads(tiles)):
                    flat[pl.ds((quad * 4 + j) * left_dev, left_dev), pl.ds(cq * 128, 128)] = value
        projected = jnp.dot(flat[...], w_ref[...], preferred_element_type=jnp.float32)
        for j in range(heads):
            value = projected[j * left_dev:(j + 1) * left_dev, :] / cover[q * heads + j]
            out_v.at[q].reshape(left_dev * heads, value.shape[1])[pl.ds(j, left_dev, stride=heads), :] = value
        out_copy(q).start()

    def out_copy(q):
        return pltpu.make_async_copy(out_v.at[q], out_ref.at[:, pl.ds(q * heads_q, heads_q), :], out_sem.at[q])

    heads_q = piece_r // CH
    last = n_z - 2
    for q in range(q_z):
        z_tick(last, q)

        @pl.when(at_end)
        def _():
            far = jnp.where(z == 0, (n_z - 1) * rows_r, 0)
            product(q, pl.multiple_of(far, rows_r), rows_r, True)

        finish(q)

    for side in range(2):
        for step in range(n_z - 1):
            for q in range(q_z):
                pl.when(z_sends(side, step))(lambda side=side, step=step, q=q: z_copy(side, step, q).wait_send())
        for step in range(n_y - 1):
            for q in range(q_y):
                pl.when(y_sends(side, step))(lambda side=side, step=step, q=q: y_copy(side, step, q).wait_send())
                pl.when(y_arrives(side, step))(lambda side=side, step=step, q=q: s_copy(side, step, q).wait_send())
    for q in range(q_y):
        s_copy(0, -1, q).wait_send()
    for q in range(q_z):
        out_copy(q).wait()


def folded(left_ref, right_ref, counts_ref, w_hbm, out_ref, w_in, w_wide, w_ref, counts_in, cover, order, left_full, left_far, right_full, right_t,
           acc, acc_far, flat, part, out_v, send, in_recv, far_recv, end_recv, own_recv, y_recv, s_recv, a_recv, own_sem):
    rows, width_l = left_ref.shape
    width_r = right_ref.shape[1]
    steps = width_r // TILE
    piece = rows // steps
    half = width_l // CORES
    quads = width_l // 128
    heads = TILE // CH
    pair = w_hbm.shape[1]
    lines = quads * heads
    early = steps // 2
    z = lax.axis_index("left")
    r = lax.axis_index("right")
    y, k = r // CORES, r % CORES
    up = z // 2
    sign = 2 * up - 1

    def fold(n, at):
        return up * at + (1 - up) * (n - 1 - at)

    zc, yc, kc = fold(4, z), fold(2, y), fold(2, k)
    inner, end = zc == 2, zc == 3
    sib_dev = {"right": r + 1 - 2 * k}
    y_dev = {"right": r + (1 - 2 * y) * CORES}

    def when(*terms):
        value = terms[0]
        for term in terms[1:]:
            value = jnp.logical_and(value, term)
        return pl.when(value)

    def z_dev(way):
        return {"left": z + way * sign}

    barrier = pltpu.get_barrier_semaphore()

    def greet(dev):
        pl.semaphore_signal(barrier, inc=1, device_id=dev, device_id_type=MESH)

    greet(sib_dev)
    greet(y_dev)
    greet(z_dev(-1))
    when(inner)(lambda: greet(z_dev(1)))
    pl.semaphore_wait(barrier, 3 + inner.astype(jnp.int32))

    def remote(src, dst, send, recv, dev):
        return pltpu.make_async_remote_copy(src_ref=src, dst_ref=dst, send_sem=send, recv_sem=recv, device_id=dev, device_id_type=MESH)

    def arrived(slot, sem):
        pltpu.make_async_copy(slot, slot, sem).wait()

    def block(at, first=0, size=rows):
        return pl.ds(pl.multiple_of(fold(4, at) * rows + first, size), size)

    def cols(q):
        return pl.ds(pl.multiple_of(q * TILE, TILE), TILE)

    def right_slot(at, q):
        return right_full.at[block(at), cols(q)]

    def in_copy(way, q):
        return remote(right_ref.at[:, cols(q)], right_slot(2, q), send.at[(way + 1) // 2], in_recv.at[0, q], z_dev(way))

    def fwd_copy(q):
        slot = right_slot(1, q)
        return remote(slot, slot, send.at[2], in_recv.at[1, q], z_dev(1))

    def cut(q):
        return ((1, 0), (1, 1), (2, 2), (4, 4))[q]

    def cut_slot(at, q, h, n):
        return right_full.at[block(at, h * (rows // n), rows // n), cols(q)]

    def mid_copy(q, h=0, n=1):
        slot = cut_slot(3, q, h, n)
        return remote(slot, slot, send.at[3], in_recv.at[1, q], z_dev(-1))

    def end_start(q):
        n, at = cut(q)
        for h in range(n):
            source = right_ref.at[pl.ds(h * (rows // n), rows // n), cols(q)]
            remote(source, cut_slot(3, q, h, n), send.at[3], end_recv.at[at + h], z_dev(-1)).start()

    def own_half():
        return pl.ds(pl.multiple_of(k * half, half), half)

    def far_copy(p):
        at = pl.ds(pl.multiple_of(p * piece, piece), piece)
        return remote(left_full.at[block(0, p * piece, piece), own_half()], left_far.at[at, own_half()], send.at[2], far_recv.at[p], z_dev(-1))

    def far_slot(p, core):
        return left_far.at[pl.ds(pl.multiple_of(p * piece, piece), piece), pl.ds(pl.multiple_of(core * half, half), half)]

    def share_copy(p):
        return remote(far_slot(p, k), far_slot(p, k), send.at[4], a_recv.at[0], sib_dev)

    def own_copy(p):
        at = pl.ds(pl.multiple_of(p * piece, piece), piece)
        slot = left_full.at[pl.ds(pl.multiple_of(r * rows + p * piece, piece), piece), :]
        return remote(left_ref.at[at, :], slot, send.at[5], own_recv.at[p], sib_dev)

    def own_arrived(p):
        other = r + 1 - 2 * k
        arrived(left_full.at[pl.ds(pl.multiple_of(other * rows + p * piece, piece), piece), :], own_recv.at[p])

    def y_slot(side, pos, p, core, count=1):
        at = 3 * side if pos == 0 else 1 + side
        return left_full.at[block(at, p * piece, count * piece), pl.ds(pl.multiple_of(core * half, half), half)]

    def y_copy(pos, p, own=False):
        slot = y_slot(yc, pos, p, k)
        source = left_ref.at[pl.ds(pl.multiple_of(p * piece, piece), piece), own_half()] if own else slot
        return remote(source, slot, send.at[6], y_recv.at[pos, p], y_dev)

    def s_copy(pos, p, group):
        slot = y_slot(1 - yc, pos, p, k)
        return remote(slot, slot, send.at[7], s_recv.at[group], sib_dev)

    def part_copy(q):
        return remote(part.at[q], part.at[q], send.at[8], far_recv.at[q], z_dev(1))

    def each(body, first=0, last=steps):
        def step(at, carry):
            body(at)
            return carry

        lax.fori_loop(first, last, step, 0)

    @when(inner)
    def _():
        @each
        def _(q):
            in_copy(-1, q).start()
            in_copy(1, q).start()

    @when(end)
    def _():
        end_start(0)
        end_start(1)

    first = kc == yc
    when(first)(lambda: each(lambda p: y_copy(0, p, True).start()))
    own_left = pltpu.make_async_copy(left_ref, left_full.at[pl.ds(pl.multiple_of(r * rows, rows), rows), :], own_sem.at[0])
    own = pltpu.make_async_copy(right_ref, right_full.at[block(zc), :], own_sem.at[1])
    weights = pltpu.make_async_copy(w_hbm, w_in, own_sem.at[2])
    counts_copy = pltpu.make_async_copy(counts_ref, counts_in, own_sem.at[3])
    each(lambda p: own_copy(p).start())
    for copy in (own_left, own, weights, counts_copy):
        copy.start()

    @each
    def _(p):
        own_arrived(p)
        when(jnp.logical_not(first))(lambda: y_copy(0, p).start())
        when(end, yc == 0, kc == 1)(lambda: far_copy(p).start())
        when(end, yc == 0, kc == 1, p == steps - 2)(lambda: end_start(2))

    own_left.wait()

    @when(end, yc == 0, kc == 0)
    def _():
        each(lambda p: far_copy(p).start(), 0, steps - 1)
        end_start(2)
        far_copy(steps - 1).start()

    each(lambda p: y_copy(1, p).start())
    when(end, yc == 0)(lambda: end_start(3))

    row = lax.broadcasted_iota(jnp.int32, (TILE, TILE), 0)
    column = lax.broadcasted_iota(jnp.int32, (TILE, TILE), 1)
    order[...] = jnp.where(column == (row % heads) * CH + row // heads, 1.0, 0.0).astype(order.dtype)
    weights.wait()
    w_wide[...] = w_in[...].astype(jnp.float32)
    for e in range(CH):
        some = w_wide[pl.ds(e, CH, stride=CH), :].astype(w_ref.dtype)
        for i in range(2):
            w_ref[pl.ds((2 * e + i) * CH, CH), i * pair:(i + 1) * pair] = some
            w_ref[pl.ds((2 * e + i) * CH, CH), (1 - i) * pair:(2 - i) * pair] = jnp.zeros_like(some)
    counts_copy.wait()
    counted = counts_in[...].astype(jnp.float32)
    for i in range(counted.shape[1]):
        cover[i // 4, i % 4] = jnp.broadcast_to(counted[:, i:i + 1], (counted.shape[0], cover.shape[3]))

    def turn(at, q):
        value = lax.dot_general(order[...], right_full[block(at), cols(q)], (((1,), (1,)), ((), ())), preferred_element_type=jnp.float32)
        right_t[cols(q), block(at)] = value.astype(right_t.dtype)

    def product(into, lines, source, left, left_rows, size, wide, add):
        for n in range(width_l // wide):
            value = jnp.dot(right_t[lines, source], left[left_rows, pl.ds(n * wide, wide)], preferred_element_type=jnp.float32)
            for one in range(wide // 128):
                some = value[:, one * 128:(one + 1) * 128]
                slab = n * (wide // 128) + one
                into[slab, size, :] = into[slab, size, :] + some if add else some

    def product_all(at, add, first=0, depth=rows):
        every = pl.ds(0, width_r)
        product(acc, every, block(at, first, depth), left_full, block(at, first, depth), every, 256, add)

    def product_one(at, q):
        product(acc, cols(q), block(at), left_full, block(at), cols(q), 512, True)

    def project(source, first_row):
        low = lax.broadcasted_iota(jnp.int32, (lines, 128), 1) < 64
        for two in range(CH // 2):
            a, b = (
                source[:, pl.ds(pl.multiple_of(first_row + e * heads, heads), heads), :].reshape(lines, 128).astype(flat.dtype)
                for e in (2 * two, 2 * two + 1)
            )
            at = pl.ds(two * 128, 128)
            flat[pl.ds(0, lines), at] = jnp.where(low, a, pltpu.roll(b, 64, 1))
            flat[pl.ds(lines, lines), at] = jnp.where(low, pltpu.roll(a, 64, 1), b)
        return jnp.dot(flat[...], w_ref[...], preferred_element_type=jnp.float32)

    def spot(i):
        return slice(i // 2 * lines, (i // 2 + 1) * lines), slice(i % 2 * pair, (i % 2 + 1) * pair)

    def emit(q, i, value):
        at = pl.ds(pl.multiple_of(q * heads, heads), heads)
        out_ref[pl.ds(i, quads, stride=4), at, :] = value / cover[:, i, at, :]

    def settle(q):
        for i in range(4):
            value = out_v[q, :, i]
            emit(q, i, value + part[(q, *spot(i))].astype(jnp.float32).reshape(value.shape))

    own.wait()
    each(lambda q: turn(zc, q))

    def pass_on(q, h):
        n, at = cut(q)
        arrived(cut_slot(3, q, h, n), end_recv.at[at + h])
        mid_copy(q, h, n).start()

    def end_arrived(q):
        arrived(right_slot(3, q), end_recv.at[q])
        mid_copy(q).start()
        turn(3, q)

    def share(p):
        arrived(far_slot(p, k), far_recv.at[p])
        share_copy(p).start()

    @each
    def _(p):
        arrived(y_slot(1 - yc, 0, p, k), y_recv.at[0, p])
        s_copy(0, p, 0).start()
        when(end, yc == 1)(lambda: far_copy(p).start())
        when(end, yc == 1, p == steps - 2)(lambda: end_start(2))
        arrived(right_slot(zc - 1, p), in_recv.at[0, p])
        when(inner)(lambda: fwd_copy(p).start())
        turn(zc - 1, p)
        when(inner, p >= 1, p <= early)(lambda: end_arrived(p - 1))

    when(end, yc == 1)(lambda: end_start(3))
    arrived(y_slot(1 - yc, 0, 0, 1 - k, steps), s_recv.at[0])
    late = 2 - yc
    groups = ((0, early), (early, early + 1), (early + 1, steps))

    def y_arrived(p):
        group = next(at for at, (_, last) in enumerate(groups) if p < last)
        arrived(y_slot(1 - yc, 1, p, k), y_recv.at[1, p])
        s_copy(1, p, 1 + group).start()

    def late_part(group):
        low, high = groups[group]
        arrived(y_slot(1 - yc, 1, low, 1 - k, high - low), s_recv.at[1 + group])
        product_all(late, True, low * piece, (high - low) * piece)

    def far_turn(q):
        arrived(right_slot(0, q), in_recv.at[1, q])
        turn(0, q)

    def far_product(q):
        product(acc_far, cols(q), block(0), left_far, pl.ds(0, rows), pl.ds(0, TILE), 512, False)

    def far_send_on(q):
        part[q] = project(acc_far, 0).astype(part.dtype)
        pl.when(k == 0)(lambda: part_copy(q).start())
        if q >= 1:
            pl.when(k == 1)(lambda: part_copy(q - 1).start())
        if q == steps - 1:
            pl.when(k == 1)(lambda: part_copy(q).start())

    def finish(q):
        value = project(acc, q * TILE)
        for i in range(4):
            out_v[q, :, i] = value[spot(i)].reshape(quads, heads, pair)

    def sent(sem, count=1):
        slot = left_full.at[pl.ds(0, count * rows), pl.ds(0, half)]
        arrived(slot, send.at[sem])

    @when(inner)
    def _():
        each(share, 0, early)
        product_all(1 + yc, False)
        for q in range(early):
            product_one(3, q)
        y_arrived(0)
        share(2)
        far_turn(0)
        product_one(0, 0)
        pass_on(2, 0)
        pass_on(2, 1)
        turn(3, 2)
        product_one(3, 2)
        y_arrived(1)
        far_turn(1)
        product_one(0, 1)
        late_part(0)
        share(3)
        pass_on(3, 0)
        far_turn(2)
        product_one(0, 2)
        pass_on(3, 1)
        arrived(left_far.at[:, pl.ds(pl.multiple_of((1 - k) * half, half), half)], a_recv.at[0])
        far_product(0)
        y_arrived(2)
        far_send_on(0)
        pass_on(3, 2)
        far_product(1)
        pass_on(3, 3)
        far_send_on(1)
        far_product(2)
        far_send_on(2)
        late_part(1)
        y_arrived(3)
        turn(3, 3)
        product_one(3, 3)
        far_turn(3)
        far_product(3)
        far_send_on(3)
        late_part(2)
        product_one(0, 3)

        @each
        def _(q):
            value = project(acc, q * TILE)
            for i in range(4):
                emit(q, i, value[spot(i)].reshape(quads, heads, pair))

        sent(0)
        sent(1)
        sent(2)
        sent(3)
        sent(4)
        sent(5, 2)
        sent(6, 2)
        sent(7, 2)
        arrived(part, send.at[8])

    @when(end)
    def _():
        product_all(3, False)
        for q in range(steps):
            y_arrived(q)
            arrived(right_slot(1, q), in_recv.at[1, q])
            turn(1, q)
            product_one(1 + yc, q)
        for group in range(len(groups)):
            late_part(group)
        each(finish)
        sent(2)
        sent(3)
        sent(5, 2)
        sent(6, 2)
        sent(7, 2)

        @each
        def _(q):
            arrived(part.at[q], far_recv.at[q])
            settle(q)


def folded_call(left_act, right_act, counts, w_out):
    rows, width_l = left_act.shape
    width_r = right_act.shape[1]
    left_dev, right_dev = counts.shape
    pair = w_out.shape[1]
    steps = width_r // TILE
    heads = TILE // CH
    full = 4 * rows
    dma = pltpu.SemaphoreType.DMA
    return pl.pallas_call(
        folded,
        out_shape=jax.ShapeDtypeStruct((left_dev, right_dev, pair), jnp.float32),
        in_specs=[pl.BlockSpec(memory_space=pl.ANY)] * 4,
        out_specs=pl.BlockSpec(memory_space=pltpu.VMEM),
        scratch_shapes=[
            pltpu.VMEM(w_out.shape, w_out.dtype),
            pltpu.VMEM(w_out.shape, jnp.float32),
            pltpu.VMEM((2 * w_out.shape[0], 2 * pair), w_out.dtype),
            pltpu.VMEM((right_dev, left_dev), counts.dtype),
            pltpu.VMEM((left_dev // 4, 4, right_dev, pair), jnp.float32),
            pltpu.VMEM((TILE, TILE), jnp.bfloat16),
            pltpu.VMEM((full, width_l), jnp.bfloat16),
            pltpu.VMEM((rows, width_l), jnp.bfloat16),
            pltpu.VMEM((full, width_r), jnp.bfloat16),
            pltpu.VMEM((width_r, full), jnp.bfloat16),
            pltpu.VMEM((width_l // 128, width_r, 128), jnp.float32),
            pltpu.VMEM((width_l // 128, TILE, 128), jnp.float32),
            pltpu.VMEM((left_dev * heads // 2, 2 * CH * CH), jnp.bfloat16),
            pltpu.VMEM((steps, left_dev * heads // 2, 2 * pair), jnp.bfloat16),
            pltpu.VMEM((steps, left_dev // 4, 4, heads, pair), jnp.float32),
            dma((9,)), dma((2, steps)), dma((steps,)), dma((8,)), dma((steps,)), dma((2, steps)), dma((4,)), dma((1,)), dma((4,)),
        ],
        compiler_params=pltpu.CompilerParams(collective_id=0, has_side_effects=True, vmem_limit_bytes=38000 * 1024),
        name="pair_mean",
    )(*(pltpu.with_memory_space_constraint(x, pltpu.HBM) for x in (left_act, right_act, counts.T, w_out)))


def solution(mesh):
    n_z, n_r = mesh.shape["left"], mesh.shape["right"]
    n_y = n_r // CORES

    def shards(left_act, right_act, counts, w_out):
        width_l, width_r = left_act.shape[1], right_act.shape[1]
        if (n_z, n_y) == (4, 2) and width_r == 4 * TILE and width_l == CORES * width_r:
            return folded_call(left_act, right_act, counts, w_out)
        rows_l, width_l = left_act.shape
        rows_r, width_r = right_act.shape
        seqs = rows_r * n_z
        left_dev, right_dev = counts.shape
        pair = w_out.shape[1]
        q_z = width_r // 256
        q_y = rows_l // max(128, rows_l // 4)
        projected = pl.pallas_call(
            functools.partial(kernel, (n_z, n_r, q_z, q_y)),
            out_shape=jax.ShapeDtypeStruct((left_dev, right_dev, pair), jnp.float32),
            in_specs=[pl.BlockSpec(memory_space=pl.ANY)] * 4,
            out_specs=pl.BlockSpec(memory_space=pl.ANY),
            scratch_shapes=[
                pltpu.VMEM(w_out.shape, w_out.dtype),
                pltpu.VMEM(counts.shape, counts.dtype),
                pltpu.VMEM((right_dev, left_dev, pair), jnp.float32),
                pltpu.VMEM((q_z, left_dev, right_dev // q_z, pair), jnp.float32),
                pltpu.VMEM((seqs, width_l), jnp.bfloat16),
                pltpu.VMEM((seqs, width_r), jnp.bfloat16),
                pltpu.VMEM((width_l, seqs), jnp.bfloat16),
                pltpu.VMEM((width_r // 128, width_l, 128), jnp.float32),
                pltpu.VMEM((width_r // q_z // CH * left_dev, CH * CH), jnp.bfloat16),
                pltpu.SemaphoreType.DMA((2, (n_z - 1) * q_z)),
                pltpu.SemaphoreType.DMA((2, (n_z - 1) * q_z)),
                pltpu.SemaphoreType.DMA((2, (n_y - 1) * q_y)),
                pltpu.SemaphoreType.DMA((2, (n_y - 1) * q_y)),
                pltpu.SemaphoreType.DMA(((2 * n_y - 1) * q_y,)),
                pltpu.SemaphoreType.DMA(((2 * n_y - 1) * q_y,)),
                pltpu.SemaphoreType.DMA((4,)),
                pltpu.SemaphoreType.DMA((q_z,)),
            ],
            compiler_params=pltpu.CompilerParams(
                collective_id=0, has_side_effects=True, vmem_limit_bytes=56 * 1024 * 1024
            ),
            name="pair_mean",
        )(left_act, right_act, counts, w_out)
        return projected

    in_specs = (
        P(("groups", "right"), "left"),
        P(("groups", "left"), "right"),
        P(("groups", "left"), "right"),
        P(),
    )
    out_specs = P(("groups", "left"), "right", None)
    return jax.shard_map(shards, mesh=mesh, in_specs=in_specs, out_specs=out_specs, check_vma=False)
```

```python
import functools

import jax
import jax.numpy as jnp
from jax import lax
from jax.experimental import pallas as pl
from jax.experimental.pallas import tpu as pltpu
from jax.sharding import PartitionSpec as P

CH = 32
CORES = 2
TILE = 256
MESH = pl.DeviceIdType.MESH


def lane_quads(tiles):
    lane = lax.broadcasted_iota(jnp.int32, tiles[0].shape, 1)
    low = lane < 64
    even = (lane % 64) < 32
    stage = [None] * 4
    for c in range(2):
        a, b = tiles[c], tiles[c + 2]
        stage[c] = jnp.where(low, a, pltpu.roll(b, 64, 1))
        stage[c + 2] = jnp.where(low, pltpu.roll(a, 64, 1), b)
    outs = [None] * 4
    for half in range(2):
        a, b = stage[2 * half], stage[2 * half + 1]
        outs[2 * half] = jnp.where(even, a, pltpu.roll(b, 32, 1))
        outs[2 * half + 1] = jnp.where(even, pltpu.roll(a, 96, 1), b)
    return outs


def kernel(sizes, left_ref, right_ref, counts_ref, w_hbm, out_ref, w_ref, counts_in, cover, out_v, left_full, right_full, left_t, acc, flat,
           z_send, z_recv, y_send, y_recv, s_send, s_recv, own_sem, out_sem):
    n_z, n_r, q_z, q_y = sizes
    n_y = n_r // CORES
    rows_l, width_l = left_ref.shape
    rows_r, width_r = right_ref.shape
    piece_r = width_r // q_z
    piece_l = rows_l // q_y
    left_dev = width_l // CH
    right_dev = width_r // CH
    seqs = left_t.shape[1]
    z = lax.axis_index("left")
    r = lax.axis_index("right")
    y = r // CORES
    k = r % CORES

    def z_dev(pos):
        return {"left": pos}

    def y_dev(pos):
        return {"right": pos * CORES + k}

    sib_dev = {"right": y * CORES + (1 - k)}

    barrier = pltpu.get_barrier_semaphore()

    def greet(dev):
        pl.semaphore_signal(barrier, inc=1, device_id=dev, device_id_type=MESH)

    greet(sib_dev)
    for pos, n, dev in ((z, n_z, z_dev), (y, n_y, y_dev)):
        pl.when(pos + 1 < n)(functools.partial(greet, dev(pos + 1)))
        pl.when(pos >= 1)(functools.partial(greet, dev(pos - 1)))
    total = 1 + (z + 1 < n_z).astype(jnp.int32) + (z >= 1).astype(jnp.int32)
    total = total + (y + 1 < n_y).astype(jnp.int32) + (y >= 1).astype(jnp.int32)
    pl.semaphore_wait(barrier, total)

    def z_slot(chunk, q):
        return right_full.at[pl.ds(pl.multiple_of(chunk * rows_r, rows_r), rows_r), pl.ds(q * piece_r, piece_r)]

    def z_copy(side, step, q):
        sign = 1 - 2 * side
        chunk = z - sign * step
        src = right_ref.at[:, pl.ds(q * piece_r, piece_r)] if step == 0 else z_slot(chunk, q)
        at = step * q_z + q
        return pltpu.make_async_remote_copy(
            src_ref=src, dst_ref=z_slot(chunk, q), send_sem=z_send.at[side, at], recv_sem=z_recv.at[side, at],
            device_id=z_dev(z + sign), device_id_type=MESH)

    def z_sends(side, step):
        near = z + 1 < n_z if side == 0 else z >= 1
        far = z - step >= 0 if side == 0 else z + step < n_z
        return jnp.logical_and(near, far)

    def z_arrives(side, step):
        return z - step - 1 >= 0 if side == 0 else z + step + 1 < n_z

    def z_wait(side, step, q):
        sign = 1 - 2 * side
        slot = z_slot(z - sign * (step + 1), q)
        pltpu.make_async_copy(slot, slot, z_recv.at[side, step * q_z + q]).wait()

    def l_slot(chunk, q):
        return left_full.at[pl.ds(pl.multiple_of(chunk * rows_l + q * piece_l, piece_l), piece_l), :]

    def l_own(q):
        return left_ref.at[pl.ds(q * piece_l, piece_l), :]

    def y_copy(side, step, q):
        sign = 1 - 2 * side
        chunk = (y - sign * step) * CORES + k
        at = step * q_y + q
        return pltpu.make_async_remote_copy(
            src_ref=l_own(q) if step == 0 else l_slot(chunk, q), dst_ref=l_slot(chunk, q),
            send_sem=y_send.at[side, at], recv_sem=y_recv.at[side, at],
            device_id=y_dev(y + sign), device_id_type=MESH)

    def y_sends(side, step):
        near = y + 1 < n_y if side == 0 else y >= 1
        far = y - step >= 0 if side == 0 else y + step < n_y
        return jnp.logical_and(near, far)

    def y_arrives(side, step):
        return y - step - 1 >= 0 if side == 0 else y + step + 1 < n_y

    def y_wait(side, step, q):
        sign = 1 - 2 * side
        slot = l_slot((y - sign * (step + 1)) * CORES + k, q)
        pltpu.make_async_copy(slot, slot, y_recv.at[side, step * q_y + q]).wait()

    def s_at(side, step, q):
        if step < 0:
            return q
        return (1 + side * (n_y - 1) + step) * q_y + q

    def s_copy(side, step, q):
        sign = 1 - 2 * side
        chunk = (y - sign * (step + 1)) * CORES + k if step >= 0 else r
        at = s_at(side, step, q)
        return pltpu.make_async_remote_copy(
            src_ref=l_own(q) if step < 0 else l_slot(chunk, q), dst_ref=l_slot(chunk, q),
            send_sem=s_send.at[at], recv_sem=s_recv.at[at],
            device_id=sib_dev, device_id_type=MESH)

    def s_wait(side, step, q):
        sign = 1 - 2 * side
        y_from = y - sign * (step + 1) if step >= 0 else y
        slot = l_slot(y_from * CORES + (1 - k), q)
        pltpu.make_async_copy(slot, slot, s_recv.at[s_at(side, step, q)]).wait()

    tile = 256

    def turn(src, first_row, chunk, q):
        col = pl.multiple_of(chunk * rows_l + q * piece_l, piece_l)

        def body(m, carry):
            at = pl.multiple_of(m * tile, tile)
            left_t[pl.ds(at, tile), pl.ds(col, piece_l)] = src[pl.ds(first_row, piece_l), pl.ds(at, tile)].T
            return carry

        lax.fori_loop(0, width_l // tile, body, 0)

    def turn_full(chunk, q):
        turn(left_full, pl.multiple_of(chunk * rows_l + q * piece_l, piece_l), chunk, q)

    for q in range(max(q_z, q_y)):
        for side in range(2):
            if q < q_z:
                pl.when(z_sends(side, 0))(lambda side=side, q=q: z_copy(side, 0, q).start())
            if q < q_y:
                pl.when(y_sends(side, 0))(lambda side=side, q=q: y_copy(side, 0, q).start())
    own_left = pltpu.make_async_copy(left_ref, left_full.at[pl.ds(pl.multiple_of(r * rows_l, rows_l), rows_l), :], own_sem.at[0])
    own = pltpu.make_async_copy(right_ref, right_full.at[pl.ds(pl.multiple_of(z * rows_r, rows_r), rows_r), :], own_sem.at[1])
    weights = pltpu.make_async_copy(w_hbm, w_ref, own_sem.at[2])
    counts_copy = pltpu.make_async_copy(counts_ref, counts_in, own_sem.at[3])
    for copy in (own_left, own, weights, counts_copy):
        copy.start()
    for q in range(q_y):
        s_copy(0, -1, q).start()
    own_left.wait()
    for q in range(q_y):
        turn_full(r, q)
    counts_copy.wait()
    counted = counts_in[...].astype(jnp.float32)
    for j in range(right_dev):
        cover[j] = jnp.broadcast_to(counted[:, j:j + 1], (left_dev, cover.shape[2]))
    for q in range(q_y):
        s_wait(0, -1, q)
        turn_full(y * CORES + (1 - k), q)

    def z_tick(step, q):
        for side in range(2):
            @pl.when(z_arrives(side, step))
            def _():
                z_wait(side, step, q)
                if step + 1 < n_z - 1:
                    pl.when(z_sends(side, step + 1))(lambda: z_copy(side, step + 1, q).start())

    def y_tick(step, q):
        for side in range(2):
            @pl.when(y_arrives(side, step))
            def _():
                y_wait(side, step, q)
                s_copy(side, step, q).start()
                if step + 1 < n_y - 1:
                    pl.when(y_sends(side, step + 1))(lambda: y_copy(side, step + 1, q).start())

        for side in range(2):
            @pl.when(y_arrives(side, step))
            def _():
                sign = 1 - 2 * side
                y_from = y - sign * (step + 1)
                turn_full(y_from * CORES + k, q)
                s_wait(side, step, q)
                turn_full(y_from * CORES + (1 - k), q)

    y_ticks = [(step, q) for step in range(n_y - 1) for q in range(q_y)]
    for t in range((n_z - 2) * q_z):
        z_tick(t // q_z, t % q_z)
        if t % 2 == 1 and y_ticks:
            y_tick(*y_ticks.pop(0))
    for tick in y_ticks:
        y_tick(*tick)
    own.wait()
    weights.wait()

    block = 1024
    at_end = jnp.logical_or(z == 0, z == n_z - 1)
    base = jnp.where(z == 0, 0, rows_r)
    base = pl.multiple_of(base, rows_r)

    def product(q, first, depth, add):
        cols = pl.ds(q * piece_r, piece_r)

        def body(m, carry):
            rows = pl.ds(pl.multiple_of(m * block, block), block)
            value = jnp.dot(left_t[rows, pl.ds(first, depth)], right_full[pl.ds(first, depth), cols],
                            preferred_element_type=jnp.float32)
            for part in range(piece_r // 128):
                some = value[:, part * 128:(part + 1) * 128]
                slab = q * (piece_r // 128) + part
                acc[slab, rows, :] = acc[slab, rows, :] + some if add else some
            return carry

        lax.fori_loop(0, width_l // block, body, 0)

    def first_part(q):
        @pl.when(at_end)
        def _():
            product(q, base, seqs - rows_r, False)

        @pl.when(jnp.logical_not(at_end))
        def _():
            product(q, 0, seqs, False)

    for q in range(q_z):
        first_part(q)

    def finish(q):
        heads = piece_r // CH
        for quad in range(heads // 4):
            slab = acc.at[q * (piece_r // 128) + quad]
            for cq in range(CH // 4):
                tiles = [slab[pl.ds(cq * 4 + c, left_dev, stride=CH), :].astype(jnp.bfloat16) for c in range(4)]
                for j, value in enumerate(lane_quads(tiles)):
                    flat[pl.ds((quad * 4 + j) * left_dev, left_dev), pl.ds(cq * 128, 128)] = value
        projected = jnp.dot(flat[...], w_ref[...], preferred_element_type=jnp.float32)
        for j in range(heads):
            value = projected[j * left_dev:(j + 1) * left_dev, :] / cover[q * heads + j]
            out_v.at[q].reshape(left_dev * heads, value.shape[1])[pl.ds(j, left_dev, stride=heads), :] = value
        out_copy(q).start()

    def out_copy(q):
        return pltpu.make_async_copy(out_v.at[q], out_ref.at[:, pl.ds(q * heads_q, heads_q), :], out_sem.at[q])

    heads_q = piece_r // CH
    last = n_z - 2
    for q in range(q_z):
        z_tick(last, q)

        @pl.when(at_end)
        def _():
            far = jnp.where(z == 0, (n_z - 1) * rows_r, 0)
            product(q, pl.multiple_of(far, rows_r), rows_r, True)

        finish(q)

    for side in range(2):
        for step in range(n_z - 1):
            for q in range(q_z):
                pl.when(z_sends(side, step))(lambda side=side, step=step, q=q: z_copy(side, step, q).wait_send())
        for step in range(n_y - 1):
            for q in range(q_y):
                pl.when(y_sends(side, step))(lambda side=side, step=step, q=q: y_copy(side, step, q).wait_send())
                pl.when(y_arrives(side, step))(lambda side=side, step=step, q=q: s_copy(side, step, q).wait_send())
    for q in range(q_y):
        s_copy(0, -1, q).wait_send()
    for q in range(q_z):
        out_copy(q).wait()


def folded(left_ref, right_ref, counts_ref, w_hbm, out_ref, w_in, w_wide, w_ref, counts_in, cover, order, left_full, left_far, right_full, right_t,
           acc, acc_far, flat, part, out_v, send, in_recv, far_recv, end_recv, own_recv, y_recv, s_recv, a_recv, own_sem):
    rows, width_l = left_ref.shape
    width_r = right_ref.shape[1]
    steps = width_r // TILE
    piece = rows // steps
    half = width_l // CORES
    quads = width_l // 128
    heads = TILE // CH
    pair = w_hbm.shape[1]
    lines = quads * heads
    early = steps // 2
    z = lax.axis_index("left")
    r = lax.axis_index("right")
    y, k = r // CORES, r % CORES
    up = z // 2
    sign = 2 * up - 1

    def fold(n, at):
        return up * at + (1 - up) * (n - 1 - at)

    zc, yc, kc = fold(4, z), fold(2, y), fold(2, k)
    inner, end = zc == 2, zc == 3
    sib_dev = {"right": r + 1 - 2 * k}
    y_dev = {"right": r + (1 - 2 * y) * CORES}

    def when(*terms):
        value = terms[0]
        for term in terms[1:]:
            value = jnp.logical_and(value, term)
        return pl.when(value)

    def z_dev(way):
        return {"left": z + way * sign}

    barrier = pltpu.get_barrier_semaphore()

    def greet(dev):
        pl.semaphore_signal(barrier, inc=1, device_id=dev, device_id_type=MESH)

    greet(sib_dev)
    greet(y_dev)
    greet(z_dev(-1))
    when(inner)(lambda: greet(z_dev(1)))
    pl.semaphore_wait(barrier, 3 + inner.astype(jnp.int32))

    def remote(src, dst, send, recv, dev):
        return pltpu.make_async_remote_copy(src_ref=src, dst_ref=dst, send_sem=send, recv_sem=recv, device_id=dev, device_id_type=MESH)

    def arrived(slot, sem):
        pltpu.make_async_copy(slot, slot, sem).wait()

    def block(at, first=0, size=rows):
        return pl.ds(pl.multiple_of(fold(4, at) * rows + first, size), size)

    def cols(q):
        return pl.ds(pl.multiple_of(q * TILE, TILE), TILE)

    def right_slot(at, q):
        return right_full.at[block(at), cols(q)]

    def in_copy(way, q):
        return remote(right_ref.at[:, cols(q)], right_slot(2, q), send.at[(way + 1) // 2], in_recv.at[0, q], z_dev(way))

    def fwd_copy(q):
        slot = right_slot(1, q)
        return remote(slot, slot, send.at[2], in_recv.at[1, q], z_dev(1))

    def cut(q):
        return ((1, 0), (1, 1), (2, 2), (4, 4))[q]

    def cut_slot(at, q, h, n):
        return right_full.at[block(at, h * (rows // n), rows // n), cols(q)]

    def mid_copy(q, h=0, n=1):
        slot = cut_slot(3, q, h, n)
        return remote(slot, slot, send.at[3], in_recv.at[1, q], z_dev(-1))

    def end_start(q):
        n, at = cut(q)
        for h in range(n):
            source = right_ref.at[pl.ds(h * (rows // n), rows // n), cols(q)]
            remote(source, cut_slot(3, q, h, n), send.at[3], end_recv.at[at + h], z_dev(-1)).start()

    def own_half():
        return pl.ds(pl.multiple_of(k * half, half), half)

    def far_copy(p):
        at = pl.ds(pl.multiple_of(p * piece, piece), piece)
        return remote(left_full.at[block(0, p * piece, piece), own_half()], left_far.at[at, own_half()], send.at[2], far_recv.at[p], z_dev(-1))

    def far_slot(p, core):
        return left_far.at[pl.ds(pl.multiple_of(p * piece, piece), piece), pl.ds(pl.multiple_of(core * half, half), half)]

    def share_copy(p):
        return remote(far_slot(p, k), far_slot(p, k), send.at[4], a_recv.at[0], sib_dev)

    def own_copy(p):
        at = pl.ds(pl.multiple_of(p * piece, piece), piece)
        slot = left_full.at[pl.ds(pl.multiple_of(r * rows + p * piece, piece), piece), :]
        return remote(left_ref.at[at, :], slot, send.at[5], own_recv.at[p], sib_dev)

    def own_arrived(p):
        other = r + 1 - 2 * k
        arrived(left_full.at[pl.ds(pl.multiple_of(other * rows + p * piece, piece), piece), :], own_recv.at[p])

    def y_slot(side, pos, p, core, count=1):
        at = 3 * side if pos == 0 else 1 + side
        return left_full.at[block(at, p * piece, count * piece), pl.ds(pl.multiple_of(core * half, half), half)]

    def y_copy(pos, p, own=False):
        slot = y_slot(yc, pos, p, k)
        source = left_ref.at[pl.ds(pl.multiple_of(p * piece, piece), piece), own_half()] if own else slot
        return remote(source, slot, send.at[6], y_recv.at[pos, p], y_dev)

    def s_copy(pos, p, group):
        slot = y_slot(1 - yc, pos, p, k)
        return remote(slot, slot, send.at[7], s_recv.at[group], sib_dev)

    def part_copy(q):
        return remote(part.at[q], part.at[q], send.at[8], far_recv.at[q], z_dev(1))

    def each(body, first=0, last=steps):
        def step(at, carry):
            body(at)
            return carry

        lax.fori_loop(first, last, step, 0)

    @when(inner)
    def _():
        @each
        def _(q):
            in_copy(-1, q).start()
            in_copy(1, q).start()

    @when(end)
    def _():
        end_start(0)
        end_start(1)

    first = kc == yc
    when(first)(lambda: each(lambda p: y_copy(0, p, True).start()))
    own_left = pltpu.make_async_copy(left_ref, left_full.at[pl.ds(pl.multiple_of(r * rows, rows), rows), :], own_sem.at[0])
    own = pltpu.make_async_copy(right_ref, right_full.at[block(zc), :], own_sem.at[1])
    weights = pltpu.make_async_copy(w_hbm, w_in, own_sem.at[2])
    counts_copy = pltpu.make_async_copy(counts_ref, counts_in, own_sem.at[3])
    each(lambda p: own_copy(p).start())
    for copy in (own_left, own, weights, counts_copy):
        copy.start()

    @each
    def _(p):
        own_arrived(p)
        when(jnp.logical_not(first))(lambda: y_copy(0, p).start())
        when(end, yc == 0, kc == 1)(lambda: far_copy(p).start())
        when(end, yc == 0, kc == 1, p == steps - 2)(lambda: end_start(2))

    own_left.wait()

    @when(end, yc == 0, kc == 0)
    def _():
        each(lambda p: far_copy(p).start(), 0, steps - 1)
        end_start(2)
        far_copy(steps - 1).start()

    each(lambda p: y_copy(1, p).start())
    when(end, yc == 0)(lambda: end_start(3))

    row = lax.broadcasted_iota(jnp.int32, (TILE, TILE), 0)
    column = lax.broadcasted_iota(jnp.int32, (TILE, TILE), 1)
    order[...] = jnp.where(column == (row % heads) * CH + row // heads, 1.0, 0.0).astype(order.dtype)
    weights.wait()
    w_wide[...] = w_in[...].astype(jnp.float32)
    for e in range(CH):
        some = w_wide[pl.ds(e, CH, stride=CH), :].astype(w_ref.dtype)
        for i in range(2):
            w_ref[pl.ds((2 * e + i) * CH, CH), i * pair:(i + 1) * pair] = some
            w_ref[pl.ds((2 * e + i) * CH, CH), (1 - i) * pair:(2 - i) * pair] = jnp.zeros_like(some)
    counts_copy.wait()
    counted = counts_in[...].astype(jnp.float32)
    for i in range(counted.shape[1]):
        cover[i // 4, i % 4] = jnp.broadcast_to(counted[:, i:i + 1], (counted.shape[0], cover.shape[3]))

    def turn(at, q):
        value = lax.dot_general(order[...], right_full[block(at), cols(q)], (((1,), (1,)), ((), ())), preferred_element_type=jnp.float32)
        right_t[cols(q), block(at)] = value.astype(right_t.dtype)

    def product(into, lines, source, left, left_rows, size, wide, add):
        for n in range(width_l // wide):
            value = jnp.dot(right_t[lines, source], left[left_rows, pl.ds(n * wide, wide)], preferred_element_type=jnp.float32)
            for one in range(wide // 128):
                some = value[:, one * 128:(one + 1) * 128]
                slab = n * (wide // 128) + one
                into[slab, size, :] = into[slab, size, :] + some if add else some

    def product_all(at, add, first=0, depth=rows):
        every = pl.ds(0, width_r)
        product(acc, every, block(at, first, depth), left_full, block(at, first, depth), every, 256, add)

    def product_one(at, q):
        product(acc, cols(q), block(at), left_full, block(at), cols(q), 512, True)

    def project(source, first_row):
        low = lax.broadcasted_iota(jnp.int32, (lines, 128), 1) < 64
        for two in range(CH // 2):
            a, b = (
                source[:, pl.ds(pl.multiple_of(first_row + e * heads, heads), heads), :].reshape(lines, 128).astype(flat.dtype)
                for e in (2 * two, 2 * two + 1)
            )
            at = pl.ds(two * 128, 128)
            flat[pl.ds(0, lines), at] = jnp.where(low, a, pltpu.roll(b, 64, 1))
            flat[pl.ds(lines, lines), at] = jnp.where(low, pltpu.roll(a, 64, 1), b)
        return jnp.dot(flat[...], w_ref[...], preferred_element_type=jnp.float32)

    def spot(i):
        return slice(i // 2 * lines, (i // 2 + 1) * lines), slice(i % 2 * pair, (i % 2 + 1) * pair)

    def emit(q, i, value):
        at = pl.ds(pl.multiple_of(q * heads, heads), heads)
        out_ref[pl.ds(i, quads, stride=4), at, :] = value / cover[:, i, at, :]

    def settle(q):
        for i in range(4):
            value = out_v[q, :, i]
            emit(q, i, value + part[(q, *spot(i))].astype(jnp.float32).reshape(value.shape))

    own.wait()
    each(lambda q: turn(zc, q))

    def pass_on(q, h):
        n, at = cut(q)
        arrived(cut_slot(3, q, h, n), end_recv.at[at + h])
        mid_copy(q, h, n).start()

    def end_arrived(q):
        arrived(right_slot(3, q), end_recv.at[q])
        mid_copy(q).start()
        turn(3, q)

    def share(p):
        arrived(far_slot(p, k), far_recv.at[p])
        share_copy(p).start()

    @each
    def _(p):
        arrived(y_slot(1 - yc, 0, p, k), y_recv.at[0, p])
        s_copy(0, p, 0).start()
        when(end, yc == 1)(lambda: far_copy(p).start())
        when(end, yc == 1, p == steps - 2)(lambda: end_start(2))
        arrived(right_slot(zc - 1, p), in_recv.at[0, p])
        when(inner)(lambda: fwd_copy(p).start())
        turn(zc - 1, p)
        when(inner, p >= 1, p <= early)(lambda: end_arrived(p - 1))

    when(end, yc == 1)(lambda: end_start(3))
    arrived(y_slot(1 - yc, 0, 0, 1 - k, steps), s_recv.at[0])
    late = 2 - yc
    groups = ((0, early), (early, early + 1), (early + 1, steps))

    def y_arrived(p):
        group = next(at for at, (_, last) in enumerate(groups) if p < last)
        arrived(y_slot(1 - yc, 1, p, k), y_recv.at[1, p])
        s_copy(1, p, 1 + group).start()

    def late_part(group):
        low, high = groups[group]
        arrived(y_slot(1 - yc, 1, low, 1 - k, high - low), s_recv.at[1 + group])
        product_all(late, True, low * piece, (high - low) * piece)

    def far_turn(q):
        arrived(right_slot(0, q), in_recv.at[1, q])
        turn(0, q)

    def far_product(q):
        product(acc_far, cols(q), block(0), left_far, pl.ds(0, rows), pl.ds(0, TILE), 512, False)

    def far_send_on(q):
        part[q] = project(acc_far, 0).astype(part.dtype)
        part_copy(q).start()

    def finish(q):
        value = project(acc, q * TILE)
        for i in range(4):
            out_v[q, :, i] = value[spot(i)].reshape(quads, heads, pair)

    def sent(sem, count=1):
        slot = left_full.at[pl.ds(0, count * rows), pl.ds(0, half)]
        arrived(slot, send.at[sem])

    @when(inner)
    def _():
        each(share, 0, early)
        product_all(1 + yc, False)
        for q in range(early):
            product_one(3, q)
        y_arrived(0)
        share(2)
        far_turn(0)
        product_one(0, 0)
        pass_on(2, 0)
        pass_on(2, 1)
        turn(3, 2)
        product_one(3, 2)
        y_arrived(1)
        far_turn(1)
        product_one(0, 1)
        late_part(0)
        share(3)
        pass_on(3, 0)
        arrived(left_far.at[:, pl.ds(pl.multiple_of((1 - k) * half, half), half)], a_recv.at[0])
        far_product(0)
        y_arrived(2)
        pass_on(3, 1)
        far_send_on(0)
        far_product(1)
        pass_on(3, 2)
        far_send_on(1)
        pass_on(3, 3)
        far_turn(2)
        far_product(2)
        far_send_on(2)
        late_part(1)
        y_arrived(3)
        turn(3, 3)
        product_one(3, 3)
        product_one(0, 2)
        far_turn(3)
        far_product(3)
        far_send_on(3)
        late_part(2)
        product_one(0, 3)

        @each
        def _(q):
            value = project(acc, q * TILE)
            for i in range(4):
                emit(q, i, value[spot(i)].reshape(quads, heads, pair))

        sent(0)
        sent(1)
        sent(2)
        sent(3)
        sent(4)
        sent(5, 2)
        sent(6, 2)
        sent(7, 2)
        arrived(part, send.at[8])

    @when(end)
    def _():
        product_all(3, False)
        for q in range(steps):
            y_arrived(q)
            arrived(right_slot(1, q), in_recv.at[1, q])
            turn(1, q)
            product_one(1 + yc, q)
        for group in range(len(groups)):
            late_part(group)
        each(finish)
        sent(2)
        sent(3)
        sent(5, 2)
        sent(6, 2)
        sent(7, 2)

        @each
        def _(q):
            arrived(part.at[q], far_recv.at[q])
            settle(q)


def folded_call(left_act, right_act, counts, w_out):
    rows, width_l = left_act.shape
    width_r = right_act.shape[1]
    left_dev, right_dev = counts.shape
    pair = w_out.shape[1]
    steps = width_r // TILE
    heads = TILE // CH
    full = 4 * rows
    dma = pltpu.SemaphoreType.DMA
    return pl.pallas_call(
        folded,
        out_shape=jax.ShapeDtypeStruct((left_dev, right_dev, pair), jnp.float32),
        in_specs=[pl.BlockSpec(memory_space=pl.ANY)] * 4,
        out_specs=pl.BlockSpec(memory_space=pltpu.VMEM),
        scratch_shapes=[
            pltpu.VMEM(w_out.shape, w_out.dtype),
            pltpu.VMEM(w_out.shape, jnp.float32),
            pltpu.VMEM((2 * w_out.shape[0], 2 * pair), w_out.dtype),
            pltpu.VMEM((right_dev, left_dev), counts.dtype),
            pltpu.VMEM((left_dev // 4, 4, right_dev, pair), jnp.float32),
            pltpu.VMEM((TILE, TILE), jnp.bfloat16),
            pltpu.VMEM((full, width_l), jnp.bfloat16),
            pltpu.VMEM((rows, width_l), jnp.bfloat16),
            pltpu.VMEM((full, width_r), jnp.bfloat16),
            pltpu.VMEM((width_r, full), jnp.bfloat16),
            pltpu.VMEM((width_l // 128, width_r, 128), jnp.float32),
            pltpu.VMEM((width_l // 128, TILE, 128), jnp.float32),
            pltpu.VMEM((left_dev * heads // 2, 2 * CH * CH), jnp.bfloat16),
            pltpu.VMEM((steps, left_dev * heads // 2, 2 * pair), jnp.bfloat16),
            pltpu.VMEM((steps, left_dev // 4, 4, heads, pair), jnp.float32),
            dma((9,)), dma((2, steps)), dma((steps,)), dma((8,)), dma((steps,)), dma((2, steps)), dma((4,)), dma((1,)), dma((4,)),
        ],
        compiler_params=pltpu.CompilerParams(collective_id=0, has_side_effects=True, vmem_limit_bytes=38000 * 1024),
        name="pair_mean",
    )(*(pltpu.with_memory_space_constraint(x, pltpu.HBM) for x in (left_act, right_act, counts.T, w_out)))


def solution(mesh):
    n_z, n_r = mesh.shape["left"], mesh.shape["right"]
    n_y = n_r // CORES

    def shards(left_act, right_act, counts, w_out):
        width_l, width_r = left_act.shape[1], right_act.shape[1]
        if (n_z, n_y) == (4, 2) and width_r == 4 * TILE and width_l == CORES * width_r:
            return folded_call(left_act, right_act, counts, w_out)
        rows_l, width_l = left_act.shape
        rows_r, width_r = right_act.shape
        seqs = rows_r * n_z
        left_dev, right_dev = counts.shape
        pair = w_out.shape[1]
        q_z = width_r // 256
        q_y = rows_l // max(128, rows_l // 4)
        projected = pl.pallas_call(
            functools.partial(kernel, (n_z, n_r, q_z, q_y)),
            out_shape=jax.ShapeDtypeStruct((left_dev, right_dev, pair), jnp.float32),
            in_specs=[pl.BlockSpec(memory_space=pl.ANY)] * 4,
            out_specs=pl.BlockSpec(memory_space=pl.ANY),
            scratch_shapes=[
                pltpu.VMEM(w_out.shape, w_out.dtype),
                pltpu.VMEM(counts.shape, counts.dtype),
                pltpu.VMEM((right_dev, left_dev, pair), jnp.float32),
                pltpu.VMEM((q_z, left_dev, right_dev // q_z, pair), jnp.float32),
                pltpu.VMEM((seqs, width_l), jnp.bfloat16),
                pltpu.VMEM((seqs, width_r), jnp.bfloat16),
                pltpu.VMEM((width_l, seqs), jnp.bfloat16),
                pltpu.VMEM((width_r // 128, width_l, 128), jnp.float32),
                pltpu.VMEM((width_r // q_z // CH * left_dev, CH * CH), jnp.bfloat16),
                pltpu.SemaphoreType.DMA((2, (n_z - 1) * q_z)),
                pltpu.SemaphoreType.DMA((2, (n_z - 1) * q_z)),
                pltpu.SemaphoreType.DMA((2, (n_y - 1) * q_y)),
                pltpu.SemaphoreType.DMA((2, (n_y - 1) * q_y)),
                pltpu.SemaphoreType.DMA(((2 * n_y - 1) * q_y,)),
                pltpu.SemaphoreType.DMA(((2 * n_y - 1) * q_y,)),
                pltpu.SemaphoreType.DMA((4,)),
                pltpu.SemaphoreType.DMA((q_z,)),
            ],
            compiler_params=pltpu.CompilerParams(
                collective_id=0, has_side_effects=True, vmem_limit_bytes=56 * 1024 * 1024
            ),
            name="pair_mean",
        )(left_act, right_act, counts, w_out)
        return projected

    in_specs = (
        P(("groups", "right"), "left"),
        P(("groups", "left"), "right"),
        P(("groups", "left"), "right"),
        P(),
    )
    out_specs = P(("groups", "left"), "right", None)
    return jax.shard_map(shards, mesh=mesh, in_specs=in_specs, out_specs=out_specs, check_vma=False)
```

```python
import functools

import jax
import jax.numpy as jnp
from jax import lax
from jax.experimental import pallas as pl
from jax.experimental.pallas import tpu as pltpu
from jax.sharding import PartitionSpec as P

CH = 32
CORES = 2
TILE = 256
MESH = pl.DeviceIdType.MESH


def lane_quads(tiles):
    lane = lax.broadcasted_iota(jnp.int32, tiles[0].shape, 1)
    low = lane < 64
    even = (lane % 64) < 32
    stage = [None] * 4
    for c in range(2):
        a, b = tiles[c], tiles[c + 2]
        stage[c] = jnp.where(low, a, pltpu.roll(b, 64, 1))
        stage[c + 2] = jnp.where(low, pltpu.roll(a, 64, 1), b)
    outs = [None] * 4
    for half in range(2):
        a, b = stage[2 * half], stage[2 * half + 1]
        outs[2 * half] = jnp.where(even, a, pltpu.roll(b, 32, 1))
        outs[2 * half + 1] = jnp.where(even, pltpu.roll(a, 96, 1), b)
    return outs


def kernel(sizes, left_ref, right_ref, counts_ref, w_hbm, out_ref, w_ref, counts_in, cover, out_v, left_full, right_full, left_t, acc, flat,
           z_send, z_recv, y_send, y_recv, s_send, s_recv, own_sem, out_sem):
    n_z, n_r, q_z, q_y = sizes
    n_y = n_r // CORES
    rows_l, width_l = left_ref.shape
    rows_r, width_r = right_ref.shape
    piece_r = width_r // q_z
    piece_l = rows_l // q_y
    left_dev = width_l // CH
    right_dev = width_r // CH
    seqs = left_t.shape[1]
    z = lax.axis_index("left")
    r = lax.axis_index("right")
    y = r // CORES
    k = r % CORES

    def z_dev(pos):
        return {"left": pos}

    def y_dev(pos):
        return {"right": pos * CORES + k}

    sib_dev = {"right": y * CORES + (1 - k)}

    barrier = pltpu.get_barrier_semaphore()

    def greet(dev):
        pl.semaphore_signal(barrier, inc=1, device_id=dev, device_id_type=MESH)

    greet(sib_dev)
    for pos, n, dev in ((z, n_z, z_dev), (y, n_y, y_dev)):
        pl.when(pos + 1 < n)(functools.partial(greet, dev(pos + 1)))
        pl.when(pos >= 1)(functools.partial(greet, dev(pos - 1)))
    total = 1 + (z + 1 < n_z).astype(jnp.int32) + (z >= 1).astype(jnp.int32)
    total = total + (y + 1 < n_y).astype(jnp.int32) + (y >= 1).astype(jnp.int32)
    pl.semaphore_wait(barrier, total)

    def z_slot(chunk, q):
        return right_full.at[pl.ds(pl.multiple_of(chunk * rows_r, rows_r), rows_r), pl.ds(q * piece_r, piece_r)]

    def z_copy(side, step, q):
        sign = 1 - 2 * side
        chunk = z - sign * step
        src = right_ref.at[:, pl.ds(q * piece_r, piece_r)] if step == 0 else z_slot(chunk, q)
        at = step * q_z + q
        return pltpu.make_async_remote_copy(
            src_ref=src, dst_ref=z_slot(chunk, q), send_sem=z_send.at[side, at], recv_sem=z_recv.at[side, at],
            device_id=z_dev(z + sign), device_id_type=MESH)

    def z_sends(side, step):
        near = z + 1 < n_z if side == 0 else z >= 1
        far = z - step >= 0 if side == 0 else z + step < n_z
        return jnp.logical_and(near, far)

    def z_arrives(side, step):
        return z - step - 1 >= 0 if side == 0 else z + step + 1 < n_z

    def z_wait(side, step, q):
        sign = 1 - 2 * side
        slot = z_slot(z - sign * (step + 1), q)
        pltpu.make_async_copy(slot, slot, z_recv.at[side, step * q_z + q]).wait()

    def l_slot(chunk, q):
        return left_full.at[pl.ds(pl.multiple_of(chunk * rows_l + q * piece_l, piece_l), piece_l), :]

    def l_own(q):
        return left_ref.at[pl.ds(q * piece_l, piece_l), :]

    def y_copy(side, step, q):
        sign = 1 - 2 * side
        chunk = (y - sign * step) * CORES + k
        at = step * q_y + q
        return pltpu.make_async_remote_copy(
            src_ref=l_own(q) if step == 0 else l_slot(chunk, q), dst_ref=l_slot(chunk, q),
            send_sem=y_send.at[side, at], recv_sem=y_recv.at[side, at],
            device_id=y_dev(y + sign), device_id_type=MESH)

    def y_sends(side, step):
        near = y + 1 < n_y if side == 0 else y >= 1
        far = y - step >= 0 if side == 0 else y + step < n_y
        return jnp.logical_and(near, far)

    def y_arrives(side, step):
        return y - step - 1 >= 0 if side == 0 else y + step + 1 < n_y

    def y_wait(side, step, q):
        sign = 1 - 2 * side
        slot = l_slot((y - sign * (step + 1)) * CORES + k, q)
        pltpu.make_async_copy(slot, slot, y_recv.at[side, step * q_y + q]).wait()

    def s_at(side, step, q):
        if step < 0:
            return q
        return (1 + side * (n_y - 1) + step) * q_y + q

    def s_copy(side, step, q):
        sign = 1 - 2 * side
        chunk = (y - sign * (step + 1)) * CORES + k if step >= 0 else r
        at = s_at(side, step, q)
        return pltpu.make_async_remote_copy(
            src_ref=l_own(q) if step < 0 else l_slot(chunk, q), dst_ref=l_slot(chunk, q),
            send_sem=s_send.at[at], recv_sem=s_recv.at[at],
            device_id=sib_dev, device_id_type=MESH)

    def s_wait(side, step, q):
        sign = 1 - 2 * side
        y_from = y - sign * (step + 1) if step >= 0 else y
        slot = l_slot(y_from * CORES + (1 - k), q)
        pltpu.make_async_copy(slot, slot, s_recv.at[s_at(side, step, q)]).wait()

    tile = 256

    def turn(src, first_row, chunk, q):
        col = pl.multiple_of(chunk * rows_l + q * piece_l, piece_l)

        def body(m, carry):
            at = pl.multiple_of(m * tile, tile)
            left_t[pl.ds(at, tile), pl.ds(col, piece_l)] = src[pl.ds(first_row, piece_l), pl.ds(at, tile)].T
            return carry

        lax.fori_loop(0, width_l // tile, body, 0)

    def turn_full(chunk, q):
        turn(left_full, pl.multiple_of(chunk * rows_l + q * piece_l, piece_l), chunk, q)

    for q in range(max(q_z, q_y)):
        for side in range(2):
            if q < q_z:
                pl.when(z_sends(side, 0))(lambda side=side, q=q: z_copy(side, 0, q).start())
            if q < q_y:
                pl.when(y_sends(side, 0))(lambda side=side, q=q: y_copy(side, 0, q).start())
    own_left = pltpu.make_async_copy(left_ref, left_full.at[pl.ds(pl.multiple_of(r * rows_l, rows_l), rows_l), :], own_sem.at[0])
    own = pltpu.make_async_copy(right_ref, right_full.at[pl.ds(pl.multiple_of(z * rows_r, rows_r), rows_r), :], own_sem.at[1])
    weights = pltpu.make_async_copy(w_hbm, w_ref, own_sem.at[2])
    counts_copy = pltpu.make_async_copy(counts_ref, counts_in, own_sem.at[3])
    for copy in (own_left, own, weights, counts_copy):
        copy.start()
    for q in range(q_y):
        s_copy(0, -1, q).start()
    own_left.wait()
    for q in range(q_y):
        turn_full(r, q)
    counts_copy.wait()
    counted = counts_in[...].astype(jnp.float32)
    for j in range(right_dev):
        cover[j] = jnp.broadcast_to(counted[:, j:j + 1], (left_dev, cover.shape[2]))
    for q in range(q_y):
        s_wait(0, -1, q)
        turn_full(y * CORES + (1 - k), q)

    def z_tick(step, q):
        for side in range(2):
            @pl.when(z_arrives(side, step))
            def _():
                z_wait(side, step, q)
                if step + 1 < n_z - 1:
                    pl.when(z_sends(side, step + 1))(lambda: z_copy(side, step + 1, q).start())

    def y_tick(step, q):
        for side in range(2):
            @pl.when(y_arrives(side, step))
            def _():
                y_wait(side, step, q)
                s_copy(side, step, q).start()
                if step + 1 < n_y - 1:
                    pl.when(y_sends(side, step + 1))(lambda: y_copy(side, step + 1, q).start())

        for side in range(2):
            @pl.when(y_arrives(side, step))
            def _():
                sign = 1 - 2 * side
                y_from = y - sign * (step + 1)
                turn_full(y_from * CORES + k, q)
                s_wait(side, step, q)
                turn_full(y_from * CORES + (1 - k), q)

    y_ticks = [(step, q) for step in range(n_y - 1) for q in range(q_y)]
    for t in range((n_z - 2) * q_z):
        z_tick(t // q_z, t % q_z)
        if t % 2 == 1 and y_ticks:
            y_tick(*y_ticks.pop(0))
    for tick in y_ticks:
        y_tick(*tick)
    own.wait()
    weights.wait()

    block = 1024
    at_end = jnp.logical_or(z == 0, z == n_z - 1)
    base = jnp.where(z == 0, 0, rows_r)
    base = pl.multiple_of(base, rows_r)

    def product(q, first, depth, add):
        cols = pl.ds(q * piece_r, piece_r)

        def body(m, carry):
            rows = pl.ds(pl.multiple_of(m * block, block), block)
            value = jnp.dot(left_t[rows, pl.ds(first, depth)], right_full[pl.ds(first, depth), cols],
                            preferred_element_type=jnp.float32)
            for part in range(piece_r // 128):
                some = value[:, part * 128:(part + 1) * 128]
                slab = q * (piece_r // 128) + part
                acc[slab, rows, :] = acc[slab, rows, :] + some if add else some
            return carry

        lax.fori_loop(0, width_l // block, body, 0)

    def first_part(q):
        @pl.when(at_end)
        def _():
            product(q, base, seqs - rows_r, False)

        @pl.when(jnp.logical_not(at_end))
        def _():
            product(q, 0, seqs, False)

    for q in range(q_z):
        first_part(q)

    def finish(q):
        heads = piece_r // CH
        for quad in range(heads // 4):
            slab = acc.at[q * (piece_r // 128) + quad]
            for cq in range(CH // 4):
                tiles = [slab[pl.ds(cq * 4 + c, left_dev, stride=CH), :].astype(jnp.bfloat16) for c in range(4)]
                for j, value in enumerate(lane_quads(tiles)):
                    flat[pl.ds((quad * 4 + j) * left_dev, left_dev), pl.ds(cq * 128, 128)] = value
        projected = jnp.dot(flat[...], w_ref[...], preferred_element_type=jnp.float32)
        for j in range(heads):
            value = projected[j * left_dev:(j + 1) * left_dev, :] / cover[q * heads + j]
            out_v.at[q].reshape(left_dev * heads, value.shape[1])[pl.ds(j, left_dev, stride=heads), :] = value
        out_copy(q).start()

    def out_copy(q):
        return pltpu.make_async_copy(out_v.at[q], out_ref.at[:, pl.ds(q * heads_q, heads_q), :], out_sem.at[q])

    heads_q = piece_r // CH
    last = n_z - 2
    for q in range(q_z):
        z_tick(last, q)

        @pl.when(at_end)
        def _():
            far = jnp.where(z == 0, (n_z - 1) * rows_r, 0)
            product(q, pl.multiple_of(far, rows_r), rows_r, True)

        finish(q)

    for side in range(2):
        for step in range(n_z - 1):
            for q in range(q_z):
                pl.when(z_sends(side, step))(lambda side=side, step=step, q=q: z_copy(side, step, q).wait_send())
        for step in range(n_y - 1):
            for q in range(q_y):
                pl.when(y_sends(side, step))(lambda side=side, step=step, q=q: y_copy(side, step, q).wait_send())
                pl.when(y_arrives(side, step))(lambda side=side, step=step, q=q: s_copy(side, step, q).wait_send())
    for q in range(q_y):
        s_copy(0, -1, q).wait_send()
    for q in range(q_z):
        out_copy(q).wait()


def folded(left_ref, right_ref, counts_ref, w_hbm, out_ref, w_in, w_wide, w_ref, counts_in, cover, order, left_full, left_far, right_full, right_t,
           acc, acc_far, flat, part, out_v, send, in_recv, far_recv, end_recv, own_recv, y_recv, s_recv, a_recv, own_sem):
    rows, width_l = left_ref.shape
    width_r = right_ref.shape[1]
    steps = width_r // TILE
    piece = rows // steps
    half = width_l // CORES
    quads = width_l // 128
    heads = TILE // CH
    pair = w_hbm.shape[1]
    lines = quads * heads
    early = steps // 2
    z = lax.axis_index("left")
    r = lax.axis_index("right")
    y, k = r // CORES, r % CORES
    up = z // 2
    sign = 2 * up - 1

    def fold(n, at):
        return up * at + (1 - up) * (n - 1 - at)

    zc, yc, kc = fold(4, z), fold(2, y), fold(2, k)
    inner, end = zc == 2, zc == 3
    sib_dev = {"right": r + 1 - 2 * k}
    y_dev = {"right": r + (1 - 2 * y) * CORES}

    def when(*terms):
        value = terms[0]
        for term in terms[1:]:
            value = jnp.logical_and(value, term)
        return pl.when(value)

    def z_dev(way):
        return {"left": z + way * sign}

    barrier = pltpu.get_barrier_semaphore()

    def greet(dev):
        pl.semaphore_signal(barrier, inc=1, device_id=dev, device_id_type=MESH)

    greet(sib_dev)
    greet(y_dev)
    greet(z_dev(-1))
    when(inner)(lambda: greet(z_dev(1)))
    pl.semaphore_wait(barrier, 3 + inner.astype(jnp.int32))

    def remote(src, dst, send, recv, dev):
        return pltpu.make_async_remote_copy(src_ref=src, dst_ref=dst, send_sem=send, recv_sem=recv, device_id=dev, device_id_type=MESH)

    def arrived(slot, sem):
        pltpu.make_async_copy(slot, slot, sem).wait()

    def block(at, first=0, size=rows):
        return pl.ds(pl.multiple_of(fold(4, at) * rows + first, size), size)

    def cols(q):
        return pl.ds(pl.multiple_of(q * TILE, TILE), TILE)

    def right_slot(at, q):
        return right_full.at[block(at), cols(q)]

    def in_copy(way, q):
        return remote(right_ref.at[:, cols(q)], right_slot(2, q), send.at[(way + 1) // 2], in_recv.at[0, q], z_dev(way))

    def fwd_copy(q):
        slot = right_slot(1, q)
        return remote(slot, slot, send.at[2], in_recv.at[1, q], z_dev(1))

    def cut(q):
        return ((1, 0), (1, 1), (2, 2), (4, 4))[q]

    def cut_slot(at, q, h, n):
        return right_full.at[block(at, h * (rows // n), rows // n), cols(q)]

    def mid_copy(q, h=0, n=1):
        slot = cut_slot(3, q, h, n)
        return remote(slot, slot, send.at[3], in_recv.at[1, q], z_dev(-1))

    def end_start(q):
        n, at = cut(q)
        for h in range(n):
            source = right_ref.at[pl.ds(h * (rows // n), rows // n), cols(q)]
            remote(source, cut_slot(3, q, h, n), send.at[3], end_recv.at[at + h], z_dev(-1)).start()

    def own_half():
        return pl.ds(pl.multiple_of(k * half, half), half)

    def far_copy(p):
        at = pl.ds(pl.multiple_of(p * piece, piece), piece)
        return remote(left_full.at[block(0, p * piece, piece), own_half()], left_far.at[at, own_half()], send.at[2], far_recv.at[p], z_dev(-1))

    def far_slot(p, core):
        return left_far.at[pl.ds(pl.multiple_of(p * piece, piece), piece), pl.ds(pl.multiple_of(core * half, half), half)]

    def share_copy(p):
        return remote(far_slot(p, k), far_slot(p, k), send.at[4], a_recv.at[0], sib_dev)

    def own_copy(p):
        at = pl.ds(pl.multiple_of(p * piece, piece), piece)
        slot = left_full.at[pl.ds(pl.multiple_of(r * rows + p * piece, piece), piece), :]
        return remote(left_ref.at[at, :], slot, send.at[5], own_recv.at[p], sib_dev)

    def own_arrived(p):
        other = r + 1 - 2 * k
        arrived(left_full.at[pl.ds(pl.multiple_of(other * rows + p * piece, piece), piece), :], own_recv.at[p])

    def y_slot(side, pos, p, core, count=1):
        at = 3 * side if pos == 0 else 1 + side
        return left_full.at[block(at, p * piece, count * piece), pl.ds(pl.multiple_of(core * half, half), half)]

    def y_copy(pos, p, own=False):
        slot = y_slot(yc, pos, p, k)
        source = left_ref.at[pl.ds(pl.multiple_of(p * piece, piece), piece), own_half()] if own else slot
        return remote(source, slot, send.at[6], y_recv.at[pos, p], y_dev)

    def s_copy(pos, p, group):
        slot = y_slot(1 - yc, pos, p, k)
        return remote(slot, slot, send.at[7], s_recv.at[group], sib_dev)

    def part_copy(q):
        return remote(part.at[q], part.at[q], send.at[8], far_recv.at[q], z_dev(1))

    def each(body, first=0, last=steps):
        def step(at, carry):
            body(at)
            return carry

        lax.fori_loop(first, last, step, 0)

    @when(inner)
    def _():
        @each
        def _(q):
            in_copy(1, q).start()
            in_copy(-1, q).start()

    @when(end)
    def _():
        end_start(0)
        end_start(1)

    first = kc == yc
    when(first)(lambda: each(lambda p: y_copy(0, p, True).start()))
    own_left = pltpu.make_async_copy(left_ref, left_full.at[pl.ds(pl.multiple_of(r * rows, rows), rows), :], own_sem.at[0])
    own = pltpu.make_async_copy(right_ref, right_full.at[block(zc), :], own_sem.at[1])
    weights = pltpu.make_async_copy(w_hbm, w_in, own_sem.at[2])
    counts_copy = pltpu.make_async_copy(counts_ref, counts_in, own_sem.at[3])
    each(lambda p: own_copy(p).start())
    for copy in (own_left, own, weights, counts_copy):
        copy.start()

    @each
    def _(p):
        own_arrived(p)
        when(jnp.logical_not(first))(lambda: y_copy(0, p).start())
        when(end, yc == 0, kc == 1)(lambda: far_copy(p).start())
        when(end, yc == 0, kc == 1, p == steps - 2)(lambda: end_start(2))

    own_left.wait()

    @when(end, yc == 0, kc == 0)
    def _():
        each(lambda p: far_copy(p).start(), 0, steps - 1)
        end_start(2)
        far_copy(steps - 1).start()

    each(lambda p: y_copy(1, p).start())
    when(end, yc == 0)(lambda: end_start(3))

    row = lax.broadcasted_iota(jnp.int32, (TILE, TILE), 0)
    column = lax.broadcasted_iota(jnp.int32, (TILE, TILE), 1)
    order[...] = jnp.where(column == (row % heads) * CH + row // heads, 1.0, 0.0).astype(order.dtype)
    weights.wait()
    w_wide[...] = w_in[...].astype(jnp.float32)
    for e in range(CH):
        some = w_wide[pl.ds(e, CH, stride=CH), :].astype(w_ref.dtype)
        for i in range(2):
            w_ref[pl.ds((2 * e + i) * CH, CH), i * pair:(i + 1) * pair] = some
            w_ref[pl.ds((2 * e + i) * CH, CH), (1 - i) * pair:(2 - i) * pair] = jnp.zeros_like(some)
    counts_copy.wait()
    counted = counts_in[...].astype(jnp.float32)
    for i in range(counted.shape[1]):
        cover[i // 4, i % 4] = jnp.broadcast_to(counted[:, i:i + 1], (counted.shape[0], cover.shape[3]))

    def turn(at, q):
        value = lax.dot_general(order[...], right_full[block(at), cols(q)], (((1,), (1,)), ((), ())), preferred_element_type=jnp.float32)
        right_t[cols(q), block(at)] = value.astype(right_t.dtype)

    def product(into, lines, source, left, left_rows, size, wide, add):
        for n in range(width_l // wide):
            value = jnp.dot(right_t[lines, source], left[left_rows, pl.ds(n * wide, wide)], preferred_element_type=jnp.float32)
            for one in range(wide // 128):
                some = value[:, one * 128:(one + 1) * 128]
                slab = n * (wide // 128) + one
                into[slab, size, :] = into[slab, size, :] + some if add else some

    def product_all(at, add, first=0, depth=rows):
        every = pl.ds(0, width_r)
        product(acc, every, block(at, first, depth), left_full, block(at, first, depth), every, 256, add)

    def product_one(at, q):
        product(acc, cols(q), block(at), left_full, block(at), cols(q), 512, True)

    def project(source, first_row):
        low = lax.broadcasted_iota(jnp.int32, (lines, 128), 1) < 64
        for two in range(CH // 2):
            a, b = (
                source[:, pl.ds(pl.multiple_of(first_row + e * heads, heads), heads), :].reshape(lines, 128).astype(flat.dtype)
                for e in (2 * two, 2 * two + 1)
            )
            at = pl.ds(two * 128, 128)
            flat[pl.ds(0, lines), at] = jnp.where(low, a, pltpu.roll(b, 64, 1))
            flat[pl.ds(lines, lines), at] = jnp.where(low, pltpu.roll(a, 64, 1), b)
        return jnp.dot(flat[...], w_ref[...], preferred_element_type=jnp.float32)

    def spot(i):
        return slice(i // 2 * lines, (i // 2 + 1) * lines), slice(i % 2 * pair, (i % 2 + 1) * pair)

    def emit(q, i, value):
        at = pl.ds(pl.multiple_of(q * heads, heads), heads)
        out_ref[pl.ds(i, quads, stride=4), at, :] = value / cover[:, i, at, :]

    def settle(q):
        for i in range(4):
            value = out_v[q, :, i]
            emit(q, i, value + part[(q, *spot(i))].astype(jnp.float32).reshape(value.shape))

    own.wait()
    each(lambda q: turn(zc, q))

    def pass_on(q, h):
        n, at = cut(q)
        arrived(cut_slot(3, q, h, n), end_recv.at[at + h])
        mid_copy(q, h, n).start()

    def end_arrived(q):
        arrived(right_slot(3, q), end_recv.at[q])
        mid_copy(q).start()
        turn(3, q)

    def share(p):
        arrived(far_slot(p, k), far_recv.at[p])
        share_copy(p).start()

    @each
    def _(p):
        arrived(y_slot(1 - yc, 0, p, k), y_recv.at[0, p])
        s_copy(0, p, 0).start()
        when(end, yc == 1)(lambda: far_copy(p).start())
        when(end, yc == 1, p == steps - 2)(lambda: end_start(2))
        arrived(right_slot(zc - 1, p), in_recv.at[0, p])
        when(inner)(lambda: fwd_copy(p).start())
        turn(zc - 1, p)
        when(inner, p >= 1, p <= early)(lambda: end_arrived(p - 1))

    when(end, yc == 1)(lambda: end_start(3))
    arrived(y_slot(1 - yc, 0, 0, 1 - k, steps), s_recv.at[0])
    late = 2 - yc
    groups = ((0, early), (early, early + 1), (early + 1, steps))

    def y_arrived(p):
        group = next(at for at, (_, last) in enumerate(groups) if p < last)
        arrived(y_slot(1 - yc, 1, p, k), y_recv.at[1, p])
        s_copy(1, p, 1 + group).start()

    def late_part(group):
        low, high = groups[group]
        arrived(y_slot(1 - yc, 1, low, 1 - k, high - low), s_recv.at[1 + group])
        product_all(late, True, low * piece, (high - low) * piece)

    def far_turn(q):
        arrived(right_slot(0, q), in_recv.at[1, q])
        turn(0, q)

    def far_product(q):
        product(acc_far, cols(q), block(0), left_far, pl.ds(0, rows), pl.ds(0, TILE), 512, False)

    def far_send_on(q):
        part[q] = project(acc_far, 0).astype(part.dtype)
        part_copy(q).start()

    def finish(q):
        value = project(acc, q * TILE)
        for i in range(4):
            out_v[q, :, i] = value[spot(i)].reshape(quads, heads, pair)

    def sent(sem, count=1):
        slot = left_full.at[pl.ds(0, count * rows), pl.ds(0, half)]
        arrived(slot, send.at[sem])

    @when(inner)
    def _():
        each(share, 0, early)
        product_all(1 + yc, False)
        for q in range(early):
            product_one(3, q)
        y_arrived(0)
        share(2)
        far_turn(0)
        product_one(0, 0)
        pass_on(2, 0)
        pass_on(2, 1)
        turn(3, 2)
        product_one(3, 2)
        y_arrived(1)
        far_turn(1)
        product_one(0, 1)
        late_part(0)
        share(3)
        pass_on(3, 0)
        arrived(left_far.at[:, pl.ds(pl.multiple_of((1 - k) * half, half), half)], a_recv.at[0])
        far_product(0)
        y_arrived(2)
        pass_on(3, 1)
        far_send_on(0)
        far_product(1)
        pass_on(3, 2)
        far_send_on(1)
        pass_on(3, 3)
        far_turn(2)
        far_product(2)
        far_send_on(2)
        late_part(1)
        y_arrived(3)
        turn(3, 3)
        product_one(3, 3)
        far_turn(3)
        far_product(3)
        far_send_on(3)
        product_one(0, 2)
        late_part(2)
        product_one(0, 3)

        @each
        def _(q):
            value = project(acc, q * TILE)
            for i in range(4):
                emit(q, i, value[spot(i)].reshape(quads, heads, pair))

        sent(0)
        sent(1)
        sent(2)
        sent(3)
        sent(4)
        sent(5, 2)
        sent(6, 2)
        sent(7, 2)
        arrived(part, send.at[8])

    @when(end)
    def _():
        product_all(3, False)
        for q in range(steps):
            y_arrived(q)
            arrived(right_slot(1, q), in_recv.at[1, q])
            turn(1, q)
            product_one(1 + yc, q)
        for group in range(len(groups)):
            late_part(group)
        each(finish)
        sent(2)
        sent(3)
        sent(5, 2)
        sent(6, 2)
        sent(7, 2)

        @each
        def _(q):
            arrived(part.at[q], far_recv.at[q])
            settle(q)


def folded_call(left_act, right_act, counts, w_out):
    rows, width_l = left_act.shape
    width_r = right_act.shape[1]
    left_dev, right_dev = counts.shape
    pair = w_out.shape[1]
    steps = width_r // TILE
    heads = TILE // CH
    full = 4 * rows
    dma = pltpu.SemaphoreType.DMA
    return pl.pallas_call(
        folded,
        out_shape=jax.ShapeDtypeStruct((left_dev, right_dev, pair), jnp.float32),
        in_specs=[pl.BlockSpec(memory_space=pl.ANY)] * 4,
        out_specs=pl.BlockSpec(memory_space=pltpu.VMEM),
        scratch_shapes=[
            pltpu.VMEM(w_out.shape, w_out.dtype),
            pltpu.VMEM(w_out.shape, jnp.float32),
            pltpu.VMEM((2 * w_out.shape[0], 2 * pair), w_out.dtype),
            pltpu.VMEM((right_dev, left_dev), counts.dtype),
            pltpu.VMEM((left_dev // 4, 4, right_dev, pair), jnp.float32),
            pltpu.VMEM((TILE, TILE), jnp.bfloat16),
            pltpu.VMEM((full, width_l), jnp.bfloat16),
            pltpu.VMEM((rows, width_l), jnp.bfloat16),
            pltpu.VMEM((full, width_r), jnp.bfloat16),
            pltpu.VMEM((width_r, full), jnp.bfloat16),
            pltpu.VMEM((width_l // 128, width_r, 128), jnp.float32),
            pltpu.VMEM((width_l // 128, TILE, 128), jnp.float32),
            pltpu.VMEM((left_dev * heads // 2, 2 * CH * CH), jnp.bfloat16),
            pltpu.VMEM((steps, left_dev * heads // 2, 2 * pair), jnp.bfloat16),
            pltpu.VMEM((steps, left_dev // 4, 4, heads, pair), jnp.float32),
            dma((9,)), dma((2, steps)), dma((steps,)), dma((8,)), dma((steps,)), dma((2, steps)), dma((4,)), dma((1,)), dma((4,)),
        ],
        compiler_params=pltpu.CompilerParams(collective_id=0, has_side_effects=True, vmem_limit_bytes=38000 * 1024),
        name="pair_mean",
    )(*(pltpu.with_memory_space_constraint(x, pltpu.HBM) for x in (left_act, right_act, counts.T, w_out)))


def solution(mesh):
    n_z, n_r = mesh.shape["left"], mesh.shape["right"]
    n_y = n_r // CORES

    def shards(left_act, right_act, counts, w_out):
        width_l, width_r = left_act.shape[1], right_act.shape[1]
        if (n_z, n_y) == (4, 2) and width_r == 4 * TILE and width_l == CORES * width_r:
            return folded_call(left_act, right_act, counts, w_out)
        rows_l, width_l = left_act.shape
        rows_r, width_r = right_act.shape
        seqs = rows_r * n_z
        left_dev, right_dev = counts.shape
        pair = w_out.shape[1]
        q_z = width_r // 256
        q_y = rows_l // max(128, rows_l // 4)
        projected = pl.pallas_call(
            functools.partial(kernel, (n_z, n_r, q_z, q_y)),
            out_shape=jax.ShapeDtypeStruct((left_dev, right_dev, pair), jnp.float32),
            in_specs=[pl.BlockSpec(memory_space=pl.ANY)] * 4,
            out_specs=pl.BlockSpec(memory_space=pl.ANY),
            scratch_shapes=[
                pltpu.VMEM(w_out.shape, w_out.dtype),
                pltpu.VMEM(counts.shape, counts.dtype),
                pltpu.VMEM((right_dev, left_dev, pair), jnp.float32),
                pltpu.VMEM((q_z, left_dev, right_dev // q_z, pair), jnp.float32),
                pltpu.VMEM((seqs, width_l), jnp.bfloat16),
                pltpu.VMEM((seqs, width_r), jnp.bfloat16),
                pltpu.VMEM((width_l, seqs), jnp.bfloat16),
                pltpu.VMEM((width_r // 128, width_l, 128), jnp.float32),
                pltpu.VMEM((width_r // q_z // CH * left_dev, CH * CH), jnp.bfloat16),
                pltpu.SemaphoreType.DMA((2, (n_z - 1) * q_z)),
                pltpu.SemaphoreType.DMA((2, (n_z - 1) * q_z)),
                pltpu.SemaphoreType.DMA((2, (n_y - 1) * q_y)),
                pltpu.SemaphoreType.DMA((2, (n_y - 1) * q_y)),
                pltpu.SemaphoreType.DMA(((2 * n_y - 1) * q_y,)),
                pltpu.SemaphoreType.DMA(((2 * n_y - 1) * q_y,)),
                pltpu.SemaphoreType.DMA((4,)),
                pltpu.SemaphoreType.DMA((q_z,)),
            ],
            compiler_params=pltpu.CompilerParams(
                collective_id=0, has_side_effects=True, vmem_limit_bytes=56 * 1024 * 1024
            ),
            name="pair_mean",
        )(left_act, right_act, counts, w_out)
        return projected

    in_specs = (
        P(("groups", "right"), "left"),
        P(("groups", "left"), "right"),
        P(("groups", "left"), "right"),
        P(),
    )
    out_specs = P(("groups", "left"), "right", None)
    return jax.shard_map(shards, mesh=mesh, in_specs=in_specs, out_specs=out_specs, check_vma=False)
```

```python
import functools

import jax
import jax.numpy as jnp
from jax import lax
from jax.experimental import pallas as pl
from jax.experimental.pallas import tpu as pltpu
from jax.sharding import PartitionSpec as P

CH = 32
CORES = 2
TILE = 256
MESH = pl.DeviceIdType.MESH


def lane_quads(tiles):
    lane = lax.broadcasted_iota(jnp.int32, tiles[0].shape, 1)
    low = lane < 64
    even = (lane % 64) < 32
    stage = [None] * 4
    for c in range(2):
        a, b = tiles[c], tiles[c + 2]
        stage[c] = jnp.where(low, a, pltpu.roll(b, 64, 1))
        stage[c + 2] = jnp.where(low, pltpu.roll(a, 64, 1), b)
    outs = [None] * 4
    for half in range(2):
        a, b = stage[2 * half], stage[2 * half + 1]
        outs[2 * half] = jnp.where(even, a, pltpu.roll(b, 32, 1))
        outs[2 * half + 1] = jnp.where(even, pltpu.roll(a, 96, 1), b)
    return outs


def kernel(sizes, left_ref, right_ref, counts_ref, w_hbm, out_ref, w_ref, counts_in, cover, out_v, left_full, right_full, left_t, acc, flat,
           z_send, z_recv, y_send, y_recv, s_send, s_recv, own_sem, out_sem):
    n_z, n_r, q_z, q_y = sizes
    n_y = n_r // CORES
    rows_l, width_l = left_ref.shape
    rows_r, width_r = right_ref.shape
    piece_r = width_r // q_z
    piece_l = rows_l // q_y
    left_dev = width_l // CH
    right_dev = width_r // CH
    seqs = left_t.shape[1]
    z = lax.axis_index("left")
    r = lax.axis_index("right")
    y = r // CORES
    k = r % CORES

    def z_dev(pos):
        return {"left": pos}

    def y_dev(pos):
        return {"right": pos * CORES + k}

    sib_dev = {"right": y * CORES + (1 - k)}

    barrier = pltpu.get_barrier_semaphore()

    def greet(dev):
        pl.semaphore_signal(barrier, inc=1, device_id=dev, device_id_type=MESH)

    greet(sib_dev)
    for pos, n, dev in ((z, n_z, z_dev), (y, n_y, y_dev)):
        pl.when(pos + 1 < n)(functools.partial(greet, dev(pos + 1)))
        pl.when(pos >= 1)(functools.partial(greet, dev(pos - 1)))
    total = 1 + (z + 1 < n_z).astype(jnp.int32) + (z >= 1).astype(jnp.int32)
    total = total + (y + 1 < n_y).astype(jnp.int32) + (y >= 1).astype(jnp.int32)
    pl.semaphore_wait(barrier, total)

    def z_slot(chunk, q):
        return right_full.at[pl.ds(pl.multiple_of(chunk * rows_r, rows_r), rows_r), pl.ds(q * piece_r, piece_r)]

    def z_copy(side, step, q):
        sign = 1 - 2 * side
        chunk = z - sign * step
        src = right_ref.at[:, pl.ds(q * piece_r, piece_r)] if step == 0 else z_slot(chunk, q)
        at = step * q_z + q
        return pltpu.make_async_remote_copy(
            src_ref=src, dst_ref=z_slot(chunk, q), send_sem=z_send.at[side, at], recv_sem=z_recv.at[side, at],
            device_id=z_dev(z + sign), device_id_type=MESH)

    def z_sends(side, step):
        near = z + 1 < n_z if side == 0 else z >= 1
        far = z - step >= 0 if side == 0 else z + step < n_z
        return jnp.logical_and(near, far)

    def z_arrives(side, step):
        return z - step - 1 >= 0 if side == 0 else z + step + 1 < n_z

    def z_wait(side, step, q):
        sign = 1 - 2 * side
        slot = z_slot(z - sign * (step + 1), q)
        pltpu.make_async_copy(slot, slot, z_recv.at[side, step * q_z + q]).wait()

    def l_slot(chunk, q):
        return left_full.at[pl.ds(pl.multiple_of(chunk * rows_l + q * piece_l, piece_l), piece_l), :]

    def l_own(q):
        return left_ref.at[pl.ds(q * piece_l, piece_l), :]

    def y_copy(side, step, q):
        sign = 1 - 2 * side
        chunk = (y - sign * step) * CORES + k
        at = step * q_y + q
        return pltpu.make_async_remote_copy(
            src_ref=l_own(q) if step == 0 else l_slot(chunk, q), dst_ref=l_slot(chunk, q),
            send_sem=y_send.at[side, at], recv_sem=y_recv.at[side, at],
            device_id=y_dev(y + sign), device_id_type=MESH)

    def y_sends(side, step):
        near = y + 1 < n_y if side == 0 else y >= 1
        far = y - step >= 0 if side == 0 else y + step < n_y
        return jnp.logical_and(near, far)

    def y_arrives(side, step):
        return y - step - 1 >= 0 if side == 0 else y + step + 1 < n_y

    def y_wait(side, step, q):
        sign = 1 - 2 * side
        slot = l_slot((y - sign * (step + 1)) * CORES + k, q)
        pltpu.make_async_copy(slot, slot, y_recv.at[side, step * q_y + q]).wait()

    def s_at(side, step, q):
        if step < 0:
            return q
        return (1 + side * (n_y - 1) + step) * q_y + q

    def s_copy(side, step, q):
        sign = 1 - 2 * side
        chunk = (y - sign * (step + 1)) * CORES + k if step >= 0 else r
        at = s_at(side, step, q)
        return pltpu.make_async_remote_copy(
            src_ref=l_own(q) if step < 0 else l_slot(chunk, q), dst_ref=l_slot(chunk, q),
            send_sem=s_send.at[at], recv_sem=s_recv.at[at],
            device_id=sib_dev, device_id_type=MESH)

    def s_wait(side, step, q):
        sign = 1 - 2 * side
        y_from = y - sign * (step + 1) if step >= 0 else y
        slot = l_slot(y_from * CORES + (1 - k), q)
        pltpu.make_async_copy(slot, slot, s_recv.at[s_at(side, step, q)]).wait()

    tile = 256

    def turn(src, first_row, chunk, q):
        col = pl.multiple_of(chunk * rows_l + q * piece_l, piece_l)

        def body(m, carry):
            at = pl.multiple_of(m * tile, tile)
            left_t[pl.ds(at, tile), pl.ds(col, piece_l)] = src[pl.ds(first_row, piece_l), pl.ds(at, tile)].T
            return carry

        lax.fori_loop(0, width_l // tile, body, 0)

    def turn_full(chunk, q):
        turn(left_full, pl.multiple_of(chunk * rows_l + q * piece_l, piece_l), chunk, q)

    for q in range(max(q_z, q_y)):
        for side in range(2):
            if q < q_z:
                pl.when(z_sends(side, 0))(lambda side=side, q=q: z_copy(side, 0, q).start())
            if q < q_y:
                pl.when(y_sends(side, 0))(lambda side=side, q=q: y_copy(side, 0, q).start())
    own_left = pltpu.make_async_copy(left_ref, left_full.at[pl.ds(pl.multiple_of(r * rows_l, rows_l), rows_l), :], own_sem.at[0])
    own = pltpu.make_async_copy(right_ref, right_full.at[pl.ds(pl.multiple_of(z * rows_r, rows_r), rows_r), :], own_sem.at[1])
    weights = pltpu.make_async_copy(w_hbm, w_ref, own_sem.at[2])
    counts_copy = pltpu.make_async_copy(counts_ref, counts_in, own_sem.at[3])
    for copy in (own_left, own, weights, counts_copy):
        copy.start()
    for q in range(q_y):
        s_copy(0, -1, q).start()
    own_left.wait()
    for q in range(q_y):
        turn_full(r, q)
    counts_copy.wait()
    counted = counts_in[...].astype(jnp.float32)
    for j in range(right_dev):
        cover[j] = jnp.broadcast_to(counted[:, j:j + 1], (left_dev, cover.shape[2]))
    for q in range(q_y):
        s_wait(0, -1, q)
        turn_full(y * CORES + (1 - k), q)

    def z_tick(step, q):
        for side in range(2):
            @pl.when(z_arrives(side, step))
            def _():
                z_wait(side, step, q)
                if step + 1 < n_z - 1:
                    pl.when(z_sends(side, step + 1))(lambda: z_copy(side, step + 1, q).start())

    def y_tick(step, q):
        for side in range(2):
            @pl.when(y_arrives(side, step))
            def _():
                y_wait(side, step, q)
                s_copy(side, step, q).start()
                if step + 1 < n_y - 1:
                    pl.when(y_sends(side, step + 1))(lambda: y_copy(side, step + 1, q).start())

        for side in range(2):
            @pl.when(y_arrives(side, step))
            def _():
                sign = 1 - 2 * side
                y_from = y - sign * (step + 1)
                turn_full(y_from * CORES + k, q)
                s_wait(side, step, q)
                turn_full(y_from * CORES + (1 - k), q)

    y_ticks = [(step, q) for step in range(n_y - 1) for q in range(q_y)]
    for t in range((n_z - 2) * q_z):
        z_tick(t // q_z, t % q_z)
        if t % 2 == 1 and y_ticks:
            y_tick(*y_ticks.pop(0))
    for tick in y_ticks:
        y_tick(*tick)
    own.wait()
    weights.wait()

    block = 1024
    at_end = jnp.logical_or(z == 0, z == n_z - 1)
    base = jnp.where(z == 0, 0, rows_r)
    base = pl.multiple_of(base, rows_r)

    def product(q, first, depth, add):
        cols = pl.ds(q * piece_r, piece_r)

        def body(m, carry):
            rows = pl.ds(pl.multiple_of(m * block, block), block)
            value = jnp.dot(left_t[rows, pl.ds(first, depth)], right_full[pl.ds(first, depth), cols],
                            preferred_element_type=jnp.float32)
            for part in range(piece_r // 128):
                some = value[:, part * 128:(part + 1) * 128]
                slab = q * (piece_r // 128) + part
                acc[slab, rows, :] = acc[slab, rows, :] + some if add else some
            return carry

        lax.fori_loop(0, width_l // block, body, 0)

    def first_part(q):
        @pl.when(at_end)
        def _():
            product(q, base, seqs - rows_r, False)

        @pl.when(jnp.logical_not(at_end))
        def _():
            product(q, 0, seqs, False)

    for q in range(q_z):
        first_part(q)

    def finish(q):
        heads = piece_r // CH
        for quad in range(heads // 4):
            slab = acc.at[q * (piece_r // 128) + quad]
            for cq in range(CH // 4):
                tiles = [slab[pl.ds(cq * 4 + c, left_dev, stride=CH), :].astype(jnp.bfloat16) for c in range(4)]
                for j, value in enumerate(lane_quads(tiles)):
                    flat[pl.ds((quad * 4 + j) * left_dev, left_dev), pl.ds(cq * 128, 128)] = value
        projected = jnp.dot(flat[...], w_ref[...], preferred_element_type=jnp.float32)
        for j in range(heads):
            value = projected[j * left_dev:(j + 1) * left_dev, :] / cover[q * heads + j]
            out_v.at[q].reshape(left_dev * heads, value.shape[1])[pl.ds(j, left_dev, stride=heads), :] = value
        out_copy(q).start()

    def out_copy(q):
        return pltpu.make_async_copy(out_v.at[q], out_ref.at[:, pl.ds(q * heads_q, heads_q), :], out_sem.at[q])

    heads_q = piece_r // CH
    last = n_z - 2
    for q in range(q_z):
        z_tick(last, q)

        @pl.when(at_end)
        def _():
            far = jnp.where(z == 0, (n_z - 1) * rows_r, 0)
            product(q, pl.multiple_of(far, rows_r), rows_r, True)

        finish(q)

    for side in range(2):
        for step in range(n_z - 1):
            for q in range(q_z):
                pl.when(z_sends(side, step))(lambda side=side, step=step, q=q: z_copy(side, step, q).wait_send())
        for step in range(n_y - 1):
            for q in range(q_y):
                pl.when(y_sends(side, step))(lambda side=side, step=step, q=q: y_copy(side, step, q).wait_send())
                pl.when(y_arrives(side, step))(lambda side=side, step=step, q=q: s_copy(side, step, q).wait_send())
    for q in range(q_y):
        s_copy(0, -1, q).wait_send()
    for q in range(q_z):
        out_copy(q).wait()


def folded(left_ref, right_ref, counts_ref, w_hbm, out_ref, w_in, w_wide, w_ref, counts_in, cover, order, left_full, left_far, right_full, right_t,
           acc, acc_far, flat, part, out_v, send, in_recv, far_recv, end_recv, own_recv, y_recv, s_recv, a_recv, own_sem):
    rows, width_l = left_ref.shape
    width_r = right_ref.shape[1]
    steps = width_r // TILE
    piece = rows // steps
    half = width_l // CORES
    quads = width_l // 128
    heads = TILE // CH
    pair = w_hbm.shape[1]
    lines = quads * heads
    early = steps // 2
    z = lax.axis_index("left")
    r = lax.axis_index("right")
    y, k = r // CORES, r % CORES
    up = z // 2
    sign = 2 * up - 1

    def fold(n, at):
        return up * at + (1 - up) * (n - 1 - at)

    zc, yc, kc = fold(4, z), fold(2, y), fold(2, k)
    inner, end = zc == 2, zc == 3
    sib_dev = {"right": r + 1 - 2 * k}
    y_dev = {"right": r + (1 - 2 * y) * CORES}

    def when(*terms):
        value = terms[0]
        for term in terms[1:]:
            value = jnp.logical_and(value, term)
        return pl.when(value)

    def z_dev(way):
        return {"left": z + way * sign}

    barrier = pltpu.get_barrier_semaphore()

    def greet(dev):
        pl.semaphore_signal(barrier, inc=1, device_id=dev, device_id_type=MESH)

    greet(sib_dev)
    greet(y_dev)
    greet(z_dev(-1))
    when(inner)(lambda: greet(z_dev(1)))
    pl.semaphore_wait(barrier, 3 + inner.astype(jnp.int32))

    def remote(src, dst, send, recv, dev):
        return pltpu.make_async_remote_copy(src_ref=src, dst_ref=dst, send_sem=send, recv_sem=recv, device_id=dev, device_id_type=MESH)

    def arrived(slot, sem):
        pltpu.make_async_copy(slot, slot, sem).wait()

    def block(at, first=0, size=rows):
        return pl.ds(pl.multiple_of(fold(4, at) * rows + first, size), size)

    def cols(q):
        return pl.ds(pl.multiple_of(q * TILE, TILE), TILE)

    def right_slot(at, q):
        return right_full.at[block(at), cols(q)]

    def in_copy(way, q):
        return remote(right_ref.at[:, cols(q)], right_slot(2, q), send.at[(way + 1) // 2], in_recv.at[0, q], z_dev(way))

    def fwd_copy(q):
        slot = right_slot(1, q)
        return remote(slot, slot, send.at[2], in_recv.at[1, q], z_dev(1))

    def cut(q):
        return ((1, 0), (1, 1), (2, 2), (4, 4))[q]

    def cut_slot(at, q, h, n):
        return right_full.at[block(at, h * (rows // n), rows // n), cols(q)]

    def mid_copy(q, h=0, n=1):
        slot = cut_slot(3, q, h, n)
        return remote(slot, slot, send.at[3], in_recv.at[1, q], z_dev(-1))

    def end_start(q):
        n, at = cut(q)
        for h in range(n):
            source = right_ref.at[pl.ds(h * (rows // n), rows // n), cols(q)]
            remote(source, cut_slot(3, q, h, n), send.at[3], end_recv.at[at + h], z_dev(-1)).start()

    def own_half():
        return pl.ds(pl.multiple_of(k * half, half), half)

    def far_copy(p):
        at = pl.ds(pl.multiple_of(p * piece, piece), piece)
        return remote(left_full.at[block(0, p * piece, piece), own_half()], left_far.at[at, own_half()], send.at[2], far_recv.at[p], z_dev(-1))

    def far_slot(p, core):
        return left_far.at[pl.ds(pl.multiple_of(p * piece, piece), piece), pl.ds(pl.multiple_of(core * half, half), half)]

    def share_copy(p):
        return remote(far_slot(p, k), far_slot(p, k), send.at[4], a_recv.at[0], sib_dev)

    def own_copy(p):
        at = pl.ds(pl.multiple_of(p * piece, piece), piece)
        slot = left_full.at[pl.ds(pl.multiple_of(r * rows + p * piece, piece), piece), :]
        return remote(left_ref.at[at, :], slot, send.at[5], own_recv.at[p], sib_dev)

    def own_arrived(p):
        other = r + 1 - 2 * k
        arrived(left_full.at[pl.ds(pl.multiple_of(other * rows + p * piece, piece), piece), :], own_recv.at[p])

    def y_slot(side, pos, p, core, count=1):
        at = 3 * side if pos == 0 else 1 + side
        return left_full.at[block(at, p * piece, count * piece), pl.ds(pl.multiple_of(core * half, half), half)]

    def y_copy(pos, p, own=False):
        slot = y_slot(yc, pos, p, k)
        source = left_ref.at[pl.ds(pl.multiple_of(p * piece, piece), piece), own_half()] if own else slot
        return remote(source, slot, send.at[6], y_recv.at[pos, p], y_dev)

    def s_copy(pos, p, group):
        slot = y_slot(1 - yc, pos, p, k)
        return remote(slot, slot, send.at[7], s_recv.at[group], sib_dev)

    def part_copy(q):
        return remote(part.at[q], part.at[q], send.at[8], far_recv.at[q], z_dev(1))

    def each(body, first=0, last=steps):
        def step(at, carry):
            body(at)
            return carry

        lax.fori_loop(first, last, step, 0)

    @when(inner)
    def _():
        @each
        def _(q):
            in_copy(1, q).start()
            in_copy(-1, q).start()

    @when(end)
    def _():
        end_start(0)
        end_start(1)

    first = kc == yc
    when(first)(lambda: each(lambda p: y_copy(0, p, True).start()))
    own_left = pltpu.make_async_copy(left_ref, left_full.at[pl.ds(pl.multiple_of(r * rows, rows), rows), :], own_sem.at[0])
    own = pltpu.make_async_copy(right_ref, right_full.at[block(zc), :], own_sem.at[1])
    weights = pltpu.make_async_copy(w_hbm, w_in, own_sem.at[2])
    counts_copy = pltpu.make_async_copy(counts_ref, counts_in, own_sem.at[3])
    each(lambda p: own_copy(p).start())
    for copy in (own_left, own, weights, counts_copy):
        copy.start()

    @each
    def _(p):
        own_arrived(p)
        when(jnp.logical_not(first))(lambda: y_copy(0, p).start())
        when(end, yc == 0, kc == 1)(lambda: far_copy(p).start())
        when(end, yc == 0, kc == 1, p == steps - 2)(lambda: end_start(2))

    own_left.wait()

    @when(end, yc == 0, kc == 0)
    def _():
        each(lambda p: far_copy(p).start(), 0, steps - 1)
        end_start(2)
        far_copy(steps - 1).start()

    each(lambda p: y_copy(1, p).start())
    when(end, yc == 0)(lambda: end_start(3))

    row = lax.broadcasted_iota(jnp.int32, (TILE, TILE), 0)
    column = lax.broadcasted_iota(jnp.int32, (TILE, TILE), 1)
    order[...] = jnp.where(column == (row % heads) * CH + row // heads, 1.0, 0.0).astype(order.dtype)
    weights.wait()
    w_wide[...] = w_in[...].astype(jnp.float32)
    for e in range(CH):
        some = w_wide[pl.ds(e, CH, stride=CH), :].astype(w_ref.dtype)
        for i in range(2):
            w_ref[pl.ds((2 * e + i) * CH, CH), i * pair:(i + 1) * pair] = some
            w_ref[pl.ds((2 * e + i) * CH, CH), (1 - i) * pair:(2 - i) * pair] = jnp.zeros_like(some)
    counts_copy.wait()
    counted = counts_in[...].astype(jnp.float32)
    for i in range(counted.shape[1]):
        cover[i // 4, i % 4] = jnp.broadcast_to(counted[:, i:i + 1], (counted.shape[0], cover.shape[3]))

    def turn(at, q):
        value = lax.dot_general(order[...], right_full[block(at), cols(q)], (((1,), (1,)), ((), ())), preferred_element_type=jnp.float32)
        right_t[cols(q), block(at)] = value.astype(right_t.dtype)

    def product(into, lines, source, left, left_rows, size, wide, add):
        for n in range(width_l // wide):
            value = jnp.dot(right_t[lines, source], left[left_rows, pl.ds(n * wide, wide)], preferred_element_type=jnp.float32)
            for one in range(wide // 128):
                some = value[:, one * 128:(one + 1) * 128]
                slab = n * (wide // 128) + one
                into[slab, size, :] = into[slab, size, :] + some if add else some

    def product_all(at, add, first=0, depth=rows):
        every = pl.ds(0, width_r)
        product(acc, every, block(at, first, depth), left_full, block(at, first, depth), every, 256, add)

    def product_one(at, q):
        product(acc, cols(q), block(at), left_full, block(at), cols(q), 512, True)

    def project(source, first_row):
        low = lax.broadcasted_iota(jnp.int32, (lines, 128), 1) < 64
        for two in range(CH // 2):
            a, b = (
                source[:, pl.ds(pl.multiple_of(first_row + e * heads, heads), heads), :].reshape(lines, 128).astype(flat.dtype)
                for e in (2 * two, 2 * two + 1)
            )
            at = pl.ds(two * 128, 128)
            flat[pl.ds(0, lines), at] = jnp.where(low, a, pltpu.roll(b, 64, 1))
            flat[pl.ds(lines, lines), at] = jnp.where(low, pltpu.roll(a, 64, 1), b)
        return jnp.dot(flat[...], w_ref[...], preferred_element_type=jnp.float32)

    def spot(i):
        return slice(i // 2 * lines, (i // 2 + 1) * lines), slice(i % 2 * pair, (i % 2 + 1) * pair)

    def emit(q, i, value):
        at = pl.ds(pl.multiple_of(q * heads, heads), heads)
        out_ref[pl.ds(i, quads, stride=4), at, :] = value / cover[:, i, at, :]

    def settle(q):
        for i in range(4):
            value = out_v[q, :, i]
            emit(q, i, value + part[(q, *spot(i))].astype(jnp.float32).reshape(value.shape))

    own.wait()
    each(lambda q: turn(zc, q))

    def pass_on(q, h):
        n, at = cut(q)
        arrived(cut_slot(3, q, h, n), end_recv.at[at + h])
        mid_copy(q, h, n).start()

    def end_arrived(q):
        arrived(right_slot(3, q), end_recv.at[q])
        mid_copy(q).start()
        turn(3, q)

    def share(p):
        arrived(far_slot(p, k), far_recv.at[p])
        share_copy(p).start()

    @each
    def _(p):
        arrived(y_slot(1 - yc, 0, p, k), y_recv.at[0, p])
        s_copy(0, p, 0).start()
        when(end, yc == 1)(lambda: far_copy(p).start())
        when(end, yc == 1, p == steps - 2)(lambda: end_start(2))
        arrived(right_slot(zc - 1, p), in_recv.at[0, p])
        when(inner)(lambda: fwd_copy(p).start())
        turn(zc - 1, p)
        when(inner, p >= 1, p <= early)(lambda: end_arrived(p - 1))

    when(end, yc == 1)(lambda: end_start(3))
    arrived(y_slot(1 - yc, 0, 0, 1 - k, steps), s_recv.at[0])
    late = 2 - yc
    groups = ((0, early), (early, early + 1), (early + 1, steps))

    def y_arrived(p):
        group = next(at for at, (_, last) in enumerate(groups) if p < last)
        arrived(y_slot(1 - yc, 1, p, k), y_recv.at[1, p])
        s_copy(1, p, 1 + group).start()

    def late_part(group):
        low, high = groups[group]
        arrived(y_slot(1 - yc, 1, low, 1 - k, high - low), s_recv.at[1 + group])
        product_all(late, True, low * piece, (high - low) * piece)

    def far_turn(q):
        arrived(right_slot(0, q), in_recv.at[1, q])
        turn(0, q)

    def far_product(q):
        product(acc_far, cols(q), block(0), left_far, pl.ds(0, rows), pl.ds(0, TILE), 512, False)

    def far_send_on(q):
        part[q] = project(acc_far, 0).astype(part.dtype)
        part_copy(q).start()

    def finish(q):
        value = project(acc, q * TILE)
        for i in range(4):
            out_v[q, :, i] = value[spot(i)].reshape(quads, heads, pair)

    def sent(sem, count=1):
        slot = left_full.at[pl.ds(0, count * rows), pl.ds(0, half)]
        arrived(slot, send.at[sem])

    @when(inner)
    def _():
        each(share, 0, early)
        product_all(1 + yc, False)
        for q in range(early):
            product_one(3, q)
        y_arrived(0)
        share(2)
        far_turn(0)
        product_one(0, 0)
        pass_on(2, 0)
        pass_on(2, 1)
        turn(3, 2)
        product_one(3, 2)
        y_arrived(1)
        far_turn(1)
        product_one(0, 1)
        late_part(0)
        share(3)
        pass_on(3, 0)
        arrived(left_far.at[:, pl.ds(pl.multiple_of((1 - k) * half, half), half)], a_recv.at[0])
        far_product(0)
        y_arrived(2)
        pass_on(3, 1)
        far_send_on(0)
        far_product(1)
        pass_on(3, 2)
        pass_on(3, 3)
        far_send_on(1)
        far_turn(2)
        far_product(2)
        far_send_on(2)
        late_part(1)
        y_arrived(3)
        turn(3, 3)
        product_one(3, 3)
        far_turn(3)
        far_product(3)
        far_send_on(3)
        product_one(0, 2)
        late_part(2)
        product_one(0, 3)

        @each
        def _(q):
            value = project(acc, q * TILE)
            for i in range(4):
                emit(q, i, value[spot(i)].reshape(quads, heads, pair))

        sent(0)
        sent(1)
        sent(2)
        sent(3)
        sent(4)
        sent(5, 2)
        sent(6, 2)
        sent(7, 2)
        arrived(part, send.at[8])

    @when(end)
    def _():
        product_all(3, False)
        for q in range(steps):
            y_arrived(q)
            arrived(right_slot(1, q), in_recv.at[1, q])
            turn(1, q)
            product_one(1 + yc, q)
        for group in range(len(groups)):
            late_part(group)
        each(finish)
        sent(2)
        sent(3)
        sent(5, 2)
        sent(6, 2)
        sent(7, 2)

        @each
        def _(q):
            arrived(part.at[q], far_recv.at[q])
            settle(q)


def folded_call(left_act, right_act, counts, w_out):
    rows, width_l = left_act.shape
    width_r = right_act.shape[1]
    left_dev, right_dev = counts.shape
    pair = w_out.shape[1]
    steps = width_r // TILE
    heads = TILE // CH
    full = 4 * rows
    dma = pltpu.SemaphoreType.DMA
    return pl.pallas_call(
        folded,
        out_shape=jax.ShapeDtypeStruct((left_dev, right_dev, pair), jnp.float32),
        in_specs=[pl.BlockSpec(memory_space=pl.ANY)] * 4,
        out_specs=pl.BlockSpec(memory_space=pltpu.VMEM),
        scratch_shapes=[
            pltpu.VMEM(w_out.shape, w_out.dtype),
            pltpu.VMEM(w_out.shape, jnp.float32),
            pltpu.VMEM((2 * w_out.shape[0], 2 * pair), w_out.dtype),
            pltpu.VMEM((right_dev, left_dev), counts.dtype),
            pltpu.VMEM((left_dev // 4, 4, right_dev, pair), jnp.float32),
            pltpu.VMEM((TILE, TILE), jnp.bfloat16),
            pltpu.VMEM((full, width_l), jnp.bfloat16),
            pltpu.VMEM((rows, width_l), jnp.bfloat16),
            pltpu.VMEM((full, width_r), jnp.bfloat16),
            pltpu.VMEM((width_r, full), jnp.bfloat16),
            pltpu.VMEM((width_l // 128, width_r, 128), jnp.float32),
            pltpu.VMEM((width_l // 128, TILE, 128), jnp.float32),
            pltpu.VMEM((left_dev * heads // 2, 2 * CH * CH), jnp.bfloat16),
            pltpu.VMEM((steps, left_dev * heads // 2, 2 * pair), jnp.bfloat16),
            pltpu.VMEM((steps, left_dev // 4, 4, heads, pair), jnp.float32),
            dma((9,)), dma((2, steps)), dma((steps,)), dma((8,)), dma((steps,)), dma((2, steps)), dma((4,)), dma((1,)), dma((4,)),
        ],
        compiler_params=pltpu.CompilerParams(collective_id=0, has_side_effects=True, vmem_limit_bytes=38000 * 1024),
        name="pair_mean",
    )(*(pltpu.with_memory_space_constraint(x, pltpu.HBM) for x in (left_act, right_act, counts.T, w_out)))


def solution(mesh):
    n_z, n_r = mesh.shape["left"], mesh.shape["right"]
    n_y = n_r // CORES

    def shards(left_act, right_act, counts, w_out):
        width_l, width_r = left_act.shape[1], right_act.shape[1]
        if (n_z, n_y) == (4, 2) and width_r == 4 * TILE and width_l == CORES * width_r:
            return folded_call(left_act, right_act, counts, w_out)
        rows_l, width_l = left_act.shape
        rows_r, width_r = right_act.shape
        seqs = rows_r * n_z
        left_dev, right_dev = counts.shape
        pair = w_out.shape[1]
        q_z = width_r // 256
        q_y = rows_l // max(128, rows_l // 4)
        projected = pl.pallas_call(
            functools.partial(kernel, (n_z, n_r, q_z, q_y)),
            out_shape=jax.ShapeDtypeStruct((left_dev, right_dev, pair), jnp.float32),
            in_specs=[pl.BlockSpec(memory_space=pl.ANY)] * 4,
            out_specs=pl.BlockSpec(memory_space=pl.ANY),
            scratch_shapes=[
                pltpu.VMEM(w_out.shape, w_out.dtype),
                pltpu.VMEM(counts.shape, counts.dtype),
                pltpu.VMEM((right_dev, left_dev, pair), jnp.float32),
                pltpu.VMEM((q_z, left_dev, right_dev // q_z, pair), jnp.float32),
                pltpu.VMEM((seqs, width_l), jnp.bfloat16),
                pltpu.VMEM((seqs, width_r), jnp.bfloat16),
                pltpu.VMEM((width_l, seqs), jnp.bfloat16),
                pltpu.VMEM((width_r // 128, width_l, 128), jnp.float32),
                pltpu.VMEM((width_r // q_z // CH * left_dev, CH * CH), jnp.bfloat16),
                pltpu.SemaphoreType.DMA((2, (n_z - 1) * q_z)),
                pltpu.SemaphoreType.DMA((2, (n_z - 1) * q_z)),
                pltpu.SemaphoreType.DMA((2, (n_y - 1) * q_y)),
                pltpu.SemaphoreType.DMA((2, (n_y - 1) * q_y)),
                pltpu.SemaphoreType.DMA(((2 * n_y - 1) * q_y,)),
                pltpu.SemaphoreType.DMA(((2 * n_y - 1) * q_y,)),
                pltpu.SemaphoreType.DMA((4,)),
                pltpu.SemaphoreType.DMA((q_z,)),
            ],
            compiler_params=pltpu.CompilerParams(
                collective_id=0, has_side_effects=True, vmem_limit_bytes=56 * 1024 * 1024
            ),
            name="pair_mean",
        )(left_act, right_act, counts, w_out)
        return projected

    in_specs = (
        P(("groups", "right"), "left"),
        P(("groups", "left"), "right"),
        P(("groups", "left"), "right"),
        P(),
    )
    out_specs = P(("groups", "left"), "right", None)
    return jax.shard_map(shards, mesh=mesh, in_specs=in_specs, out_specs=out_specs, check_vma=False)
```
